32 devices in a mesh: dp: 8 (over y, x, core), seq: 4 (over z).
Axes of the slice: x: 2, y: 2, z: 4, core: 2. Of those that a mesh axis runs over, the one named last changes fastest.
Arguments:
- tokens: bfloat16 [8, 512, 1024], P('dp', 'seq'), may hold values from -6 to 6
- prefix_len: int32 [8], P('dp'), may hold values from 51 to 256
- routes: int32 [8, 512, 8], P('dp', 'seq'), may hold values from 0 to 15, all different within a row; in each aligned block of 128 rows (0 to 127, 128 to 255, ..., all dimensions but the last counted through in order) at most 96 rows name the same one
- cotangent: bfloat16 [8, 512, 1024], P('dp', 'seq'), may hold values from -6 to 6
- query_matrix: bfloat16 [1024, 1024], P(('dp', 'seq')), may hold values from -0.1875 to 0.1875
- key_matrix: bfloat16 [1024, 512], P(('dp', 'seq')), may hold values from -0.1875 to 0.1875
- value_matrix: bfloat16 [1024, 512], P(('dp', 'seq')), may hold values from -0.1875 to 0.1875
- output_matrix: bfloat16 [1024, 1024], P(('dp', 'seq')), may hold values from -2 to 2
- attention_gain: bfloat16 [1024], P(('dp', 'seq')), may hold values from 0.5 to 1.5
- expert_gain: bfloat16 [1024], P(('dp', 'seq')), may hold values from 0.5 to 1.5
- router_matrix: bfloat16 [1024, 16], P(('dp', 'seq')), may hold values from -0.09375 to 0.09375
- gate_up_weight: bfloat16 [1024, 16, 1024], P(('dp', 'seq')), may hold values from -0.1875 to 0.1875
- down_weight: bfloat16 [1024, 16, 512], P(('dp', 'seq')), may hold values from -2 to 2
Outputs:
- mixed: bfloat16 [8, 512, 1024], P('dp', 'seq')
- tokens_grad: float32 [8, 512, 1024], P('dp', 'seq')
- query_weight_grad: float32 [1024, 1024], P(('dp', 'seq'))
- key_weight_grad: float32 [1024, 512], P(('dp', 'seq'))
- value_weight_grad: float32 [1024, 512], P(('dp', 'seq'))
- output_weight_grad: float32 [1024, 1024], P(('dp', 'seq'))
- attention_gain_grad: float32 [1024], P(('dp', 'seq'))
- expert_gain_grad: float32 [1024], P(('dp', 'seq'))
- router_weight_grad: float32 [1024, 16], P(('dp', 'seq'))
- gate_up_weight_grad: float32 [1024, 16, 1024], P(('dp', 'seq'))
- down_weight_grad: float32 [1024, 16, 512], P(('dp', 'seq'))
The draws below stay inside these ranges and needn't reach their ends.
Inputs may be any that keep to these rules, and one draw needn't show every extreme that they name: `routes`: each token names 8 different experts. Among the 128 rows of one device no expert is named by more than 96 tokens, and in some device one expert is named by exactly 96.
All inputs are finite; a program needn't handle non-finite values.
Results may differ from the reference program's by a relative error of at most 0.02.
Values may be sent and summed in bfloat16 or wider, within the bound.
A program may use at most 384 MiB of HBM per device.

```python
import math
import jax
import jax.numpy as jnp
import numpy as np
from jax import lax

D = 1024
QUERY_HEAD_COUNT = 16
KEY_VALUE_HEADS = 8
HEAD_WIDTH = 64
FF = 512
TOP = 8
EXPERTS = 16
TOK_DEV = 128
SEQ_LEN = 512
SEQS = 8
CAPACITY = 96


def touch_ends(values, own_key, low, largest):
    longest = values.shape.index(max(values.shape))
    spots = []
    for shift in (0, 1):
        where = [jax.random.randint(jax.random.fold_in(own_key, axis), (), 0, length) for axis, length in enumerate(values.shape)]
        where[longest] = (where[longest] + shift) % values.shape[longest]
        spots.append(tuple(where))
    return values.at[spots[0]].set(low).at[spots[1]].set(largest)


def level_of(rng, dims, split, smallest, largest):
    loudness = 1.0
    for position, shards_of in split:
        draws = jax.random.uniform(jax.random.fold_in(jax.random.fold_in(rng, 6), position), (shards_of,), jnp.float32, smallest / len(split), largest / len(split))
        loudness = loudness * jnp.repeat(jnp.exp(draws), dims[position] // shards_of).reshape((-1,) + (1,) * (len(dims) - 1 - position))
    return loudness


def shared_out(own_key, own, number, rows, count, top, bound, lean):
    sequence = jax.random.permutation(own_key, count)
    heavy_load, ordinary = load_shares(count, rows * top, bound, lean, True), load_shares(count, rows * top, bound, lean, False)
    places = jnp.arange(count)

    def named(sizes, turn):
        used = int((sizes > 0).sum())
        fixed = max(1, used // 4)
        passed = fixed + (places - fixed + turn * (used - fixed)) % max(1, count - fixed)
        return jnp.zeros((count,), jnp.int32).at[sequence[jnp.where(places < fixed, places, passed)]].set(jnp.asarray(sizes, jnp.int32))

    sizes = jnp.where(number % 4 == 0, named(heavy_load, number // 4), named(ordinary, number - number // 4 - 1))
    mixed = jax.random.permutation(jax.random.fold_in(own, 3), count)
    giver, taker = mixed[0:count // 2 * 2:2], mixed[1:count // 2 * 2:2]
    slack = jnp.minimum(sizes[giver] - 1, bound - sizes[taker]) // 2
    slack = jnp.where((giver == sequence[0]) | (taker == sequence[0]) | (sizes[taker] == 0), 0, jnp.maximum(slack, 0))
    passed = jax.random.randint(jax.random.fold_in(own, 4), (count // 2,), 0, 1 << 20) % (slack + 1)
    sizes = sizes.at[giver].add(-passed).at[taker].add(passed)
    labels = jnp.searchsorted(jnp.cumsum(sizes), jnp.arange(rows * top), side="right").astype(jnp.int32)
    listing = labels.reshape(top, rows).T
    listing = listing[jax.random.permutation(jax.random.fold_in(own, 1), rows)]
    turn = jax.random.randint(jax.random.fold_in(own, 2), (rows, 1), 0, top)
    return jnp.take_along_axis(listing, (jnp.arange(top)[None, :] + turn) % top, axis=1)


def load_shares(number_of, total, reach, lean, full):
    weights = [(1 << 20) // math.isqrt(rank ** lean) + 1 for rank in range(1, number_of + 1)]
    largest = reach if full else min(reach, max(-(-total // number_of), total * weights[0] // sum(weights)))
    least = 1 if total - largest >= number_of - 1 else 0
    holding, surplus = [largest] + [least] * (number_of - 1), total - largest - least * (number_of - 1)
    while surplus > 0:
        candidates = [i for i in range(1, number_of) if holding[i] < largest] or [i for i in range(1, number_of) if holding[i] < reach]
        whole, budget = sum([weights[i] for i in candidates]), surplus
        for i in candidates:
            addition = min(reach - holding[i], max(1, budget * weights[i] // whole), surplus)
            holding[i] = holding[i] + addition
            surplus = surplus - addition
    return np.array(holding)


def gaussian(own_key, extent, scale, limit, shards=(), kind=jnp.bfloat16):
    factor_of = level_of(own_key, extent, shards, -0.22, 0.18) if shards else 1.0
    values = jax.random.normal(own_key, extent, jnp.float32) * scale * factor_of
    return jnp.minimum(jnp.maximum(values, -limit), limit).astype(kind)


def setup_inputs(seed: int = 0) -> dict:
    splits = jax.random.split(jax.random.key(seed), 14)
    tokens = gaussian(splits[0], (SEQS, SEQ_LEN, D), 1.0, 6.0, ((0, 8), (1, 4)))
    prefix_len = touch_ends(jax.random.randint(splits[1], (SEQS,), SEQ_LEN // 10, SEQ_LEN // 2 + 1), jax.random.fold_in(splits[1], 1), SEQ_LEN // 10, (SEQ_LEN // 2 + 1) - 1).astype(jnp.int32)
    routes_keys = jax.random.split(jax.random.fold_in(splits[2], 1), SEQS * SEQ_LEN // TOK_DEV)
    routes_turns = jax.random.permutation(jax.random.fold_in(splits[2], 3), SEQS * SEQ_LEN // TOK_DEV)
    routes = jax.vmap(lambda own, number: shared_out(jax.random.fold_in(splits[2], 2), own, number, TOK_DEV, EXPERTS, TOP, CAPACITY, 1))(routes_keys, routes_turns).reshape((SEQS, SEQ_LEN, TOP))
    cotangent = gaussian(splits[3], (SEQS, SEQ_LEN, D), 1.0, 6.0, ((0, 8), (1, 4)))
    query_matrix = gaussian(splits[4], (D, QUERY_HEAD_COUNT * HEAD_WIDTH), D ** -0.5, 0.1875, ((0, 32),))
    key_matrix = gaussian(splits[5], (D, KEY_VALUE_HEADS * HEAD_WIDTH), D ** -0.5, 0.1875, ((0, 32),))
    value_matrix = gaussian(splits[6], (D, KEY_VALUE_HEADS * HEAD_WIDTH), D ** -0.5, 0.1875, ((0, 32),))
    output_matrix = gaussian(splits[7], (D, QUERY_HEAD_COUNT * HEAD_WIDTH), ((SEQ_LEN // 4) ** 0.5 * (QUERY_HEAD_COUNT * HEAD_WIDTH) ** -0.5), 2.0, ((0, 32),))
    attention_gain = jnp.clip(1.0 + 0.1 * jax.random.normal(splits[8], (D,), jnp.float32), 0.5, 1.5).astype(jnp.bfloat16)
    expert_gain = jnp.clip(1.0 + 0.1 * jax.random.normal(splits[9], (D,), jnp.float32), 0.5, 1.5).astype(jnp.bfloat16)
    router_matrix = gaussian(splits[10], (D, EXPERTS), (0.5 * D ** -0.5), 0.09375, ((0, 32),))
    gate_up_weight = gaussian(splits[11], (D, EXPERTS, 2 * FF), D ** -0.5, 0.1875, ((0, 32),))
    down_weight = gaussian(splits[12], (D, EXPERTS, FF), (8 * FF ** -0.5), 2.0, ((0, 32),))
    return dict(tokens=tokens, prefix_len=prefix_len, routes=routes, cotangent=cotangent, query_matrix=query_matrix, key_matrix=key_matrix, value_matrix=value_matrix, output_matrix=output_matrix, attention_gain=attention_gain, expert_gain=expert_gain, router_matrix=router_matrix, gate_up_weight=gate_up_weight, down_weight=down_weight)


NORM_EPS = 1e-06
HIGHEST_PRECISION = lax.Precision.HIGHEST
LOW_SCORE = -1e+30

@jax.custom_vjp
def lowered_value(v):
    return lax.optimization_barrier(v.astype(jnp.bfloat16)).astype(jnp.float32)

@jax.custom_vjp
def lowered_backward(v):
    return v

def low_keep(v):
    return (lowered_value(v), None)

def low_pass(kept, grad):
    return (grad,)

def back_keep(v):
    return (v, None)

def back_low(kept, grad):
    return (lowered_value(grad),)
lowered_value.defvjp(low_keep, low_pass)
lowered_backward.defvjp(back_keep, back_low)

def matrix_product(formula, left, right):
    return jnp.einsum(formula, left, right, precision=HIGHEST_PRECISION)

def rotary_tables(positions, head_dim):
    half_dim = head_dim // 2
    frequency = jnp.exp(jnp.arange(half_dim, dtype=jnp.float32) * (-2.0 * math.log(10000.0) / head_dim))
    angles = positions.astype(jnp.float32)[:, None] * frequency[None, :]
    return (jnp.cos(angles), jnp.sin(angles))

def rotate(value_rows, cosine, sine_table):
    half_dim = value_rows.shape[-1] // 2
    first_half = value_rows[..., :half_dim]
    second = value_rows[..., half_dim:]
    cos_heads = cosine[:, None, :]
    sin_heads = sine_table[:, None, :]
    return jnp.concatenate([first_half * cos_heads - second * sin_heads, second * cos_heads + first_half * sin_heads], axis=-1)

def attend_sequence(queries, keys, value_rows, prefix_end):
    length_total = queries.shape[0]
    head_group = queries.shape[2]
    block_size = math.gcd(length_total, 512)
    key_places = jnp.arange(length_total, dtype=jnp.int32)
    score_scale = HEAD_WIDTH ** (-0.5)

    def one_block(block_item):
        query_block, block_start = block_item
        scores = lowered_backward(matrix_product('bhgd,khd->hgbk', query_block, keys) * score_scale)
        query_places = block_start + jnp.arange(block_size, dtype=jnp.int32)
        allowed = (key_places[None, :] <= query_places[:, None]) | (key_places[None, :] < prefix_end)
        scores = jnp.where(allowed, scores, LOW_SCORE)
        weights = jax.nn.softmax(scores, axis=-1)
        return matrix_product('hgbk,khd->bhgd', lowered_value(weights), value_rows)
    blocks = queries.reshape(length_total // block_size, block_size, KEY_VALUE_HEADS, head_group, HEAD_WIDTH)
    starts = (jnp.arange(length_total // block_size) * block_size).astype(jnp.int32)
    outputs = lax.map(jax.checkpoint(one_block), (blocks, starts))
    return outputs.reshape(length_total, KEY_VALUE_HEADS, head_group, HEAD_WIDTH)

def decoder_layer(hidden, query_matrix, key_matrix, value_matrix, output_matrix, attention_gain, expert_gain, router_matrix, gate_up_weight, down_weight, prefix_len, chosen):
    sequence_count, length_total, model_width = hidden.shape
    head_group = QUERY_HEAD_COUNT // KEY_VALUE_HEADS
    inverse_attention = lax.rsqrt(lax.optimization_barrier(jnp.mean(hidden * hidden, -1, keepdims=True)) + NORM_EPS)
    attention_input = lowered_value(hidden * inverse_attention * attention_gain)
    positions = jnp.arange(length_total, dtype=jnp.int32)
    cosine, sine_table = rotary_tables(positions, HEAD_WIDTH)
    query_projected = lowered_backward(matrix_product('hqb,bi->hqi', attention_input, query_matrix)).reshape(sequence_count, length_total, QUERY_HEAD_COUNT, HEAD_WIDTH)
    queries = lowered_value(rotate(query_projected, cosine, sine_table)).reshape(sequence_count, length_total, KEY_VALUE_HEADS, head_group, HEAD_WIDTH)
    key_projected = lowered_backward(matrix_product('hqb,bi->hqi', attention_input, key_matrix)).reshape(sequence_count, length_total, KEY_VALUE_HEADS, HEAD_WIDTH)
    keys = lowered_value(rotate(key_projected, cosine, sine_table))
    value_rows = lowered_value(lowered_backward(matrix_product('hqb,bi->hqi', attention_input, value_matrix))).reshape(sequence_count, length_total, KEY_VALUE_HEADS, HEAD_WIDTH)

    def one_sequence(sequence_item):
        return attend_sequence(sequence_item[0], sequence_item[1], sequence_item[2], sequence_item[3])
    attended = lax.map(one_sequence, (queries, keys, value_rows, prefix_len))
    attention_lowered = lowered_value(lowered_backward(attended.reshape(sequence_count, length_total, QUERY_HEAD_COUNT * HEAD_WIDTH)))
    branch_output = lowered_backward(matrix_product('aqf,xf->aqx', attention_lowered, output_matrix))
    middle = hidden + branch_output
    inverse_expert = lax.rsqrt(lax.optimization_barrier(jnp.mean(middle * middle, -1, keepdims=True)) + NORM_EPS)
    expert_input = lowered_value(middle * inverse_expert * expert_gain)
    router_logits = lowered_backward(matrix_product('wtx,xc->wtc', expert_input, router_matrix))
    router_probs = jax.nn.softmax(router_logits, axis=-1)
    gates = router_probs * chosen
    flat_in = expert_input.reshape(-1, model_width)
    flat_gates = gates.reshape(-1, EXPERTS)
    block_size = math.gcd(flat_in.shape[0], 2048)
    ff_width = down_weight.shape[2]

    def expert_mix(block_item):
        block_in, block_gates = block_item
        mid_linear = lowered_backward(matrix_product('bd,def->bef', block_in, gate_up_weight))
        activation = lowered_value(jax.nn.silu(mid_linear[..., :ff_width]) * mid_linear[..., ff_width:])
        expert_out = lowered_backward(matrix_product('bef,def->bed', activation, down_weight))
        return matrix_product('be,bed->bd', block_gates, expert_out)
    mixed_experts = lax.map(jax.checkpoint(expert_mix), (flat_in.reshape(-1, block_size, model_width), flat_gates.reshape(-1, block_size, EXPERTS)))
    return middle + mixed_experts.reshape(sequence_count, length_total, model_width)

def reference(tokens, prefix_len, routes, cotangent, query_matrix, key_matrix, value_matrix, output_matrix, attention_gain, expert_gain, router_matrix, gate_up_weight, down_weight):
    chosen = lax.optimization_barrier(jnp.sum((routes[..., None] == jnp.arange(EXPERTS, dtype=jnp.int32)).astype(jnp.float32), -2))

    def forward(hidden, query_f, key_f, value_f, output_f, attention_f, expert_f, router_f, gate_up_f, down_f):
        return decoder_layer(hidden, query_f, key_f, value_f, output_f, attention_f, expert_f, router_f, gate_up_f, down_f, prefix_len, chosen)
    primal = (tokens.astype(jnp.float32), query_matrix.astype(jnp.float32), key_matrix.astype(jnp.float32), value_matrix.astype(jnp.float32), output_matrix.astype(jnp.float32), attention_gain.astype(jnp.float32), expert_gain.astype(jnp.float32), router_matrix.astype(jnp.float32), gate_up_weight.astype(jnp.float32), down_weight.astype(jnp.float32))
    result, pullback = jax.vjp(forward, *primal)
    gradients = pullback(cotangent.astype(jnp.float32))
    return (result.astype(jnp.bfloat16), gradients[0], gradients[1], gradients[2], gradients[3], gradients[4], gradients[5], gradients[6], gradients[7], gradients[8], gradients[9])
```

```python
import math

import jax
import jax.numpy as jnp
import numpy as np
from jax import lax
from jax.experimental import pallas as pl
from jax.experimental.pallas import tpu as pltpu
from jax.sharding import PartitionSpec as P

HEAD_WIDTH = 64
CAPACITY = 96


NORM_EPS = 1e-06
LOW_SCORE = -1e30
LANES = 128
HALF = HEAD_WIDTH // 2
SCORE_SCALE = HEAD_WIDTH ** (-0.5)
EXPERT_COUNT = 16
KEY_HEADS = 8
MESH = pl.DeviceIdType.MESH


def rotary_tables(positions, head_dim):
    half_dim = head_dim // 2
    frequency = jnp.exp(
        jnp.arange(half_dim, dtype=jnp.float32) * (-2.0 * math.log(10000.0) / head_dim)
    )
    angles = positions.astype(jnp.float32)[:, None] * frequency[None, :]
    return (jnp.cos(angles), jnp.sin(angles))


def rotate(value_rows, cosine, sine_table):
    half_dim = value_rows.shape[-1] // 2
    first_half = value_rows[..., :half_dim]
    second = value_rows[..., half_dim:]
    cos_heads = cosine[:, None, :]
    sin_heads = sine_table[:, None, :]
    return jnp.concatenate(
        [first_half * cos_heads - second * sin_heads, second * cos_heads + first_half * sin_heads],
        axis=-1,
    )


def norm_back(grad_normed, normed, inverse):
    return inverse * (grad_normed - normed * jnp.mean(grad_normed * normed, -1, keepdims=True))


def keep_state(running):
    return running


def swiglu(mid_linear, ff_width):
    return (jax.nn.silu(mid_linear[..., :ff_width]) * mid_linear[..., ff_width:]).astype(
        jnp.bfloat16
    )


def swiglu_back(act_grad, mid_linear, ff_width):
    gate_part = mid_linear[..., :ff_width]
    up_part = mid_linear[..., ff_width:]
    sigmoid = jax.nn.sigmoid(gate_part)
    gate_slope = sigmoid * (1.0 + gate_part * (1.0 - sigmoid))
    return jnp.concatenate(
        [act_grad * up_part * gate_slope, act_grad * gate_part * sigmoid], axis=-1
    ).astype(jnp.bfloat16)


def over_key_blocks(pieces, block_fn, running):
    piece_rows = pieces[0].shape[0]
    block_size = math.gcd(piece_rows, 512)
    shaped = tuple(
        (piece.reshape(piece_rows // block_size, block_size, piece.shape[1]) for piece in pieces)
    )
    offsets = block_size * jnp.arange(piece_rows // block_size, dtype=jnp.int32)

    def advance(carried, block_item):
        return (block_fn(carried, block_item[0], block_item[1], block_item[2]), None)

    result_state, unused = lax.scan(advance, running, (shaped[0], shaped[1], offsets))
    return result_state


def per_device(
    tokens,
    prefix_len,
    routes,
    cotangent,
    query_matrix,
    key_matrix,
    value_matrix,
    output_matrix,
    attention_gain,
    expert_gain,
    router_matrix,
    gate_up_weight,
    down_weight,
):
    hidden = tokens[0].astype(jnp.float32)
    tok_rows, model_width = hidden.shape
    params = (
        lax.all_gather(query_matrix, ("dp", "seq"), axis=0, tiled=True),
        lax.all_gather(key_matrix, ("dp", "seq"), axis=0, tiled=True),
        lax.all_gather(value_matrix, ("dp", "seq"), axis=0, tiled=True),
        lax.all_gather(output_matrix, ("dp", "seq"), axis=0, tiled=True),
        lax.all_gather(attention_gain, ("dp", "seq"), axis=0, tiled=True),
        lax.all_gather(expert_gain, ("dp", "seq"), axis=0, tiled=True),
        lax.all_gather(router_matrix, ("dp", "seq"), axis=0, tiled=True),
    )
    query_full, key_full, value_full, output_full, gain_attention, gain_expert, router_full = params
    head_dim = HEAD_WIDTH
    query_width = query_full.shape[1]
    key_width = key_full.shape[1]
    query_heads = query_width // head_dim
    key_groups = key_width // head_dim
    head_group = query_heads // key_groups
    score_scale = head_dim ** (-0.5)
    first_place = lax.axis_index("seq") * tok_rows
    positions = first_place + jnp.arange(tok_rows, dtype=jnp.int32)
    last_place = first_place + tok_rows - 1
    prefix_end = prefix_len[0]
    cosine, sine_table = rotary_tables(positions, head_dim)
    inverse_attention = lax.rsqrt(jnp.mean(hidden * hidden, -1, keepdims=True) + NORM_EPS)
    normed_attention = hidden * inverse_attention
    attention_input = (normed_attention * gain_attention.astype(jnp.float32)).astype(jnp.bfloat16)
    query_projected = jnp.dot(
        attention_input, query_full, preferred_element_type=jnp.float32
    ).reshape(tok_rows, query_heads, head_dim)
    queries = (
        rotate(query_projected, cosine, sine_table)
        .astype(jnp.bfloat16)
        .reshape(tok_rows, key_groups, head_group, head_dim)
    )
    key_projected = jnp.dot(attention_input, key_full, preferred_element_type=jnp.float32).reshape(
        tok_rows, key_groups, head_dim
    )
    keys_local = (
        rotate(key_projected, cosine, sine_table).astype(jnp.bfloat16).reshape(tok_rows, key_width)
    )
    values_local = jnp.dot(attention_input, value_full, preferred_element_type=jnp.float32).astype(
        jnp.bfloat16
    )

    def block_scores(key_block, key_start):
        block_size = key_block.shape[0]
        key_heads = key_block.reshape(block_size, key_groups, head_dim)
        key_places = key_start + jnp.arange(block_size, dtype=jnp.int32)
        allowed = (key_places[None, :] <= positions[:, None]) | (key_places[None, :] < prefix_end)
        scores = (
            jnp.einsum("qhgd,khd->hgqk", queries, key_heads, preferred_element_type=jnp.float32)
            * score_scale
        )
        return (jnp.where(allowed, scores, -jnp.inf), key_heads)

    def attend(running, key_block, value_block, key_start):

        def compute(carried):
            run_max, run_sum, weighted = carried
            scores, key_heads = block_scores(key_block, key_start)
            value_heads = value_block.reshape(key_block.shape[0], key_groups, head_dim)
            new_max = jnp.maximum(run_max, jnp.max(scores, -1))
            weights = jnp.exp(scores - new_max[..., None])
            factor = jnp.exp(run_max - new_max)
            new_sum = run_sum * factor + jnp.sum(weights, -1)
            new_weighted = weighted * factor[..., None] + jnp.einsum(
                "hgqk,khd->hgqd",
                weights.astype(jnp.bfloat16),
                value_heads,
                preferred_element_type=jnp.float32,
            )
            return (new_max, new_sum, new_weighted)

        visible = (key_start <= last_place) | (key_start < prefix_end)
        return lax.cond(visible, compute, keep_state, running)

    stat_shape = (key_groups, head_group, tok_rows)
    start_state = (
        jnp.full(stat_shape, LOW_SCORE, jnp.float32),
        jnp.zeros(stat_shape, jnp.float32),
        jnp.zeros(stat_shape + (head_dim,), jnp.float32),
    )
    run_max, run_sum, weighted = over_key_blocks(
        (
            lax.all_gather(keys_local, "seq", axis=0, tiled=True),
            lax.all_gather(values_local, "seq", axis=0, tiled=True),
        ),
        attend,
        start_state,
    )
    log_total = run_max + jnp.log(run_sum)
    attended_heads = weighted / run_sum[..., None]
    attention_lowered = (
        attended_heads.transpose(2, 0, 1, 3).reshape(tok_rows, query_width).astype(jnp.bfloat16)
    )
    branch_output = jnp.einsum(
        "tc,dc->td", attention_lowered, output_full, preferred_element_type=jnp.float32
    )
    middle = hidden + branch_output
    inverse_expert = lax.rsqrt(jnp.mean(middle * middle, -1, keepdims=True) + NORM_EPS)
    normed_expert = middle * inverse_expert
    expert_input = (normed_expert * gain_expert.astype(jnp.float32)).astype(jnp.bfloat16)
    router_logits = jnp.dot(expert_input, router_full, preferred_element_type=jnp.float32)
    router_probs = jax.nn.softmax(router_logits, axis=-1)
    expert_count = router_full.shape[1]
    route_ids = routes[0]
    expert_range = jnp.arange(expert_count, dtype=jnp.int32)
    route_hits = jnp.sum(
        (route_ids[:, :, None] == expert_range[None, None, :]).astype(jnp.int32), 1
    )
    slot_rank = jnp.cumsum(route_hits, 0) - 1
    slot_target = jnp.where(route_hits > 0, slot_rank, CAPACITY)
    token_index = jnp.broadcast_to(
        jnp.arange(tok_rows, dtype=jnp.int32)[:, None], (tok_rows, expert_count)
    )
    expert_index = jnp.broadcast_to(expert_range[None, :], (tok_rows, expert_count))
    slot_table = (
        jnp.zeros((expert_count, CAPACITY), jnp.int32)
        .at[expert_index, slot_target]
        .set(token_index, mode="drop")
    )
    slot_live = jnp.arange(CAPACITY, dtype=jnp.int32)[None, :] < jnp.sum(route_hits, 0)[:, None]
    expert_column = expert_range[:, None]
    dispatched = expert_input[slot_table]
    slot_gates = jnp.where(slot_live, router_probs[slot_table, expert_column], 0.0)
    ff_width = down_weight.shape[2]
    grad_mid = cotangent[0].astype(jnp.float32)
    slot_grad = grad_mid[slot_table]
    out_grad = (slot_gates[..., None] * slot_grad).astype(jnp.bfloat16)
    gate_up_full, down_full = (
        lax.all_gather(gate_up_weight, ("dp", "seq"), axis=0, tiled=True),
        lax.all_gather(down_weight, ("dp", "seq"), axis=0, tiled=True),
    )
    mid_linear = jnp.einsum(
        "ecd,def->ecf", dispatched, gate_up_full, preferred_element_type=jnp.float32
    )
    activation = swiglu(mid_linear, ff_width)
    expert_out = jnp.einsum(
        "ecf,def->ecd", activation, down_full, preferred_element_type=jnp.float32
    )
    flat_slots = slot_table.reshape(-1)
    combined = (
        jnp.zeros((tok_rows, model_width), jnp.float32)
        .at[flat_slots]
        .add((slot_gates[..., None] * expert_out).reshape(-1, model_width))
    )
    mixed = (middle + combined).astype(jnp.bfloat16)
    gate_grad = jnp.where(slot_live, jnp.sum(expert_out * slot_grad, -1), 0.0)
    act_grad = jnp.einsum("ecd,def->ecf", out_grad, down_full, preferred_element_type=jnp.float32)
    mid_grad = swiglu_back(act_grad, mid_linear, ff_width)
    gate_up_term = jnp.einsum(
        "ecd,ecf->def", dispatched, mid_grad, preferred_element_type=jnp.float32
    )
    down_term = jnp.einsum("ecd,ecf->def", out_grad, activation, preferred_element_type=jnp.float32)
    summed_terms = lax.psum_scatter(
        jnp.concatenate([gate_up_term, down_term], axis=-1),
        ("dp", "seq"),
        scatter_dimension=0,
        tiled=True,
    )
    gate_up_weight_grad = summed_terms[..., : 2 * ff_width]
    down_weight_grad = summed_terms[..., 2 * ff_width :]
    dispatched_grad = jnp.einsum(
        "ecf,def->ecd", mid_grad, gate_up_full, preferred_element_type=jnp.float32
    )
    expert_in_grad = (
        jnp.zeros((tok_rows, model_width), jnp.float32)
        .at[flat_slots]
        .add(dispatched_grad.reshape(-1, model_width))
    )
    prob_grad = (
        jnp.zeros((tok_rows, expert_count), jnp.float32)
        .at[slot_table, expert_column]
        .add(gate_grad)
    )
    logit_grad = (
        router_probs * (prob_grad - jnp.sum(router_probs * prob_grad, -1, keepdims=True))
    ).astype(jnp.bfloat16)
    router_term = jnp.einsum(
        "td,te->de", expert_input, logit_grad, preferred_element_type=jnp.float32
    )
    expert_in_grad = expert_in_grad + jnp.einsum(
        "te,de->td", logit_grad, router_full, preferred_element_type=jnp.float32
    )
    expert_gain_term = jnp.sum(expert_in_grad * normed_expert, 0)
    grad_res = grad_mid + norm_back(
        expert_in_grad * gain_expert.astype(jnp.float32), normed_expert, inverse_expert
    )
    branch_grad = grad_res.astype(jnp.bfloat16)
    output_term = jnp.einsum(
        "td,tc->dc", branch_grad, attention_lowered, preferred_element_type=jnp.float32
    )
    attended_grad = jnp.dot(branch_grad, output_full, preferred_element_type=jnp.float32).astype(
        jnp.bfloat16
    )
    attended_grad_heads = attended_grad.reshape(
        tok_rows, key_groups, head_group, head_dim
    ).transpose(1, 2, 0, 3)
    delta = jnp.sum(attended_grad_heads.astype(jnp.float32) * attended_heads, -1)
    seq_total = tok_rows * lax.axis_size("seq")

    def attend_back(running, key_block, value_block, key_start):

        def compute(carried):
            query_sum, key_sum, value_sum = carried
            block_size = key_block.shape[0]
            scores, key_heads = block_scores(key_block, key_start)
            value_heads = value_block.reshape(block_size, key_groups, head_dim)
            probs_full = jnp.exp(scores - log_total[..., None])
            probs_low = probs_full.astype(jnp.bfloat16)
            value_piece = jnp.einsum(
                "hgqk,hgqd->khd", probs_low, attended_grad_heads, preferred_element_type=jnp.float32
            ).reshape(block_size, key_width)
            prob_part = jnp.einsum(
                "hgqd,khd->hgqk",
                attended_grad_heads,
                value_heads,
                preferred_element_type=jnp.float32,
            )
            score_grad = (probs_full * (prob_part - delta[..., None])).astype(jnp.bfloat16)
            query_sum = (
                query_sum
                + jnp.einsum(
                    "hgqk,khd->hgqd", score_grad, key_heads, preferred_element_type=jnp.float32
                )
                * score_scale
            )
            key_piece = (
                jnp.einsum(
                    "hgqk,qhgd->khd", score_grad, queries, preferred_element_type=jnp.float32
                )
                * score_scale
            ).reshape(block_size, key_width)
            key_sum = lax.dynamic_update_slice_in_dim(
                key_sum,
                lax.dynamic_slice_in_dim(key_sum, key_start, block_size, 0) + key_piece,
                key_start,
                0,
            )
            value_sum = lax.dynamic_update_slice_in_dim(
                value_sum,
                lax.dynamic_slice_in_dim(value_sum, key_start, block_size, 0) + value_piece,
                key_start,
                0,
            )
            return (query_sum, key_sum, value_sum)

        visible = (key_start <= last_place) | (key_start < prefix_end)
        return lax.cond(visible, compute, keep_state, running)

    back_start = (
        jnp.zeros(stat_shape + (head_dim,), jnp.float32),
        jnp.zeros((seq_total, key_width), jnp.float32),
        jnp.zeros((seq_total, key_width), jnp.float32),
    )
    query_sum, key_sum, value_sum = over_key_blocks(
        (
            lax.all_gather(keys_local, "seq", axis=0, tiled=True),
            lax.all_gather(values_local, "seq", axis=0, tiled=True),
        ),
        attend_back,
        back_start,
    )
    key_part, value_part = (
        lax.psum_scatter(
            key_sum.astype(jnp.bfloat16), "seq", scatter_dimension=0, tiled=True
        ).astype(jnp.float32),
        lax.psum_scatter(
            value_sum.astype(jnp.bfloat16), "seq", scatter_dimension=0, tiled=True
        ).astype(jnp.float32),
    )
    query_rows = query_sum.transpose(2, 0, 1, 3).reshape(tok_rows, query_heads, head_dim)
    query_grad = (
        rotate(query_rows, cosine, -sine_table).reshape(tok_rows, query_width).astype(jnp.bfloat16)
    )
    key_grad = (
        rotate(key_part.reshape(tok_rows, key_groups, head_dim), cosine, -sine_table)
        .reshape(tok_rows, key_width)
        .astype(jnp.bfloat16)
    )
    value_grad = value_part.astype(jnp.bfloat16)
    query_term = jnp.einsum(
        "td,tc->dc", attention_input, query_grad, preferred_element_type=jnp.float32
    )
    key_term = jnp.einsum(
        "td,tc->dc", attention_input, key_grad, preferred_element_type=jnp.float32
    )
    value_term = jnp.einsum(
        "td,tc->dc", attention_input, value_grad, preferred_element_type=jnp.float32
    )
    attention_in_grad = jnp.einsum(
        "tc,dc->td", query_grad, query_full, preferred_element_type=jnp.float32
    )
    attention_in_grad = attention_in_grad + jnp.einsum(
        "tc,dc->td", key_grad, key_full, preferred_element_type=jnp.float32
    )
    attention_in_grad = attention_in_grad + jnp.einsum(
        "tc,dc->td", value_grad, value_full, preferred_element_type=jnp.float32
    )
    attention_gain_term = jnp.sum(attention_in_grad * normed_attention, 0)
    tokens_grad = grad_res + norm_back(
        attention_in_grad * gain_attention.astype(jnp.float32), normed_attention, inverse_attention
    )
    summed_grads = (
        lax.psum_scatter(query_term, ("dp", "seq"), scatter_dimension=0, tiled=True),
        lax.psum_scatter(key_term, ("dp", "seq"), scatter_dimension=0, tiled=True),
        lax.psum_scatter(value_term, ("dp", "seq"), scatter_dimension=0, tiled=True),
        lax.psum_scatter(output_term, ("dp", "seq"), scatter_dimension=0, tiled=True),
        lax.psum_scatter(attention_gain_term, ("dp", "seq"), scatter_dimension=0, tiled=True),
        lax.psum_scatter(expert_gain_term, ("dp", "seq"), scatter_dimension=0, tiled=True),
        lax.psum_scatter(router_term, ("dp", "seq"), scatter_dimension=0, tiled=True),
    )
    return (
        mixed[None],
        tokens_grad[None],
        summed_grads[0],
        summed_grads[1],
        summed_grads[2],
        summed_grads[3],
        summed_grads[4],
        summed_grads[5],
        summed_grads[6],
        gate_up_weight_grad,
        down_weight_grad,
    )


def matmul(left, right, contract):
    return lax.dot_general(
        left, right, (contract, ((), ())), preferred_element_type=jnp.float32
    )


ROWS_BY_COLS = ((1,), (0,))
ROWS_BY_ROWS = ((1,), (1,))
COLS_BY_COLS = ((0,), (0,))


def split_sum_columns(terms):
    ones = jnp.ones((terms.shape[0], LANES), jnp.bfloat16)
    high = terms.astype(jnp.bfloat16)
    low = (terms - high.astype(jnp.float32)).astype(jnp.bfloat16)
    return matmul(high, ones, COLS_BY_COLS) + matmul(low, ones, COLS_BY_COLS)


def turned(value_rows):
    width = value_rows.shape[1]
    lane = lax.broadcasted_iota(jnp.int32, value_rows.shape, 1)
    ahead = pltpu.roll(value_rows, width - HALF, 1)
    behind = pltpu.roll(value_rows, HALF, 1)
    return jnp.where(lane % HEAD_WIDTH < HALF, -ahead, behind)


def spin(value_rows, cosine, sine_table):
    repeats = value_rows.shape[1] // LANES
    cos_all = jnp.concatenate([cosine] * repeats, 1) if repeats > 1 else cosine
    sin_all = jnp.concatenate([sine_table] * repeats, 1) if repeats > 1 else sine_table
    return value_rows * cos_all + turned(value_rows) * sin_all


def shape_of(*dims, kind=jnp.bfloat16):
    return jax.ShapeDtypeStruct(dims, kind)


VMEM_SPEC = pl.BlockSpec(memory_space=pltpu.VMEM)
SMEM_SPEC = pl.BlockSpec(memory_space=pltpu.SMEM)
ANY_SPEC = pl.BlockSpec(memory_space=pl.ANY)


class Place:
    def __init__(self):
        self.dp = lax.axis_index("dp")
        self.z = lax.axis_index("seq")
        self.lines = lax.axis_size("seq")
        self.chips = lax.axis_size("dp") // 2
        self.chip = self.dp // 2
        self.core = self.dp % 2

    def line_peer(self, step):
        return (self.dp, (self.z + step) % self.lines)

    def chip_peer(self, step):
        return (((self.chip + step) % self.chips) * 2 + self.core, self.z)

    def sibling(self):
        return (self.chip * 2 + 1 - self.core, self.z)


def meet(peers):
    barrier = pltpu.get_barrier_semaphore()
    for peer in peers:
        pl.semaphore_signal(barrier, inc=1, device_id=peer, device_id_type=MESH)
    pl.semaphore_wait(barrier, len(peers))


def send(source, target, send_sem, recv_sem, peer):
    copy = pltpu.make_async_remote_copy(
        src_ref=source,
        dst_ref=target,
        send_sem=send_sem,
        recv_sem=recv_sem,
        device_id=peer,
        device_id_type=MESH,
    )
    copy.start()
    return copy


def all_peers(here):
    return (
        [here.line_peer(k) for k in range(1, here.lines)]
        + [here.chip_peer(k) for k in range(1, here.chips)]
        + [here.sibling()]
    )


def comm_params(ident, limit=56):
    return pltpu.CompilerParams(
        collective_id=ident, has_side_effects=True, vmem_limit_bytes=limit << 20
    )


class Spread:
    def __init__(self, here, pick, slot, local_sem, sends, recvs):
        self.here, self.pick, self.slot = here, pick, slot
        self.local_sem, self.sends, self.recvs = local_sem, sends, recvs

    def start(self):
        here = self.here
        mine = self.slot(here.chip, here.core, here.z)
        self.own = pltpu.make_async_copy(self.pick(here.z), mine, self.local_sem)
        self.own.start()
        self.line = [
            send(
                self.pick((here.z + k) % here.lines),
                mine,
                self.sends.at[k - 1],
                self.recvs.at[k - 1],
                here.line_peer(k),
            )
            for k in range(1, here.lines)
        ]

    def chips(self):
        here = self.here
        self.own.wait()
        for copy in self.line:
            copy.wait_recv()
        mine = self.slot(here.chip, here.core, None)
        base = here.lines - 1
        self.plane = [
            send(mine, mine, self.sends.at[base + k - 1], self.recvs.at[base + k - 1], here.chip_peer(k))
            for k in range(1, here.chips)
        ]
        base = base + here.chips - 1
        self.across = [send(mine, mine, self.sends.at[base], self.recvs.at[base], here.sibling())]

    def cores(self):
        here = self.here
        base = here.lines - 1 + here.chips - 1
        for k in range(1, here.chips):
            self.plane[k - 1].wait_recv()
            source = (here.chip - k + here.chips) % here.chips
            block = self.slot(source, here.core, None)
            self.across.append(
                send(block, block, self.sends.at[base + k], self.recvs.at[base + k], here.sibling())
            )

    def finish(self):
        for copy in self.across:
            copy.wait_recv()
        for copy in self.line + self.plane + self.across:
            copy.wait_send()


def spread_count(lines, chips):
    return lines - 1 + chips - 1 + chips


class LineGather:
    def __init__(self, here, source, slot, local_sem, sends, recvs):
        self.here, self.source, self.slot = here, source, slot
        self.local_sem, self.sends, self.recvs = local_sem, sends, recvs

    def start(self):
        here = self.here
        mine = self.slot(here.z)
        self.own = pltpu.make_async_copy(self.source, mine, self.local_sem)
        self.own.start()
        self.line = [
            send(self.source, mine, self.sends.at[k - 1], self.recvs.at[k - 1], here.line_peer(k))
            for k in range(1, here.lines)
        ]

    def finish(self):
        self.own.wait()
        for copy in self.line:
            copy.wait()


class LineSwap:
    def __init__(self, here, pick, received, sends, recvs):
        self.here, self.pick, self.received = here, pick, received
        self.sends, self.recvs = sends, recvs

    def start(self):
        here = self.here
        self.line = [
            send(
                self.pick((here.z + k) % here.lines),
                self.received(k),
                self.sends.at[k - 1],
                self.recvs.at[k - 1],
                here.line_peer(k),
            )
            for k in range(1, here.lines)
        ]

    def finish(self):
        for copy in self.line:
            copy.wait()


def front_kernel(tokens, rows, tokens_all, weights, local_sem, sends, recvs, tok_sends, tok_recvs):
    here = Place()
    meet(all_peers(here))
    gather = LineGather(here, tokens, lambda z: tokens_all.at[z], local_sem.at[0], tok_sends, tok_recvs)

    def slot(chip, core, z):
        return weights.at[chip, core] if z is None else weights.at[chip, core, z]

    spread = Spread(here, lambda z: rows.at[z], slot, local_sem.at[1], sends, recvs)
    spread.start()
    gather.start()
    spread.chips()
    spread.cores()
    spread.finish()
    gather.finish()


def supply_kernel(
    out_rows, expert_rows, marked, out_full, expert_full, marked_all, local_sem, o_sends, o_recvs, e_sends, e_recvs, m_sends, m_recvs
):
    here = Place()
    meet(all_peers(here))

    def out_slot(chip, core, z):
        return out_full.at[chip, core] if z is None else out_full.at[chip, core, z]

    def expert_slot(chip, core, z):
        return expert_full.at[:, chip, core] if z is None else expert_full.at[:, chip, core, z]

    outs = Spread(here, lambda z: out_rows, out_slot, local_sem.at[0], o_sends, o_recvs)
    experts = Spread(here, lambda z: expert_rows.at[z], expert_slot, local_sem.at[1], e_sends, e_recvs)
    marks = LineGather(here, marked, lambda z: marked_all.at[z], local_sem.at[2], m_sends, m_recvs)
    outs.start()
    experts.start()
    marks.start()
    outs.chips()
    experts.chips()
    outs.cores()
    experts.cores()
    outs.finish()
    experts.finish()
    marks.finish()


def attend_kernel(prefix, tokens, weights, gain, cosine, sine_table, att_in, queries, keys, values, attended, attended_low, log_total):
    rows_all, width = tokens.shape
    qkv_width = 2 * queries.shape[1]
    q_width, kv_width = queries.shape[1], keys.shape[1]
    block = rows_all // lax.axis_size("seq")
    for start in range(0, rows_all, block):
        here = pl.ds(start, block)
        hidden = tokens[here, :].astype(jnp.float32)
        inverse = lax.rsqrt(jnp.mean(hidden * hidden, -1, keepdims=True) + NORM_EPS)
        normed = (hidden * inverse * gain[...]).astype(jnp.bfloat16)
        att_in[here, :] = normed
        linear = matmul(normed, weights[:, :qkv_width], ROWS_BY_COLS)
        cos_rows, sin_rows = cosine[here, :], sine_table[here, :]
        queries[here, :] = spin(linear[:, :q_width], cos_rows, sin_rows).astype(jnp.bfloat16)
        keys[here, :] = spin(linear[:, q_width : q_width + kv_width], cos_rows, sin_rows).astype(
            jnp.bfloat16
        )
        values[here, :] = linear[:, q_width + kv_width :].astype(jnp.bfloat16)
    prefix_end = prefix[0]
    heads = q_width // HEAD_WIDTH
    group = q_width // kv_width
    for start in range(0, rows_all, block):
        here = pl.ds(start, block)
        reach = max(rows_all // 2, start + block)
        query_place = start + lax.broadcasted_iota(jnp.int32, (block, reach), 0)
        key_place = lax.broadcasted_iota(jnp.int32, (block, reach), 1)
        allowed = (key_place <= query_place) | (key_place < prefix_end)
        lanes = lax.broadcasted_iota(jnp.int32, (block, LANES), 1)
        totals = jnp.zeros((block, LANES), jnp.float32)
        outputs = []
        for head in range(heads):
            low = head // group * HEAD_WIDTH
            scores = matmul(
                queries[here, head * HEAD_WIDTH : (head + 1) * HEAD_WIDTH],
                keys[:reach, low : low + HEAD_WIDTH],
                ROWS_BY_ROWS,
            )
            scores = jnp.where(allowed, scores * SCORE_SCALE, LOW_SCORE)
            largest = jnp.max(scores, -1, keepdims=True)
            powers = jnp.exp(scores - largest)
            total = jnp.sum(powers, -1, keepdims=True)
            product = matmul(
                powers.astype(jnp.bfloat16), values[:reach, low : low + HEAD_WIDTH], ROWS_BY_COLS
            )
            outputs.append(product / total)
            totals = jnp.where(lanes == head, largest + jnp.log(total), totals)
        joined = jnp.concatenate(outputs, 1)
        attended[here, :] = joined
        attended_low[here, :] = joined.astype(jnp.bfloat16)
        log_total[here, :] = totals


def gather_kernel(block, gathered, local_sem, sends, recvs):
    here = Place()
    meet([here.line_peer(k) for k in range(1, here.lines)])
    gather = LineGather(here, block, lambda z: gathered.at[z], local_sem, sends, recvs)
    gather.start()
    gather.finish()


def middle_kernel(tokens, attended_all, out_full, gain, router, expert_in, probs, middle):
    rows_all = tokens.shape[0]
    lines = attended_all.shape[0]
    block = rows_all // lines
    cols = attended_all.shape[2]
    for start in range(0, rows_all, block):
        here = pl.ds(start, block)
        total = tokens[here, :].astype(jnp.float32)
        branch = matmul(attended_all[0, here, :], out_full[:, :cols], ROWS_BY_ROWS)
        for line in range(1, lines):
            branch = branch + matmul(
                attended_all[line, here, :], out_full[:, line * cols : (line + 1) * cols], ROWS_BY_ROWS
            )
        total = total + branch
        inverse = lax.rsqrt(jnp.mean(total * total, -1, keepdims=True) + NORM_EPS)
        lowered = (total * inverse * gain[...]).astype(jnp.bfloat16)
        expert_in[here, :] = lowered
        logits = matmul(lowered, router[...], ROWS_BY_COLS)
        lane = lax.broadcasted_iota(jnp.int32, logits.shape, 1)
        logits = jnp.where(lane < EXPERT_COUNT, logits, LOW_SCORE)
        powers = jnp.exp(logits - jnp.max(logits, -1, keepdims=True))
        powers = jnp.where(lane < EXPERT_COUNT, powers, 0.0)
        probs[here, :] = powers / jnp.sum(powers, -1, keepdims=True)
        middle[here, :] = total


def expert_kernel(expert_in, marked, probs, weights, mixed_part, in_grad, gate_grad, weight_grad, mix_sum, grad_sum):
    step = pl.program_id(0)
    mine = lax.axis_index("seq") * pl.num_programs(0) + step
    width = expert_in.shape[1]
    ff_width = (weights.shape[2] - width) // 1
    ff_width = weights.shape[2] // 3
    half = expert_in.shape[0] // 2

    @pl.when(step == 0)
    def clear():
        mix_sum[...] = jnp.zeros_like(mix_sum)
        grad_sum[...] = jnp.zeros_like(grad_sum)
        gate_grad[...] = jnp.zeros_like(gate_grad)

    gate_up = weights[0, :, : 2 * ff_width]
    down = weights[0, :, 2 * ff_width :]
    acts, out_grads, mids = [], [], []
    for start in (0, half):
        here = pl.ds(start, half)
        inputs = expert_in[here, :]
        chosen = marked[here, width:].astype(jnp.float32)
        lane = lax.broadcasted_iota(jnp.int32, chosen.shape, 1)
        own = lane == mine
        picked = jnp.sum(jnp.where(own, chosen, 0.0), -1, keepdims=True)
        gate = jnp.sum(jnp.where(own, probs[here, :] * chosen, 0.0), -1, keepdims=True)
        linear = matmul(inputs, gate_up, ROWS_BY_COLS)
        gate_part, up_part = linear[:, :ff_width], linear[:, ff_width:]
        sigmoid = 1.0 / (1.0 + jnp.exp(-gate_part))
        silu = gate_part * sigmoid
        act = (silu * up_part).astype(jnp.bfloat16)
        out = matmul(act, down, ROWS_BY_ROWS)
        grad_mid = marked[here, :width].astype(jnp.float32)
        column = jnp.sum(out * grad_mid, -1, keepdims=True) * picked
        gate_grad[here, :] = gate_grad[here, :] + jnp.where(own, column, 0.0)
        mix_sum[here, :] = mix_sum[here, :] + gate * out
        out_grad = (gate * grad_mid).astype(jnp.bfloat16)
        act_grad = matmul(out_grad, down, ROWS_BY_COLS)
        mid = jnp.concatenate(
            [
                act_grad * up_part * (sigmoid * (1.0 + gate_part * (1.0 - sigmoid))),
                act_grad * silu,
            ],
            1,
        ).astype(jnp.bfloat16)
        grad_sum[here, :] = grad_sum[here, :] + matmul(mid, gate_up, ROWS_BY_ROWS)
        acts.append(act)
        out_grads.append(out_grad)
        mids.append(mid)
    act, out_grad, mid = (jnp.concatenate(pieces, 0) for pieces in (acts, out_grads, mids))
    weight_grad[0, :, : 2 * ff_width] = matmul(expert_in[...], mid, COLS_BY_COLS).astype(jnp.bfloat16)
    weight_grad[0, :, 2 * ff_width :] = matmul(out_grad, act, COLS_BY_COLS).astype(jnp.bfloat16)

    @pl.when(step == pl.num_programs(0) - 1)
    def store():
        mixed_part[...] = mix_sum[...].astype(jnp.bfloat16)
        in_grad[...] = grad_sum[...].astype(jnp.bfloat16)


def settle_kernel(
    mixed_part, in_grad, gate_grad, middle, mixed, in_total, gate_total, got_mix, got_grad, got_gate, m_sends, m_recvs, x_sends, x_recvs, g_sends, g_recvs
):
    here = Place()
    meet([here.line_peer(k) for k in range(1, here.lines)])
    swaps = [
        LineSwap(here, lambda z: in_grad.at[z], lambda k: got_grad.at[k - 1], x_sends, x_recvs),
        LineSwap(here, lambda z: gate_grad.at[z], lambda k: got_gate.at[k - 1], g_sends, g_recvs),
        LineSwap(here, lambda z: mixed_part.at[z], lambda k: got_mix.at[k - 1], m_sends, m_recvs),
    ]
    for swap in swaps:
        swap.start()
    for swap in swaps:
        swap.finish()
    total = in_grad[here.z].astype(jnp.float32)
    gates = gate_grad[here.z]
    sum_mix = middle[here.z] + mixed_part[here.z].astype(jnp.float32)
    for k in range(here.lines - 1):
        total = total + got_grad[k].astype(jnp.float32)
        gates = gates + got_gate[k]
        sum_mix = sum_mix + got_mix[k].astype(jnp.float32)
    in_total[...] = total
    gate_total[...] = gates
    mixed[...] = sum_mix.astype(jnp.bfloat16)


def branch_kernel(
    in_total, gate_total, probs, expert_in, cotangent, middle, gain, router, attended_all, out_full, grad_res, out_term, attended_grad
):
    z = lax.axis_index("seq")
    lines, cols = attended_all.shape[0], attended_all.shape[3]
    prob = probs[z]
    gates = gate_total[...]
    logit_grad = (prob * (gates - jnp.sum(prob * gates, -1, keepdims=True))).astype(jnp.bfloat16)
    router_term = matmul(expert_in[z], logit_grad, COLS_BY_COLS)
    grad = in_total[...] + matmul(logit_grad, router[...], ROWS_BY_ROWS)
    hidden = middle[z]
    inverse = lax.rsqrt(jnp.mean(hidden * hidden, -1, keepdims=True) + NORM_EPS)
    normed = hidden * inverse
    gain_term = split_sum_columns(grad * normed)
    lane = lax.broadcasted_iota(jnp.int32, router_term.shape, 1)
    tail = lines * cols
    out_term[:, tail:] = jnp.where(lane == EXPERT_COUNT, gain_term, router_term).astype(jnp.bfloat16)
    scaled = grad * gain[...]
    result = cotangent[...].astype(jnp.float32) + inverse * (
        scaled - normed * jnp.mean(scaled * normed, -1, keepdims=True)
    )
    grad_res[...] = result
    branch = result.astype(jnp.bfloat16)
    for line in range(lines):
        out_term[:, line * cols : (line + 1) * cols] = matmul(
            branch, attended_all[line, z], COLS_BY_COLS
        ).astype(jnp.bfloat16)
        attended_grad[line] = matmul(
            branch, out_full[:, line * cols : (line + 1) * cols], ROWS_BY_COLS
        ).astype(jnp.bfloat16)


def exchange_kernel(blocks, swapped, local_sem, sends, recvs):
    here = Place()
    meet([here.line_peer(k) for k in range(1, here.lines)])
    own = pltpu.make_async_copy(blocks.at[here.z], swapped.at[here.z], local_sem)
    own.start()
    swap = LineSwap(here, lambda z: blocks.at[z], lambda k: swapped.at[here.z], sends, recvs)
    swap.start()
    own.wait()
    swap.finish()


def attend_back_kernel(
    prefix, tokens, att_in, weights, gain, cosine, sine_table, queries, keys, values, attended, log_total, attended_grad, qkv_term, in_part, joined_grad, key_sum, value_sum
):
    rows_all, width = tokens.shape
    q_width, kv_width = queries.shape[1], keys.shape[1]
    qkv_width = q_width + 2 * kv_width
    heads = q_width // HEAD_WIDTH
    group = q_width // kv_width
    block = rows_all // lax.axis_size("seq")
    prefix_end = prefix[0]
    key_sum[...] = jnp.zeros_like(key_sum)
    value_sum[...] = jnp.zeros_like(value_sum)
    for start in range(0, rows_all, block):
        here = pl.ds(start, block)
        reach = max(rows_all // 2, start + block)
        query_place = start + lax.broadcasted_iota(jnp.int32, (block, reach), 0)
        key_place = lax.broadcasted_iota(jnp.int32, (block, reach), 1)
        allowed = (key_place <= query_place) | (key_place < prefix_end)
        query_grads = []
        for head in range(heads):
            own = slice(head * HEAD_WIDTH, (head + 1) * HEAD_WIDTH)
            low = head // group * HEAD_WIDTH
            shared = slice(low, low + HEAD_WIDTH)
            query, key = queries[here, own], keys[:reach, shared]
            grad = attended_grad[here, own]
            scores = matmul(query, key, ROWS_BY_ROWS) * SCORE_SCALE
            prob = jnp.where(allowed, jnp.exp(scores - log_total[here, head : head + 1]), 0.0)
            delta = jnp.sum(grad.astype(jnp.float32) * attended[here, own], -1, keepdims=True)
            prob_part = matmul(grad, values[:reach, shared], ROWS_BY_ROWS)
            score_grad = (prob * (prob_part - delta)).astype(jnp.bfloat16)
            value_sum[:reach, shared] = value_sum[:reach, shared] + matmul(
                prob.astype(jnp.bfloat16), grad, COLS_BY_COLS
            )
            key_sum[:reach, shared] = key_sum[:reach, shared] + matmul(score_grad, query, COLS_BY_COLS)
            query_grads.append(matmul(score_grad, key, ROWS_BY_COLS))
        query_grad = jnp.concatenate(query_grads, 1) * SCORE_SCALE
        joined_grad[here, :q_width] = spin(query_grad, cosine[here, :], -sine_table[here, :]).astype(
            jnp.bfloat16
        )
    joined_grad[:, q_width : q_width + kv_width] = spin(
        key_sum[...] * SCORE_SCALE, cosine[...], -sine_table[...]
    ).astype(jnp.bfloat16)
    joined_grad[:, q_width + kv_width :] = value_sum[...].astype(jnp.bfloat16)
    qkv_term[:, :qkv_width] = matmul(att_in[...], joined_grad[...], COLS_BY_COLS).astype(jnp.bfloat16)
    gain_term = jnp.zeros((width, LANES), jnp.float32)
    for start in range(0, rows_all, block):
        here = pl.ds(start, block)
        hidden = tokens[here, :].astype(jnp.float32)
        normed = hidden * lax.rsqrt(jnp.mean(hidden * hidden, -1, keepdims=True) + NORM_EPS)
        part = matmul(joined_grad[here, :], weights[:, :qkv_width], ROWS_BY_ROWS)
        in_part[here, :] = part.astype(jnp.bfloat16)
        gain_term = gain_term + split_sum_columns(part * normed)
    qkv_term[:, qkv_width:] = gain_term.astype(jnp.bfloat16)


def tokens_kernel(in_part, grad_res, tokens, gain, tokens_grad, got, sends, recvs):
    here = Place()
    meet([here.line_peer(k) for k in range(1, here.lines)])
    swap = LineSwap(here, lambda z: in_part.at[z], lambda k: got.at[k - 1], sends, recvs)
    swap.start()
    swap.finish()
    total = in_part[here.z].astype(jnp.float32)
    for k in range(here.lines - 1):
        total = total + got[k].astype(jnp.float32)
    hidden = tokens[...].astype(jnp.float32)
    inverse = lax.rsqrt(jnp.mean(hidden * hidden, -1, keepdims=True) + NORM_EPS)
    normed = hidden * inverse
    scaled = total * gain[...]
    tokens_grad[...] = grad_res[...] + inverse * (
        scaled - normed * jnp.mean(scaled * normed, -1, keepdims=True)
    )


def reduce_kernel(
    experts, outs, qkvs, expert_out, out_out, qkv_out,
    e_core, e_sum, e_chips, e_half, e_line,
    o_core, o_sum, o_chips, o_half, o_line,
    q_core, q_sum, q_chips, q_half, q_line,
    e_sends, e_recvs, o_sends, o_recvs, q_sends, q_recvs,
):
    here = Place()
    meet(all_peers(here))
    other = 1 - here.core
    lines, chips = here.lines, here.chips
    first = [
        send(outs.at[:, other], o_core, o_sends.at[0], o_recvs.at[0], here.sibling()),
        send(qkvs.at[:, other], q_core, q_sends.at[0], q_recvs.at[0], here.sibling()),
        send(experts.at[:, :, other], e_core, e_sends.at[0], e_recvs.at[0], here.sibling()),
    ]

    def added(left, right):
        return (left.astype(jnp.float32) + right.astype(jnp.float32)).astype(jnp.bfloat16)

    def plane(total, received, sends, recvs, pick):
        return [
            send(
                pick(total, (here.chip + k) % chips),
                received.at[k - 1],
                sends.at[k],
                recvs.at[k],
                here.chip_peer(k),
            )
            for k in range(1, chips)
        ]

    def line(half, received, sends, recvs, pick):
        return [
            send(
                pick(half, (here.z + k) % lines),
                received.at[k - 1],
                sends.at[chips - 1 + k],
                recvs.at[chips - 1 + k],
                here.line_peer(k),
            )
            for k in range(1, lines)
        ]

    first[0].wait()
    o_sum[...] = added(outs[:, here.core], o_core[...])
    o_plane = plane(o_sum, o_chips, o_sends, o_recvs, lambda ref, chip: ref.at[chip])
    first[1].wait()
    q_sum[...] = added(qkvs[:, here.core], q_core[...])
    q_plane = plane(q_sum, q_chips, q_sends, q_recvs, lambda ref, chip: ref.at[chip])
    first[2].wait()
    for expert in range(experts.shape[0]):
        e_sum[expert] = added(experts[expert, :, here.core], e_core[expert])
    e_plane = plane(e_sum, e_chips, e_sends, e_recvs, lambda ref, chip: ref.at[:, chip])

    def collected(own, received):
        total = own.astype(jnp.float32)
        for k in range(chips - 1):
            total = total + received(k).astype(jnp.float32)
        return total.astype(jnp.bfloat16)

    for copy in o_plane:
        copy.wait()
    o_half[...] = collected(o_sum[here.chip], lambda k: o_chips[k])
    o_lines = line(o_half, o_line, o_sends, o_recvs, lambda ref, z: ref.at[z])
    for copy in q_plane:
        copy.wait()
    q_half[...] = collected(q_sum[here.chip], lambda k: q_chips[k])
    q_lines = line(q_half, q_line, q_sends, q_recvs, lambda ref, z: ref.at[z])
    for copy in e_plane:
        copy.wait()
    for expert in range(experts.shape[0]):
        e_half[expert] = collected(e_sum[expert, here.chip], lambda k: e_chips[k, expert])
    e_lines = [
        send(
            e_half.at[:, (here.z + k) % lines],
            e_line.at[here.z],
            e_sends.at[chips - 1 + k],
            e_recvs.at[chips - 1 + k],
            here.line_peer(k),
        )
        for k in range(1, lines)
    ]
    for copy in o_lines:
        copy.wait()
    total = o_half[here.z].astype(jnp.float32)
    for k in range(lines - 1):
        total = total + o_line[k].astype(jnp.float32)
    out_out[...] = total
    for copy in q_lines:
        copy.wait()
    qkv_out[here.z] = q_half[here.z].astype(jnp.float32)
    for k in range(1, lines):
        qkv_out[(here.z + lines - k) % lines] = q_line[k - 1].astype(jnp.float32)
    for copy in e_lines:
        copy.wait()
    e_line[here.z] = e_half[:, here.z]
    expert_out[...] = e_line[...].astype(jnp.float32)


def fast_device(
    tokens, prefix_len, routes, cotangent, query_matrix, key_matrix, value_matrix, output_matrix,
    attention_gain, expert_gain, router_matrix, gate_up_weight, down_weight,
):
    lines = lax.axis_size("seq")
    chips = lax.axis_size("dp") // 2
    tok_rows, width = tokens.shape[1:]
    rows_all = lines * tok_rows
    depth = query_matrix.shape[0]
    query_width, key_width = query_matrix.shape[1], key_matrix.shape[1]
    q_cols, kv_cols = query_width // lines, key_width // lines
    qkv_cols = q_cols + 2 * kv_cols
    expert_count = router_matrix.shape[1]
    own_experts = expert_count // lines
    ff_width = down_weight.shape[2]
    all_ff = 3 * ff_width
    row_cols = qkv_cols + LANES
    half_dim = HEAD_WIDTH // 2

    places = np.arange(rows_all, dtype=np.float32)
    frequency = np.exp(
        np.arange(half_dim, dtype=np.float32) * np.float32(-2.0 * math.log(10000.0) / HEAD_WIDTH)
    ).astype(np.float32)
    angles = places[:, None] * frequency[None, :]
    cosine = jnp.asarray(np.tile(np.cos(angles), (1, LANES // half_dim)), jnp.float32)
    sine_table = jnp.asarray(np.tile(np.sin(angles), (1, LANES // half_dim)), jnp.float32)

    def by_line(matrix, cols):
        return matrix.reshape(depth, lines, cols).transpose(1, 0, 2)

    small = jnp.concatenate(
        [router_matrix, attention_gain[:, None], expert_gain[:, None],
         jnp.zeros((depth, LANES - expert_count - 2), jnp.bfloat16)], 1,
    )
    rows = jnp.concatenate(
        [by_line(query_matrix, q_cols), by_line(key_matrix, kv_cols), by_line(value_matrix, kv_cols),
         jnp.broadcast_to(small[None], (lines, depth, LANES))], 2,
    )
    DMA = pltpu.SemaphoreType.DMA
    count = spread_count(lines, chips)
    tokens_all, weights = pl.pallas_call(
        front_kernel,
        name="front",
        out_shape=(shape_of(lines, tok_rows, width), shape_of(chips, 2, lines, depth, row_cols)),
        in_specs=[ANY_SPEC] * 2,
        out_specs=(ANY_SPEC,) * 2,
        scratch_shapes=[DMA((2,)), DMA((count,)), DMA((count,)), DMA((lines,)), DMA((lines,))],
        compiler_params=comm_params(1),
    )(tokens[0], rows)
    weights = weights.reshape(width, row_cols)
    gains = weights[:, qkv_cols + expert_count : qkv_cols + expert_count + 2].astype(jnp.float32).T
    gain_attention, gain_expert = gains[0:1], gains[1:2]
    router = weights[:, qkv_cols:]
    router = jnp.where(jnp.arange(LANES)[None, :] < expert_count, router, 0)
    tokens_all = tokens_all.reshape(rows_all, width)

    att_in, queries, keys, values, attended, attended_low, log_total = pl.pallas_call(
        attend_kernel,
        name="attend",
        out_shape=(
            shape_of(rows_all, width), shape_of(rows_all, q_cols), shape_of(rows_all, kv_cols), shape_of(rows_all, kv_cols),
            shape_of(rows_all, q_cols, kind=jnp.float32), shape_of(rows_all, q_cols), shape_of(rows_all, LANES, kind=jnp.float32),
        ),
        in_specs=[SMEM_SPEC] + [VMEM_SPEC] * 5,
        out_specs=(VMEM_SPEC,) * 7,
        compiler_params=pltpu.CompilerParams(vmem_limit_bytes=56 << 20),
    )(prefix_len, tokens_all, weights, gain_attention, cosine, sine_table)

    attended_all = pl.pallas_call(
        gather_kernel,
        name="attended_gather",
        out_shape=shape_of(lines, rows_all, q_cols),
        in_specs=[ANY_SPEC],
        out_specs=ANY_SPEC,
        scratch_shapes=[DMA(()), DMA((lines,)), DMA((lines,))],
        compiler_params=comm_params(2),
    )(attended_low)

    chosen = jnp.sum(
        (routes[0][:, :, None] == jnp.arange(LANES, dtype=jnp.int32)[None, None, :]).astype(jnp.bfloat16), 1
    )
    marked = jnp.concatenate([cotangent[0], chosen], 1)
    expert_rows = jnp.concatenate([gate_up_weight, down_weight], 2).transpose(1, 0, 2)
    expert_rows = expert_rows.reshape(lines, own_experts, depth, all_ff)
    out_full, expert_full, marked_all = pl.pallas_call(
        supply_kernel,
        name="supply",
        out_shape=(
            shape_of(chips, 2, lines, depth, query_width),
            shape_of(own_experts, chips, 2, lines, depth, all_ff),
            shape_of(lines, tok_rows, width + LANES),
        ),
        in_specs=[ANY_SPEC] * 3,
        out_specs=(ANY_SPEC,) * 3,
        scratch_shapes=[DMA((3,))] + [DMA((count,))] * 4 + [DMA((lines,))] * 2,
        compiler_params=comm_params(3),
    )(output_matrix, expert_rows, marked)
    out_full = out_full.reshape(width, query_width)
    expert_full = expert_full.reshape(own_experts, width, all_ff)
    marked_all = marked_all.reshape(rows_all, width + LANES)

    expert_in, probs, middle = pl.pallas_call(
        middle_kernel,
        name="middle",
        out_shape=(
            shape_of(rows_all, width), shape_of(rows_all, LANES, kind=jnp.float32), shape_of(rows_all, width, kind=jnp.float32),
        ),
        in_specs=[VMEM_SPEC] * 5,
        out_specs=(VMEM_SPEC,) * 3,
        compiler_params=pltpu.CompilerParams(vmem_limit_bytes=56 << 20),
    )(tokens_all, attended_all, out_full, gain_expert, router)

    whole = lambda *dims: pl.BlockSpec(dims, lambda e: (0,) * len(dims))
    each = pl.BlockSpec((1, width, all_ff), lambda e: (e, 0, 0))
    mixed_part, in_grad, gate_grad, expert_grad = pl.pallas_call(
        expert_kernel,
        name="experts",
        grid=(own_experts,),
        out_shape=(
            shape_of(rows_all, width), shape_of(rows_all, width), shape_of(rows_all, LANES, kind=jnp.float32),
            shape_of(own_experts, width, all_ff),
        ),
        in_specs=[whole(rows_all, width), whole(rows_all, width + LANES), whole(rows_all, LANES), each],
        out_specs=(whole(rows_all, width), whole(rows_all, width), whole(rows_all, LANES), each),
        scratch_shapes=[pltpu.VMEM((rows_all, width), jnp.float32)] * 2,
        compiler_params=pltpu.CompilerParams(vmem_limit_bytes=56 << 20, dimension_semantics=("arbitrary",)),
    )(expert_in, marked_all, probs, expert_full)

    line_shape = (lines, tok_rows)
    mixed, in_total, gate_total = pl.pallas_call(
        settle_kernel,
        name="settle",
        out_shape=(
            shape_of(tok_rows, width), shape_of(tok_rows, width, kind=jnp.float32), shape_of(tok_rows, LANES, kind=jnp.float32),
        ),
        in_specs=[VMEM_SPEC] * 4,
        out_specs=(VMEM_SPEC,) * 3,
        scratch_shapes=[
            pltpu.VMEM((lines - 1, tok_rows, width), jnp.bfloat16), pltpu.VMEM((lines - 1, tok_rows, width), jnp.bfloat16),
            pltpu.VMEM((lines - 1, tok_rows, LANES), jnp.float32),
        ] + [DMA((lines,))] * 6,
        compiler_params=comm_params(4),
    )(mixed_part.reshape(*line_shape, width), in_grad.reshape(*line_shape, width), gate_grad.reshape(*line_shape, LANES),
      middle.reshape(*line_shape, width))

    grad_res, out_term, attended_grad = pl.pallas_call(
        branch_kernel,
        name="branch",
        out_shape=(
            shape_of(tok_rows, width, kind=jnp.float32), shape_of(width, query_width + LANES), shape_of(lines, tok_rows, q_cols),
        ),
        in_specs=[VMEM_SPEC] * 10,
        out_specs=(VMEM_SPEC,) * 3,
        compiler_params=pltpu.CompilerParams(vmem_limit_bytes=56 << 20),
    )(in_total, gate_total, probs.reshape(*line_shape, LANES), expert_in.reshape(*line_shape, width), cotangent[0],
      middle.reshape(*line_shape, width), gain_expert, router, attended_all.reshape(lines, lines, tok_rows, q_cols), out_full)

    attended_grad = pl.pallas_call(
        exchange_kernel,
        name="exchange",
        out_shape=shape_of(lines, tok_rows, q_cols),
        in_specs=[ANY_SPEC],
        out_specs=ANY_SPEC,
        scratch_shapes=[DMA(()), DMA((lines,)), DMA((lines,))],
        compiler_params=comm_params(5),
    )(attended_grad).reshape(rows_all, q_cols)

    qkv_term, in_part = pl.pallas_call(
        attend_back_kernel,
        name="attend_back",
        out_shape=(shape_of(width, row_cols), shape_of(rows_all, width)),
        in_specs=[SMEM_SPEC] + [VMEM_SPEC] * 12,
        out_specs=(VMEM_SPEC,) * 2,
        scratch_shapes=[
            pltpu.VMEM((rows_all, qkv_cols), jnp.bfloat16), pltpu.VMEM((rows_all, kv_cols), jnp.float32),
            pltpu.VMEM((rows_all, kv_cols), jnp.float32),
        ],
        compiler_params=pltpu.CompilerParams(vmem_limit_bytes=56 << 20),
    )(prefix_len, tokens_all, att_in, weights, gain_attention, cosine, sine_table, queries, keys, values, attended, log_total, attended_grad)

    tokens_grad = pl.pallas_call(
        tokens_kernel,
        name="tokens_grad",
        out_shape=shape_of(tok_rows, width, kind=jnp.float32),
        in_specs=[VMEM_SPEC] * 4,
        out_specs=VMEM_SPEC,
        scratch_shapes=[pltpu.VMEM((lines - 1, tok_rows, width), jnp.bfloat16)] + [DMA((lines,))] * 2,
        compiler_params=comm_params(6),
    )(in_part.reshape(*line_shape, width), grad_res, tokens[0], gain_attention)

    def buffers(cols, lead=()):
        low = jnp.bfloat16
        return [
            pltpu.VMEM((*lead, chips, lines, depth, cols), low), pltpu.VMEM((*lead, chips, lines, depth, cols), low),
            pltpu.VMEM((chips - 1, *lead, lines, depth, cols), low), pltpu.VMEM((*lead, lines, depth, cols), low),
        ]

    steps = chips + lines
    expert_sum, out_sum, qkv_sum = pl.pallas_call(
        reduce_kernel,
        name="reduce",
        out_shape=(
            shape_of(lines, own_experts, depth, all_ff, kind=jnp.float32), shape_of(depth, query_width + LANES, kind=jnp.float32),
            shape_of(lines, depth, row_cols, kind=jnp.float32),
        ),
        in_specs=[VMEM_SPEC] * 3,
        out_specs=(VMEM_SPEC,) * 3,
        scratch_shapes=buffers(all_ff, (own_experts,)) + [pltpu.VMEM((lines, own_experts, depth, all_ff), jnp.bfloat16)]
        + buffers(query_width + LANES) + [pltpu.VMEM((lines - 1, depth, query_width + LANES), jnp.bfloat16)]
        + buffers(row_cols) + [pltpu.VMEM((lines - 1, depth, row_cols), jnp.bfloat16)]
        + [DMA((steps,))] * 6,
        compiler_params=comm_params(7, 60),
    )(expert_grad.reshape(own_experts, chips, 2, lines, depth, all_ff), out_term.reshape(chips, 2, lines, depth, query_width + LANES),
      qkv_term.reshape(chips, 2, lines, depth, row_cols))

    def joined(start, cols):
        return qkv_sum[:, :, start : start + cols].transpose(1, 0, 2).reshape(depth, lines * cols)

    expert_sum = expert_sum.reshape(expert_count, depth, all_ff)
    return (
        mixed[None],
        tokens_grad[None],
        joined(0, q_cols),
        joined(q_cols, kv_cols),
        joined(q_cols + kv_cols, kv_cols),
        out_sum[:, :query_width],
        jnp.sum(qkv_sum[:, :, qkv_cols], 0),
        out_sum[:, query_width + expert_count],
        out_sum[:, query_width : query_width + expert_count],
        expert_sum[:, :, : 2 * ff_width].transpose(1, 0, 2),
        expert_sum[:, :, 2 * ff_width :].transpose(1, 0, 2),
    )


def solution(mesh):
    lines, chips = mesh.shape["seq"], mesh.shape["dp"] // 2
    even = KEY_HEADS % (2 * lines) == 0 and EXPERT_COUNT % lines == 0 and mesh.shape["dp"] == 2 * chips
    return jax.shard_map(
        fast_device if even else per_device,
        mesh=mesh,
        in_specs=(
            P("dp", "seq", None),
            P("dp"),
            P("dp", "seq", None),
            P("dp", "seq", None),
            P(("dp", "seq"), None),
            P(("dp", "seq"), None),
            P(("dp", "seq"), None),
            P(("dp", "seq"), None),
            P(("dp", "seq")),
            P(("dp", "seq")),
            P(("dp", "seq"), None),
            P(("dp", "seq"), None, None),
            P(("dp", "seq"), None, None),
        ),
        out_specs=(
            P("dp", "seq", None),
            P("dp", "seq", None),
            P(("dp", "seq"), None),
            P(("dp", "seq"), None),
            P(("dp", "seq"), None),
            P(("dp", "seq"), None),
            P(("dp", "seq")),
            P(("dp", "seq")),
            P(("dp", "seq"), None),
            P(("dp", "seq"), None, None),
            P(("dp", "seq"), None, None),
        ),
        check_vma=False,
    )
```

```python
import math

import jax
import jax.numpy as jnp
import numpy as np
from jax import lax
from jax.experimental import pallas as pl
from jax.experimental.pallas import tpu as pltpu
from jax.sharding import PartitionSpec as P

HEAD_WIDTH = 64
CAPACITY = 96


NORM_EPS = 1e-06
LOW_SCORE = -1e30
LANES = 128
HALF = HEAD_WIDTH // 2
SCORE_SCALE = HEAD_WIDTH ** (-0.5)
EXPERT_COUNT = 16
KEY_HEADS = 8
MESH = pl.DeviceIdType.MESH


def rotary_tables(positions, head_dim):
    half_dim = head_dim // 2
    frequency = jnp.exp(
        jnp.arange(half_dim, dtype=jnp.float32) * (-2.0 * math.log(10000.0) / head_dim)
    )
    angles = positions.astype(jnp.float32)[:, None] * frequency[None, :]
    return (jnp.cos(angles), jnp.sin(angles))


def rotate(value_rows, cosine, sine_table):
    half_dim = value_rows.shape[-1] // 2
    first_half = value_rows[..., :half_dim]
    second = value_rows[..., half_dim:]
    cos_heads = cosine[:, None, :]
    sin_heads = sine_table[:, None, :]
    return jnp.concatenate(
        [first_half * cos_heads - second * sin_heads, second * cos_heads + first_half * sin_heads],
        axis=-1,
    )


def norm_back(grad_normed, normed, inverse):
    return inverse * (grad_normed - normed * jnp.mean(grad_normed * normed, -1, keepdims=True))


def keep_state(running):
    return running


def swiglu(mid_linear, ff_width):
    return (jax.nn.silu(mid_linear[..., :ff_width]) * mid_linear[..., ff_width:]).astype(
        jnp.bfloat16
    )


def swiglu_back(act_grad, mid_linear, ff_width):
    gate_part = mid_linear[..., :ff_width]
    up_part = mid_linear[..., ff_width:]
    sigmoid = jax.nn.sigmoid(gate_part)
    gate_slope = sigmoid * (1.0 + gate_part * (1.0 - sigmoid))
    return jnp.concatenate(
        [act_grad * up_part * gate_slope, act_grad * gate_part * sigmoid], axis=-1
    ).astype(jnp.bfloat16)


def over_key_blocks(pieces, block_fn, running):
    piece_rows = pieces[0].shape[0]
    block_size = math.gcd(piece_rows, 512)
    shaped = tuple(
        (piece.reshape(piece_rows // block_size, block_size, piece.shape[1]) for piece in pieces)
    )
    offsets = block_size * jnp.arange(piece_rows // block_size, dtype=jnp.int32)

    def advance(carried, block_item):
        return (block_fn(carried, block_item[0], block_item[1], block_item[2]), None)

    result_state, unused = lax.scan(advance, running, (shaped[0], shaped[1], offsets))
    return result_state


def per_device(
    tokens,
    prefix_len,
    routes,
    cotangent,
    query_matrix,
    key_matrix,
    value_matrix,
    output_matrix,
    attention_gain,
    expert_gain,
    router_matrix,
    gate_up_weight,
    down_weight,
):
    hidden = tokens[0].astype(jnp.float32)
    tok_rows, model_width = hidden.shape
    params = (
        lax.all_gather(query_matrix, ("dp", "seq"), axis=0, tiled=True),
        lax.all_gather(key_matrix, ("dp", "seq"), axis=0, tiled=True),
        lax.all_gather(value_matrix, ("dp", "seq"), axis=0, tiled=True),
        lax.all_gather(output_matrix, ("dp", "seq"), axis=0, tiled=True),
        lax.all_gather(attention_gain, ("dp", "seq"), axis=0, tiled=True),
        lax.all_gather(expert_gain, ("dp", "seq"), axis=0, tiled=True),
        lax.all_gather(router_matrix, ("dp", "seq"), axis=0, tiled=True),
    )
    query_full, key_full, value_full, output_full, gain_attention, gain_expert, router_full = params
    head_dim = HEAD_WIDTH
    query_width = query_full.shape[1]
    key_width = key_full.shape[1]
    query_heads = query_width // head_dim
    key_groups = key_width // head_dim
    head_group = query_heads // key_groups
    score_scale = head_dim ** (-0.5)
    first_place = lax.axis_index("seq") * tok_rows
    positions = first_place + jnp.arange(tok_rows, dtype=jnp.int32)
    last_place = first_place + tok_rows - 1
    prefix_end = prefix_len[0]
    cosine, sine_table = rotary_tables(positions, head_dim)
    inverse_attention = lax.rsqrt(jnp.mean(hidden * hidden, -1, keepdims=True) + NORM_EPS)
    normed_attention = hidden * inverse_attention
    attention_input = (normed_attention * gain_attention.astype(jnp.float32)).astype(jnp.bfloat16)
    query_projected = jnp.dot(
        attention_input, query_full, preferred_element_type=jnp.float32
    ).reshape(tok_rows, query_heads, head_dim)
    queries = (
        rotate(query_projected, cosine, sine_table)
        .astype(jnp.bfloat16)
        .reshape(tok_rows, key_groups, head_group, head_dim)
    )
    key_projected = jnp.dot(attention_input, key_full, preferred_element_type=jnp.float32).reshape(
        tok_rows, key_groups, head_dim
    )
    keys_local = (
        rotate(key_projected, cosine, sine_table).astype(jnp.bfloat16).reshape(tok_rows, key_width)
    )
    values_local = jnp.dot(attention_input, value_full, preferred_element_type=jnp.float32).astype(
        jnp.bfloat16
    )

    def block_scores(key_block, key_start):
        block_size = key_block.shape[0]
        key_heads = key_block.reshape(block_size, key_groups, head_dim)
        key_places = key_start + jnp.arange(block_size, dtype=jnp.int32)
        allowed = (key_places[None, :] <= positions[:, None]) | (key_places[None, :] < prefix_end)
        scores = (
            jnp.einsum("qhgd,khd->hgqk", queries, key_heads, preferred_element_type=jnp.float32)
            * score_scale
        )
        return (jnp.where(allowed, scores, -jnp.inf), key_heads)

    def attend(running, key_block, value_block, key_start):

        def compute(carried):
            run_max, run_sum, weighted = carried
            scores, key_heads = block_scores(key_block, key_start)
            value_heads = value_block.reshape(key_block.shape[0], key_groups, head_dim)
            new_max = jnp.maximum(run_max, jnp.max(scores, -1))
            weights = jnp.exp(scores - new_max[..., None])
            factor = jnp.exp(run_max - new_max)
            new_sum = run_sum * factor + jnp.sum(weights, -1)
            new_weighted = weighted * factor[..., None] + jnp.einsum(
                "hgqk,khd->hgqd",
                weights.astype(jnp.bfloat16),
                value_heads,
                preferred_element_type=jnp.float32,
            )
            return (new_max, new_sum, new_weighted)

        visible = (key_start <= last_place) | (key_start < prefix_end)
        return lax.cond(visible, compute, keep_state, running)

    stat_shape = (key_groups, head_group, tok_rows)
    start_state = (
        jnp.full(stat_shape, LOW_SCORE, jnp.float32),
        jnp.zeros(stat_shape, jnp.float32),
        jnp.zeros(stat_shape + (head_dim,), jnp.float32),
    )
    run_max, run_sum, weighted = over_key_blocks(
        (
            lax.all_gather(keys_local, "seq", axis=0, tiled=True),
            lax.all_gather(values_local, "seq", axis=0, tiled=True),
        ),
        attend,
        start_state,
    )
    log_total = run_max + jnp.log(run_sum)
    attended_heads = weighted / run_sum[..., None]
    attention_lowered = (
        attended_heads.transpose(2, 0, 1, 3).reshape(tok_rows, query_width).astype(jnp.bfloat16)
    )
    branch_output = jnp.einsum(
        "tc,dc->td", attention_lowered, output_full, preferred_element_type=jnp.float32
    )
    middle = hidden + branch_output
    inverse_expert = lax.rsqrt(jnp.mean(middle * middle, -1, keepdims=True) + NORM_EPS)
    normed_expert = middle * inverse_expert
    expert_input = (normed_expert * gain_expert.astype(jnp.float32)).astype(jnp.bfloat16)
    router_logits = jnp.dot(expert_input, router_full, preferred_element_type=jnp.float32)
    router_probs = jax.nn.softmax(router_logits, axis=-1)
    expert_count = router_full.shape[1]
    route_ids = routes[0]
    expert_range = jnp.arange(expert_count, dtype=jnp.int32)
    route_hits = jnp.sum(
        (route_ids[:, :, None] == expert_range[None, None, :]).astype(jnp.int32), 1
    )
    slot_rank = jnp.cumsum(route_hits, 0) - 1
    slot_target = jnp.where(route_hits > 0, slot_rank, CAPACITY)
    token_index = jnp.broadcast_to(
        jnp.arange(tok_rows, dtype=jnp.int32)[:, None], (tok_rows, expert_count)
    )
    expert_index = jnp.broadcast_to(expert_range[None, :], (tok_rows, expert_count))
    slot_table = (
        jnp.zeros((expert_count, CAPACITY), jnp.int32)
        .at[expert_index, slot_target]
        .set(token_index, mode="drop")
    )
    slot_live = jnp.arange(CAPACITY, dtype=jnp.int32)[None, :] < jnp.sum(route_hits, 0)[:, None]
    expert_column = expert_range[:, None]
    dispatched = expert_input[slot_table]
    slot_gates = jnp.where(slot_live, router_probs[slot_table, expert_column], 0.0)
    ff_width = down_weight.shape[2]
    grad_mid = cotangent[0].astype(jnp.float32)
    slot_grad = grad_mid[slot_table]
    out_grad = (slot_gates[..., None] * slot_grad).astype(jnp.bfloat16)
    gate_up_full, down_full = (
        lax.all_gather(gate_up_weight, ("dp", "seq"), axis=0, tiled=True),
        lax.all_gather(down_weight, ("dp", "seq"), axis=0, tiled=True),
    )
    mid_linear = jnp.einsum(
        "ecd,def->ecf", dispatched, gate_up_full, preferred_element_type=jnp.float32
    )
    activation = swiglu(mid_linear, ff_width)
    expert_out = jnp.einsum(
        "ecf,def->ecd", activation, down_full, preferred_element_type=jnp.float32
    )
    flat_slots = slot_table.reshape(-1)
    combined = (
        jnp.zeros((tok_rows, model_width), jnp.float32)
        .at[flat_slots]
        .add((slot_gates[..., None] * expert_out).reshape(-1, model_width))
    )
    mixed = (middle + combined).astype(jnp.bfloat16)
    gate_grad = jnp.where(slot_live, jnp.sum(expert_out * slot_grad, -1), 0.0)
    act_grad = jnp.einsum("ecd,def->ecf", out_grad, down_full, preferred_element_type=jnp.float32)
    mid_grad = swiglu_back(act_grad, mid_linear, ff_width)
    gate_up_term = jnp.einsum(
        "ecd,ecf->def", dispatched, mid_grad, preferred_element_type=jnp.float32
    )
    down_term = jnp.einsum("ecd,ecf->def", out_grad, activation, preferred_element_type=jnp.float32)
    summed_terms = lax.psum_scatter(
        jnp.concatenate([gate_up_term, down_term], axis=-1),
        ("dp", "seq"),
        scatter_dimension=0,
        tiled=True,
    )
    gate_up_weight_grad = summed_terms[..., : 2 * ff_width]
    down_weight_grad = summed_terms[..., 2 * ff_width :]
    dispatched_grad = jnp.einsum(
        "ecf,def->ecd", mid_grad, gate_up_full, preferred_element_type=jnp.float32
    )
    expert_in_grad = (
        jnp.zeros((tok_rows, model_width), jnp.float32)
        .at[flat_slots]
        .add(dispatched_grad.reshape(-1, model_width))
    )
    prob_grad = (
        jnp.zeros((tok_rows, expert_count), jnp.float32)
        .at[slot_table, expert_column]
        .add(gate_grad)
    )
    logit_grad = (
        router_probs * (prob_grad - jnp.sum(router_probs * prob_grad, -1, keepdims=True))
    ).astype(jnp.bfloat16)
    router_term = jnp.einsum(
        "td,te->de", expert_input, logit_grad, preferred_element_type=jnp.float32
    )
    expert_in_grad = expert_in_grad + jnp.einsum(
        "te,de->td", logit_grad, router_full, preferred_element_type=jnp.float32
    )
    expert_gain_term = jnp.sum(expert_in_grad * normed_expert, 0)
    grad_res = grad_mid + norm_back(
        expert_in_grad * gain_expert.astype(jnp.float32), normed_expert, inverse_expert
    )
    branch_grad = grad_res.astype(jnp.bfloat16)
    output_term = jnp.einsum(
        "td,tc->dc", branch_grad, attention_lowered, preferred_element_type=jnp.float32
    )
    attended_grad = jnp.dot(branch_grad, output_full, preferred_element_type=jnp.float32).astype(
        jnp.bfloat16
    )
    attended_grad_heads = attended_grad.reshape(
        tok_rows, key_groups, head_group, head_dim
    ).transpose(1, 2, 0, 3)
    delta = jnp.sum(attended_grad_heads.astype(jnp.float32) * attended_heads, -1)
    seq_total = tok_rows * lax.axis_size("seq")

    def attend_back(running, key_block, value_block, key_start):

        def compute(carried):
            query_sum, key_sum, value_sum = carried
            block_size = key_block.shape[0]
            scores, key_heads = block_scores(key_block, key_start)
            value_heads = value_block.reshape(block_size, key_groups, head_dim)
            probs_full = jnp.exp(scores - log_total[..., None])
            probs_low = probs_full.astype(jnp.bfloat16)
            value_piece = jnp.einsum(
                "hgqk,hgqd->khd", probs_low, attended_grad_heads, preferred_element_type=jnp.float32
            ).reshape(block_size, key_width)
            prob_part = jnp.einsum(
                "hgqd,khd->hgqk",
                attended_grad_heads,
                value_heads,
                preferred_element_type=jnp.float32,
            )
            score_grad = (probs_full * (prob_part - delta[..., None])).astype(jnp.bfloat16)
            query_sum = (
                query_sum
                + jnp.einsum(
                    "hgqk,khd->hgqd", score_grad, key_heads, preferred_element_type=jnp.float32
                )
                * score_scale
            )
            key_piece = (
                jnp.einsum(
                    "hgqk,qhgd->khd", score_grad, queries, preferred_element_type=jnp.float32
                )
                * score_scale
            ).reshape(block_size, key_width)
            key_sum = lax.dynamic_update_slice_in_dim(
                key_sum,
                lax.dynamic_slice_in_dim(key_sum, key_start, block_size, 0) + key_piece,
                key_start,
                0,
            )
            value_sum = lax.dynamic_update_slice_in_dim(
                value_sum,
                lax.dynamic_slice_in_dim(value_sum, key_start, block_size, 0) + value_piece,
                key_start,
                0,
            )
            return (query_sum, key_sum, value_sum)

        visible = (key_start <= last_place) | (key_start < prefix_end)
        return lax.cond(visible, compute, keep_state, running)

    back_start = (
        jnp.zeros(stat_shape + (head_dim,), jnp.float32),
        jnp.zeros((seq_total, key_width), jnp.float32),
        jnp.zeros((seq_total, key_width), jnp.float32),
    )
    query_sum, key_sum, value_sum = over_key_blocks(
        (
            lax.all_gather(keys_local, "seq", axis=0, tiled=True),
            lax.all_gather(values_local, "seq", axis=0, tiled=True),
        ),
        attend_back,
        back_start,
    )
    key_part, value_part = (
        lax.psum_scatter(
            key_sum.astype(jnp.bfloat16), "seq", scatter_dimension=0, tiled=True
        ).astype(jnp.float32),
        lax.psum_scatter(
            value_sum.astype(jnp.bfloat16), "seq", scatter_dimension=0, tiled=True
        ).astype(jnp.float32),
    )
    query_rows = query_sum.transpose(2, 0, 1, 3).reshape(tok_rows, query_heads, head_dim)
    query_grad = (
        rotate(query_rows, cosine, -sine_table).reshape(tok_rows, query_width).astype(jnp.bfloat16)
    )
    key_grad = (
        rotate(key_part.reshape(tok_rows, key_groups, head_dim), cosine, -sine_table)
        .reshape(tok_rows, key_width)
        .astype(jnp.bfloat16)
    )
    value_grad = value_part.astype(jnp.bfloat16)
    query_term = jnp.einsum(
        "td,tc->dc", attention_input, query_grad, preferred_element_type=jnp.float32
    )
    key_term = jnp.einsum(
        "td,tc->dc", attention_input, key_grad, preferred_element_type=jnp.float32
    )
    value_term = jnp.einsum(
        "td,tc->dc", attention_input, value_grad, preferred_element_type=jnp.float32
    )
    attention_in_grad = jnp.einsum(
        "tc,dc->td", query_grad, query_full, preferred_element_type=jnp.float32
    )
    attention_in_grad = attention_in_grad + jnp.einsum(
        "tc,dc->td", key_grad, key_full, preferred_element_type=jnp.float32
    )
    attention_in_grad = attention_in_grad + jnp.einsum(
        "tc,dc->td", value_grad, value_full, preferred_element_type=jnp.float32
    )
    attention_gain_term = jnp.sum(attention_in_grad * normed_attention, 0)
    tokens_grad = grad_res + norm_back(
        attention_in_grad * gain_attention.astype(jnp.float32), normed_attention, inverse_attention
    )
    summed_grads = (
        lax.psum_scatter(query_term, ("dp", "seq"), scatter_dimension=0, tiled=True),
        lax.psum_scatter(key_term, ("dp", "seq"), scatter_dimension=0, tiled=True),
        lax.psum_scatter(value_term, ("dp", "seq"), scatter_dimension=0, tiled=True),
        lax.psum_scatter(output_term, ("dp", "seq"), scatter_dimension=0, tiled=True),
        lax.psum_scatter(attention_gain_term, ("dp", "seq"), scatter_dimension=0, tiled=True),
        lax.psum_scatter(expert_gain_term, ("dp", "seq"), scatter_dimension=0, tiled=True),
        lax.psum_scatter(router_term, ("dp", "seq"), scatter_dimension=0, tiled=True),
    )
    return (
        mixed[None],
        tokens_grad[None],
        summed_grads[0],
        summed_grads[1],
        summed_grads[2],
        summed_grads[3],
        summed_grads[4],
        summed_grads[5],
        summed_grads[6],
        gate_up_weight_grad,
        down_weight_grad,
    )


def matmul(left, right, contract):
    return lax.dot_general(
        left, right, (contract, ((), ())), preferred_element_type=jnp.float32
    )


ROWS_BY_COLS = ((1,), (0,))
ROWS_BY_ROWS = ((1,), (1,))
COLS_BY_COLS = ((0,), (0,))


def split_sum_columns(terms):
    ones = jnp.ones((terms.shape[0], LANES), jnp.bfloat16)
    high = terms.astype(jnp.bfloat16)
    low = (terms - high.astype(jnp.float32)).astype(jnp.bfloat16)
    return matmul(high, ones, COLS_BY_COLS) + matmul(low, ones, COLS_BY_COLS)


def turned(value_rows):
    width = value_rows.shape[1]
    lane = lax.broadcasted_iota(jnp.int32, value_rows.shape, 1)
    ahead = pltpu.roll(value_rows, width - HALF, 1)
    behind = pltpu.roll(value_rows, HALF, 1)
    return jnp.where(lane % HEAD_WIDTH < HALF, -ahead, behind)


def spin(value_rows, cosine, sine_table):
    repeats = value_rows.shape[1] // LANES
    cos_all = jnp.concatenate([cosine] * repeats, 1) if repeats > 1 else cosine
    sin_all = jnp.concatenate([sine_table] * repeats, 1) if repeats > 1 else sine_table
    return value_rows * cos_all + turned(value_rows) * sin_all


def inverse_rms(value_rows):
    return lax.rsqrt(jnp.mean(value_rows * value_rows, -1, keepdims=True) + NORM_EPS)


def shape_of(*dims, kind=jnp.bfloat16):
    return jax.ShapeDtypeStruct(dims, kind)


VMEM_SPEC = pl.BlockSpec(memory_space=pltpu.VMEM)
SMEM_SPEC = pl.BlockSpec(memory_space=pltpu.SMEM)
ANY_SPEC = pl.BlockSpec(memory_space=pl.ANY)


class Place:
    def __init__(self):
        self.dp = lax.axis_index("dp")
        self.z = lax.axis_index("seq")
        self.lines = lax.axis_size("seq")
        self.chips = lax.axis_size("dp") // 2
        self.chip = self.dp // 2
        self.core = self.dp % 2
        self.other = 1 - self.core

    def ahead(self, step):
        return (self.z + step) % self.lines

    def behind(self, step):
        return (self.z + self.lines - step) % self.lines

    def line_peer(self, step):
        return (self.dp, self.ahead(step))

    def chip_ahead(self, step):
        return (self.chip + step) % self.chips

    def chip_behind(self, step):
        return (self.chip + self.chips - step) % self.chips

    def chip_peer(self, step):
        return (self.chip_ahead(step) * 2 + self.core, self.z)

    def sibling(self):
        return (self.chip * 2 + self.other, self.z)


def meet(peers):
    barrier = pltpu.get_barrier_semaphore()
    for peer in peers:
        pl.semaphore_signal(barrier, inc=1, device_id=peer, device_id_type=MESH)
    pl.semaphore_wait(barrier, len(peers))


def send(source, target, send_sem, recv_sem, peer):
    copy = pltpu.make_async_remote_copy(
        src_ref=source,
        dst_ref=target,
        send_sem=send_sem,
        recv_sem=recv_sem,
        device_id=peer,
        device_id_type=MESH,
    )
    copy.start()
    return copy


def move(source, target, sem):
    copy = pltpu.make_async_copy(source, target, sem)
    copy.start()
    return copy


def all_peers(here):
    return (
        [here.line_peer(k) for k in range(1, here.lines)]
        + [here.chip_peer(k) for k in range(1, here.chips)]
        + [here.sibling()]
    )


def comm_params(ident, limit=56):
    return pltpu.CompilerParams(
        collective_id=ident, has_side_effects=True, vmem_limit_bytes=limit << 20
    )


class Spread:
    def __init__(self, here, pick, target, depth, local_sem, sends, recvs):
        self.here, self.pick, self.target, self.depth = here, pick, target, depth
        self.local_sem, self.sends, self.recvs = local_sem, sends, recvs

    def row(self):
        here = self.here
        first = (here.dp * here.lines + here.z) * self.depth
        return self.target.at[pl.ds(pl.multiple_of(first, self.depth), self.depth)]

    def chip_rows(self, chip):
        here = self.here
        count = here.lines * self.depth
        first = (chip * 2 + here.core) * count
        return self.target.at[pl.ds(pl.multiple_of(first, count), count)]

    def start(self):
        here = self.here
        mine = self.row()
        self.own = move(self.pick(here.z), mine, self.local_sem)
        self.line = [
            send(
                self.pick(here.ahead(k)), mine, self.sends.at[k - 1], self.recvs.at[k - 1], here.line_peer(k)
            )
            for k in range(1, here.lines)
        ]

    def chips(self):
        here = self.here
        self.own.wait()
        for copy in self.line:
            copy.wait_recv()
        mine = self.chip_rows(here.chip)
        base = here.lines - 1
        self.plane = [
            send(mine, mine, self.sends.at[base + k - 1], self.recvs.at[base + k - 1], here.chip_peer(k))
            for k in range(1, here.chips)
        ]
        base = base + here.chips - 1
        self.across = [send(mine, mine, self.sends.at[base], self.recvs.at[base], here.sibling())]

    def cores(self):
        here = self.here
        base = here.lines - 1 + here.chips - 1
        for k in range(1, here.chips):
            self.plane[k - 1].wait_recv()
            block = self.chip_rows(here.chip_behind(k))
            self.across.append(
                send(block, block, self.sends.at[base + k], self.recvs.at[base + k], here.sibling())
            )

    def finish(self):
        for copy in self.across:
            copy.wait_recv()

    def close(self):
        for copy in self.line + self.plane + self.across:
            copy.wait_send()


def spread_count(lines, chips):
    return lines - 1 + chips - 1 + chips


class LineGather:
    def __init__(self, here, source, target, local_sem, sends, recvs):
        self.here, self.source, self.target = here, source, target
        self.local_sem, self.sends, self.recvs = local_sem, sends, recvs

    def start(self):
        here = self.here
        mine = self.target.at[here.z]
        self.own = move(self.source, mine, self.local_sem)
        self.line = [
            send(self.source, mine, self.sends.at[k - 1], self.recvs.at[k - 1], here.line_peer(k))
            for k in range(1, here.lines)
        ]

    def arrived(self, step):
        if step == 0:
            self.own.wait()
        else:
            self.line[step - 1].wait_recv()

    def finish(self):
        for step in range(self.here.lines):
            self.arrived(step)

    def close(self):
        for copy in self.line:
            copy.wait_send()


class LineSwap:
    def __init__(self, here, pick, received, sends, recvs):
        self.here, self.pick, self.received = here, pick, received
        self.sends, self.recvs = sends, recvs

    def start(self):
        here = self.here
        self.line = [
            send(
                self.pick(here.ahead(k)), self.received(k, here.z), self.sends.at[k - 1], self.recvs.at[k - 1], here.line_peer(k)
            )
            for k in range(1, here.lines)
        ]

    def finish(self):
        for copy in self.line:
            copy.wait_recv()

    def close(self):
        for copy in self.line:
            copy.wait_send()


def forward_kernel(
    prefix, tokens, rows, out_rows, expert_rows, cotangent, chosen_rows, cosine, sine_table,
    mixed_o, tokens_o, weights_o, out_o, cot_o, att_in_o, qkv_o, attended_o, log_o, attended_own_o,
    expert_in_o, probs_o, middle_o, mids_o, gated_o, in_grad_o, gate_grad_o,
    tokens_all, weights, out_full, experts, cot_all, chosen_all, att_in, qkv, attended, attended_all,
    log_total, expert_in, probs, middle, slopes, acts, gated, mids, part_mix, part_grad, gate_grad, got_mix, mixed,
    local_sem, r_sends, r_recvs, o_sends, o_recvs, e_sends, e_recvs, t_sends, t_recvs, c_sends, c_recvs,
    k_sends, k_recvs, a_sends, a_recvs, m_sends, m_recvs, out_sem,
):
    here = Place()
    lines = here.lines
    tok_rows, width = tokens.shape
    rows_all = lines * tok_rows
    depth = rows.shape[1]
    own_experts = experts.shape[0]
    ff_width = experts.shape[2] // 3
    qkv_cols = qkv.shape[1]
    kv_cols = qkv_cols // 4
    q_cols = 2 * kv_cols
    stores = []

    def store(source, target):
        stores.append(move(source, target, out_sem.at[len(stores)]))

    meet(all_peers(here))
    rows_spread = Spread(here, lambda z: rows.at[z], weights, depth, local_sem.at[0], r_sends, r_recvs)
    token_gather = LineGather(here, tokens, tokens_all, local_sem.at[1], t_sends, t_recvs)
    out_spread = Spread(here, lambda z: out_rows, out_full, depth, local_sem.at[2], o_sends, o_recvs)
    chosen_gather = LineGather(here, chosen_rows, chosen_all, local_sem.at[3], k_sends, k_recvs)
    cot_gather = LineGather(here, cotangent, cot_all, local_sem.at[4], c_sends, c_recvs)
    expert_spreads = [
        Spread(
            here, lambda z, e=e: expert_rows.at[z, e], experts.at[e], depth, local_sem.at[5 + e], e_sends.at[e], e_recvs.at[e]
        )
        for e in range(own_experts)
    ]
    rows_spread.start()
    token_gather.start()
    rows_spread.chips()
    out_spread.start()
    rows_spread.cores()
    rows_spread.finish()
    expert_spreads[0].start()
    store(weights, weights_o)
    columns = weights[:, qkv_cols:].astype(jnp.float32).T
    gain_attention = columns[EXPERT_COUNT : EXPERT_COUNT + 1, :]
    gain_expert = columns[EXPERT_COUNT + 1 : EXPERT_COUNT + 2, :]

    for step in range(lines):
        token_gather.arrived(step)
        source = here.behind(step)
        block = pl.ds(pl.multiple_of(source * tok_rows, tok_rows), tok_rows)
        hidden = tokens_all[source].astype(jnp.float32)
        normed = (hidden * inverse_rms(hidden) * gain_attention).astype(jnp.bfloat16)
        att_in[block, :] = normed
        linear = matmul(normed, weights[:, :qkv_cols], ROWS_BY_COLS)
        turned_part = linear[:, : q_cols + kv_cols]
        qkv[block, : q_cols + kv_cols] = spin(turned_part, cosine[block, :], sine_table[block, :]).astype(
            jnp.bfloat16
        )
        qkv[block, q_cols + kv_cols :] = linear[:, q_cols + kv_cols :].astype(jnp.bfloat16)
    store(tokens_all, tokens_o)
    store(att_in, att_in_o)
    store(qkv, qkv_o)
    out_spread.chips()

    prefix_end = prefix[0]
    heads = q_cols // HEAD_WIDTH
    group = q_cols // kv_cols
    attended_sends = []
    for number in range(lines):
        start = number * tok_rows
        block = pl.ds(start, tok_rows)
        reach = max(rows_all // 2, start + tok_rows)
        query_place = start + lax.broadcasted_iota(jnp.int32, (tok_rows, reach), 0)
        key_place = lax.broadcasted_iota(jnp.int32, (tok_rows, reach), 1)
        allowed = (key_place <= query_place) | (key_place < prefix_end)
        lanes = lax.broadcasted_iota(jnp.int32, (tok_rows, LANES), 1)
        totals = jnp.zeros((tok_rows, LANES), jnp.float32)
        outputs = []
        for head in range(heads):
            key_at = q_cols + head // group * HEAD_WIDTH
            value_at = key_at + kv_cols
            scores = matmul(
                qkv[block, head * HEAD_WIDTH : (head + 1) * HEAD_WIDTH],
                qkv[:reach, key_at : key_at + HEAD_WIDTH],
                ROWS_BY_ROWS,
            )
            scores = jnp.where(allowed, scores * SCORE_SCALE, LOW_SCORE)
            largest = jnp.max(scores, -1, keepdims=True)
            powers = jnp.exp(scores - largest)
            total = jnp.sum(powers, -1, keepdims=True)
            product = matmul(
                powers.astype(jnp.bfloat16), qkv[:reach, value_at : value_at + HEAD_WIDTH], ROWS_BY_COLS
            )
            outputs.append(product / total)
            totals = jnp.where(lanes == head, largest + jnp.log(total), totals)
        joined = jnp.concatenate(outputs, 1)
        attended[block, :] = joined
        log_total[block, :] = totals
        mine = attended_all.at[here.z, block]
        attended_all[here.z, block, :] = joined.astype(jnp.bfloat16)
        attended_sends.append(
            [
                send(mine, mine, a_sends.at[number, k - 1], a_recvs.at[number, k - 1], here.line_peer(k))
                for k in range(1, lines)
            ]
        )
        if number == lines // 2:
            out_spread.cores()
    store(attended, attended_o)
    store(log_total, log_o)
    chosen_gather.start()
    expert_spreads[0].chips()
    out_spread.finish()
    store(out_full, out_o)
    chosen_gather.finish()

    for number in range(lines):
        block = pl.ds(number * tok_rows, tok_rows)
        for copy in attended_sends[number]:
            copy.wait_recv()
        branch = matmul(attended_all[0, block, :], out_full[:, :q_cols], ROWS_BY_ROWS)
        for line in range(1, lines):
            branch = branch + matmul(
                attended_all[line, block, :], out_full[:, line * q_cols : (line + 1) * q_cols], ROWS_BY_ROWS
            )
        total = tokens_all[number].astype(jnp.float32) + branch
        lowered = (total * inverse_rms(total) * gain_expert).astype(jnp.bfloat16)
        expert_in[number] = lowered
        logits = matmul(lowered, weights[:, qkv_cols:], ROWS_BY_COLS)
        lane = lax.broadcasted_iota(jnp.int32, logits.shape, 1)
        logits = jnp.where(lane < EXPERT_COUNT, logits, LOW_SCORE)
        powers = jnp.exp(logits - jnp.max(logits, -1, keepdims=True))
        powers = jnp.where(lane < EXPERT_COUNT, powers, 0.0)
        probs[number] = powers / jnp.sum(powers, -1, keepdims=True)
        middle[number] = total
        if number == 1:
            expert_spreads[1].start()
    store(expert_in, expert_in_o)
    store(probs.at[here.z], probs_o)
    store(middle.at[here.z], middle_o)
    store(attended_all.at[:, pl.ds(pl.multiple_of(here.z * tok_rows, tok_rows), tok_rows)], attended_own_o)

    def chosen_of(number):
        marks = chosen_all[number].astype(jnp.float32)
        filler = jnp.zeros((LANES - marks.shape[0], marks.shape[1]), jnp.float32)
        return jnp.concatenate([marks, filler], 0).T

    def gate_columns(number, e):
        chosen = chosen_of(number)
        lane = lax.broadcasted_iota(jnp.int32, chosen.shape, 1)
        own = lane == here.z * own_experts + e
        picked = jnp.sum(jnp.where(own, chosen, 0.0), -1, keepdims=True)
        gate = jnp.sum(jnp.where(own, probs[number] * chosen, 0.0), -1, keepdims=True)
        return own, picked, gate

    pairs = [(a, a + 2) for a in range(0, lines, 2)]

    def expert_forward(e):
        for low, high in pairs:
            block = pl.ds(low * tok_rows, (high - low) * tok_rows)
            inputs = jnp.concatenate([expert_in[n] for n in range(low, high)], 0)
            linear = matmul(inputs, experts[e, :, : 2 * ff_width], ROWS_BY_COLS)
            gate_part, up_part = linear[:, :ff_width], linear[:, ff_width:]
            sigmoid = 1.0 / (1.0 + jnp.exp(-gate_part))
            silu = gate_part * sigmoid
            act = silu * up_part
            slopes[e, block, :ff_width] = up_part * (sigmoid * (1.0 + gate_part * (1.0 - sigmoid)))
            slopes[e, block, ff_width:] = silu
            acts[e, block, :] = act.astype(jnp.bfloat16)
            gate = jnp.concatenate([gate_columns(n, e)[2] for n in range(low, high)], 0)
            gated[e, block, :] = (gate * act).astype(jnp.bfloat16)

    expert_spreads[0].cores()
    expert_spreads[1].chips()
    expert_spreads[2].start()
    expert_spreads[0].finish()
    expert_forward(0)
    expert_spreads[2].chips()
    expert_spreads[3].start()
    expert_spreads[1].cores()
    expert_spreads[1].finish()
    expert_forward(1)
    expert_spreads[3].chips()
    cot_gather.start()
    expert_spreads[2].cores()
    expert_spreads[2].finish()
    expert_forward(2)
    expert_spreads[3].cores()
    expert_spreads[3].finish()
    expert_forward(3)
    store(gated, gated_o)

    for low, high in pairs:
        block = pl.ds(low * tok_rows, (high - low) * tok_rows)
        total = matmul(gated[0, block, :], experts[0, :, 2 * ff_width :], ROWS_BY_ROWS)
        for e in range(1, own_experts):
            total = total + matmul(gated[e, block, :], experts[e, :, 2 * ff_width :], ROWS_BY_ROWS)
        for n in range(low, high):
            part_mix[n] = total[(n - low) * tok_rows : (n - low + 1) * tok_rows, :].astype(jnp.bfloat16)
    mix_swap = LineSwap(here, lambda z: part_mix.at[z], lambda k, z: got_mix.at[k - 1], m_sends, m_recvs)
    mix_swap.start()

    cot_gather.finish()
    store(cot_all, cot_o)
    for low, high in pairs:
        block = pl.ds(low * tok_rows, (high - low) * tok_rows)
        grad_mid = jnp.concatenate([cot_all[n] for n in range(low, high)], 0)
        total = None
        gate_cols = [jnp.zeros((tok_rows, LANES), jnp.float32) for n in range(low, high)]
        for e in range(own_experts):
            act_grad = matmul(grad_mid, experts[e, :, 2 * ff_width :], ROWS_BY_COLS)
            column = jnp.sum(act_grad * acts[e, block, :].astype(jnp.float32), -1, keepdims=True)
            gates = []
            for n in range(low, high):
                own, picked, gate = gate_columns(n, e)
                part = column[(n - low) * tok_rows : (n - low + 1) * tok_rows, :]
                gate_cols[n - low] = jnp.where(own, part * picked, gate_cols[n - low])
                gates.append(gate)
            act_grad = act_grad * jnp.concatenate(gates, 0)
            mid = jnp.concatenate(
                [act_grad * slopes[e, block, :ff_width], act_grad * slopes[e, block, ff_width:]], 1
            ).astype(jnp.bfloat16)
            mids[e, block, :] = mid
            term = matmul(mid, experts[e, :, : 2 * ff_width], ROWS_BY_ROWS)
            total = term if total is None else total + term
        for n in range(low, high):
            part_grad[n] = total[(n - low) * tok_rows : (n - low + 1) * tok_rows, :].astype(jnp.bfloat16)
            gate_grad[n] = gate_cols[n - low]
    store(mids, mids_o)
    store(part_grad, in_grad_o)
    store(gate_grad, gate_grad_o)

    mix_swap.finish()
    total = middle[here.z] + part_mix[here.z].astype(jnp.float32)
    for k in range(lines - 1):
        total = total + got_mix[k].astype(jnp.float32)
    mixed[...] = total.astype(jnp.bfloat16)
    store(mixed, mixed_o)
    for group_of in [rows_spread, token_gather, out_spread, chosen_gather, cot_gather, mix_swap] + expert_spreads:
        group_of.close()
    for block_sends in attended_sends:
        for copy in block_sends:
            copy.wait_send()
    for copy in stores:
        copy.wait()


class Fold:
    def __init__(self, here, terms, crossed, landed, half, sends, recvs):
        self.here, self.terms, self.crossed, self.landed, self.half = here, terms, crossed, landed, half
        self.sends, self.recvs = sends, recvs

    def start(self):
        here = self.here
        self.first = send(
            self.terms.at[:, here.other], self.crossed, self.sends.at[0], self.recvs.at[0], here.sibling()
        )

    def chips(self):
        here = self.here
        self.first.wait_recv()
        for chip in range(here.chips):
            self.terms[chip, here.core] = (
                self.terms[chip, here.core].astype(jnp.float32) + self.crossed[chip].astype(jnp.float32)
            ).astype(jnp.bfloat16)
        self.plane = [
            send(
                self.terms.at[here.chip_ahead(k), here.core], self.landed.at[k - 1], self.sends.at[k], self.recvs.at[k], here.chip_peer(k)
            )
            for k in range(1, here.chips)
        ]

    def finish(self):
        here = self.here
        for copy in self.plane:
            copy.wait_recv()
        for line in range(here.lines):
            total = self.terms[here.chip, here.core, line].astype(jnp.float32)
            for k in range(here.chips - 1):
                total = total + self.landed[k, line].astype(jnp.float32)
            self.half[line] = total.astype(jnp.bfloat16)

    def close(self):
        for copy in [self.first] + self.plane:
            copy.wait_send()


def backward_kernel(
    prefix, cosine, sine_table, tokens_i, weights_i, out_i, cot_i, att_in_i, qkv_i, attended_i, log_i, attended_own_i,
    expert_in_i, probs_i, middle_i, mids_i, gated_i, in_grad_i, gate_grad_i,
    tokens_grad_o, expert_o, out_o, qkv_o,
    tokens_all, weights, out_full, cot_all, att_in, qkv, attended, log_total, attended_own, expert_in, probs, middle,
    mids, gated, in_grad, gate_grad, got_grad, got_gate, grad_res, attended_grad, attended_grad_all, joined_grad,
    key_sum, value_sum, in_part, got_part, tokens_grad,
    e_terms, e_crossed, e_landed, e_half, e_lines,
    o_terms, o_crossed, o_landed, o_half, o_lines, o_sum,
    q_terms, q_crossed, q_landed, q_half, q_lines,
    load_sem, mid_sem, x_sends, x_recvs, g_sends, g_recvs, b_sends, b_recvs, p_sends, p_recvs,
    e_sends, e_recvs, o_sends, o_recvs, q_sends, q_recvs, el_sends, el_recvs, ol_sends, ol_recvs, ql_sends, ql_recvs, out_sem,
):
    here = Place()
    lines, chips = here.lines, here.chips
    tok_rows, width = tokens_all.shape[1:]
    rows_all = lines * tok_rows
    depth = e_terms.shape[4]
    own_experts = e_terms.shape[0]
    ff_width = e_terms.shape[5] // 3
    qkv_cols = qkv.shape[1]
    kv_cols = qkv_cols // 4
    q_cols = 2 * kv_cols
    query_width = lines * q_cols

    def slot_loads(e):
        return [
            move(mids_i.at[e], mids.at[e % 2], mid_sem.at[0, e % 2]),
            move(gated_i.at[e], gated.at[e % 2], mid_sem.at[1, e % 2]),
        ]

    loads = {}
    for number, (name, source, target) in enumerate(
        [
            ("expert_in", expert_in_i, expert_in), ("cot", cot_i, cot_all), ("in_grad", in_grad_i, in_grad), ("gate", gate_grad_i, gate_grad),
            ("probs", probs_i, probs), ("middle", middle_i, middle), ("weights", weights_i, weights), ("out", out_i, out_full),
            ("own", attended_own_i, attended_own), ("tokens", tokens_i, tokens_all), ("att_in", att_in_i, att_in), ("qkv", qkv_i, qkv),
            ("attended", attended_i, attended), ("log", log_i, log_total),
        ]
    ):
        loads[name] = move(source, target, load_sem.at[number])
    slots = [slot_loads(0), slot_loads(1)]
    meet(all_peers(here))
    grad_swap = LineSwap(here, lambda z: in_grad_i.at[z], lambda k, z: got_grad.at[k - 1], x_sends, x_recvs)
    gate_swap = LineSwap(here, lambda z: gate_grad_i.at[z], lambda k, z: got_gate.at[k - 1], g_sends, g_recvs)
    gate_swap.start()
    grad_swap.start()

    folds = [
        Fold(here, e_terms.at[e], e_crossed.at[e], e_landed.at[e], e_half.at[e], e_sends.at[e], e_recvs.at[e])
        for e in range(own_experts)
    ]
    out_fold = Fold(here, o_terms, o_crossed, o_landed, o_half, o_sends, o_recvs)
    qkv_fold = Fold(here, q_terms, q_crossed, q_landed, q_half, q_sends, q_recvs)
    five = (chips, 2, lines, depth)

    def line_swaps(e):
        return LineSwap(here, lambda z: e_half.at[e, z], lambda k, z: e_lines.at[z, e], el_sends.at[e], el_recvs.at[e])

    expert_swaps = [line_swaps(e) for e in range(own_experts)]
    loads["expert_in"].wait()
    loads["cot"].wait()
    inputs = expert_in[...].reshape(rows_all, width)
    grad_mid = cot_all[...].reshape(rows_all, width)
    for e in range(own_experts):
        for load in slots[e % 2]:
            load.wait()
        e_terms[e, ..., : 2 * ff_width] = (
            matmul(inputs, mids[e % 2], COLS_BY_COLS).astype(jnp.bfloat16).reshape(*five, 2 * ff_width)
        )
        e_terms[e, ..., 2 * ff_width :] = (
            matmul(grad_mid, gated[e % 2], COLS_BY_COLS).astype(jnp.bfloat16).reshape(*five, ff_width)
        )
        if e + 2 < own_experts:
            slots[e % 2] = slot_loads(e + 2)
        folds[e].start()
        if e > 0:
            folds[e - 1].chips()

    for name in ("in_grad", "gate", "probs", "middle", "weights", "out", "own"):
        loads[name].wait()
    gate_swap.finish()
    grad_swap.finish()
    gates = gate_grad[here.z]
    grad = in_grad[here.z].astype(jnp.float32)
    for k in range(lines - 1):
        gates = gates + got_gate[k]
        grad = grad + got_grad[k].astype(jnp.float32)
    columns = weights[:, qkv_cols:].astype(jnp.float32).T
    gain_attention = columns[EXPERT_COUNT : EXPERT_COUNT + 1, :]
    gain_expert = columns[EXPERT_COUNT + 1 : EXPERT_COUNT + 2, :]
    prob = probs[...]
    logit_grad = (prob * (gates - jnp.sum(prob * gates, -1, keepdims=True))).astype(jnp.bfloat16)
    router_term = matmul(expert_in[here.z], logit_grad, COLS_BY_COLS)
    grad = grad + matmul(logit_grad, weights[:, qkv_cols:], ROWS_BY_ROWS)
    hidden = middle[...]
    inverse = inverse_rms(hidden)
    normed = hidden * inverse
    gain_term = split_sum_columns(grad * normed)
    lane = lax.broadcasted_iota(jnp.int32, router_term.shape, 1)
    scaled = grad * gain_expert
    result = cot_all[here.z].astype(jnp.float32) + inverse * (
        scaled - normed * jnp.mean(scaled * normed, -1, keepdims=True)
    )
    grad_res[...] = result
    branch = result.astype(jnp.bfloat16)
    for line in range(lines):
        attended_grad[line] = matmul(
            branch, out_full[:, line * q_cols : (line + 1) * q_cols], ROWS_BY_COLS
        ).astype(jnp.bfloat16)
    attended_swap = LineSwap(
        here, lambda z: attended_grad.at[z], lambda k, z: attended_grad_all.at[z], b_sends, b_recvs
    )
    attended_swap.start()
    attended_grad_all[here.z] = attended_grad[here.z]
    for line in range(lines):
        o_terms[..., line * q_cols : (line + 1) * q_cols] = (
            matmul(branch, attended_own[line], COLS_BY_COLS).astype(jnp.bfloat16).reshape(*five, q_cols)
        )
    o_terms[..., query_width:] = (
        jnp.where(lane == EXPERT_COUNT, gain_term, router_term).astype(jnp.bfloat16).reshape(*five, LANES)
    )
    out_fold.start()
    folds[own_experts - 1].chips()

    for name in ("tokens", "att_in", "qkv", "attended", "log"):
        loads[name].wait()
    folds[0].finish()
    expert_swaps[0].start()
    out_fold.chips()
    attended_swap.finish()
    prefix_end = prefix[0]
    heads = q_cols // HEAD_WIDTH
    group = q_cols // kv_cols
    key_sum[...] = jnp.zeros_like(key_sum)
    value_sum[...] = jnp.zeros_like(value_sum)
    for number in range(lines):
        start = number * tok_rows
        block = pl.ds(start, tok_rows)
        reach = max(rows_all // 2, start + tok_rows)
        query_place = start + lax.broadcasted_iota(jnp.int32, (tok_rows, reach), 0)
        key_place = lax.broadcasted_iota(jnp.int32, (tok_rows, reach), 1)
        allowed = (key_place <= query_place) | (key_place < prefix_end)
        query_grads = []
        for head in range(heads):
            own = slice(head * HEAD_WIDTH, (head + 1) * HEAD_WIDTH)
            low = head // group * HEAD_WIDTH
            shared = slice(low, low + HEAD_WIDTH)
            query = qkv[block, own]
            key = qkv[:reach, q_cols + low : q_cols + low + HEAD_WIDTH]
            value = qkv[:reach, q_cols + kv_cols + low : q_cols + kv_cols + low + HEAD_WIDTH]
            grad = attended_grad_all[number, :, own]
            scores = matmul(query, key, ROWS_BY_ROWS) * SCORE_SCALE
            prob = jnp.where(allowed, jnp.exp(scores - log_total[block, head : head + 1]), 0.0)
            delta = jnp.sum(grad.astype(jnp.float32) * attended[block, own], -1, keepdims=True)
            prob_part = matmul(grad, value, ROWS_BY_ROWS)
            score_grad = (prob * (prob_part - delta)).astype(jnp.bfloat16)
            value_sum[:reach, shared] = value_sum[:reach, shared] + matmul(
                prob.astype(jnp.bfloat16), grad, COLS_BY_COLS
            )
            key_sum[:reach, shared] = key_sum[:reach, shared] + matmul(score_grad, query, COLS_BY_COLS)
            query_grads.append(matmul(score_grad, key, ROWS_BY_COLS))
        query_grad = jnp.concatenate(query_grads, 1) * SCORE_SCALE
        joined_grad[block, :q_cols] = spin(query_grad, cosine[block, :], -sine_table[block, :]).astype(
            jnp.bfloat16
        )
    joined_grad[:, q_cols : q_cols + kv_cols] = spin(
        key_sum[...] * SCORE_SCALE, cosine[...], -sine_table[...]
    ).astype(jnp.bfloat16)
    joined_grad[:, q_cols + kv_cols :] = value_sum[...].astype(jnp.bfloat16)
    gain_term = jnp.zeros((width, LANES), jnp.float32)
    part_sends = []
    for number in range(lines):
        block = pl.ds(number * tok_rows, tok_rows)
        hidden = tokens_all[number].astype(jnp.float32)
        normed = hidden * inverse_rms(hidden)
        part = matmul(joined_grad[block, :], weights[:, :qkv_cols], ROWS_BY_ROWS)
        in_part[number] = part.astype(jnp.bfloat16)
        gain_term = gain_term + split_sum_columns(part * normed)
    part_swap = LineSwap(here, lambda z: in_part.at[z], lambda k, z: got_part.at[k - 1], p_sends, p_recvs)
    part_swap.start()
    q_terms[..., :qkv_cols] = (
        matmul(att_in[...], joined_grad[...], COLS_BY_COLS).astype(jnp.bfloat16).reshape(*five, qkv_cols)
    )
    q_terms[..., qkv_cols:] = gain_term.astype(jnp.bfloat16).reshape(*five, LANES)
    qkv_fold.start()
    out_fold.finish()
    out_swap = LineSwap(here, lambda z: o_half.at[z], lambda k, z: o_lines.at[k - 1], ol_sends, ol_recvs)
    out_swap.start()
    qkv_fold.chips()
    for e in range(1, own_experts):
        folds[e].finish()
        expert_swaps[e].start()
    qkv_fold.finish()
    qkv_swap = LineSwap(here, lambda z: q_half.at[z], lambda k, z: q_lines.at[z], ql_sends, ql_recvs)
    qkv_swap.start()

    part_swap.finish()
    total = in_part[here.z].astype(jnp.float32)
    for k in range(lines - 1):
        total = total + got_part[k].astype(jnp.float32)
    hidden = tokens_all[here.z].astype(jnp.float32)
    inverse = inverse_rms(hidden)
    normed = hidden * inverse
    scaled = total * gain_attention
    tokens_grad[...] = grad_res[...] + inverse * (
        scaled - normed * jnp.mean(scaled * normed, -1, keepdims=True)
    )
    stores = [move(tokens_grad, tokens_grad_o, out_sem.at[0])]
    out_swap.finish()
    total = o_half[here.z].astype(jnp.float32)
    for k in range(lines - 1):
        total = total + o_lines[k].astype(jnp.float32)
    o_sum[...] = total
    stores.append(move(o_sum, out_o, out_sem.at[1]))
    q_lines[here.z] = q_half[here.z]
    qkv_swap.finish()
    stores.append(move(q_lines, qkv_o, out_sem.at[2]))
    for e in range(own_experts):
        e_lines[here.z, e] = e_half[e, here.z]
        expert_swaps[e].finish()
    stores.append(move(e_lines, expert_o, out_sem.at[3]))
    for group_of in (
        [grad_swap, gate_swap, attended_swap, part_swap, out_swap, qkv_swap, out_fold, qkv_fold] + folds + expert_swaps
    ):
        group_of.close()
    for copy in stores:
        copy.wait()


def fast_device(
    tokens, prefix_len, routes, cotangent, query_matrix, key_matrix, value_matrix, output_matrix,
    attention_gain, expert_gain, router_matrix, gate_up_weight, down_weight,
):
    lines = lax.axis_size("seq")
    chips = lax.axis_size("dp") // 2
    tok_rows, width = tokens.shape[1:]
    rows_all = lines * tok_rows
    depth = query_matrix.shape[0]
    query_width, key_width = query_matrix.shape[1], key_matrix.shape[1]
    q_cols, kv_cols = query_width // lines, key_width // lines
    qkv_cols = q_cols + 2 * kv_cols
    expert_count = router_matrix.shape[1]
    own_experts = expert_count // lines
    ff_width = down_weight.shape[2]
    all_ff = 3 * ff_width
    row_cols = qkv_cols + LANES
    out_cols = query_width + LANES
    half_dim = HEAD_WIDTH // 2
    low, full = jnp.bfloat16, jnp.float32
    DMA = pltpu.SemaphoreType.DMA

    places = np.arange(rows_all, dtype=np.float32)
    frequency = np.exp(
        np.arange(half_dim, dtype=np.float32) * np.float32(-2.0 * math.log(10000.0) / HEAD_WIDTH)
    ).astype(np.float32)
    angles = places[:, None] * frequency[None, :]
    cosine = jnp.asarray(np.tile(np.cos(angles), (1, LANES // half_dim)), jnp.float32)
    sine_table = jnp.asarray(np.tile(np.sin(angles), (1, LANES // half_dim)), jnp.float32)

    def by_line(matrix, cols):
        return matrix.reshape(depth, lines, cols).transpose(1, 0, 2)

    small = jnp.concatenate(
        [router_matrix, attention_gain[:, None], expert_gain[:, None],
         jnp.zeros((depth, LANES - expert_count - 2), jnp.bfloat16)], 1,
    )
    rows = jnp.concatenate(
        [by_line(query_matrix, q_cols), by_line(key_matrix, kv_cols), by_line(value_matrix, kv_cols),
         jnp.broadcast_to(small[None], (lines, depth, LANES))], 2,
    )
    expert_ids = jnp.arange(expert_count, dtype=jnp.int32)
    chosen_rows = jnp.sum((routes[0].T[None] == expert_ids[:, None, None]).astype(jnp.bfloat16), 1)
    expert_rows = jnp.concatenate([gate_up_weight, down_weight], 2).transpose(1, 0, 2)
    expert_rows = expert_rows.reshape(lines, own_experts, depth, all_ff)
    count = spread_count(lines, chips)

    def scratch(*dims, kind=low):
        return pltpu.VMEM(dims, kind)

    kept = [
        ((lines, tok_rows, width), low), ((width, row_cols), low), ((width, query_width), low), ((lines, tok_rows, width), low),
        ((rows_all, width), low), ((rows_all, qkv_cols), low), ((rows_all, q_cols), full), ((rows_all, LANES), full),
        ((lines, tok_rows, q_cols), low), ((lines, tok_rows, width), low), ((tok_rows, LANES), full), ((tok_rows, width), full),
        ((own_experts, rows_all, 2 * ff_width), low), ((own_experts, rows_all, ff_width), low), ((lines, tok_rows, width), low),
        ((lines, tok_rows, LANES), full),
    ]
    results = pl.pallas_call(
        forward_kernel,
        name="forward",
        out_shape=tuple(jax.ShapeDtypeStruct(dims, kind) for dims, kind in [((tok_rows, width), low)] + kept),
        in_specs=[SMEM_SPEC] + [ANY_SPEC] * 6 + [VMEM_SPEC] * 2,
        out_specs=(ANY_SPEC,) * (len(kept) + 1),
        scratch_shapes=[
            scratch(lines, tok_rows, width), scratch(width, row_cols), scratch(width, query_width),
            scratch(own_experts, width, all_ff), scratch(lines, tok_rows, width), scratch(lines, expert_count, tok_rows),
            scratch(rows_all, width), scratch(rows_all, qkv_cols), scratch(rows_all, q_cols, kind=full),
            scratch(lines, rows_all, q_cols), scratch(rows_all, LANES, kind=full), scratch(lines, tok_rows, width),
            scratch(lines, tok_rows, LANES, kind=full), scratch(lines, tok_rows, width, kind=full),
            scratch(own_experts, rows_all, 2 * ff_width, kind=full), scratch(own_experts, rows_all, ff_width),
            scratch(own_experts, rows_all, ff_width), scratch(own_experts, rows_all, 2 * ff_width),
            scratch(lines, tok_rows, width), scratch(lines, tok_rows, width), scratch(lines, tok_rows, LANES, kind=full),
            scratch(lines - 1, tok_rows, width), scratch(tok_rows, width),
            DMA((5 + own_experts,)), DMA((count,)), DMA((count,)), DMA((count,)), DMA((count,)),
            DMA((own_experts, count)), DMA((own_experts, count)), DMA((lines,)), DMA((lines,)), DMA((lines,)), DMA((lines,)),
            DMA((lines,)), DMA((lines,)), DMA((lines, lines)), DMA((lines, lines)), DMA((lines,)), DMA((lines,)),
            DMA((len(kept) + 1,)),
        ],
        compiler_params=comm_params(1, 62),
    )(prefix_len, tokens[0], rows, output_matrix, expert_rows, cotangent[0], chosen_rows, cosine, sine_table)
    mixed = results[0]

    five = (chips, 2, lines, depth)
    four = (chips, lines, depth)
    tokens_grad, expert_sum, out_sum, qkv_sum = pl.pallas_call(
        backward_kernel,
        name="backward",
        out_shape=(
            shape_of(tok_rows, width, kind=full), shape_of(lines, own_experts, depth, all_ff), shape_of(depth, out_cols, kind=full),
            shape_of(lines, depth, row_cols),
        ),
        in_specs=[SMEM_SPEC] + [VMEM_SPEC] * 2 + [ANY_SPEC] * len(kept),
        out_specs=(ANY_SPEC,) * 4,
        scratch_shapes=[
            pltpu.VMEM(dims, kind) for dims, kind in kept[:12]
        ] + [
            scratch(2, rows_all, 2 * ff_width), scratch(2, rows_all, ff_width),
            scratch(lines, tok_rows, width), scratch(lines, tok_rows, LANES, kind=full),
            scratch(lines - 1, tok_rows, width), scratch(lines - 1, tok_rows, LANES, kind=full), scratch(tok_rows, width, kind=full),
            scratch(lines, tok_rows, q_cols), scratch(lines, tok_rows, q_cols), scratch(rows_all, qkv_cols),
            scratch(rows_all, kv_cols, kind=full), scratch(rows_all, kv_cols, kind=full),
            scratch(lines, tok_rows, width), scratch(lines - 1, tok_rows, width), scratch(tok_rows, width, kind=full),
            scratch(own_experts, *five, all_ff), scratch(own_experts, *four, all_ff), scratch(own_experts, chips - 1, lines, depth, all_ff),
            scratch(own_experts, lines, depth, all_ff), scratch(lines, own_experts, depth, all_ff),
            scratch(*five, out_cols), scratch(*four, out_cols), scratch(chips - 1, lines, depth, out_cols), scratch(lines, depth, out_cols),
            scratch(lines - 1, depth, out_cols), scratch(depth, out_cols, kind=full),
            scratch(*five, row_cols), scratch(*four, row_cols), scratch(chips - 1, lines, depth, row_cols), scratch(lines, depth, row_cols),
            scratch(lines, depth, row_cols),
            DMA((len(kept),)), DMA((2, 2)), DMA((lines,)), DMA((lines,)), DMA((lines,)), DMA((lines,)), DMA((lines,)), DMA((lines,)),
            DMA((lines,)), DMA((lines,)),
            DMA((own_experts, chips)), DMA((own_experts, chips)), DMA((chips,)), DMA((chips,)), DMA((chips,)), DMA((chips,)),
            DMA((own_experts, lines)), DMA((own_experts, lines)), DMA((lines,)), DMA((lines,)), DMA((lines,)), DMA((lines,)), DMA((4,)),
        ],
        compiler_params=comm_params(2, 62),
    )(prefix_len, cosine, sine_table, *results[1:])

    def joined(start, cols):
        return qkv_sum[:, :, start : start + cols].transpose(1, 0, 2).reshape(depth, lines * cols).astype(full)

    expert_sum = expert_sum.reshape(expert_count, depth, all_ff)
    return (
        mixed[None],
        tokens_grad[None],
        joined(0, q_cols),
        joined(q_cols, kv_cols),
        joined(q_cols + kv_cols, kv_cols),
        out_sum[:, :query_width],
        jnp.sum(qkv_sum[:, :, qkv_cols].astype(full), 0),
        out_sum[:, query_width + expert_count],
        out_sum[:, query_width : query_width + expert_count],
        expert_sum[:, :, : 2 * ff_width].transpose(1, 0, 2).astype(full),
        expert_sum[:, :, 2 * ff_width :].transpose(1, 0, 2).astype(full),
    )


def solution(mesh):
    lines, chips = mesh.shape["seq"], mesh.shape["dp"] // 2
    even = KEY_HEADS % (2 * lines) == 0 and EXPERT_COUNT % lines == 0 and mesh.shape["dp"] == 2 * chips
    return jax.shard_map(
        fast_device if even else per_device,
        mesh=mesh,
        in_specs=(
            P("dp", "seq", None),
            P("dp"),
            P("dp", "seq", None),
            P("dp", "seq", None),
            P(("dp", "seq"), None),
            P(("dp", "seq"), None),
            P(("dp", "seq"), None),
            P(("dp", "seq"), None),
            P(("dp", "seq")),
            P(("dp", "seq")),
            P(("dp", "seq"), None),
            P(("dp", "seq"), None, None),
            P(("dp", "seq"), None, None),
        ),
        out_specs=(
            P("dp", "seq", None),
            P("dp", "seq", None),
            P(("dp", "seq"), None),
            P(("dp", "seq"), None),
            P(("dp", "seq"), None),
            P(("dp", "seq"), None),
            P(("dp", "seq")),
            P(("dp", "seq")),
            P(("dp", "seq"), None),
            P(("dp", "seq"), None, None),
            P(("dp", "seq"), None, None),
        ),
        check_vma=False,
    )
```

```python
import math

import jax
import jax.numpy as jnp
import numpy as np
from jax import lax
from jax.experimental import pallas as pl
from jax.experimental.pallas import tpu as pltpu
from jax.sharding import PartitionSpec as P

HEAD_WIDTH = 64
CAPACITY = 96


NORM_EPS = 1e-06
LOW_SCORE = -1e30
LANES = 128
HALF = HEAD_WIDTH // 2
SCORE_SCALE = HEAD_WIDTH ** (-0.5)
EXPERT_COUNT = 16
KEY_HEADS = 8
MESH = pl.DeviceIdType.MESH


def rotary_tables(positions, head_dim):
    half_dim = head_dim // 2
    frequency = jnp.exp(
        jnp.arange(half_dim, dtype=jnp.float32) * (-2.0 * math.log(10000.0) / head_dim)
    )
    angles = positions.astype(jnp.float32)[:, None] * frequency[None, :]
    return (jnp.cos(angles), jnp.sin(angles))


def rotate(value_rows, cosine, sine_table):
    half_dim = value_rows.shape[-1] // 2
    first_half = value_rows[..., :half_dim]
    second = value_rows[..., half_dim:]
    cos_heads = cosine[:, None, :]
    sin_heads = sine_table[:, None, :]
    return jnp.concatenate(
        [first_half * cos_heads - second * sin_heads, second * cos_heads + first_half * sin_heads],
        axis=-1,
    )


def norm_back(grad_normed, normed, inverse):
    return inverse * (grad_normed - normed * jnp.mean(grad_normed * normed, -1, keepdims=True))


def keep_state(running):
    return running


def swiglu(mid_linear, ff_width):
    return (jax.nn.silu(mid_linear[..., :ff_width]) * mid_linear[..., ff_width:]).astype(
        jnp.bfloat16
    )


def swiglu_back(act_grad, mid_linear, ff_width):
    gate_part = mid_linear[..., :ff_width]
    up_part = mid_linear[..., ff_width:]
    sigmoid = jax.nn.sigmoid(gate_part)
    gate_slope = sigmoid * (1.0 + gate_part * (1.0 - sigmoid))
    return jnp.concatenate(
        [act_grad * up_part * gate_slope, act_grad * gate_part * sigmoid], axis=-1
    ).astype(jnp.bfloat16)


def over_key_blocks(pieces, block_fn, running):
    piece_rows = pieces[0].shape[0]
    block_size = math.gcd(piece_rows, 512)
    shaped = tuple(
        (piece.reshape(piece_rows // block_size, block_size, piece.shape[1]) for piece in pieces)
    )
    offsets = block_size * jnp.arange(piece_rows // block_size, dtype=jnp.int32)

    def advance(carried, block_item):
        return (block_fn(carried, block_item[0], block_item[1], block_item[2]), None)

    result_state, unused = lax.scan(advance, running, (shaped[0], shaped[1], offsets))
    return result_state


def per_device(
    tokens,
    prefix_len,
    routes,
    cotangent,
    query_matrix,
    key_matrix,
    value_matrix,
    output_matrix,
    attention_gain,
    expert_gain,
    router_matrix,
    gate_up_weight,
    down_weight,
):
    hidden = tokens[0].astype(jnp.float32)
    tok_rows, model_width = hidden.shape
    params = (
        lax.all_gather(query_matrix, ("dp", "seq"), axis=0, tiled=True),
        lax.all_gather(key_matrix, ("dp", "seq"), axis=0, tiled=True),
        lax.all_gather(value_matrix, ("dp", "seq"), axis=0, tiled=True),
        lax.all_gather(output_matrix, ("dp", "seq"), axis=0, tiled=True),
        lax.all_gather(attention_gain, ("dp", "seq"), axis=0, tiled=True),
        lax.all_gather(expert_gain, ("dp", "seq"), axis=0, tiled=True),
        lax.all_gather(router_matrix, ("dp", "seq"), axis=0, tiled=True),
    )
    query_full, key_full, value_full, output_full, gain_attention, gain_expert, router_full = params
    head_dim = HEAD_WIDTH
    query_width = query_full.shape[1]
    key_width = key_full.shape[1]
    query_heads = query_width // head_dim
    key_groups = key_width // head_dim
    head_group = query_heads // key_groups
    score_scale = head_dim ** (-0.5)
    first_place = lax.axis_index("seq") * tok_rows
    positions = first_place + jnp.arange(tok_rows, dtype=jnp.int32)
    last_place = first_place + tok_rows - 1
    prefix_end = prefix_len[0]
    cosine, sine_table = rotary_tables(positions, head_dim)
    inverse_attention = lax.rsqrt(jnp.mean(hidden * hidden, -1, keepdims=True) + NORM_EPS)
    normed_attention = hidden * inverse_attention
    attention_input = (normed_attention * gain_attention.astype(jnp.float32)).astype(jnp.bfloat16)
    query_projected = jnp.dot(
        attention_input, query_full, preferred_element_type=jnp.float32
    ).reshape(tok_rows, query_heads, head_dim)
    queries = (
        rotate(query_projected, cosine, sine_table)
        .astype(jnp.bfloat16)
        .reshape(tok_rows, key_groups, head_group, head_dim)
    )
    key_projected = jnp.dot(attention_input, key_full, preferred_element_type=jnp.float32).reshape(
        tok_rows, key_groups, head_dim
    )
    keys_local = (
        rotate(key_projected, cosine, sine_table).astype(jnp.bfloat16).reshape(tok_rows, key_width)
    )
    values_local = jnp.dot(attention_input, value_full, preferred_element_type=jnp.float32).astype(
        jnp.bfloat16
    )

    def block_scores(key_block, key_start):
        block_size = key_block.shape[0]
        key_heads = key_block.reshape(block_size, key_groups, head_dim)
        key_places = key_start + jnp.arange(block_size, dtype=jnp.int32)
        allowed = (key_places[None, :] <= positions[:, None]) | (key_places[None, :] < prefix_end)
        scores = (
            jnp.einsum("qhgd,khd->hgqk", queries, key_heads, preferred_element_type=jnp.float32)
            * score_scale
        )
        return (jnp.where(allowed, scores, -jnp.inf), key_heads)

    def attend(running, key_block, value_block, key_start):

        def compute(carried):
            run_max, run_sum, weighted = carried
            scores, key_heads = block_scores(key_block, key_start)
            value_heads = value_block.reshape(key_block.shape[0], key_groups, head_dim)
            new_max = jnp.maximum(run_max, jnp.max(scores, -1))
            weights = jnp.exp(scores - new_max[..., None])
            factor = jnp.exp(run_max - new_max)
            new_sum = run_sum * factor + jnp.sum(weights, -1)
            new_weighted = weighted * factor[..., None] + jnp.einsum(
                "hgqk,khd->hgqd",
                weights.astype(jnp.bfloat16),
                value_heads,
                preferred_element_type=jnp.float32,
            )
            return (new_max, new_sum, new_weighted)

        visible = (key_start <= last_place) | (key_start < prefix_end)
        return lax.cond(visible, compute, keep_state, running)

    stat_shape = (key_groups, head_group, tok_rows)
    start_state = (
        jnp.full(stat_shape, LOW_SCORE, jnp.float32),
        jnp.zeros(stat_shape, jnp.float32),
        jnp.zeros(stat_shape + (head_dim,), jnp.float32),
    )
    run_max, run_sum, weighted = over_key_blocks(
        (
            lax.all_gather(keys_local, "seq", axis=0, tiled=True),
            lax.all_gather(values_local, "seq", axis=0, tiled=True),
        ),
        attend,
        start_state,
    )
    log_total = run_max + jnp.log(run_sum)
    attended_heads = weighted / run_sum[..., None]
    attention_lowered = (
        attended_heads.transpose(2, 0, 1, 3).reshape(tok_rows, query_width).astype(jnp.bfloat16)
    )
    branch_output = jnp.einsum(
        "tc,dc->td", attention_lowered, output_full, preferred_element_type=jnp.float32
    )
    middle = hidden + branch_output
    inverse_expert = lax.rsqrt(jnp.mean(middle * middle, -1, keepdims=True) + NORM_EPS)
    normed_expert = middle * inverse_expert
    expert_input = (normed_expert * gain_expert.astype(jnp.float32)).astype(jnp.bfloat16)
    router_logits = jnp.dot(expert_input, router_full, preferred_element_type=jnp.float32)
    router_probs = jax.nn.softmax(router_logits, axis=-1)
    expert_count = router_full.shape[1]
    route_ids = routes[0]
    expert_range = jnp.arange(expert_count, dtype=jnp.int32)
    route_hits = jnp.sum(
        (route_ids[:, :, None] == expert_range[None, None, :]).astype(jnp.int32), 1
    )
    slot_rank = jnp.cumsum(route_hits, 0) - 1
    slot_target = jnp.where(route_hits > 0, slot_rank, CAPACITY)
    token_index = jnp.broadcast_to(
        jnp.arange(tok_rows, dtype=jnp.int32)[:, None], (tok_rows, expert_count)
    )
    expert_index = jnp.broadcast_to(expert_range[None, :], (tok_rows, expert_count))
    slot_table = (
        jnp.zeros((expert_count, CAPACITY), jnp.int32)
        .at[expert_index, slot_target]
        .set(token_index, mode="drop")
    )
    slot_live = jnp.arange(CAPACITY, dtype=jnp.int32)[None, :] < jnp.sum(route_hits, 0)[:, None]
    expert_column = expert_range[:, None]
    dispatched = expert_input[slot_table]
    slot_gates = jnp.where(slot_live, router_probs[slot_table, expert_column], 0.0)
    ff_width = down_weight.shape[2]
    grad_mid = cotangent[0].astype(jnp.float32)
    slot_grad = grad_mid[slot_table]
    out_grad = (slot_gates[..., None] * slot_grad).astype(jnp.bfloat16)
    gate_up_full, down_full = (
        lax.all_gather(gate_up_weight, ("dp", "seq"), axis=0, tiled=True),
        lax.all_gather(down_weight, ("dp", "seq"), axis=0, tiled=True),
    )
    mid_linear = jnp.einsum(
        "ecd,def->ecf", dispatched, gate_up_full, preferred_element_type=jnp.float32
    )
    activation = swiglu(mid_linear, ff_width)
    expert_out = jnp.einsum(
        "ecf,def->ecd", activation, down_full, preferred_element_type=jnp.float32
    )
    flat_slots = slot_table.reshape(-1)
    combined = (
        jnp.zeros((tok_rows, model_width), jnp.float32)
        .at[flat_slots]
        .add((slot_gates[..., None] * expert_out).reshape(-1, model_width))
    )
    mixed = (middle + combined).astype(jnp.bfloat16)
    gate_grad = jnp.where(slot_live, jnp.sum(expert_out * slot_grad, -1), 0.0)
    act_grad = jnp.einsum("ecd,def->ecf", out_grad, down_full, preferred_element_type=jnp.float32)
    mid_grad = swiglu_back(act_grad, mid_linear, ff_width)
    gate_up_term = jnp.einsum(
        "ecd,ecf->def", dispatched, mid_grad, preferred_element_type=jnp.float32
    )
    down_term = jnp.einsum("ecd,ecf->def", out_grad, activation, preferred_element_type=jnp.float32)
    summed_terms = lax.psum_scatter(
        jnp.concatenate([gate_up_term, down_term], axis=-1),
        ("dp", "seq"),
        scatter_dimension=0,
        tiled=True,
    )
    gate_up_weight_grad = summed_terms[..., : 2 * ff_width]
    down_weight_grad = summed_terms[..., 2 * ff_width :]
    dispatched_grad = jnp.einsum(
        "ecf,def->ecd", mid_grad, gate_up_full, preferred_element_type=jnp.float32
    )
    expert_in_grad = (
        jnp.zeros((tok_rows, model_width), jnp.float32)
        .at[flat_slots]
        .add(dispatched_grad.reshape(-1, model_width))
    )
    prob_grad = (
        jnp.zeros((tok_rows, expert_count), jnp.float32)
        .at[slot_table, expert_column]
        .add(gate_grad)
    )
    logit_grad = (
        router_probs * (prob_grad - jnp.sum(router_probs * prob_grad, -1, keepdims=True))
    ).astype(jnp.bfloat16)
    router_term = jnp.einsum(
        "td,te->de", expert_input, logit_grad, preferred_element_type=jnp.float32
    )
    expert_in_grad = expert_in_grad + jnp.einsum(
        "te,de->td", logit_grad, router_full, preferred_element_type=jnp.float32
    )
    expert_gain_term = jnp.sum(expert_in_grad * normed_expert, 0)
    grad_res = grad_mid + norm_back(
        expert_in_grad * gain_expert.astype(jnp.float32), normed_expert, inverse_expert
    )
    branch_grad = grad_res.astype(jnp.bfloat16)
    output_term = jnp.einsum(
        "td,tc->dc", branch_grad, attention_lowered, preferred_element_type=jnp.float32
    )
    attended_grad = jnp.dot(branch_grad, output_full, preferred_element_type=jnp.float32).astype(
        jnp.bfloat16
    )
    attended_grad_heads = attended_grad.reshape(
        tok_rows, key_groups, head_group, head_dim
    ).transpose(1, 2, 0, 3)
    delta = jnp.sum(attended_grad_heads.astype(jnp.float32) * attended_heads, -1)
    seq_total = tok_rows * lax.axis_size("seq")

    def attend_back(running, key_block, value_block, key_start):

        def compute(carried):
            query_sum, key_sum, value_sum = carried
            block_size = key_block.shape[0]
            scores, key_heads = block_scores(key_block, key_start)
            value_heads = value_block.reshape(block_size, key_groups, head_dim)
            probs_full = jnp.exp(scores - log_total[..., None])
            probs_low = probs_full.astype(jnp.bfloat16)
            value_piece = jnp.einsum(
                "hgqk,hgqd->khd", probs_low, attended_grad_heads, preferred_element_type=jnp.float32
            ).reshape(block_size, key_width)
            prob_part = jnp.einsum(
                "hgqd,khd->hgqk",
                attended_grad_heads,
                value_heads,
                preferred_element_type=jnp.float32,
            )
            score_grad = (probs_full * (prob_part - delta[..., None])).astype(jnp.bfloat16)
            query_sum = (
                query_sum
                + jnp.einsum(
                    "hgqk,khd->hgqd", score_grad, key_heads, preferred_element_type=jnp.float32
                )
                * score_scale
            )
            key_piece = (
                jnp.einsum(
                    "hgqk,qhgd->khd", score_grad, queries, preferred_element_type=jnp.float32
                )
                * score_scale
            ).reshape(block_size, key_width)
            key_sum = lax.dynamic_update_slice_in_dim(
                key_sum,
                lax.dynamic_slice_in_dim(key_sum, key_start, block_size, 0) + key_piece,
                key_start,
                0,
            )
            value_sum = lax.dynamic_update_slice_in_dim(
                value_sum,
                lax.dynamic_slice_in_dim(value_sum, key_start, block_size, 0) + value_piece,
                key_start,
                0,
            )
            return (query_sum, key_sum, value_sum)

        visible = (key_start <= last_place) | (key_start < prefix_end)
        return lax.cond(visible, compute, keep_state, running)

    back_start = (
        jnp.zeros(stat_shape + (head_dim,), jnp.float32),
        jnp.zeros((seq_total, key_width), jnp.float32),
        jnp.zeros((seq_total, key_width), jnp.float32),
    )
    query_sum, key_sum, value_sum = over_key_blocks(
        (
            lax.all_gather(keys_local, "seq", axis=0, tiled=True),
            lax.all_gather(values_local, "seq", axis=0, tiled=True),
        ),
        attend_back,
        back_start,
    )
    key_part, value_part = (
        lax.psum_scatter(
            key_sum.astype(jnp.bfloat16), "seq", scatter_dimension=0, tiled=True
        ).astype(jnp.float32),
        lax.psum_scatter(
            value_sum.astype(jnp.bfloat16), "seq", scatter_dimension=0, tiled=True
        ).astype(jnp.float32),
    )
    query_rows = query_sum.transpose(2, 0, 1, 3).reshape(tok_rows, query_heads, head_dim)
    query_grad = (
        rotate(query_rows, cosine, -sine_table).reshape(tok_rows, query_width).astype(jnp.bfloat16)
    )
    key_grad = (
        rotate(key_part.reshape(tok_rows, key_groups, head_dim), cosine, -sine_table)
        .reshape(tok_rows, key_width)
        .astype(jnp.bfloat16)
    )
    value_grad = value_part.astype(jnp.bfloat16)
    query_term = jnp.einsum(
        "td,tc->dc", attention_input, query_grad, preferred_element_type=jnp.float32
    )
    key_term = jnp.einsum(
        "td,tc->dc", attention_input, key_grad, preferred_element_type=jnp.float32
    )
    value_term = jnp.einsum(
        "td,tc->dc", attention_input, value_grad, preferred_element_type=jnp.float32
    )
    attention_in_grad = jnp.einsum(
        "tc,dc->td", query_grad, query_full, preferred_element_type=jnp.float32
    )
    attention_in_grad = attention_in_grad + jnp.einsum(
        "tc,dc->td", key_grad, key_full, preferred_element_type=jnp.float32
    )
    attention_in_grad = attention_in_grad + jnp.einsum(
        "tc,dc->td", value_grad, value_full, preferred_element_type=jnp.float32
    )
    attention_gain_term = jnp.sum(attention_in_grad * normed_attention, 0)
    tokens_grad = grad_res + norm_back(
        attention_in_grad * gain_attention.astype(jnp.float32), normed_attention, inverse_attention
    )
    summed_grads = (
        lax.psum_scatter(query_term, ("dp", "seq"), scatter_dimension=0, tiled=True),
        lax.psum_scatter(key_term, ("dp", "seq"), scatter_dimension=0, tiled=True),
        lax.psum_scatter(value_term, ("dp", "seq"), scatter_dimension=0, tiled=True),
        lax.psum_scatter(output_term, ("dp", "seq"), scatter_dimension=0, tiled=True),
        lax.psum_scatter(attention_gain_term, ("dp", "seq"), scatter_dimension=0, tiled=True),
        lax.psum_scatter(expert_gain_term, ("dp", "seq"), scatter_dimension=0, tiled=True),
        lax.psum_scatter(router_term, ("dp", "seq"), scatter_dimension=0, tiled=True),
    )
    return (
        mixed[None],
        tokens_grad[None],
        summed_grads[0],
        summed_grads[1],
        summed_grads[2],
        summed_grads[3],
        summed_grads[4],
        summed_grads[5],
        summed_grads[6],
        gate_up_weight_grad,
        down_weight_grad,
    )


def matmul(left, right, contract):
    return lax.dot_general(
        left, right, (contract, ((), ())), preferred_element_type=jnp.float32
    )


ROWS_BY_COLS = ((1,), (0,))
ROWS_BY_ROWS = ((1,), (1,))
COLS_BY_COLS = ((0,), (0,))


def split_sum_columns(terms):
    ones = jnp.ones((terms.shape[0], LANES), jnp.bfloat16)
    high = terms.astype(jnp.bfloat16)
    low = (terms - high.astype(jnp.float32)).astype(jnp.bfloat16)
    return matmul(high, ones, COLS_BY_COLS) + matmul(low, ones, COLS_BY_COLS)


def turned(value_rows):
    width = value_rows.shape[1]
    lane = lax.broadcasted_iota(jnp.int32, value_rows.shape, 1)
    ahead = pltpu.roll(value_rows, width - HALF, 1)
    behind = pltpu.roll(value_rows, HALF, 1)
    return jnp.where(lane % HEAD_WIDTH < HALF, -ahead, behind)


def spin(value_rows, cosine, sine_table):
    repeats = value_rows.shape[1] // LANES
    cos_all = jnp.concatenate([cosine] * repeats, 1) if repeats > 1 else cosine
    sin_all = jnp.concatenate([sine_table] * repeats, 1) if repeats > 1 else sine_table
    return value_rows * cos_all + turned(value_rows) * sin_all


def inverse_rms(value_rows):
    return lax.rsqrt(jnp.mean(value_rows * value_rows, -1, keepdims=True) + NORM_EPS)


def shape_of(*dims, kind=jnp.bfloat16):
    return jax.ShapeDtypeStruct(dims, kind)


VMEM_SPEC = pl.BlockSpec(memory_space=pltpu.VMEM)
SMEM_SPEC = pl.BlockSpec(memory_space=pltpu.SMEM)
ANY_SPEC = pl.BlockSpec(memory_space=pl.ANY)


class Place:
    def __init__(self):
        self.dp = lax.axis_index("dp")
        self.z = lax.axis_index("seq")
        self.lines = lax.axis_size("seq")
        self.chips = lax.axis_size("dp") // 2
        self.chip = self.dp // 2
        self.core = self.dp % 2
        self.other = 1 - self.core
        self.chip_x = self.chip + 1 - 2 * (self.chip % 2)
        self.chip_y = (self.chip + 2) % 4
        self.chip_diag = 3 - self.chip

    def ahead(self, step):
        return (self.z + step) % self.lines

    def behind(self, step):
        return (self.z + self.lines - step) % self.lines

    def line_peer(self, step):
        return (self.dp, self.ahead(step))

    def on_chip(self, chip):
        return (chip * 2 + self.core, self.z)

    def sibling(self):
        return (self.chip * 2 + self.other, self.z)


def meet(peers):
    barrier = pltpu.get_barrier_semaphore()
    for peer in peers:
        pl.semaphore_signal(barrier, inc=1, device_id=peer, device_id_type=MESH)
    pl.semaphore_wait(barrier, len(peers))


def send(source, target, send_sem, recv_sem, peer):
    copy = pltpu.make_async_remote_copy(
        src_ref=source,
        dst_ref=target,
        send_sem=send_sem,
        recv_sem=recv_sem,
        device_id=peer,
        device_id_type=MESH,
    )
    copy.start()
    return copy


def move(source, target, sem):
    copy = pltpu.make_async_copy(source, target, sem)
    copy.start()
    return copy


def all_peers(here):
    return (
        [here.line_peer(k) for k in range(1, here.lines)]
        + [here.on_chip(chip) for chip in (here.chip_x, here.chip_y, here.chip_diag)]
        + [here.sibling()]
    )


def comm_params(ident, limit=56):
    return pltpu.CompilerParams(
        collective_id=ident, has_side_effects=True, vmem_limit_bytes=limit << 20
    )


class Spread:
    def __init__(self, here, pick, target, depth, local_sem, sends, recvs):
        self.here, self.pick, self.target, self.depth = here, pick, target, depth
        self.local_sem, self.sends, self.recvs = local_sem, sends, recvs
        self.used = 0

    def put(self, source, target, peer):
        copy = send(source, target, self.sends.at[self.used], self.recvs.at[self.used], peer)
        self.used += 1
        return copy

    def row(self):
        here = self.here
        first = (here.dp * here.lines + here.z) * self.depth
        return self.target.at[pl.ds(pl.multiple_of(first, self.depth), self.depth)]

    def chip_rows(self, chip, part=None):
        here = self.here
        count = here.lines * self.depth
        first = (chip * 2 + here.core) * count
        if part is not None:
            first, count = first + part * (count // 2), count // 2
        return self.target.at[pl.ds(pl.multiple_of(first, count), count)]

    def start(self):
        here = self.here
        mine = self.row()
        self.own = move(self.pick(here.z), mine, self.local_sem)
        self.line = [
            self.put(self.pick(here.ahead(k)), mine, here.line_peer(k)) for k in range(1, here.lines)
        ]

    def chips(self):
        here = self.here
        self.own.wait()
        for copy in self.line:
            copy.wait_recv()
        mine = self.chip_rows(here.chip)
        self.plane = [
            self.put(mine, mine, here.on_chip(here.chip_x)),
            self.put(mine, mine, here.on_chip(here.chip_y)),
        ]
        self.across = [self.put(mine, mine, here.sibling())]

    def turn(self):
        here = self.here
        self.corner = []
        for copy, origin, onward, part in (
            (self.plane[0], here.chip_x, here.chip_y, 0),
            (self.plane[1], here.chip_y, here.chip_x, 1),
        ):
            copy.wait_recv()
            half = self.chip_rows(origin, part)
            self.corner.append(self.put(half, half, here.on_chip(onward)))
            block = self.chip_rows(origin)
            self.across.append(self.put(block, block, here.sibling()))

    def cores(self):
        here = self.here
        for copy in self.corner:
            copy.wait_recv()
        block = self.chip_rows(here.chip_diag)
        self.across.append(self.put(block, block, here.sibling()))

    def finish(self):
        for copy in self.across:
            copy.wait_recv()

    def close(self):
        for copy in self.line + self.plane + self.corner + self.across:
            copy.wait_send()


def spread_count(lines):
    return lines - 1 + 2 + 2 + 4


class LineGather:
    def __init__(self, here, view, sends, recvs, source=None):
        self.here, self.view, self.source = here, view, source
        self.sends, self.recvs = sends, recvs

    def copy(self, way, hop, block, source=None):
        here = self.here
        step = 1 if way == 0 else here.lines - 1
        return pltpu.make_async_remote_copy(
            src_ref=self.view(block) if source is None else source,
            dst_ref=self.view(block),
            send_sem=self.sends.at[way, hop - 1],
            recv_sem=self.recvs.at[way, hop - 1],
            device_id=here.line_peer(step),
            device_id_type=MESH,
        )

    def start(self):
        here = self.here

        @pl.when(here.z < here.lines - 1)
        def rightward():
            self.copy(0, 1, here.z, self.source).start()

        @pl.when(here.z > 0)
        def leftward():
            self.copy(1, 1, here.z, self.source).start()

    def step(self, hop):
        here = self.here
        lines = here.lines

        @pl.when(here.z >= hop)
        def from_left():
            block = here.behind(hop)
            self.copy(0, hop, block).wait_recv()
            if hop < lines - 1:

                @pl.when(here.z < lines - 1)
                def onward():
                    self.copy(0, hop + 1, block).start()

        @pl.when(here.z + hop < lines)
        def from_right():
            block = here.ahead(hop)
            self.copy(1, hop, block).wait_recv()
            if hop < lines - 1:

                @pl.when(here.z > 0)
                def onward():
                    self.copy(1, hop + 1, block).start()

    def close(self):
        here = self.here
        lines = here.lines
        for hop in range(1, lines):

            @pl.when((here.z >= hop - 1) & (here.z < lines - 1))
            def rightward():
                self.copy(0, hop, here.behind(hop - 1)).wait_send()

            @pl.when((here.z + hop - 1 < lines) & (here.z > 0))
            def leftward():
                self.copy(1, hop, here.ahead(hop - 1)).wait_send()


class LineSpread:
    def __init__(self, here, view, sends, recvs, source=None):
        self.here, self.view, self.source = here, view, source
        self.sends, self.recvs = sends, recvs

    def start(self):
        here = self.here
        mine = self.view(here.z)
        self.line = [
            send(
                mine if self.source is None else self.source, mine, self.sends.at[k - 1], self.recvs.at[k - 1], here.line_peer(k)
            )
            for k in range(1, here.lines)
        ]

    def arrived(self, step):
        self.line[step - 1].wait_recv()

    def finish(self):
        for copy in self.line:
            copy.wait_recv()

    def close(self):
        for copy in self.line:
            copy.wait_send()


class LineSum:
    def __init__(self, here, parts, landed, sends, recvs):
        self.here, self.parts, self.landed = here, parts, landed
        self.sends, self.recvs = sends, recvs

    def copy(self, way, hops):
        here = self.here
        step = 1 if way == 0 else here.lines - 1
        block = here.ahead(hops) if way == 0 else here.behind(hops)
        return pltpu.make_async_remote_copy(
            src_ref=self.parts.at[block],
            dst_ref=self.landed.at[way, hops - 1],
            send_sem=self.sends.at[way, hops - 1],
            recv_sem=self.recvs.at[way, hops - 1],
            device_id=here.line_peer(step),
            device_id_type=MESH,
        )

    def arrival(self, way, left):
        return self.copy(way, left + 1)

    def step(self, hops):
        here = self.here
        lines = here.lines

        def pass_on(way, first):
            block = here.ahead(hops) if way == 0 else here.behind(hops)
            if hops < lines - 1:

                @pl.when(jnp.logical_not(first))
                def add():
                    self.arrival(way, hops).wait_recv()
                    self.parts[block] = (
                        self.parts[block].astype(jnp.float32) + self.landed[way, hops].astype(jnp.float32)
                    ).astype(self.parts.dtype)

            self.copy(way, hops).start()

        @pl.when(here.z + hops < lines)
        def rightward():
            pass_on(0, here.z == 0)

        @pl.when(here.z >= hops)
        def leftward():
            pass_on(1, here.z == lines - 1)

    def finish(self, total):
        here = self.here
        total[...] = self.parts[here.z].astype(jnp.float32)

        @pl.when(here.z > 0)
        def from_left():
            self.arrival(0, 0).wait_recv()
            total[...] = total[...] + self.landed[0, 0].astype(jnp.float32)

        @pl.when(here.z < here.lines - 1)
        def from_right():
            self.arrival(1, 0).wait_recv()
            total[...] = total[...] + self.landed[1, 0].astype(jnp.float32)

    def close(self):
        here = self.here
        for hops in range(1, here.lines):

            @pl.when(here.z + hops < here.lines)
            def rightward():
                self.copy(0, hops).wait_send()

            @pl.when(here.z >= hops)
            def leftward():
                self.copy(1, hops).wait_send()


class LineSwap:
    def __init__(self, here, pick, received, sends, recvs):
        self.here, self.pick, self.received = here, pick, received
        self.sends, self.recvs = sends, recvs

    def start(self):
        here = self.here
        self.line = [
            send(
                self.pick(here.ahead(k)), self.received(k, here.z), self.sends.at[k - 1], self.recvs.at[k - 1], here.line_peer(k)
            )
            for k in range(1, here.lines)
        ]

    def finish(self):
        for copy in self.line:
            copy.wait_recv()

    def close(self):
        for copy in self.line:
            copy.wait_send()


def padded_square(block):
    filler = jnp.zeros((LANES - block.shape[0], LANES), jnp.float32)
    return jnp.concatenate([block, filler], 0).T


def row_order(depth, experts, by_expert):
    count = depth * experts
    place = lax.broadcasted_iota(jnp.int32, (count, count), 0)
    source = lax.broadcasted_iota(jnp.int32, (count, count), 1)
    if by_expert:
        wanted = place % depth * experts + place // depth
    else:
        wanted = place % experts * depth + place // experts
    return (source == wanted).astype(jnp.bfloat16)


def forward_kernel(
    prefix, tokens, query_rows, key_rows, value_rows, out_rows, router_cols, attention_gain, expert_gain, gate_up_rows, down_rows,
    cotangent, routes, cosine, sine_table,
    part_mix_o, tokens_o, weights_o, out_o, cot_o, att_in_o, qkv_o, attended_o, log_o, attended_own_o,
    expert_in_o, probs_o, middle_o, mids_o, gated_o, in_grad_o, gate_grad_o,
    gate_up, down, square, rows, expert_rows, tokens_all, weights, out_full, experts, cot_all, chosen_all, att_in, qkv, attended, attended_all,
    log_total, expert_in, probs, middle, slopes, acts, gated, mids, part_mix, part_grad, gate_grad,
    local_sem, r_sends, r_recvs, o_sends, o_recvs, e_sends, e_recvs, t_sends, t_recvs, c_sends, c_recvs,
    k_sends, k_recvs, a_sends, a_recvs, out_sem,
):
    here = Place()
    lines = here.lines
    tok_rows, width = tokens.shape
    rows_all = lines * tok_rows
    depth = rows.shape[1]
    own_experts = experts.shape[0]
    ff_width = experts.shape[2] // 3
    qkv_cols = qkv.shape[1]
    kv_cols = qkv_cols // 4
    q_cols = 2 * kv_cols
    stores = []

    def store(source, target):
        stores.append(move(source, target, out_sem.at[len(stores)]))

    gate_up_load = move(gate_up_rows, gate_up, local_sem.at[0])
    down_load = move(down_rows, down, local_sem.at[1])
    token_load = move(tokens, tokens_all.at[here.z], local_sem.at[2])
    cot_load = move(cotangent, cot_all.at[here.z], local_sem.at[3])

    square[...] = jnp.zeros_like(square)
    square[:EXPERT_COUNT, :depth] = router_cols[...].astype(jnp.float32)
    square[EXPERT_COUNT : EXPERT_COUNT + 1, :depth] = attention_gain[...].astype(jnp.float32)
    square[EXPERT_COUNT + 1 : EXPERT_COUNT + 2, :depth] = expert_gain[...].astype(jnp.float32)
    small = square[...].T[:depth, :].astype(jnp.bfloat16)
    for line in range(lines):
        rows[line, :, :q_cols] = query_rows[:, line * q_cols : (line + 1) * q_cols]
        rows[line, :, q_cols : q_cols + kv_cols] = key_rows[:, line * kv_cols : (line + 1) * kv_cols]
        rows[line, :, q_cols + kv_cols : qkv_cols] = value_rows[:, line * kv_cols : (line + 1) * kv_cols]
        rows[line, :, qkv_cols:] = small
    meet(all_peers(here))
    rows_spread = Spread(here, lambda z: rows.at[z], weights, depth, local_sem.at[4], r_sends, r_recvs)
    half = tok_rows // 2
    token_gathers = [
        LineGather(
            here, lambda z, n=n: tokens_all.at[z, pl.ds(n * half, half)], t_sends.at[n], t_recvs.at[n], tokens.at[pl.ds(n * half, half)]
        )
        for n in range(2)
    ]
    out_spread = Spread(here, lambda z: out_rows, out_full, depth, local_sem.at[5], o_sends, o_recvs)
    chosen_swap = LineSwap(
        here, lambda z: chosen_all.at[here.z], lambda k, z: chosen_all.at[z], k_sends, k_recvs
    )
    cot_gather = LineSpread(here, lambda z: cot_all.at[z], c_sends, c_recvs, cotangent)
    expert_spreads = [
        Spread(
            here,
            lambda z, e=e: expert_rows.at[pl.ds(pl.multiple_of((z * own_experts + e) * depth, depth), depth)],
            experts.at[e], depth, local_sem.at[6 + e], e_sends.at[e], e_recvs.at[e],
        )
        for e in range(own_experts)
    ]
    rows_spread.start()
    for gather in token_gathers:
        gather.start()
    expert_id = lax.broadcasted_iota(jnp.int32, (EXPERT_COUNT, tok_rows), 0)
    chosen = jnp.zeros((EXPERT_COUNT, tok_rows), jnp.float32)
    for number in range(routes.shape[0]):
        chosen = chosen + (routes[number : number + 1, :] == expert_id).astype(jnp.float32)
    chosen_all[here.z] = chosen.astype(jnp.bfloat16)
    chosen_swap.start()
    rows_spread.chips()
    gate_up_load.wait()
    down_load.wait()
    order = row_order(depth, EXPERT_COUNT, True)
    expert_rows[:, : 2 * ff_width] = matmul(
        order, gate_up[...].reshape(depth * EXPERT_COUNT, 2 * ff_width), ROWS_BY_COLS
    ).astype(jnp.bfloat16)
    expert_rows[:, 2 * ff_width :] = matmul(
        order, down[...].reshape(depth * EXPERT_COUNT, ff_width), ROWS_BY_COLS
    ).astype(jnp.bfloat16)
    token_gathers[0].step(1)
    rows_spread.turn()
    token_gathers[1].step(1)
    for hop in range(2, lines - 1):
        token_gathers[0].step(hop)
        rows_spread.cores()
        token_gathers[1].step(hop)
    out_spread.start()
    for spread in expert_spreads[: own_experts // 2]:
        spread.start()
    rows_spread.finish()
    store(weights, weights_o)
    columns = weights[:, qkv_cols:].astype(jnp.float32).T
    gain_attention = columns[EXPERT_COUNT : EXPERT_COUNT + 1, :]
    gain_expert = columns[EXPERT_COUNT + 1 : EXPERT_COUNT + 2, :]

    def project(source):
        block = pl.ds(pl.multiple_of(source * tok_rows, tok_rows), tok_rows)
        hidden = tokens_all[source].astype(jnp.float32)
        normed = (hidden * inverse_rms(hidden) * gain_attention).astype(jnp.bfloat16)
        att_in[block, :] = normed
        linear = matmul(normed, weights[:, :qkv_cols], ROWS_BY_COLS)
        turned_part = linear[:, : q_cols + kv_cols]
        qkv[block, : q_cols + kv_cols] = spin(turned_part, cosine[block, :], sine_table[block, :]).astype(
            jnp.bfloat16
        )
        qkv[block, q_cols + kv_cols :] = linear[:, q_cols + kv_cols :].astype(jnp.bfloat16)

    token_load.wait()
    project(here.z)
    for step in range(1, lines - 1):

        @pl.when(here.z >= step)
        def left():
            project(here.behind(step))

        @pl.when(here.z + step < lines)
        def right():
            project(here.ahead(step))

    for gather in token_gathers:
        gather.step(lines - 1)

    @pl.when(here.z == lines - 1)
    def first():
        project(0)

    @pl.when(here.z == 0)
    def last():
        project(lines - 1)

    out_spread.chips()
    store(tokens_all, tokens_o)
    store(att_in, att_in_o)
    store(qkv, qkv_o)

    prefix_end = prefix[0]
    heads = q_cols // HEAD_WIDTH
    group = q_cols // kv_cols

    def attend(number):
        start = number * tok_rows
        block = pl.ds(start, tok_rows)
        reach = max(rows_all // 2, start + tok_rows)
        query_place = start + lax.broadcasted_iota(jnp.int32, (tok_rows, reach), 0)
        key_place = lax.broadcasted_iota(jnp.int32, (tok_rows, reach), 1)
        allowed = (key_place <= query_place) | (key_place < prefix_end)
        lanes = lax.broadcasted_iota(jnp.int32, (tok_rows, LANES), 1)
        totals = jnp.zeros((tok_rows, LANES), jnp.float32)
        outputs = []
        for head in range(heads):
            key_at = q_cols + head // group * HEAD_WIDTH
            value_at = key_at + kv_cols
            scores = matmul(
                qkv[block, head * HEAD_WIDTH : (head + 1) * HEAD_WIDTH],
                qkv[:reach, key_at : key_at + HEAD_WIDTH],
                ROWS_BY_ROWS,
            )
            scores = jnp.where(allowed, scores * SCORE_SCALE, LOW_SCORE)
            largest = jnp.max(scores, -1, keepdims=True)
            powers = jnp.exp(scores - largest)
            total = jnp.sum(powers, -1, keepdims=True)
            product = matmul(
                powers.astype(jnp.bfloat16), qkv[:reach, value_at : value_at + HEAD_WIDTH], ROWS_BY_COLS
            )
            outputs.append(product / total)
            totals = jnp.where(lanes == head, largest + jnp.log(total), totals)
        joined = jnp.concatenate(outputs, 1)
        attended[block, :] = joined
        log_total[block, :] = totals
        attended_all[here.z, block, :] = joined.astype(jnp.bfloat16)

    def mix_in(number):
        block = pl.ds(number * tok_rows, tok_rows)
        branch = matmul(attended_all[0, block, :], out_full[:, :q_cols], ROWS_BY_ROWS)
        for line in range(1, lines):
            branch = branch + matmul(
                attended_all[line, block, :], out_full[:, line * q_cols : (line + 1) * q_cols], ROWS_BY_ROWS
            )
        total = tokens_all[number].astype(jnp.float32) + branch
        lowered = (total * inverse_rms(total) * gain_expert).astype(jnp.bfloat16)
        expert_in[number] = lowered
        logits = matmul(lowered, weights[:, qkv_cols:], ROWS_BY_COLS)
        lane = lax.broadcasted_iota(jnp.int32, logits.shape, 1)
        logits = jnp.where(lane < EXPERT_COUNT, logits, LOW_SCORE)
        powers = jnp.exp(logits - jnp.max(logits, -1, keepdims=True))
        powers = jnp.where(lane < EXPERT_COUNT, powers, 0.0)
        probs[number] = powers / jnp.sum(powers, -1, keepdims=True)
        middle[number] = total

    attended_gathers = [
        LineSpread(
            here, lambda z, n=n: attended_all.at[z, pl.ds(n * tok_rows, tok_rows)], a_sends.at[n], a_recvs.at[n]
        )
        for n in range(lines)
    ]
    for turn in range(lines):
        attend(turn)
        attended_gathers[turn].start()
    for spread in expert_spreads[own_experts // 2 :]:
        spread.start()
    cot_gather.start()
    out_spread.turn()
    expert_spreads[0].chips()
    out_spread.cores()
    expert_spreads[1].chips()
    expert_spreads[0].turn()
    expert_spreads[0].cores()
    out_spread.finish()
    for number in range(lines):
        attended_gathers[number].finish()
        mix_in(number)
        if number == lines // 2:
            expert_spreads[1].turn()
    store(out_full, out_o)
    store(attended, attended_o)
    store(log_total, log_o)
    store(expert_in, expert_in_o)
    store(probs.at[here.z], probs_o)
    store(middle.at[here.z], middle_o)
    store(attended_all.at[:, pl.ds(pl.multiple_of(here.z * tok_rows, tok_rows), tok_rows)], attended_own_o)

    def gate_columns(number, e):
        chosen = padded_square(chosen_all[number].astype(jnp.float32))
        lane = lax.broadcasted_iota(jnp.int32, chosen.shape, 1)
        own = lane == here.z * own_experts + e
        picked = jnp.sum(jnp.where(own, chosen, 0.0), -1, keepdims=True)
        gate = jnp.sum(jnp.where(own, probs[number] * chosen, 0.0), -1, keepdims=True)
        return own, picked, gate

    pairs = [(a, a + 2) for a in range(0, lines, 2)]

    def expert_forward(e):
        for low, high in pairs:
            block = pl.ds(low * tok_rows, (high - low) * tok_rows)
            inputs = jnp.concatenate([expert_in[n] for n in range(low, high)], 0)
            linear = matmul(inputs, experts[e, :, : 2 * ff_width], ROWS_BY_COLS)
            gate_part, up_part = linear[:, :ff_width], linear[:, ff_width:]
            sigmoid = 1.0 / (1.0 + jnp.exp(-gate_part))
            silu = gate_part * sigmoid
            act = silu * up_part
            slopes[e, block, :ff_width] = up_part * (sigmoid * (1.0 + gate_part * (1.0 - sigmoid)))
            slopes[e, block, ff_width:] = silu
            acts[e, block, :] = act.astype(jnp.bfloat16)
            gate = jnp.concatenate([gate_columns(n, e)[2] for n in range(low, high)], 0)
            gated[e, block, :] = (gate * act).astype(jnp.bfloat16)

    chosen_swap.finish()
    expert_spreads[1].cores()
    expert_spreads[0].finish()
    expert_forward(0)
    expert_spreads[2].chips()
    expert_spreads[1].finish()
    expert_forward(1)
    expert_spreads[3].chips()
    expert_spreads[2].turn()
    expert_spreads[2].cores()
    expert_spreads[2].finish()
    expert_forward(2)
    expert_spreads[3].turn()
    expert_spreads[3].cores()
    expert_spreads[3].finish()
    expert_forward(3)
    store(gated, gated_o)

    for low, high in pairs:
        block = pl.ds(low * tok_rows, (high - low) * tok_rows)
        total = matmul(gated[0, block, :], experts[0, :, 2 * ff_width :], ROWS_BY_ROWS)
        for e in range(1, own_experts):
            total = total + matmul(gated[e, block, :], experts[e, :, 2 * ff_width :], ROWS_BY_ROWS)
        for n in range(low, high):
            part_mix[n] = total[(n - low) * tok_rows : (n - low + 1) * tok_rows, :].astype(jnp.bfloat16)
    store(part_mix, part_mix_o)

    cot_load.wait()
    cot_gather.finish()
    store(cot_all, cot_o)

    def expert_back(low):
        block = pl.ds(pl.multiple_of(low * tok_rows, 2 * tok_rows), 2 * tok_rows)
        grad_mid = jnp.concatenate([cot_all[low], cot_all[low + 1]], 0)
        total = None
        gate_cols = [jnp.zeros((tok_rows, LANES), jnp.float32)] * 2
        for e in range(own_experts):
            act_grad = matmul(grad_mid, experts[e, :, 2 * ff_width :], ROWS_BY_COLS)
            column = jnp.sum(act_grad * acts[e, block, :].astype(jnp.float32), -1, keepdims=True)
            gates = []
            for n in range(2):
                own, picked, gate = gate_columns(low + n, e)
                part = column[n * tok_rows : (n + 1) * tok_rows, :]
                gate_cols[n] = jnp.where(own, part * picked, gate_cols[n])
                gates.append(gate)
            act_grad = act_grad * jnp.concatenate(gates, 0)
            mid = jnp.concatenate(
                [act_grad * slopes[e, block, :ff_width], act_grad * slopes[e, block, ff_width:]], 1
            ).astype(jnp.bfloat16)
            mids[e, block, :] = mid
            term = matmul(mid, experts[e, :, : 2 * ff_width], ROWS_BY_ROWS)
            total = term if total is None else total + term
        for n in range(2):
            part_grad[low + n] = total[n * tok_rows : (n + 1) * tok_rows, :].astype(jnp.bfloat16)
            gate_grad[low + n] = gate_cols[n].T[:EXPERT_COUNT, :]

    for low in range(0, lines, 2):
        expert_back(low)
    store(mids, mids_o)
    store(part_grad, in_grad_o)
    store(gate_grad, gate_grad_o)
    for group_of in (
        [rows_spread, out_spread, chosen_swap, cot_gather] + token_gathers + expert_spreads + attended_gathers
    ):
        group_of.close()
    for copy in stores:
        copy.wait()


class Fold:
    def __init__(self, here, terms, crossed, landed, last, half, sends, recvs):
        self.here, self.terms, self.crossed = here, terms, crossed
        self.landed, self.last, self.half = landed, last, half
        self.sends, self.recvs = sends, recvs
        middle = here.lines // 2
        self.parts = [(0, middle), (middle, here.lines)]

    def start(self):
        here = self.here
        self.first = send(
            self.terms.at[:, here.other], self.crossed, self.sends.at[0], self.recvs.at[0], here.sibling()
        )

    def chips(self):
        here = self.here
        self.first.wait_recv()
        for chip in range(here.chips):
            self.terms[chip, here.core] = (
                self.terms[chip, here.core].astype(jnp.float32) + self.crossed[chip].astype(jnp.float32)
            ).astype(jnp.bfloat16)
        self.one, self.straight = [], []
        for number, near in enumerate((here.chip_x, here.chip_y)):
            low, high = self.parts[number]
            for slot, chip, group in ((1, here.chip_diag, self.one), (0, near, self.straight)):
                place = 1 + number * 2 + slot
                group.append(
                    send(
                        self.terms.at[chip, here.core, low:high], self.landed.at[number, slot],
                        self.sends.at[place], self.recvs.at[place], here.on_chip(near),
                    )
                )

    def turn(self):
        here = self.here
        self.two = []
        for number, onward in enumerate((here.chip_y, here.chip_x)):
            low, high = self.parts[number]
            self.one[number].wait_recv()
            self.terms[onward, here.core, low:high] = (
                self.terms[onward, here.core, low:high].astype(jnp.float32)
                + self.landed[number, 1].astype(jnp.float32)
            ).astype(jnp.bfloat16)
            place = 5 + number
            self.two.append(
                send(
                    self.terms.at[onward, here.core, low:high], self.last.at[number],
                    self.sends.at[place], self.recvs.at[place], here.on_chip(onward),
                )
            )

    def finish(self):
        here = self.here
        for number in range(2):
            low, high = self.parts[number]
            self.straight[number].wait_recv()
            self.two[number].wait_recv()
            self.half[low:high] = (
                self.terms[here.chip, here.core, low:high].astype(jnp.float32)
                + self.landed[number, 0].astype(jnp.float32)
                + self.last[number].astype(jnp.float32)
            ).astype(jnp.bfloat16)

    def close(self):
        for copy in [self.first] + self.one + self.straight + self.two:
            copy.wait_send()


def backward_kernel(
    prefix, cosine, sine_table, tokens_i, weights_i, out_i, cot_i, att_in_i, qkv_i, attended_i, log_i, attended_own_i,
    expert_in_i, probs_i, middle_i, mids_i, gated_i, in_grad_i, gate_grad_i, part_mix_i,
    mixed_o, tokens_grad_o, query_o, key_o, value_o, out_o, attention_gain_o, expert_gain_o, router_o, expert_o,
    tokens_all, weights, out_full, cot_all, att_in, qkv, attended, log_total, attended_own, expert_in, probs, middle,
    mids, gated, in_grad, gate_grad, got_grad, got_gate, grad_res, attended_grad, attended_grad_all, joined_grad,
    key_sum, value_sum, in_part, got_part, part_mix, got_mix, mixed, tokens_grad,
    e_terms, e_crossed, e_landed, e_last, e_half, e_lines,
    o_terms, o_crossed, o_landed, o_last, o_half, o_lines,
    q_terms, q_crossed, q_landed, q_last, q_half, q_lines,
    query_s, key_s, value_s, out_s, attention_gain_s, expert_gain_s, router_s,
    load_sem, mid_sem, x_sends, x_recvs, g_sends, g_recvs, b_sends, b_recvs, p_sends, p_recvs,
    e_sends, e_recvs, o_sends, o_recvs, q_sends, q_recvs, el_sends, el_recvs, ol_sends, ol_recvs, ql_sends, ql_recvs, m_sends, m_recvs, out_sem,
):
    here = Place()
    lines, chips = here.lines, here.chips
    tok_rows, width = tokens_all.shape[1:]
    rows_all = lines * tok_rows
    depth = e_terms.shape[4]
    own_experts = e_terms.shape[0]
    ff_width = e_terms.shape[5] // 3
    qkv_cols = qkv.shape[1]
    kv_cols = qkv_cols // 4
    q_cols = 2 * kv_cols
    query_width = lines * q_cols
    five = (chips, 2, lines, depth)

    def slot_loads(e):
        return [
            move(mids_i.at[e], mids.at[e % 2], mid_sem.at[0, e % 2]),
            move(gated_i.at[e], gated.at[e % 2], mid_sem.at[1, e % 2]),
        ]

    loads = {}

    def load(name, source, target):
        loads[name] = move(source, target, load_sem.at[len(loads)])

    load("in_grad", in_grad_i, in_grad)
    load("expert_in", expert_in_i, expert_in)
    load("cot", cot_i, cot_all)
    slots = [slot_loads(0), slot_loads(1)]
    load("gate", gate_grad_i, gate_grad)
    load("probs", probs_i, probs)
    load("middle", middle_i, middle)
    load("weights", weights_i, weights)
    load("out", out_i, out_full)
    load("own", attended_own_i, attended_own)
    load("mix", part_mix_i, part_mix)
    load("tokens", tokens_i, tokens_all)
    load("att_in", att_in_i, att_in)
    load("qkv", qkv_i, qkv)
    load("attended", attended_i, attended)
    load("log", log_i, log_total)
    meet(all_peers(here))
    grad_swap = LineSum(here, in_grad, got_grad, x_sends, x_recvs)
    gate_swap = LineSwap(here, lambda z: gate_grad_i.at[z], lambda k, z: got_gate.at[k - 1], g_sends, g_recvs)
    attended_swap = LineSwap(
        here, lambda z: attended_grad.at[z], lambda k, z: attended_grad_all.at[z], b_sends, b_recvs
    )
    part_swap = LineSum(here, in_part, got_part, p_sends, p_recvs)
    mix_swap = LineSum(here, part_mix, got_mix, m_sends, m_recvs)
    folds = [
        Fold(
            here, e_terms.at[e], e_crossed.at[e], e_landed.at[e], e_last.at[e], e_half.at[e], e_sends.at[e], e_recvs.at[e]
        )
        for e in range(own_experts)
    ]
    out_fold = Fold(here, o_terms, o_crossed, o_landed, o_last, o_half, o_sends, o_recvs)
    qkv_fold = Fold(here, q_terms, q_crossed, q_landed, q_last, q_half, q_sends, q_recvs)
    expert_swaps = [
        LineSwap(
            here, lambda z, e=e: e_half.at[e, z], lambda k, z, e=e: e_lines.at[z, e], el_sends.at[e], el_recvs.at[e]
        )
        for e in range(own_experts)
    ]
    out_swap = LineSwap(here, lambda z: o_half.at[z], lambda k, z: o_lines.at[k - 1], ol_sends, ol_recvs)
    qkv_swap = LineSwap(here, lambda z: q_half.at[z], lambda k, z: q_lines.at[z], ql_sends, ql_recvs)

    loads["in_grad"].wait()
    grad_swap.step(lines - 1)
    gate_swap.start()
    loads["expert_in"].wait()
    loads["cot"].wait()
    for e in range(own_experts):
        for copy in slots[e % 2]:
            copy.wait()
        e_terms[e, ..., : 2 * ff_width] = (
            matmul(expert_in[...].reshape(rows_all, width), mids[e % 2], COLS_BY_COLS)
            .astype(jnp.bfloat16)
            .reshape(*five, 2 * ff_width)
        )
        e_terms[e, ..., 2 * ff_width :] = (
            matmul(cot_all[...].reshape(rows_all, width), gated[e % 2], COLS_BY_COLS)
            .astype(jnp.bfloat16)
            .reshape(*five, ff_width)
        )
        if e + 2 < own_experts:
            slots[e % 2] = slot_loads(e + 2)
        folds[e].start()
        if 1 <= lines - 2 - e:
            grad_swap.step(lines - 2 - e)
        if e == 1:
            folds[0].chips()

    for name in ("gate", "probs", "middle", "weights", "out", "own"):
        loads[name].wait()
    folds[0].turn()
    folds[1].chips()
    gate_swap.finish()
    grad_swap.finish(grad_res)
    gate_rows = gate_grad[here.z]
    for k in range(lines - 1):
        gate_rows = gate_rows + got_gate[k]
    gates = padded_square(gate_rows)
    grad = grad_res[...]
    columns = weights[:, qkv_cols:].astype(jnp.float32).T
    gain_attention = columns[EXPERT_COUNT : EXPERT_COUNT + 1, :]
    gain_expert = columns[EXPERT_COUNT + 1 : EXPERT_COUNT + 2, :]
    prob = probs[...]
    logit_grad = (prob * (gates - jnp.sum(prob * gates, -1, keepdims=True))).astype(jnp.bfloat16)
    grad = grad + matmul(logit_grad, weights[:, qkv_cols:], ROWS_BY_ROWS)
    hidden = middle[...]
    inverse = inverse_rms(hidden)
    normed = hidden * inverse
    scaled = grad * gain_expert
    result = cot_all[here.z].astype(jnp.float32) + inverse * (
        scaled - normed * jnp.mean(scaled * normed, -1, keepdims=True)
    )
    grad_res[...] = result
    branch = result.astype(jnp.bfloat16)
    for line in range(lines):
        attended_grad[line] = matmul(
            branch, out_full[:, line * q_cols : (line + 1) * q_cols], ROWS_BY_COLS
        ).astype(jnp.bfloat16)
    attended_swap.start()
    loads["mix"].wait()
    mix_swap.step(lines - 1)
    folds[0].finish()
    expert_swaps[0].start()
    attended_grad_all[here.z] = attended_grad[here.z]
    router_term = matmul(expert_in[here.z], logit_grad, COLS_BY_COLS)
    gain_term = split_sum_columns(grad * normed)
    lane = lax.broadcasted_iota(jnp.int32, router_term.shape, 1)
    for line in range(lines):
        o_terms[..., line * q_cols : (line + 1) * q_cols] = (
            matmul(branch, attended_own[line], COLS_BY_COLS).astype(jnp.bfloat16).reshape(*five, q_cols)
        )
    o_terms[..., query_width:] = (
        jnp.where(lane == EXPERT_COUNT, gain_term, router_term).astype(jnp.bfloat16).reshape(*five, LANES)
    )
    out_fold.start()
    for name in ("tokens", "att_in", "qkv", "attended", "log"):
        loads[name].wait()
    folds[1].turn()
    folds[2].chips()
    attended_swap.finish()
    for hops in range(lines - 2, 1, -1):
        mix_swap.step(hops)

    prefix_end = prefix[0]
    heads = q_cols // HEAD_WIDTH
    group = q_cols // kv_cols
    key_sum[...] = jnp.zeros_like(key_sum)
    value_sum[...] = jnp.zeros_like(value_sum)

    def attend_back(number):
        start = number * tok_rows
        block = pl.ds(start, tok_rows)
        reach = max(rows_all // 2, start + tok_rows)
        query_place = start + lax.broadcasted_iota(jnp.int32, (tok_rows, reach), 0)
        key_place = lax.broadcasted_iota(jnp.int32, (tok_rows, reach), 1)
        allowed = (key_place <= query_place) | (key_place < prefix_end)
        query_grads = []
        for head in range(heads):
            own = slice(head * HEAD_WIDTH, (head + 1) * HEAD_WIDTH)
            low = head // group * HEAD_WIDTH
            shared = slice(low, low + HEAD_WIDTH)
            query = qkv[block, own]
            key = qkv[:reach, q_cols + low : q_cols + low + HEAD_WIDTH]
            value = qkv[:reach, q_cols + kv_cols + low : q_cols + kv_cols + low + HEAD_WIDTH]
            grad = attended_grad_all[number, :, own]
            scores = matmul(query, key, ROWS_BY_ROWS) * SCORE_SCALE
            prob = jnp.where(allowed, jnp.exp(scores - log_total[block, head : head + 1]), 0.0)
            delta = jnp.sum(grad.astype(jnp.float32) * attended[block, own], -1, keepdims=True)
            prob_part = matmul(grad, value, ROWS_BY_ROWS)
            score_grad = (prob * (prob_part - delta)).astype(jnp.bfloat16)
            value_sum[:reach, shared] = value_sum[:reach, shared] + matmul(
                prob.astype(jnp.bfloat16), grad, COLS_BY_COLS
            )
            key_sum[:reach, shared] = key_sum[:reach, shared] + matmul(score_grad, query, COLS_BY_COLS)
            query_grads.append(matmul(score_grad, key, ROWS_BY_COLS))
        query_grad = jnp.concatenate(query_grads, 1) * SCORE_SCALE
        joined_grad[block, :q_cols] = spin(query_grad, cosine[block, :], -sine_table[block, :]).astype(
            jnp.bfloat16
        )

    for number in range(lines):
        attend_back(number)
        if number == lines - 2:
            folds[1].finish()
            expert_swaps[1].start()
    folds[2].turn()
    folds[3].chips()
    joined_grad[:, q_cols : q_cols + kv_cols] = spin(
        key_sum[...] * SCORE_SCALE, cosine[...], -sine_table[...]
    ).astype(jnp.bfloat16)
    joined_grad[:, q_cols + kv_cols :] = value_sum[...].astype(jnp.bfloat16)
    gain_term = jnp.zeros((width, LANES), jnp.float32)
    for number in range(lines):
        block = pl.ds(number * tok_rows, tok_rows)
        hidden = tokens_all[number].astype(jnp.float32)
        normed = hidden * inverse_rms(hidden)
        part = matmul(joined_grad[block, :], weights[:, :qkv_cols], ROWS_BY_ROWS)
        in_part[number] = part.astype(jnp.bfloat16)
        gain_term = gain_term + split_sum_columns(part * normed)
    part_swap.step(lines - 1)
    q_terms[..., :qkv_cols] = (
        matmul(att_in[...], joined_grad[...], COLS_BY_COLS).astype(jnp.bfloat16).reshape(*five, qkv_cols)
    )
    q_terms[..., qkv_cols:] = gain_term.astype(jnp.bfloat16).reshape(*five, LANES)
    qkv_fold.start()
    mix_swap.step(1)
    out_fold.chips()
    qkv_fold.chips()
    folds[2].finish()
    expert_swaps[2].start()
    for hops in range(lines - 2, 1, -1):
        part_swap.step(hops)
    folds[3].turn()
    out_fold.turn()
    qkv_fold.turn()
    part_swap.step(1)
    folds[3].finish()
    expert_swaps[3].start()
    out_fold.finish()
    out_swap.start()
    qkv_fold.finish()
    qkv_swap.start()

    stores = []

    def store(source, target):
        stores.append(move(source, target, out_sem.at[len(stores)]))

    mix_swap.finish(tokens_grad)
    mixed[...] = (tokens_grad[...] + middle[...]).astype(jnp.bfloat16)
    store(mixed, mixed_o)
    part_swap.finish(tokens_grad)
    hidden = tokens_all[here.z].astype(jnp.float32)
    inverse = inverse_rms(hidden)
    normed = hidden * inverse
    scaled = tokens_grad[...] * gain_attention
    tokens_grad[...] = grad_res[...] + inverse * (
        scaled - normed * jnp.mean(scaled * normed, -1, keepdims=True)
    )
    store(tokens_grad, tokens_grad_o)
    out_swap.finish()
    total = o_half[here.z].astype(jnp.float32)
    for k in range(lines - 1):
        total = total + o_lines[k].astype(jnp.float32)
    out_s[...] = total[:, :query_width]
    tail = padded_square(total[:, query_width:])
    router_s[...] = tail[:EXPERT_COUNT, :depth]
    expert_gain_s[...] = tail[EXPERT_COUNT : EXPERT_COUNT + 1, :depth]
    store(out_s, out_o)
    store(router_s, router_o)
    store(expert_gain_s, expert_gain_o)
    q_lines[here.z] = q_half[here.z]
    qkv_swap.finish()
    gain_columns = jnp.zeros((depth, LANES), jnp.float32)
    for line in range(lines):
        query_s[:, line * q_cols : (line + 1) * q_cols] = q_lines[line, :, :q_cols].astype(jnp.float32)
        key_s[:, line * kv_cols : (line + 1) * kv_cols] = q_lines[line, :, q_cols : q_cols + kv_cols].astype(
            jnp.float32
        )
        value_s[:, line * kv_cols : (line + 1) * kv_cols] = q_lines[line, :, q_cols + kv_cols : qkv_cols].astype(
            jnp.float32
        )
        gain_columns = gain_columns + q_lines[line, :, qkv_cols:].astype(jnp.float32)
    attention_gain_s[...] = padded_square(gain_columns)[:1, :depth]
    store(query_s, query_o)
    store(key_s, key_o)
    store(value_s, value_o)
    store(attention_gain_s, attention_gain_o)
    for e in range(own_experts):
        e_lines[here.z, e] = e_half[e, here.z]
        expert_swaps[e].finish()
    store(e_lines, expert_o)
    for group_of in (
        [grad_swap, gate_swap, attended_swap, part_swap, mix_swap, out_swap, qkv_swap, out_fold, qkv_fold] + folds + expert_swaps
    ):
        group_of.close()
    for copy in stores:
        copy.wait()


def deliver_kernel(*refs):
    count = (len(refs) - 4) // 3
    sources, targets, held = refs[:count], refs[count : 2 * count + 1], refs[2 * count + 1 : 3 * count + 1]
    gate_up, down, sems = refs[3 * count + 1 :]
    loads = [move(sources[n], held[n], sems.at[0, n]) for n in range(count)]
    stores = []
    depth, expert_count = gate_up.shape[:2]
    order = row_order(depth, expert_count, False)
    loads[count - 1].wait()
    rows = held[count - 1][...].reshape(expert_count * depth, gate_up.shape[2] + down.shape[2])
    gate_up[...] = matmul(order, rows[:, : gate_up.shape[2]], ROWS_BY_COLS).reshape(gate_up.shape)
    stores.append(move(gate_up, targets[count - 1], sems.at[1, count - 1]))
    down[...] = matmul(order, rows[:, gate_up.shape[2] :], ROWS_BY_COLS).reshape(down.shape)
    stores.append(move(down, targets[count], sems.at[1, count]))
    for n in range(count - 1):
        loads[n].wait()
        stores.append(move(held[n], targets[n], sems.at[1, n]))
    for copy in stores:
        copy.wait()


def fast_device(
    tokens, prefix_len, routes, cotangent, query_matrix, key_matrix, value_matrix, output_matrix,
    attention_gain, expert_gain, router_matrix, gate_up_weight, down_weight,
):
    lines = lax.axis_size("seq")
    chips = lax.axis_size("dp") // 2
    tok_rows, width = tokens.shape[1:]
    rows_all = lines * tok_rows
    depth = query_matrix.shape[0]
    query_width, key_width = query_matrix.shape[1], key_matrix.shape[1]
    q_cols, kv_cols = query_width // lines, key_width // lines
    qkv_cols = q_cols + 2 * kv_cols
    expert_count = router_matrix.shape[1]
    own_experts = expert_count // lines
    ff_width = down_weight.shape[2]
    all_ff = 3 * ff_width
    row_cols = qkv_cols + LANES
    out_cols = query_width + LANES
    half_dim = HEAD_WIDTH // 2
    low, full = jnp.bfloat16, jnp.float32

    places = np.arange(rows_all, dtype=np.float32)
    frequency = np.exp(
        np.arange(half_dim, dtype=np.float32) * np.float32(-2.0 * math.log(10000.0) / HEAD_WIDTH)
    ).astype(np.float32)
    angles = places[:, None] * frequency[None, :]
    cosine = jnp.asarray(np.tile(np.cos(angles), (1, LANES // half_dim)), jnp.float32)
    sine_table = jnp.asarray(np.tile(np.sin(angles), (1, LANES // half_dim)), jnp.float32)

    count = spread_count(lines)

    def scratch(*dims, kind=low):
        return pltpu.VMEM(dims, kind)

    def pair(*dims):
        return [pltpu.SemaphoreType.DMA(dims)] * 2

    DMA = pltpu.SemaphoreType.DMA
    by_token = (lines, tok_rows)
    kept = [
        ((*by_token, width), low), ((width, row_cols), low), ((width, query_width), low), ((*by_token, width), low),
        ((rows_all, width), low), ((rows_all, qkv_cols), low), ((rows_all, q_cols), full), ((rows_all, LANES), full),
        ((*by_token, q_cols), low), ((*by_token, width), low), ((tok_rows, LANES), full), ((tok_rows, width), full),
        ((own_experts, rows_all, 2 * ff_width), low), ((own_experts, rows_all, ff_width), low), ((*by_token, width), low),
        ((lines, expert_count, tok_rows), full),
    ]
    results = pl.pallas_call(
        forward_kernel,
        name="forward",
        out_shape=tuple(jax.ShapeDtypeStruct(dims, kind) for dims, kind in [((*by_token, width), low)] + kept),
        in_specs=[SMEM_SPEC, ANY_SPEC] + [VMEM_SPEC] * 3 + [ANY_SPEC] + [VMEM_SPEC] * 3 + [ANY_SPEC] * 3 + [VMEM_SPEC] * 3,
        out_specs=(ANY_SPEC,) * (len(kept) + 1),
        scratch_shapes=[
            scratch(depth, expert_count, 2 * ff_width), scratch(depth, expert_count, ff_width), scratch(LANES, LANES, kind=full),
            scratch(lines, depth, row_cols), scratch(expert_count * depth, all_ff),
            scratch(*by_token, width), scratch(width, row_cols), scratch(width, query_width),
            scratch(own_experts, width, all_ff), scratch(*by_token, width), scratch(lines, expert_count, tok_rows),
            scratch(rows_all, width), scratch(rows_all, qkv_cols), scratch(rows_all, q_cols, kind=full),
            scratch(lines, rows_all, q_cols), scratch(rows_all, LANES, kind=full), scratch(*by_token, width),
            scratch(*by_token, LANES, kind=full), scratch(*by_token, width, kind=full),
            scratch(own_experts, rows_all, 2 * ff_width, kind=full), scratch(own_experts, rows_all, ff_width),
            scratch(own_experts, rows_all, ff_width), scratch(own_experts, rows_all, 2 * ff_width),
            scratch(*by_token, width), scratch(*by_token, width), scratch(lines, expert_count, tok_rows, kind=full),
            DMA((6 + own_experts,)),
            *pair(count), *pair(count), *pair(own_experts, count), *pair(2, 2, lines - 1), *pair(lines), *pair(lines),
            *pair(lines, lines), DMA((len(kept) + 1,)),
        ],
        compiler_params=comm_params(1, 63),
    )(
        prefix_len, tokens[0], query_matrix, key_matrix, value_matrix, output_matrix, router_matrix.T,
        attention_gain.reshape(1, depth), expert_gain.reshape(1, depth), gate_up_weight, down_weight, cotangent[0], routes[0].T,
        cosine, sine_table,
    )
    five = (chips, 2, lines, depth)
    four = (chips, lines, depth)
    landed = (2, 2, lines // 2, depth)
    last = (2, lines // 2, depth)
    ends = [
        ((tok_rows, width), low), ((tok_rows, width), full), ((depth, query_width), full), ((depth, key_width), full),
        ((depth, key_width), full), ((depth, query_width), full), ((1, depth), full), ((1, depth), full), ((expert_count, depth), full),
        ((lines, own_experts, depth, all_ff), low),
    ]

    def fold_scratch(cols, lead=()):
        return [
            scratch(*lead, *dims, cols) for dims in (five, four, landed, last, (lines, depth))
        ]

    results = pl.pallas_call(
        backward_kernel,
        name="backward",
        out_shape=tuple(jax.ShapeDtypeStruct(dims, kind) for dims, kind in ends),
        in_specs=[SMEM_SPEC] + [VMEM_SPEC] * 2 + [ANY_SPEC] * (len(kept) + 1),
        out_specs=(ANY_SPEC,) * len(ends),
        scratch_shapes=[
            pltpu.VMEM(dims, kind) for dims, kind in kept[:12]
        ] + [
            scratch(2, rows_all, 2 * ff_width), scratch(2, rows_all, ff_width),
            scratch(*by_token, width), scratch(lines, expert_count, tok_rows, kind=full),
            scratch(2, lines - 1, tok_rows, width), scratch(lines - 1, expert_count, tok_rows, kind=full),
            scratch(tok_rows, width, kind=full),
            scratch(*by_token, q_cols), scratch(*by_token, q_cols), scratch(rows_all, qkv_cols),
            scratch(rows_all, kv_cols, kind=full), scratch(rows_all, kv_cols, kind=full),
            scratch(*by_token, width), scratch(2, lines - 1, tok_rows, width),
            scratch(*by_token, width), scratch(2, lines - 1, tok_rows, width), scratch(tok_rows, width), scratch(tok_rows, width, kind=full),
            *fold_scratch(all_ff, (own_experts,)), scratch(lines, own_experts, depth, all_ff),
            *fold_scratch(out_cols), scratch(lines - 1, depth, out_cols),
            *fold_scratch(row_cols), scratch(lines, depth, row_cols),
            *[scratch(*dims, kind=kind) for dims, kind in ends[2:-1]],
            DMA((len(kept) + 1,)), DMA((2, 2)), *pair(2, lines - 1), *pair(lines), *pair(lines), *pair(2, lines - 1),
            *pair(own_experts, 7), *pair(7), *pair(7), *pair(own_experts, lines), *pair(lines), *pair(lines), *pair(2, lines - 1), DMA((len(ends),)),
        ],
        compiler_params=comm_params(2, 63),
    )(prefix_len, cosine, sine_table, *results[1:], results[0])
    last_ends = [((depth, expert_count, 2 * ff_width), full), ((depth, expert_count, ff_width), full)]
    results = pl.pallas_call(
        deliver_kernel,
        name="deliver",
        out_shape=tuple(jax.ShapeDtypeStruct(dims, kind) for dims, kind in ends[:-1] + last_ends),
        in_specs=[ANY_SPEC] * len(ends),
        out_specs=(ANY_SPEC,) * (len(ends) + 1),
        scratch_shapes=[pltpu.VMEM(dims, kind) for dims, kind in ends + last_ends] + [DMA((2, len(ends) + 1))],
        compiler_params=pltpu.CompilerParams(vmem_limit_bytes=63 << 20),
    )(*results)
    mixed, tokens_grad, query_grad, key_grad, value_grad, out_grad, attention_gain_grad, expert_gain_grad, router_grad, gate_up_grad, down_grad = results
    return (
        mixed[None],
        tokens_grad[None],
        query_grad,
        key_grad,
        value_grad,
        out_grad,
        attention_gain_grad.reshape(depth),
        expert_gain_grad.reshape(depth),
        router_grad.T,
        gate_up_grad,
        down_grad,
    )


def solution(mesh):
    lines, chips = mesh.shape["seq"], mesh.shape["dp"] // 2
    even = KEY_HEADS % (2 * lines) == 0 and EXPERT_COUNT % lines == 0 and chips == 4
    return jax.shard_map(
        fast_device if even else per_device,
        mesh=mesh,
        in_specs=(
            P("dp", "seq", None),
            P("dp"),
            P("dp", "seq", None),
            P("dp", "seq", None),
            P(("dp", "seq"), None),
            P(("dp", "seq"), None),
            P(("dp", "seq"), None),
            P(("dp", "seq"), None),
            P(("dp", "seq")),
            P(("dp", "seq")),
            P(("dp", "seq"), None),
            P(("dp", "seq"), None, None),
            P(("dp", "seq"), None, None),
        ),
        out_specs=(
            P("dp", "seq", None),
            P("dp", "seq", None),
            P(("dp", "seq"), None),
            P(("dp", "seq"), None),
            P(("dp", "seq"), None),
            P(("dp", "seq"), None),
            P(("dp", "seq")),
            P(("dp", "seq")),
            P(("dp", "seq"), None),
            P(("dp", "seq"), None, None),
            P(("dp", "seq"), None, None),
        ),
        check_vma=False,
    )
```

```python
import math

import jax
import jax.numpy as jnp
import numpy as np
from jax import lax
from jax.experimental import pallas as pl
from jax.experimental.pallas import tpu as pltpu
from jax.sharding import PartitionSpec as P

HEAD_WIDTH = 64
CAPACITY = 96


NORM_EPS = 1e-06
LOW_SCORE = -1e30
LANES = 128
HALF = HEAD_WIDTH // 2
SCORE_SCALE = HEAD_WIDTH ** (-0.5)
EXPERT_COUNT = 16
KEY_HEADS = 8
MESH = pl.DeviceIdType.MESH


def rotary_tables(positions, head_dim):
    half_dim = head_dim // 2
    frequency = jnp.exp(
        jnp.arange(half_dim, dtype=jnp.float32) * (-2.0 * math.log(10000.0) / head_dim)
    )
    angles = positions.astype(jnp.float32)[:, None] * frequency[None, :]
    return (jnp.cos(angles), jnp.sin(angles))


def rotate(value_rows, cosine, sine_table):
    half_dim = value_rows.shape[-1] // 2
    first_half = value_rows[..., :half_dim]
    second = value_rows[..., half_dim:]
    cos_heads = cosine[:, None, :]
    sin_heads = sine_table[:, None, :]
    return jnp.concatenate(
        [first_half * cos_heads - second * sin_heads, second * cos_heads + first_half * sin_heads],
        axis=-1,
    )


def norm_back(grad_normed, normed, inverse):
    return inverse * (grad_normed - normed * jnp.mean(grad_normed * normed, -1, keepdims=True))


def keep_state(running):
    return running


def swiglu(mid_linear, ff_width):
    return (jax.nn.silu(mid_linear[..., :ff_width]) * mid_linear[..., ff_width:]).astype(
        jnp.bfloat16
    )


def swiglu_back(act_grad, mid_linear, ff_width):
    gate_part = mid_linear[..., :ff_width]
    up_part = mid_linear[..., ff_width:]
    sigmoid = jax.nn.sigmoid(gate_part)
    gate_slope = sigmoid * (1.0 + gate_part * (1.0 - sigmoid))
    return jnp.concatenate(
        [act_grad * up_part * gate_slope, act_grad * gate_part * sigmoid], axis=-1
    ).astype(jnp.bfloat16)


def over_key_blocks(pieces, block_fn, running):
    piece_rows = pieces[0].shape[0]
    block_size = math.gcd(piece_rows, 512)
    shaped = tuple(
        (piece.reshape(piece_rows // block_size, block_size, piece.shape[1]) for piece in pieces)
    )
    offsets = block_size * jnp.arange(piece_rows // block_size, dtype=jnp.int32)

    def advance(carried, block_item):
        return (block_fn(carried, block_item[0], block_item[1], block_item[2]), None)

    result_state, unused = lax.scan(advance, running, (shaped[0], shaped[1], offsets))
    return result_state


def per_device(
    tokens,
    prefix_len,
    routes,
    cotangent,
    query_matrix,
    key_matrix,
    value_matrix,
    output_matrix,
    attention_gain,
    expert_gain,
    router_matrix,
    gate_up_weight,
    down_weight,
):
    hidden = tokens[0].astype(jnp.float32)
    tok_rows, model_width = hidden.shape
    params = (
        lax.all_gather(query_matrix, ("dp", "seq"), axis=0, tiled=True),
        lax.all_gather(key_matrix, ("dp", "seq"), axis=0, tiled=True),
        lax.all_gather(value_matrix, ("dp", "seq"), axis=0, tiled=True),
        lax.all_gather(output_matrix, ("dp", "seq"), axis=0, tiled=True),
        lax.all_gather(attention_gain, ("dp", "seq"), axis=0, tiled=True),
        lax.all_gather(expert_gain, ("dp", "seq"), axis=0, tiled=True),
        lax.all_gather(router_matrix, ("dp", "seq"), axis=0, tiled=True),
    )
    query_full, key_full, value_full, output_full, gain_attention, gain_expert, router_full = params
    head_dim = HEAD_WIDTH
    query_width = query_full.shape[1]
    key_width = key_full.shape[1]
    query_heads = query_width // head_dim
    key_groups = key_width // head_dim
    head_group = query_heads // key_groups
    score_scale = head_dim ** (-0.5)
    first_place = lax.axis_index("seq") * tok_rows
    positions = first_place + jnp.arange(tok_rows, dtype=jnp.int32)
    last_place = first_place + tok_rows - 1
    prefix_end = prefix_len[0]
    cosine, sine_table = rotary_tables(positions, head_dim)
    inverse_attention = lax.rsqrt(jnp.mean(hidden * hidden, -1, keepdims=True) + NORM_EPS)
    normed_attention = hidden * inverse_attention
    attention_input = (normed_attention * gain_attention.astype(jnp.float32)).astype(jnp.bfloat16)
    query_projected = jnp.dot(
        attention_input, query_full, preferred_element_type=jnp.float32
    ).reshape(tok_rows, query_heads, head_dim)
    queries = (
        rotate(query_projected, cosine, sine_table)
        .astype(jnp.bfloat16)
        .reshape(tok_rows, key_groups, head_group, head_dim)
    )
    key_projected = jnp.dot(attention_input, key_full, preferred_element_type=jnp.float32).reshape(
        tok_rows, key_groups, head_dim
    )
    keys_local = (
        rotate(key_projected, cosine, sine_table).astype(jnp.bfloat16).reshape(tok_rows, key_width)
    )
    values_local = jnp.dot(attention_input, value_full, preferred_element_type=jnp.float32).astype(
        jnp.bfloat16
    )

    def block_scores(key_block, key_start):
        block_size = key_block.shape[0]
        key_heads = key_block.reshape(block_size, key_groups, head_dim)
        key_places = key_start + jnp.arange(block_size, dtype=jnp.int32)
        allowed = (key_places[None, :] <= positions[:, None]) | (key_places[None, :] < prefix_end)
        scores = (
            jnp.einsum("qhgd,khd->hgqk", queries, key_heads, preferred_element_type=jnp.float32)
            * score_scale
        )
        return (jnp.where(allowed, scores, -jnp.inf), key_heads)

    def attend(running, key_block, value_block, key_start):

        def compute(carried):
            run_max, run_sum, weighted = carried
            scores, key_heads = block_scores(key_block, key_start)
            value_heads = value_block.reshape(key_block.shape[0], key_groups, head_dim)
            new_max = jnp.maximum(run_max, jnp.max(scores, -1))
            weights = jnp.exp(scores - new_max[..., None])
            factor = jnp.exp(run_max - new_max)
            new_sum = run_sum * factor + jnp.sum(weights, -1)
            new_weighted = weighted * factor[..., None] + jnp.einsum(
                "hgqk,khd->hgqd",
                weights.astype(jnp.bfloat16),
                value_heads,
                preferred_element_type=jnp.float32,
            )
            return (new_max, new_sum, new_weighted)

        visible = (key_start <= last_place) | (key_start < prefix_end)
        return lax.cond(visible, compute, keep_state, running)

    stat_shape = (key_groups, head_group, tok_rows)
    start_state = (
        jnp.full(stat_shape, LOW_SCORE, jnp.float32),
        jnp.zeros(stat_shape, jnp.float32),
        jnp.zeros(stat_shape + (head_dim,), jnp.float32),
    )
    run_max, run_sum, weighted = over_key_blocks(
        (
            lax.all_gather(keys_local, "seq", axis=0, tiled=True),
            lax.all_gather(values_local, "seq", axis=0, tiled=True),
        ),
        attend,
        start_state,
    )
    log_total = run_max + jnp.log(run_sum)
    attended_heads = weighted / run_sum[..., None]
    attention_lowered = (
        attended_heads.transpose(2, 0, 1, 3).reshape(tok_rows, query_width).astype(jnp.bfloat16)
    )
    branch_output = jnp.einsum(
        "tc,dc->td", attention_lowered, output_full, preferred_element_type=jnp.float32
    )
    middle = hidden + branch_output
    inverse_expert = lax.rsqrt(jnp.mean(middle * middle, -1, keepdims=True) + NORM_EPS)
    normed_expert = middle * inverse_expert
    expert_input = (normed_expert * gain_expert.astype(jnp.float32)).astype(jnp.bfloat16)
    router_logits = jnp.dot(expert_input, router_full, preferred_element_type=jnp.float32)
    router_probs = jax.nn.softmax(router_logits, axis=-1)
    expert_count = router_full.shape[1]
    route_ids = routes[0]
    expert_range = jnp.arange(expert_count, dtype=jnp.int32)
    route_hits = jnp.sum(
        (route_ids[:, :, None] == expert_range[None, None, :]).astype(jnp.int32), 1
    )
    slot_rank = jnp.cumsum(route_hits, 0) - 1
    slot_target = jnp.where(route_hits > 0, slot_rank, CAPACITY)
    token_index = jnp.broadcast_to(
        jnp.arange(tok_rows, dtype=jnp.int32)[:, None], (tok_rows, expert_count)
    )
    expert_index = jnp.broadcast_to(expert_range[None, :], (tok_rows, expert_count))
    slot_table = (
        jnp.zeros((expert_count, CAPACITY), jnp.int32)
        .at[expert_index, slot_target]
        .set(token_index, mode="drop")
    )
    slot_live = jnp.arange(CAPACITY, dtype=jnp.int32)[None, :] < jnp.sum(route_hits, 0)[:, None]
    expert_column = expert_range[:, None]
    dispatched = expert_input[slot_table]
    slot_gates = jnp.where(slot_live, router_probs[slot_table, expert_column], 0.0)
    ff_width = down_weight.shape[2]
    grad_mid = cotangent[0].astype(jnp.float32)
    slot_grad = grad_mid[slot_table]
    out_grad = (slot_gates[..., None] * slot_grad).astype(jnp.bfloat16)
    gate_up_full, down_full = (
        lax.all_gather(gate_up_weight, ("dp", "seq"), axis=0, tiled=True),
        lax.all_gather(down_weight, ("dp", "seq"), axis=0, tiled=True),
    )
    mid_linear = jnp.einsum(
        "ecd,def->ecf", dispatched, gate_up_full, preferred_element_type=jnp.float32
    )
    activation = swiglu(mid_linear, ff_width)
    expert_out = jnp.einsum(
        "ecf,def->ecd", activation, down_full, preferred_element_type=jnp.float32
    )
    flat_slots = slot_table.reshape(-1)
    combined = (
        jnp.zeros((tok_rows, model_width), jnp.float32)
        .at[flat_slots]
        .add((slot_gates[..., None] * expert_out).reshape(-1, model_width))
    )
    mixed = (middle + combined).astype(jnp.bfloat16)
    gate_grad = jnp.where(slot_live, jnp.sum(expert_out * slot_grad, -1), 0.0)
    act_grad = jnp.einsum("ecd,def->ecf", out_grad, down_full, preferred_element_type=jnp.float32)
    mid_grad = swiglu_back(act_grad, mid_linear, ff_width)
    gate_up_term = jnp.einsum(
        "ecd,ecf->def", dispatched, mid_grad, preferred_element_type=jnp.float32
    )
    down_term = jnp.einsum("ecd,ecf->def", out_grad, activation, preferred_element_type=jnp.float32)
    summed_terms = lax.psum_scatter(
        jnp.concatenate([gate_up_term, down_term], axis=-1),
        ("dp", "seq"),
        scatter_dimension=0,
        tiled=True,
    )
    gate_up_weight_grad = summed_terms[..., : 2 * ff_width]
    down_weight_grad = summed_terms[..., 2 * ff_width :]
    dispatched_grad = jnp.einsum(
        "ecf,def->ecd", mid_grad, gate_up_full, preferred_element_type=jnp.float32
    )
    expert_in_grad = (
        jnp.zeros((tok_rows, model_width), jnp.float32)
        .at[flat_slots]
        .add(dispatched_grad.reshape(-1, model_width))
    )
    prob_grad = (
        jnp.zeros((tok_rows, expert_count), jnp.float32)
        .at[slot_table, expert_column]
        .add(gate_grad)
    )
    logit_grad = (
        router_probs * (prob_grad - jnp.sum(router_probs * prob_grad, -1, keepdims=True))
    ).astype(jnp.bfloat16)
    router_term = jnp.einsum(
        "td,te->de", expert_input, logit_grad, preferred_element_type=jnp.float32
    )
    expert_in_grad = expert_in_grad + jnp.einsum(
        "te,de->td", logit_grad, router_full, preferred_element_type=jnp.float32
    )
    expert_gain_term = jnp.sum(expert_in_grad * normed_expert, 0)
    grad_res = grad_mid + norm_back(
        expert_in_grad * gain_expert.astype(jnp.float32), normed_expert, inverse_expert
    )
    branch_grad = grad_res.astype(jnp.bfloat16)
    output_term = jnp.einsum(
        "td,tc->dc", branch_grad, attention_lowered, preferred_element_type=jnp.float32
    )
    attended_grad = jnp.dot(branch_grad, output_full, preferred_element_type=jnp.float32).astype(
        jnp.bfloat16
    )
    attended_grad_heads = attended_grad.reshape(
        tok_rows, key_groups, head_group, head_dim
    ).transpose(1, 2, 0, 3)
    delta = jnp.sum(attended_grad_heads.astype(jnp.float32) * attended_heads, -1)
    seq_total = tok_rows * lax.axis_size("seq")

    def attend_back(running, key_block, value_block, key_start):

        def compute(carried):
            query_sum, key_sum, value_sum = carried
            block_size = key_block.shape[0]
            scores, key_heads = block_scores(key_block, key_start)
            value_heads = value_block.reshape(block_size, key_groups, head_dim)
            probs_full = jnp.exp(scores - log_total[..., None])
            probs_low = probs_full.astype(jnp.bfloat16)
            value_piece = jnp.einsum(
                "hgqk,hgqd->khd", probs_low, attended_grad_heads, preferred_element_type=jnp.float32
            ).reshape(block_size, key_width)
            prob_part = jnp.einsum(
                "hgqd,khd->hgqk",
                attended_grad_heads,
                value_heads,
                preferred_element_type=jnp.float32,
            )
            score_grad = (probs_full * (prob_part - delta[..., None])).astype(jnp.bfloat16)
            query_sum = (
                query_sum
                + jnp.einsum(
                    "hgqk,khd->hgqd", score_grad, key_heads, preferred_element_type=jnp.float32
                )
                * score_scale
            )
            key_piece = (
                jnp.einsum(
                    "hgqk,qhgd->khd", score_grad, queries, preferred_element_type=jnp.float32
                )
                * score_scale
            ).reshape(block_size, key_width)
            key_sum = lax.dynamic_update_slice_in_dim(
                key_sum,
                lax.dynamic_slice_in_dim(key_sum, key_start, block_size, 0) + key_piece,
                key_start,
                0,
            )
            value_sum = lax.dynamic_update_slice_in_dim(
                value_sum,
                lax.dynamic_slice_in_dim(value_sum, key_start, block_size, 0) + value_piece,
                key_start,
                0,
            )
            return (query_sum, key_sum, value_sum)

        visible = (key_start <= last_place) | (key_start < prefix_end)
        return lax.cond(visible, compute, keep_state, running)

    back_start = (
        jnp.zeros(stat_shape + (head_dim,), jnp.float32),
        jnp.zeros((seq_total, key_width), jnp.float32),
        jnp.zeros((seq_total, key_width), jnp.float32),
    )
    query_sum, key_sum, value_sum = over_key_blocks(
        (
            lax.all_gather(keys_local, "seq", axis=0, tiled=True),
            lax.all_gather(values_local, "seq", axis=0, tiled=True),
        ),
        attend_back,
        back_start,
    )
    key_part, value_part = (
        lax.psum_scatter(
            key_sum.astype(jnp.bfloat16), "seq", scatter_dimension=0, tiled=True
        ).astype(jnp.float32),
        lax.psum_scatter(
            value_sum.astype(jnp.bfloat16), "seq", scatter_dimension=0, tiled=True
        ).astype(jnp.float32),
    )
    query_rows = query_sum.transpose(2, 0, 1, 3).reshape(tok_rows, query_heads, head_dim)
    query_grad = (
        rotate(query_rows, cosine, -sine_table).reshape(tok_rows, query_width).astype(jnp.bfloat16)
    )
    key_grad = (
        rotate(key_part.reshape(tok_rows, key_groups, head_dim), cosine, -sine_table)
        .reshape(tok_rows, key_width)
        .astype(jnp.bfloat16)
    )
    value_grad = value_part.astype(jnp.bfloat16)
    query_term = jnp.einsum(
        "td,tc->dc", attention_input, query_grad, preferred_element_type=jnp.float32
    )
    key_term = jnp.einsum(
        "td,tc->dc", attention_input, key_grad, preferred_element_type=jnp.float32
    )
    value_term = jnp.einsum(
        "td,tc->dc", attention_input, value_grad, preferred_element_type=jnp.float32
    )
    attention_in_grad = jnp.einsum(
        "tc,dc->td", query_grad, query_full, preferred_element_type=jnp.float32
    )
    attention_in_grad = attention_in_grad + jnp.einsum(
        "tc,dc->td", key_grad, key_full, preferred_element_type=jnp.float32
    )
    attention_in_grad = attention_in_grad + jnp.einsum(
        "tc,dc->td", value_grad, value_full, preferred_element_type=jnp.float32
    )
    attention_gain_term = jnp.sum(attention_in_grad * normed_attention, 0)
    tokens_grad = grad_res + norm_back(
        attention_in_grad * gain_attention.astype(jnp.float32), normed_attention, inverse_attention
    )
    summed_grads = (
        lax.psum_scatter(query_term, ("dp", "seq"), scatter_dimension=0, tiled=True),
        lax.psum_scatter(key_term, ("dp", "seq"), scatter_dimension=0, tiled=True),
        lax.psum_scatter(value_term, ("dp", "seq"), scatter_dimension=0, tiled=True),
        lax.psum_scatter(output_term, ("dp", "seq"), scatter_dimension=0, tiled=True),
        lax.psum_scatter(attention_gain_term, ("dp", "seq"), scatter_dimension=0, tiled=True),
        lax.psum_scatter(expert_gain_term, ("dp", "seq"), scatter_dimension=0, tiled=True),
        lax.psum_scatter(router_term, ("dp", "seq"), scatter_dimension=0, tiled=True),
    )
    return (
        mixed[None],
        tokens_grad[None],
        summed_grads[0],
        summed_grads[1],
        summed_grads[2],
        summed_grads[3],
        summed_grads[4],
        summed_grads[5],
        summed_grads[6],
        gate_up_weight_grad,
        down_weight_grad,
    )


def matmul(left, right, contract):
    return lax.dot_general(
        left, right, (contract, ((), ())), preferred_element_type=jnp.float32
    )


ROWS_BY_COLS = ((1,), (0,))
ROWS_BY_ROWS = ((1,), (1,))
COLS_BY_COLS = ((0,), (0,))


def split_sum_columns(terms):
    ones = jnp.ones((terms.shape[0], LANES), jnp.bfloat16)
    high = terms.astype(jnp.bfloat16)
    low = (terms - high.astype(jnp.float32)).astype(jnp.bfloat16)
    return matmul(high, ones, COLS_BY_COLS) + matmul(low, ones, COLS_BY_COLS)


def turned(value_rows):
    width = value_rows.shape[1]
    lane = lax.broadcasted_iota(jnp.int32, value_rows.shape, 1)
    ahead = pltpu.roll(value_rows, width - HALF, 1)
    behind = pltpu.roll(value_rows, HALF, 1)
    return jnp.where(lane % HEAD_WIDTH < HALF, -ahead, behind)


def spin(value_rows, cosine, sine_table):
    repeats = value_rows.shape[1] // LANES
    cos_all = jnp.concatenate([cosine] * repeats, 1) if repeats > 1 else cosine
    sin_all = jnp.concatenate([sine_table] * repeats, 1) if repeats > 1 else sine_table
    return value_rows * cos_all + turned(value_rows) * sin_all


def inverse_rms(value_rows):
    return lax.rsqrt(jnp.mean(value_rows * value_rows, -1, keepdims=True) + NORM_EPS)


def shape_of(*dims, kind=jnp.bfloat16):
    return jax.ShapeDtypeStruct(dims, kind)


VMEM_SPEC = pl.BlockSpec(memory_space=pltpu.VMEM)
SMEM_SPEC = pl.BlockSpec(memory_space=pltpu.SMEM)
ANY_SPEC = pl.BlockSpec(memory_space=pl.ANY)


class Place:
    def __init__(self):
        self.dp = lax.axis_index("dp")
        self.z = lax.axis_index("seq")
        self.lines = lax.axis_size("seq")
        self.chips = lax.axis_size("dp") // 2
        self.chip = self.dp // 2
        self.core = self.dp % 2
        self.other = 1 - self.core
        self.chip_x = self.chip + 1 - 2 * (self.chip % 2)
        self.chip_y = (self.chip + 2) % 4
        self.chip_diag = 3 - self.chip

    def ahead(self, step):
        return (self.z + step) % self.lines

    def behind(self, step):
        return (self.z + self.lines - step) % self.lines

    def line_peer(self, step):
        return (self.dp, self.ahead(step))

    def on_chip(self, chip):
        return (chip * 2 + self.core, self.z)

    def sibling(self):
        return (self.chip * 2 + self.other, self.z)


def meet(peers):
    barrier = pltpu.get_barrier_semaphore()
    for peer in peers:
        pl.semaphore_signal(barrier, inc=1, device_id=peer, device_id_type=MESH)
    pl.semaphore_wait(barrier, len(peers))


def send(source, target, send_sem, recv_sem, peer):
    copy = pltpu.make_async_remote_copy(
        src_ref=source,
        dst_ref=target,
        send_sem=send_sem,
        recv_sem=recv_sem,
        device_id=peer,
        device_id_type=MESH,
    )
    copy.start()
    return copy


def move(source, target, sem):
    copy = pltpu.make_async_copy(source, target, sem)
    copy.start()
    return copy


def all_peers(here):
    return (
        [here.line_peer(k) for k in range(1, here.lines)]
        + [here.on_chip(chip) for chip in (here.chip_x, here.chip_y, here.chip_diag)]
        + [here.sibling()]
    )


def comm_params(ident, limit=56):
    return pltpu.CompilerParams(
        collective_id=ident, has_side_effects=True, vmem_limit_bytes=limit << 20
    )


class Spread:
    def __init__(self, here, pick, target, depth, local_sem, sends, recvs):
        self.here, self.pick, self.target, self.depth = here, pick, target, depth
        self.local_sem, self.sends, self.recvs = local_sem, sends, recvs
        self.used = 0

    def put(self, source, target, peer):
        copy = send(source, target, self.sends.at[self.used], self.recvs.at[self.used], peer)
        self.used += 1
        return copy

    def row(self):
        here = self.here
        if len(self.target.shape) > 2:
            return self.target.at[here.chip, here.core, here.z]
        first = (here.dp * here.lines + here.z) * self.depth
        return self.target.at[pl.ds(pl.multiple_of(first, self.depth), self.depth)]

    def chip_rows(self, chip, part=None):
        here = self.here
        if len(self.target.shape) > 2:
            if part is None:
                return self.target.at[chip, here.core]
            return self.target.at[chip, here.core, pl.ds(part * (here.lines // 2), here.lines // 2)]
        count = here.lines * self.depth
        first = (chip * 2 + here.core) * count
        if part is not None:
            first, count = first + part * (count // 2), count // 2
        return self.target.at[pl.ds(pl.multiple_of(first, count), count)]

    def start(self):
        here = self.here
        mine = self.row()
        self.own = move(self.pick(here.z), mine, self.local_sem)
        self.line = [
            self.put(self.pick(here.ahead(k)), mine, here.line_peer(k)) for k in range(1, here.lines)
        ]

    def chips(self):
        here = self.here
        self.own.wait()
        for copy in self.line:
            copy.wait_recv()
        mine = self.chip_rows(here.chip)
        self.plane = [
            self.put(mine, mine, here.on_chip(here.chip_x)),
            self.put(mine, mine, here.on_chip(here.chip_y)),
        ]
        self.across = [self.put(mine, mine, here.sibling())]

    def turn(self):
        here = self.here
        self.corner = []
        for copy, origin, onward, part in (
            (self.plane[0], here.chip_x, here.chip_y, 0),
            (self.plane[1], here.chip_y, here.chip_x, 1),
        ):
            copy.wait_recv()
            half = self.chip_rows(origin, part)
            self.corner.append(self.put(half, half, here.on_chip(onward)))
            block = self.chip_rows(origin)
            self.across.append(self.put(block, block, here.sibling()))

    def cores(self):
        here = self.here
        for copy in self.corner:
            copy.wait_recv()
        block = self.chip_rows(here.chip_diag)
        self.across.append(self.put(block, block, here.sibling()))

    def finish(self):
        for copy in self.across:
            copy.wait_recv()

    def close(self):
        for copy in self.line + self.plane + self.corner + self.across:
            copy.wait_send()


def spread_count(lines):
    return lines - 1 + 2 + 2 + 4


class LineGather:
    def __init__(self, here, view, sends, recvs, source=None):
        self.here, self.view, self.source = here, view, source
        self.sends, self.recvs = sends, recvs

    def copy(self, way, hop, block, source=None):
        here = self.here
        step = 1 if way == 0 else here.lines - 1
        return pltpu.make_async_remote_copy(
            src_ref=self.view(block) if source is None else source,
            dst_ref=self.view(block),
            send_sem=self.sends.at[way, hop - 1],
            recv_sem=self.recvs.at[way, hop - 1],
            device_id=here.line_peer(step),
            device_id_type=MESH,
        )

    def start(self):
        here = self.here

        @pl.when(here.z < here.lines - 1)
        def rightward():
            self.copy(0, 1, here.z, self.source).start()

        @pl.when(here.z > 0)
        def leftward():
            self.copy(1, 1, here.z, self.source).start()

    def step(self, hop):
        here = self.here
        lines = here.lines

        @pl.when(here.z >= hop)
        def from_left():
            block = here.behind(hop)
            self.copy(0, hop, block).wait_recv()
            if hop < lines - 1:

                @pl.when(here.z < lines - 1)
                def onward():
                    self.copy(0, hop + 1, block).start()

        @pl.when(here.z + hop < lines)
        def from_right():
            block = here.ahead(hop)
            self.copy(1, hop, block).wait_recv()
            if hop < lines - 1:

                @pl.when(here.z > 0)
                def onward():
                    self.copy(1, hop + 1, block).start()

    def close(self):
        here = self.here
        lines = here.lines
        for hop in range(1, lines):

            @pl.when((here.z >= hop - 1) & (here.z < lines - 1))
            def rightward():
                self.copy(0, hop, here.behind(hop - 1)).wait_send()

            @pl.when((here.z + hop - 1 < lines) & (here.z > 0))
            def leftward():
                self.copy(1, hop, here.ahead(hop - 1)).wait_send()


class LineSpread:
    def __init__(self, here, view, sends, recvs, source=None):
        self.here, self.view, self.source = here, view, source
        self.sends, self.recvs = sends, recvs

    def start(self):
        here = self.here
        mine = self.view(here.z)
        self.line = [
            send(
                mine if self.source is None else self.source, mine, self.sends.at[k - 1], self.recvs.at[k - 1], here.line_peer(k)
            )
            for k in range(1, here.lines)
        ]

    def arrived(self, step):
        self.line[step - 1].wait_recv()

    def finish(self):
        for copy in self.line:
            copy.wait_recv()

    def close(self):
        for copy in self.line:
            copy.wait_send()


class LineSum:
    def __init__(self, here, parts, landed, rows, sends, recvs):
        self.here, self.parts, self.landed, self.rows = here, parts, landed, rows
        self.sends, self.recvs = sends, recvs

    def copy(self, way, hops):
        here = self.here
        step = 1 if way == 0 else here.lines - 1
        block = here.ahead(hops) if way == 0 else here.behind(hops)
        return pltpu.make_async_remote_copy(
            src_ref=self.parts.at[block, self.rows],
            dst_ref=self.landed.at[way, hops - 1, self.rows],
            send_sem=self.sends.at[way, hops - 1],
            recv_sem=self.recvs.at[way, hops - 1],
            device_id=here.line_peer(step),
            device_id_type=MESH,
        )

    def step(self, hops):
        here = self.here
        lines = here.lines

        def pass_on(way, first):
            block = here.ahead(hops) if way == 0 else here.behind(hops)
            if hops < lines - 1:

                @pl.when(jnp.logical_not(first))
                def add():
                    self.copy(way, hops + 1).wait_recv()
                    self.parts[block, self.rows] = (
                        self.parts[block, self.rows].astype(jnp.float32)
                        + self.landed[way, hops, self.rows].astype(jnp.float32)
                    ).astype(self.parts.dtype)

            self.copy(way, hops).start()

        @pl.when(here.z + hops < lines)
        def rightward():
            pass_on(0, here.z == 0)

        @pl.when(here.z >= hops)
        def leftward():
            pass_on(1, here.z == lines - 1)

    def finish(self, total):
        here = self.here
        rows = self.rows
        total[rows, :] = self.parts[here.z, rows].astype(jnp.float32)

        @pl.when(here.z > 0)
        def from_left():
            self.copy(0, 1).wait_recv()
            total[rows, :] = total[rows, :] + self.landed[0, 0, rows].astype(jnp.float32)

        @pl.when(here.z < here.lines - 1)
        def from_right():
            self.copy(1, 1).wait_recv()
            total[rows, :] = total[rows, :] + self.landed[1, 0, rows].astype(jnp.float32)

    def close(self):
        here = self.here
        for hops in range(1, here.lines):

            @pl.when(here.z + hops < here.lines)
            def rightward():
                self.copy(0, hops).wait_send()

            @pl.when(here.z >= hops)
            def leftward():
                self.copy(1, hops).wait_send()


class Halves:
    def __init__(self, *members):
        self.members = members

    def start(self):
        for member in self.members:
            member.start()

    def step(self, hops):
        for member in self.members:
            member.step(hops)

    def finish(self, total):
        for member in self.members:
            member.finish(total)

    def close(self):
        for member in self.members:
            member.close()


class LineSwap:
    def __init__(self, here, pick, received, sends, recvs):
        self.here, self.pick, self.received = here, pick, received
        self.sends, self.recvs = sends, recvs

    def start(self):
        here = self.here
        self.line = [
            send(
                self.pick(here.ahead(k)), self.received(k, here.z), self.sends.at[k - 1], self.recvs.at[k - 1], here.line_peer(k)
            )
            for k in range(1, here.lines)
        ]

    def finish(self):
        for copy in self.line:
            copy.wait_recv()

    def close(self):
        for copy in self.line:
            copy.wait_send()


def padded_square(block):
    filler = jnp.zeros((LANES - block.shape[0], LANES), jnp.float32)
    return jnp.concatenate([block, filler], 0).T


def row_order(depth, experts, by_expert):
    count = depth * experts
    place = lax.broadcasted_iota(jnp.int32, (count, count), 0)
    source = lax.broadcasted_iota(jnp.int32, (count, count), 1)
    if by_expert:
        wanted = place % depth * experts + place // depth
    else:
        wanted = place % experts * depth + place // experts
    return (source == wanted).astype(jnp.bfloat16)


class Fold:
    def __init__(self, here, terms, crossed, landed, last, sends, recvs):
        self.here, self.terms, self.crossed = here, terms, crossed
        self.landed, self.last = landed, last
        self.sends, self.recvs = sends, recvs
        middle = here.lines // 2
        self.parts = [(0, middle), (middle, here.lines)]

    def start(self):
        here = self.here
        self.first = send(
            self.terms.at[:, here.other], self.crossed, self.sends.at[0], self.recvs.at[0], here.sibling()
        )

    def chips(self):
        here = self.here
        self.first.wait_recv()
        for chip in range(here.chips):
            self.terms[chip, here.core] = (
                self.terms[chip, here.core].astype(jnp.float32) + self.crossed[chip].astype(jnp.float32)
            ).astype(jnp.bfloat16)
        self.one, self.straight = [], []
        for number, near in enumerate((here.chip_x, here.chip_y)):
            low, high = self.parts[number]
            for slot, chip, group in ((1, here.chip_diag, self.one), (0, near, self.straight)):
                place = 1 + number * 2 + slot
                group.append(
                    send(
                        self.terms.at[chip, here.core, low:high], self.landed.at[number, slot],
                        self.sends.at[place], self.recvs.at[place], here.on_chip(near),
                    )
                )

    def turn(self):
        here = self.here
        self.two = []
        for number, onward in enumerate((here.chip_y, here.chip_x)):
            low, high = self.parts[number]
            self.one[number].wait_recv()
            self.terms[onward, here.core, low:high] = (
                self.terms[onward, here.core, low:high].astype(jnp.float32)
                + self.landed[number, 1].astype(jnp.float32)
            ).astype(jnp.bfloat16)
            place = 5 + number
            self.two.append(
                send(
                    self.terms.at[onward, here.core, low:high], self.last.at[number],
                    self.sends.at[place], self.recvs.at[place], here.on_chip(onward),
                )
            )

    def finish(self):
        here = self.here
        for number in range(2):
            low, high = self.parts[number]
            self.straight[number].wait_recv()
            self.two[number].wait_recv()
            self.terms[here.chip, here.core, low:high] = (
                self.terms[here.chip, here.core, low:high].astype(jnp.float32)
                + self.landed[number, 0].astype(jnp.float32)
                + self.last[number].astype(jnp.float32)
            ).astype(jnp.bfloat16)

    def sums(self, z):
        return self.terms.at[self.here.chip, self.here.core, z]

    def close(self):
        for copy in [self.first] + self.one + self.straight + self.two:
            copy.wait_send()


def layer_kernel(
    prefix, tokens, query_rows, key_rows, value_rows, out_rows, router_cols, attention_gain, expert_gain, gate_up_rows, down_rows,
    cotangent, routes, cosine, sine_table,
    mixed_o, tokens_grad_o, query_o, key_o, value_o, out_o, attention_gain_o, expert_gain_o, router_o, expert_o,
    square, rows, expert_rows, tokens_all, weights, out_full, terms, cot_all, chosen_all, att_in, qkv, attended, attended_all,
    log_total, expert_in, probs, middle, slopes, acts, mids, part_mix, got_mix, mix_total, mixed, part_grad, got_grad,
    gate_grad, got_gate, grad_res, attended_grad, attended_grad_all, joined_grad, key_sum, value_sum, e_landed, e_last,
    o_terms, o_crossed, o_landed, o_last, o_lines, q_terms, q_crossed, q_landed, q_last, q_lines,
    query_s, key_s, value_s, out_s, attention_gain_s, expert_gain_s, router_s,
    local_sem, r_sends, r_recvs, o_sends, o_recvs, e_sends, e_recvs, t_sends, t_recvs, c_sends, c_recvs, k_sends, k_recvs,
    a_sends, a_recvs, m_sends, m_recvs, x_sends, x_recvs, g_sends, g_recvs, b_sends, b_recvs, p_sends, p_recvs,
    f_sends, f_recvs, of_sends, of_recvs, q_sends, q_recvs, el_sends, el_recvs, ol_sends, ol_recvs, ql_sends, ql_recvs,
    free_sem, out_sem,
):
    here = Place()
    lines = here.lines
    tok_rows, width = tokens.shape
    rows_all = lines * tok_rows
    depth = rows.shape[1]
    own_experts = terms.shape[0]
    ff_width = terms.shape[5] // 3
    chips = here.chips
    five = (chips, 2, lines, depth)
    four = (chips, lines, depth)
    query_width = lines * (qkv.shape[1] // 2)
    qkv_cols = qkv.shape[1]
    kv_cols = qkv_cols // 4
    q_cols = 2 * kv_cols
    stores = []

    def store(source, target):
        stores.append(move(source, target, out_sem.at[len(stores)]))

    gate_up_load = move(gate_up_rows, mids.at[0, ..., : 2 * ff_width], local_sem.at[0])
    down_load = move(down_rows, mids.at[0, ..., 2 * ff_width :], local_sem.at[1])
    token_load = move(tokens, tokens_all.at[here.z], local_sem.at[2])
    cot_load = move(cotangent, cot_all.at[here.z], local_sem.at[3])

    square[...] = jnp.zeros_like(square)
    square[:EXPERT_COUNT, :depth] = router_cols[...].astype(jnp.float32)
    square[EXPERT_COUNT : EXPERT_COUNT + 1, :depth] = attention_gain[...].astype(jnp.float32)
    square[EXPERT_COUNT + 1 : EXPERT_COUNT + 2, :depth] = expert_gain[...].astype(jnp.float32)
    small = square[...].T[:depth, :].astype(jnp.bfloat16)
    for line in range(lines):
        rows[line, :, :q_cols] = query_rows[:, line * q_cols : (line + 1) * q_cols]
        rows[line, :, q_cols : q_cols + kv_cols] = key_rows[:, line * kv_cols : (line + 1) * kv_cols]
        rows[line, :, q_cols + kv_cols : qkv_cols] = value_rows[:, line * kv_cols : (line + 1) * kv_cols]
        rows[line, :, qkv_cols:] = small
    meet(all_peers(here))
    rows_spread = Spread(here, lambda z: rows.at[z], weights, depth, local_sem.at[4], r_sends, r_recvs)
    half = tok_rows // 2
    token_gathers = [
        LineGather(
            here, lambda z, n=n: tokens_all.at[z, pl.ds(n * half, half)], t_sends.at[n], t_recvs.at[n], tokens.at[pl.ds(n * half, half)]
        )
        for n in range(2)
    ]
    out_spread = Spread(here, lambda z: out_rows, out_full, depth, local_sem.at[5], o_sends, o_recvs)
    chosen_swap = LineSwap(
        here, lambda z: chosen_all.at[here.z], lambda k, z: chosen_all.at[z], k_sends, k_recvs
    )
    cot_gather = LineGather(here, lambda z: cot_all.at[z], c_sends, c_recvs, cotangent)
    expert_spreads = [
        Spread(
            here,
            lambda z, e=e: expert_rows.at[z, e], terms.at[e], depth, local_sem.at[6 + e], e_sends.at[e], e_recvs.at[e],
        )
        for e in range(own_experts)
    ]
    rows_spread.start()
    for gather in token_gathers:
        gather.start()
    expert_id = lax.broadcasted_iota(jnp.int32, (EXPERT_COUNT, tok_rows), 0)
    chosen = jnp.zeros((EXPERT_COUNT, tok_rows), jnp.float32)
    for number in range(routes.shape[0]):
        chosen = chosen + (routes[number : number + 1, :] == expert_id).astype(jnp.float32)
    chosen_all[here.z] = chosen.astype(jnp.bfloat16)
    chosen_swap.start()
    rows_spread.chips()
    gate_up_load.wait()
    down_load.wait()
    order = row_order(depth, EXPERT_COUNT, True)
    expert_rows[...] = (
        matmul(order, mids[0].reshape(depth * EXPERT_COUNT, 3 * ff_width), ROWS_BY_COLS)
        .astype(jnp.bfloat16)
        .reshape(expert_rows.shape)
    )
    token_gathers[0].step(1)
    rows_spread.turn()
    token_gathers[1].step(1)
    for hop in range(2, lines - 1):
        token_gathers[0].step(hop)
        rows_spread.cores()
        token_gathers[1].step(hop)
    out_spread.start()
    for spread in expert_spreads:
        spread.start()
    rows_spread.finish()
    columns = weights[:, qkv_cols:].astype(jnp.float32).T
    gain_attention = columns[EXPERT_COUNT : EXPERT_COUNT + 1, :]
    gain_expert = columns[EXPERT_COUNT + 1 : EXPERT_COUNT + 2, :]

    def project(source):
        block = pl.ds(pl.multiple_of(source * tok_rows, tok_rows), tok_rows)
        hidden = tokens_all[source].astype(jnp.float32)
        normed = (hidden * inverse_rms(hidden) * gain_attention).astype(jnp.bfloat16)
        att_in[block, :] = normed
        linear = matmul(normed, weights[:, :qkv_cols], ROWS_BY_COLS)
        turned_part = linear[:, : q_cols + kv_cols]
        qkv[block, : q_cols + kv_cols] = spin(turned_part, cosine[block, :], sine_table[block, :]).astype(
            jnp.bfloat16
        )
        qkv[block, q_cols + kv_cols :] = linear[:, q_cols + kv_cols :].astype(jnp.bfloat16)

    token_load.wait()
    project(here.z)
    for step in range(1, lines - 1):

        @pl.when(here.z >= step)
        def left():
            project(here.behind(step))

        @pl.when(here.z + step < lines)
        def right():
            project(here.ahead(step))

    for gather in token_gathers:
        gather.step(lines - 1)

    @pl.when(here.z == lines - 1)
    def first():
        project(0)

    @pl.when(here.z == 0)
    def last():
        project(lines - 1)

    out_spread.chips()

    prefix_end = prefix[0]
    heads = q_cols // HEAD_WIDTH
    group = q_cols // kv_cols

    def attend(number):
        start = number * tok_rows
        block = pl.ds(start, tok_rows)
        reach = max(rows_all // 2, start + tok_rows)
        query_place = start + lax.broadcasted_iota(jnp.int32, (tok_rows, reach), 0)
        key_place = lax.broadcasted_iota(jnp.int32, (tok_rows, reach), 1)
        allowed = (key_place <= query_place) | (key_place < prefix_end)
        lanes = lax.broadcasted_iota(jnp.int32, (tok_rows, LANES), 1)
        totals = jnp.zeros((tok_rows, LANES), jnp.float32)
        outputs = []
        for head in range(heads):
            key_at = q_cols + head // group * HEAD_WIDTH
            value_at = key_at + kv_cols
            scores = matmul(
                qkv[block, head * HEAD_WIDTH : (head + 1) * HEAD_WIDTH],
                qkv[:reach, key_at : key_at + HEAD_WIDTH],
                ROWS_BY_ROWS,
            )
            scores = jnp.where(allowed, scores * SCORE_SCALE, LOW_SCORE)
            largest = jnp.max(scores, -1, keepdims=True)
            powers = jnp.exp(scores - largest)
            total = jnp.sum(powers, -1, keepdims=True)
            product = matmul(
                powers.astype(jnp.bfloat16), qkv[:reach, value_at : value_at + HEAD_WIDTH], ROWS_BY_COLS
            )
            outputs.append(product / total)
            totals = jnp.where(lanes == head, largest + jnp.log(total), totals)
        joined = jnp.concatenate(outputs, 1)
        attended[block, :] = joined
        log_total[block, :] = totals
        attended_all[here.z, block, :] = joined.astype(jnp.bfloat16)

    def mix_in(number):
        block = pl.ds(number * tok_rows, tok_rows)
        branch = matmul(attended_all[0, block, :], out_full[:, :q_cols], ROWS_BY_ROWS)
        for line in range(1, lines):
            branch = branch + matmul(
                attended_all[line, block, :], out_full[:, line * q_cols : (line + 1) * q_cols], ROWS_BY_ROWS
            )
        total = tokens_all[number].astype(jnp.float32) + branch
        lowered = (total * inverse_rms(total) * gain_expert).astype(jnp.bfloat16)
        expert_in[number] = lowered
        logits = matmul(lowered, weights[:, qkv_cols:], ROWS_BY_COLS)
        lane = lax.broadcasted_iota(jnp.int32, logits.shape, 1)
        logits = jnp.where(lane < EXPERT_COUNT, logits, LOW_SCORE)
        powers = jnp.exp(logits - jnp.max(logits, -1, keepdims=True))
        powers = jnp.where(lane < EXPERT_COUNT, powers, 0.0)
        probs[number] = powers / jnp.sum(powers, -1, keepdims=True)

        @pl.when(here.z == number)
        def keep():
            middle[...] = total


    attended_gathers = [
        LineSpread(
            here, lambda z, n=n: attended_all.at[z, pl.ds(n * tok_rows, tok_rows)], a_sends.at[n], a_recvs.at[n]
        )
        for n in range(lines)
    ]
    for turn in range(lines):
        attend(turn)
        attended_gathers[turn].start()
    out_spread.turn()
    expert_spreads[0].chips()
    out_spread.cores()
    expert_spreads[0].turn()
    expert_spreads[1].chips()
    expert_spreads[0].cores()
    out_spread.finish()
    expert_spreads[2].chips()
    expert_spreads[1].turn()
    expert_spreads[3].chips()
    expert_spreads[1].cores()
    expert_spreads[2].turn()

    def mix_arrived(number):
        attended_gathers[number].finish()
        mix_in(number)

    mix_arrived(0)
    mix_arrived(1)
    cot_gather.start()
    expert_spreads[2].cores()
    for number in range(2, lines):
        mix_arrived(number)

    def gate_columns(number, e):
        chosen = padded_square(chosen_all[number].astype(jnp.float32))
        lane = lax.broadcasted_iota(jnp.int32, chosen.shape, 1)
        own = lane == here.z * own_experts + e
        picked = jnp.sum(jnp.where(own, chosen, 0.0), -1, keepdims=True)
        gate = jnp.sum(jnp.where(own, probs[number] * chosen, 0.0), -1, keepdims=True)
        return own, picked, gate

    pairs = [(a, a + 2) for a in range(0, lines, 2)]

    def gate_up_of(e):
        return terms[e, ..., : 2 * ff_width].reshape(width, 2 * ff_width)

    def down_of(e):
        return terms[e, ..., 2 * ff_width :].reshape(width, ff_width)

    def expert_forward(e):
        for low, high in pairs:
            block = pl.ds(low * tok_rows, (high - low) * tok_rows)
            inputs = jnp.concatenate([expert_in[n] for n in range(low, high)], 0)
            linear = matmul(inputs, gate_up_of(e), ROWS_BY_COLS)
            gate_part, up_part = linear[:, :ff_width], linear[:, ff_width:]
            sigmoid = 1.0 / (1.0 + jnp.exp(-gate_part))
            silu = gate_part * sigmoid
            act = silu * up_part
            slopes[e, block, :ff_width] = (
                up_part * (sigmoid * (1.0 + gate_part * (1.0 - sigmoid)))
            ).astype(jnp.bfloat16)
            slopes[e, block, ff_width:] = silu.astype(jnp.bfloat16)
            acts[e, block, :] = act.astype(jnp.bfloat16)
            gate = jnp.concatenate([gate_columns(n, e)[2] for n in range(low, high)], 0)
            mids[e, low:high, ..., 2 * ff_width :] = (
                (gate * act).astype(jnp.bfloat16).reshape(high - low, lines, depth, ff_width)
            )

    chosen_swap.finish()
    expert_spreads[3].turn()
    expert_spreads[0].finish()
    expert_forward(0)
    expert_spreads[1].finish()
    expert_forward(1)
    cot_gather.step(1)
    expert_spreads[3].cores()
    expert_spreads[2].finish()
    expert_forward(2)
    expert_spreads[3].finish()
    expert_forward(3)

    def line_sum(parts, landed, sends, recvs):
        return Halves(
            *[
                LineSum(here, parts, landed, pl.ds(n * half, half), sends.at[n], recvs.at[n])
                for n in range(2)
            ]
        )

    for low, high in pairs:
        total = None
        for e in range(own_experts):
            gated = mids[e, low:high, ..., 2 * ff_width :].reshape((high - low) * tok_rows, ff_width)
            term = matmul(gated, down_of(e), ROWS_BY_ROWS)
            total = term if total is None else total + term
        for n in range(low, high):
            part_mix[n] = total[(n - low) * tok_rows : (n - low + 1) * tok_rows, :].astype(jnp.bfloat16)
    mix_swap = line_sum(part_mix, got_mix, m_sends, m_recvs)
    mix_swap.step(lines - 1)

    cot_load.wait()
    for hop in range(2, lines - 1):
        cot_gather.step(hop)

    def expert_back(low):
        block = pl.ds(pl.multiple_of(low * tok_rows, 2 * tok_rows), 2 * tok_rows)
        grad_mid = jnp.concatenate([cot_all[low], cot_all[low + 1]], 0)
        total = None
        gate_cols = [jnp.zeros((tok_rows, LANES), jnp.float32)] * 2
        for e in range(own_experts):
            act_grad = matmul(grad_mid, down_of(e), ROWS_BY_COLS)
            column = jnp.sum(act_grad * acts[e, block, :].astype(jnp.float32), -1, keepdims=True)
            gates = []
            for n in range(2):
                own, picked, gate = gate_columns(low + n, e)
                part = column[n * tok_rows : (n + 1) * tok_rows, :]
                gate_cols[n] = jnp.where(own, part * picked, gate_cols[n])
                gates.append(gate)
            act_grad = act_grad * jnp.concatenate(gates, 0)
            slope = slopes[e, block, :].astype(jnp.float32)
            mid = jnp.concatenate(
                [act_grad * slope[:, :ff_width], act_grad * slope[:, ff_width:]], 1
            ).astype(jnp.bfloat16)
            mids[e, pl.ds(low, 2), ..., : 2 * ff_width] = mid.reshape(2, lines, depth, 2 * ff_width)
            term = matmul(mid, gate_up_of(e), ROWS_BY_ROWS)
            total = term if total is None else total + term
        for n in range(2):
            part_grad[low + n] = total[n * tok_rows : (n + 1) * tok_rows, :].astype(jnp.bfloat16)
            gate_grad[low + n] = gate_cols[n].T[:EXPERT_COUNT, :]

    expert_back(here.z // 2 * 2)
    mix_swap.step(lines - 2)
    cot_gather.step(lines - 1)
    for number in range(1, lines // 2):
        expert_back((here.z // 2 + number) % (lines // 2) * 2)
    for group_of in [rows_spread, out_spread, chosen_swap, cot_gather] + token_gathers + expert_spreads + attended_gathers:
        group_of.close()
    grad_swap = line_sum(part_grad, got_grad, x_sends, x_recvs)
    gate_swap = LineSwap(here, lambda z: gate_grad.at[z], lambda k, z: got_gate.at[k - 1], g_sends, g_recvs)
    attended_swap = LineSwap(
        here, lambda z: attended_grad.at[z], lambda k, z: attended_grad_all.at[z], b_sends, b_recvs
    )
    part_swap = line_sum(part_mix, got_mix, p_sends, p_recvs)
    folds = [
        Fold(here, terms.at[e], mids.at[e], e_landed.at[e], e_last.at[e], f_sends.at[e], f_recvs.at[e])
        for e in range(own_experts)
    ]
    out_fold = Fold(here, o_terms, o_crossed, o_landed, o_last, of_sends, of_recvs)
    qkv_fold = Fold(here, q_terms, q_crossed, q_landed, q_last, q_sends, q_recvs)
    expert_swaps = [
        LineSwap(here, folds[e].sums, lambda k, z, e=e: expert_rows.at[z, e], el_sends.at[e], el_recvs.at[e])
        for e in range(own_experts)
    ]
    out_swap = LineSwap(here, out_fold.sums, lambda k, z: o_lines.at[k - 1], ol_sends, ol_recvs)
    qkv_swap = LineSwap(here, qkv_fold.sums, lambda k, z: q_lines.at[z], ql_sends, ql_recvs)

    grad_swap.step(lines - 1)
    gate_swap.start()
    for e in range(own_experts):
        terms[e, ..., : 2 * ff_width] = (
            matmul(
                expert_in[...].reshape(rows_all, width),
                mids[e, ..., : 2 * ff_width].reshape(rows_all, 2 * ff_width),
                COLS_BY_COLS,
            )
            .astype(jnp.bfloat16)
            .reshape(*five, 2 * ff_width)
        )
        terms[e, ..., 2 * ff_width :] = (
            matmul(
                cot_all[...].reshape(rows_all, width),
                mids[e, ..., 2 * ff_width :].reshape(rows_all, ff_width),
                COLS_BY_COLS,
            )
            .astype(jnp.bfloat16)
            .reshape(*five, ff_width)
        )
        pl.semaphore_signal(free_sem.at[e], inc=1, device_id=here.sibling(), device_id_type=MESH)
        pl.semaphore_wait(free_sem.at[e], 1)
        folds[e].start()
        if e == 0:
            for hops in range(lines - 3, 0, -1):
                mix_swap.step(hops)
            grad_swap.step(lines - 2)
            folds[0].chips()
        if e == 1:
            for hops in range(lines - 3, 0, -1):
                grad_swap.step(hops)
        if e == 2:
            folds[0].turn()
            folds[1].chips()
            mix_swap.finish(mix_total)
            mixed[...] = (mix_total[...] + middle[...]).astype(jnp.bfloat16)
            store(mixed, mixed_o)

    gate_swap.finish()
    grad_swap.finish(grad_res)
    gate_rows = gate_grad[here.z]
    for k in range(lines - 1):
        gate_rows = gate_rows + got_gate[k]
    gates = padded_square(gate_rows)
    grad = grad_res[...]
    prob = probs[here.z]
    logit_grad = (prob * (gates - jnp.sum(prob * gates, -1, keepdims=True))).astype(jnp.bfloat16)
    grad = grad + matmul(logit_grad, weights[:, qkv_cols:], ROWS_BY_ROWS)
    hidden = middle[...]
    inverse = inverse_rms(hidden)
    normed = hidden * inverse
    scaled = grad * gain_expert
    result = cot_all[here.z].astype(jnp.float32) + inverse * (
        scaled - normed * jnp.mean(scaled * normed, -1, keepdims=True)
    )
    grad_res[...] = result
    branch = result.astype(jnp.bfloat16)
    for line in range(lines):
        attended_grad[line] = matmul(
            branch, out_full[:, line * q_cols : (line + 1) * q_cols], ROWS_BY_COLS
        ).astype(jnp.bfloat16)
    attended_swap.start()
    folds[0].finish()
    expert_swaps[0].start()
    attended_grad_all[here.z] = attended_grad[here.z]
    own_block = pl.ds(pl.multiple_of(here.z * tok_rows, tok_rows), tok_rows)
    router_term = matmul(expert_in[here.z], logit_grad, COLS_BY_COLS)
    gain_term = split_sum_columns(grad * normed)
    lane = lax.broadcasted_iota(jnp.int32, router_term.shape, 1)
    for line in range(lines):
        o_terms[..., line * q_cols : (line + 1) * q_cols] = (
            matmul(branch, attended_all[line, own_block, :], COLS_BY_COLS).astype(jnp.bfloat16).reshape(*five, q_cols)
        )
    o_terms[..., query_width:] = (
        jnp.where(lane == EXPERT_COUNT, gain_term, router_term).astype(jnp.bfloat16).reshape(*five, LANES)
    )
    out_fold.start()
    folds[1].turn()
    folds[2].chips()
    attended_swap.finish()

    key_sum[...] = jnp.zeros_like(key_sum)
    value_sum[...] = jnp.zeros_like(value_sum)

    def attend_back(number):
        start = number * tok_rows
        block = pl.ds(start, tok_rows)
        reach = max(rows_all // 2, start + tok_rows)
        query_place = start + lax.broadcasted_iota(jnp.int32, (tok_rows, reach), 0)
        key_place = lax.broadcasted_iota(jnp.int32, (tok_rows, reach), 1)
        allowed = (key_place <= query_place) | (key_place < prefix_end)
        query_grads = []
        for head in range(heads):
            own = slice(head * HEAD_WIDTH, (head + 1) * HEAD_WIDTH)
            low = head // group * HEAD_WIDTH
            shared = slice(low, low + HEAD_WIDTH)
            query = qkv[block, own]
            key = qkv[:reach, q_cols + low : q_cols + low + HEAD_WIDTH]
            value = qkv[:reach, q_cols + kv_cols + low : q_cols + kv_cols + low + HEAD_WIDTH]
            grad = attended_grad_all[number, :, own]
            scores = matmul(query, key, ROWS_BY_ROWS) * SCORE_SCALE
            prob = jnp.where(allowed, jnp.exp(scores - log_total[block, head : head + 1]), 0.0)
            delta = jnp.sum(grad.astype(jnp.float32) * attended[block, own], -1, keepdims=True)
            prob_part = matmul(grad, value, ROWS_BY_ROWS)
            score_grad = (prob * (prob_part - delta)).astype(jnp.bfloat16)
            value_sum[:reach, shared] = value_sum[:reach, shared] + matmul(
                prob.astype(jnp.bfloat16), grad, COLS_BY_COLS
            )
            key_sum[:reach, shared] = key_sum[:reach, shared] + matmul(score_grad, query, COLS_BY_COLS)
            query_grads.append(matmul(score_grad, key, ROWS_BY_COLS))
        query_grad = jnp.concatenate(query_grads, 1) * SCORE_SCALE
        joined_grad[block, :q_cols] = spin(query_grad, cosine[block, :], -sine_table[block, :]).astype(
            jnp.bfloat16
        )

    for number in range(lines):
        attend_back(number)
        if number == lines - 2:
            folds[1].finish()
            expert_swaps[1].start()
    folds[2].turn()
    folds[3].chips()
    joined_grad[:, q_cols : q_cols + kv_cols] = spin(
        key_sum[...] * SCORE_SCALE, cosine[...], -sine_table[...]
    ).astype(jnp.bfloat16)
    joined_grad[:, q_cols + kv_cols :] = value_sum[...].astype(jnp.bfloat16)
    mix_swap.close()
    gain_term = jnp.zeros((width, LANES), jnp.float32)
    for number in range(lines):
        block = pl.ds(number * tok_rows, tok_rows)
        hidden = tokens_all[number].astype(jnp.float32)
        normed = hidden * inverse_rms(hidden)
        part = matmul(joined_grad[block, :], weights[:, :qkv_cols], ROWS_BY_ROWS)
        part_mix[number] = part.astype(jnp.bfloat16)
        gain_term = gain_term + split_sum_columns(part * normed)
    part_swap.step(lines - 1)
    q_terms[..., :qkv_cols] = (
        matmul(att_in[...], joined_grad[...], COLS_BY_COLS).astype(jnp.bfloat16).reshape(*five, qkv_cols)
    )
    q_terms[..., qkv_cols:] = gain_term.astype(jnp.bfloat16).reshape(*five, LANES)
    qkv_fold.start()
    out_fold.chips()
    qkv_fold.chips()
    folds[2].finish()
    expert_swaps[2].start()
    for hops in range(lines - 2, 1, -1):
        part_swap.step(hops)
    folds[3].turn()
    out_fold.turn()
    qkv_fold.turn()
    part_swap.step(1)
    folds[3].finish()
    expert_swaps[3].start()
    out_fold.finish()
    out_swap.start()
    qkv_fold.finish()
    qkv_swap.start()

    part_swap.finish(mix_total)
    hidden = tokens_all[here.z].astype(jnp.float32)
    inverse = inverse_rms(hidden)
    normed = hidden * inverse
    scaled = mix_total[...] * gain_attention
    mix_total[...] = grad_res[...] + inverse * (
        scaled - normed * jnp.mean(scaled * normed, -1, keepdims=True)
    )
    store(mix_total, tokens_grad_o)
    out_swap.finish()
    total = o_terms[here.chip, here.core, here.z].astype(jnp.float32)
    for k in range(lines - 1):
        total = total + o_lines[k].astype(jnp.float32)
    out_s[...] = total[:, :query_width]
    tail = padded_square(total[:, query_width:])
    router_s[...] = tail[:EXPERT_COUNT, :depth]
    expert_gain_s[...] = tail[EXPERT_COUNT : EXPERT_COUNT + 1, :depth]
    store(out_s, out_o)
    store(router_s, router_o)
    store(expert_gain_s, expert_gain_o)
    q_lines[here.z] = q_terms[here.chip, here.core, here.z]
    qkv_swap.finish()
    gain_columns = jnp.zeros((depth, LANES), jnp.float32)
    for line in range(lines):
        query_s[:, line * q_cols : (line + 1) * q_cols] = q_lines[line, :, :q_cols].astype(jnp.float32)
        key_s[:, line * kv_cols : (line + 1) * kv_cols] = q_lines[line, :, q_cols : q_cols + kv_cols].astype(
            jnp.float32
        )
        value_s[:, line * kv_cols : (line + 1) * kv_cols] = q_lines[line, :, q_cols + kv_cols : qkv_cols].astype(
            jnp.float32
        )
        gain_columns = gain_columns + q_lines[line, :, qkv_cols:].astype(jnp.float32)
    attention_gain_s[...] = padded_square(gain_columns)[:1, :depth]
    store(query_s, query_o)
    store(key_s, key_o)
    store(value_s, value_o)
    store(attention_gain_s, attention_gain_o)
    for e in range(own_experts):
        expert_rows[here.z, e] = terms[e, here.chip, here.core, here.z]
        expert_swaps[e].finish()
    store(expert_rows, expert_o)
    for group_of in (
        [grad_swap, gate_swap, attended_swap, part_swap, out_swap, qkv_swap, out_fold, qkv_fold] + folds + expert_swaps
    ):
        group_of.close()
    for copy in stores:
        copy.wait()


def deliver_kernel(*refs):
    count = (len(refs) - 4) // 3
    sources, targets, held = refs[:count], refs[count : 2 * count + 1], refs[2 * count + 1 : 3 * count + 1]
    gate_up, down, sems = refs[3 * count + 1 :]
    loads = [move(sources[n], held[n], sems.at[0, n]) for n in range(count)]
    stores = []
    depth, expert_count = gate_up.shape[:2]
    order = row_order(depth, expert_count, False)
    loads[count - 1].wait()
    rows = held[count - 1][...].reshape(expert_count * depth, gate_up.shape[2] + down.shape[2])
    gate_up[...] = matmul(order, rows[:, : gate_up.shape[2]], ROWS_BY_COLS).reshape(gate_up.shape)
    stores.append(move(gate_up, targets[count - 1], sems.at[1, count - 1]))
    down[...] = matmul(order, rows[:, gate_up.shape[2] :], ROWS_BY_COLS).reshape(down.shape)
    stores.append(move(down, targets[count], sems.at[1, count]))
    for n in range(count - 1):
        loads[n].wait()
        stores.append(move(held[n], targets[n], sems.at[1, n]))
    for copy in stores:
        copy.wait()


def fast_device(
    tokens, prefix_len, routes, cotangent, query_matrix, key_matrix, value_matrix, output_matrix,
    attention_gain, expert_gain, router_matrix, gate_up_weight, down_weight,
):
    lines = lax.axis_size("seq")
    chips = lax.axis_size("dp") // 2
    tok_rows, width = tokens.shape[1:]
    rows_all = lines * tok_rows
    depth = query_matrix.shape[0]
    query_width, key_width = query_matrix.shape[1], key_matrix.shape[1]
    q_cols, kv_cols = query_width // lines, key_width // lines
    qkv_cols = q_cols + 2 * kv_cols
    expert_count = router_matrix.shape[1]
    own_experts = expert_count // lines
    ff_width = down_weight.shape[2]
    all_ff = 3 * ff_width
    row_cols = qkv_cols + LANES
    out_cols = query_width + LANES
    half_dim = HEAD_WIDTH // 2
    low, full = jnp.bfloat16, jnp.float32

    places = np.arange(rows_all, dtype=np.float32)
    frequency = np.exp(
        np.arange(half_dim, dtype=np.float32) * np.float32(-2.0 * math.log(10000.0) / HEAD_WIDTH)
    ).astype(np.float32)
    angles = places[:, None] * frequency[None, :]
    cosine = jnp.asarray(np.tile(np.cos(angles), (1, LANES // half_dim)), jnp.float32)
    sine_table = jnp.asarray(np.tile(np.sin(angles), (1, LANES // half_dim)), jnp.float32)

    count = spread_count(lines)

    def scratch(*dims, kind=low):
        return pltpu.VMEM(dims, kind)

    def pair(*dims):
        return [pltpu.SemaphoreType.DMA(dims)] * 2

    DMA = pltpu.SemaphoreType.DMA
    by_token = (lines, tok_rows)
    five = (chips, 2, lines, depth)
    four = (chips, lines, depth)
    landed = (2, 2, lines // 2, depth)
    last = (2, lines // 2, depth)
    ends = [
        ((tok_rows, width), low), ((tok_rows, width), full), ((depth, query_width), full), ((depth, key_width), full),
        ((depth, key_width), full), ((depth, query_width), full), ((1, depth), full), ((1, depth), full), ((expert_count, depth), full),
        ((lines, own_experts, depth, all_ff), low),
    ]

    def fold_scratch(cols):
        return [scratch(*dims, cols) for dims in (five, four, landed, last)]

    results = pl.pallas_call(
        layer_kernel,
        name="layer",
        out_shape=tuple(jax.ShapeDtypeStruct(dims, kind) for dims, kind in ends),
        in_specs=[SMEM_SPEC, ANY_SPEC] + [VMEM_SPEC] * 3 + [ANY_SPEC] + [VMEM_SPEC] * 3 + [ANY_SPEC] * 3 + [VMEM_SPEC] * 3,
        out_specs=(ANY_SPEC,) * len(ends),
        scratch_shapes=[
            scratch(LANES, LANES, kind=full), scratch(lines, depth, row_cols), scratch(lines, own_experts, depth, all_ff),
            scratch(*by_token, width), scratch(width, row_cols), scratch(width, query_width), scratch(own_experts, *five, all_ff),
            scratch(*by_token, width), scratch(lines, expert_count, tok_rows), scratch(rows_all, width), scratch(rows_all, qkv_cols),
            scratch(rows_all, q_cols, kind=full), scratch(lines, rows_all, q_cols), scratch(rows_all, LANES, kind=full),
            scratch(*by_token, width), scratch(*by_token, LANES, kind=full), scratch(tok_rows, width, kind=full),
            scratch(own_experts, rows_all, 2 * ff_width), scratch(own_experts, rows_all, ff_width), scratch(own_experts, *four, all_ff),
            scratch(*by_token, width), scratch(2, lines - 1, tok_rows, width), scratch(tok_rows, width, kind=full), scratch(tok_rows, width),
            scratch(*by_token, width), scratch(2, lines - 1, tok_rows, width),
            scratch(lines, expert_count, tok_rows, kind=full), scratch(lines - 1, expert_count, tok_rows, kind=full),
            scratch(tok_rows, width, kind=full), scratch(*by_token, q_cols), scratch(*by_token, q_cols), scratch(rows_all, qkv_cols),
            scratch(rows_all, kv_cols, kind=full), scratch(rows_all, kv_cols, kind=full),
            scratch(own_experts, *landed, all_ff), scratch(own_experts, *last, all_ff),
            *fold_scratch(out_cols), scratch(lines - 1, depth, out_cols),
            *fold_scratch(row_cols), scratch(lines, depth, row_cols),
            *[scratch(*dims, kind=kind) for dims, kind in ends[2:-1]],
            DMA((6 + own_experts,)),
            *pair(count), *pair(count), *pair(own_experts, count), *pair(2, 2, lines - 1), *pair(2, lines - 1), *pair(lines),
            *pair(lines, lines), *pair(2, 2, lines - 1), *pair(2, 2, lines - 1), *pair(lines), *pair(lines), *pair(2, 2, lines - 1),
            *pair(own_experts, 7), *pair(7), *pair(7), *pair(own_experts, lines), *pair(lines), *pair(lines),
            pltpu.SemaphoreType.REGULAR((own_experts,)), DMA((len(ends),)),
        ],
        compiler_params=comm_params(1, 63),
    )(
        prefix_len, tokens[0], query_matrix, key_matrix, value_matrix, output_matrix, router_matrix.T,
        attention_gain.reshape(1, depth), expert_gain.reshape(1, depth), gate_up_weight.reshape(*four, 2 * ff_width),
        down_weight.reshape(*four, ff_width), cotangent[0], routes[0].T, cosine, sine_table,
    )
    last_ends = [((depth, expert_count, 2 * ff_width), full), ((depth, expert_count, ff_width), full)]
    results = pl.pallas_call(
        deliver_kernel,
        name="deliver",
        out_shape=tuple(jax.ShapeDtypeStruct(dims, kind) for dims, kind in ends[:-1] + last_ends),
        in_specs=[ANY_SPEC] * len(ends),
        out_specs=(ANY_SPEC,) * (len(ends) + 1),
        scratch_shapes=[pltpu.VMEM(dims, kind) for dims, kind in ends + last_ends] + [DMA((2, len(ends) + 1))],
        compiler_params=pltpu.CompilerParams(vmem_limit_bytes=63 << 20),
    )(*results)
    mixed, tokens_grad, query_grad, key_grad, value_grad, out_grad, attention_gain_grad, expert_gain_grad, router_grad, gate_up_grad, down_grad = results
    return (
        mixed[None],
        tokens_grad[None],
        query_grad,
        key_grad,
        value_grad,
        out_grad,
        attention_gain_grad.reshape(depth),
        expert_gain_grad.reshape(depth),
        router_grad.T,
        gate_up_grad,
        down_grad,
    )


def solution(mesh):
    lines, chips = mesh.shape["seq"], mesh.shape["dp"] // 2
    even = KEY_HEADS % (2 * lines) == 0 and EXPERT_COUNT % lines == 0 and chips == lines
    return jax.shard_map(
        fast_device if even else per_device,
        mesh=mesh,
        in_specs=(
            P("dp", "seq", None),
            P("dp"),
            P("dp", "seq", None),
            P("dp", "seq", None),
            P(("dp", "seq"), None),
            P(("dp", "seq"), None),
            P(("dp", "seq"), None),
            P(("dp", "seq"), None),
            P(("dp", "seq")),
            P(("dp", "seq")),
            P(("dp", "seq"), None),
            P(("dp", "seq"), None, None),
            P(("dp", "seq"), None, None),
        ),
        out_specs=(
            P("dp", "seq", None),
            P("dp", "seq", None),
            P(("dp", "seq"), None),
            P(("dp", "seq"), None),
            P(("dp", "seq"), None),
            P(("dp", "seq"), None),
            P(("dp", "seq")),
            P(("dp", "seq")),
            P(("dp", "seq"), None),
            P(("dp", "seq"), None, None),
            P(("dp", "seq"), None, None),
        ),
        check_vma=False,
    )
```

```python
import math

import jax
import jax.numpy as jnp
import numpy as np
from jax import lax
from jax.experimental import pallas as pl
from jax.experimental.pallas import tpu as pltpu
from jax.sharding import PartitionSpec as P

HEAD_WIDTH = 64
CAPACITY = 96


NORM_EPS = 1e-06
LOW_SCORE = -1e30
LANES = 128
HALF = HEAD_WIDTH // 2
SCORE_SCALE = HEAD_WIDTH ** (-0.5)
EXPERT_COUNT = 16
KEY_HEADS = 8
MESH = pl.DeviceIdType.MESH


def rotary_tables(positions, head_dim):
    half_dim = head_dim // 2
    frequency = jnp.exp(
        jnp.arange(half_dim, dtype=jnp.float32) * (-2.0 * math.log(10000.0) / head_dim)
    )
    angles = positions.astype(jnp.float32)[:, None] * frequency[None, :]
    return (jnp.cos(angles), jnp.sin(angles))


def rotate(value_rows, cosine, sine_table):
    half_dim = value_rows.shape[-1] // 2
    first_half = value_rows[..., :half_dim]
    second = value_rows[..., half_dim:]
    cos_heads = cosine[:, None, :]
    sin_heads = sine_table[:, None, :]
    return jnp.concatenate(
        [first_half * cos_heads - second * sin_heads, second * cos_heads + first_half * sin_heads],
        axis=-1,
    )


def norm_back(grad_normed, normed, inverse):
    return inverse * (grad_normed - normed * jnp.mean(grad_normed * normed, -1, keepdims=True))


def keep_state(running):
    return running


def swiglu(mid_linear, ff_width):
    return (jax.nn.silu(mid_linear[..., :ff_width]) * mid_linear[..., ff_width:]).astype(
        jnp.bfloat16
    )


def swiglu_back(act_grad, mid_linear, ff_width):
    gate_part = mid_linear[..., :ff_width]
    up_part = mid_linear[..., ff_width:]
    sigmoid = jax.nn.sigmoid(gate_part)
    gate_slope = sigmoid * (1.0 + gate_part * (1.0 - sigmoid))
    return jnp.concatenate(
        [act_grad * up_part * gate_slope, act_grad * gate_part * sigmoid], axis=-1
    ).astype(jnp.bfloat16)


def over_key_blocks(pieces, block_fn, running):
    piece_rows = pieces[0].shape[0]
    block_size = math.gcd(piece_rows, 512)
    shaped = tuple(
        (piece.reshape(piece_rows // block_size, block_size, piece.shape[1]) for piece in pieces)
    )
    offsets = block_size * jnp.arange(piece_rows // block_size, dtype=jnp.int32)

    def advance(carried, block_item):
        return (block_fn(carried, block_item[0], block_item[1], block_item[2]), None)

    result_state, unused = lax.scan(advance, running, (shaped[0], shaped[1], offsets))
    return result_state


def per_device(
    tokens,
    prefix_len,
    routes,
    cotangent,
    query_matrix,
    key_matrix,
    value_matrix,
    output_matrix,
    attention_gain,
    expert_gain,
    router_matrix,
    gate_up_weight,
    down_weight,
):
    hidden = tokens[0].astype(jnp.float32)
    tok_rows, model_width = hidden.shape
    params = (
        lax.all_gather(query_matrix, ("dp", "seq"), axis=0, tiled=True),
        lax.all_gather(key_matrix, ("dp", "seq"), axis=0, tiled=True),
        lax.all_gather(value_matrix, ("dp", "seq"), axis=0, tiled=True),
        lax.all_gather(output_matrix, ("dp", "seq"), axis=0, tiled=True),
        lax.all_gather(attention_gain, ("dp", "seq"), axis=0, tiled=True),
        lax.all_gather(expert_gain, ("dp", "seq"), axis=0, tiled=True),
        lax.all_gather(router_matrix, ("dp", "seq"), axis=0, tiled=True),
    )
    query_full, key_full, value_full, output_full, gain_attention, gain_expert, router_full = params
    head_dim = HEAD_WIDTH
    query_width = query_full.shape[1]
    key_width = key_full.shape[1]
    query_heads = query_width // head_dim
    key_groups = key_width // head_dim
    head_group = query_heads // key_groups
    score_scale = head_dim ** (-0.5)
    first_place = lax.axis_index("seq") * tok_rows
    positions = first_place + jnp.arange(tok_rows, dtype=jnp.int32)
    last_place = first_place + tok_rows - 1
    prefix_end = prefix_len[0]
    cosine, sine_table = rotary_tables(positions, head_dim)
    inverse_attention = lax.rsqrt(jnp.mean(hidden * hidden, -1, keepdims=True) + NORM_EPS)
    normed_attention = hidden * inverse_attention
    attention_input = (normed_attention * gain_attention.astype(jnp.float32)).astype(jnp.bfloat16)
    query_projected = jnp.dot(
        attention_input, query_full, preferred_element_type=jnp.float32
    ).reshape(tok_rows, query_heads, head_dim)
    queries = (
        rotate(query_projected, cosine, sine_table)
        .astype(jnp.bfloat16)
        .reshape(tok_rows, key_groups, head_group, head_dim)
    )
    key_projected = jnp.dot(attention_input, key_full, preferred_element_type=jnp.float32).reshape(
        tok_rows, key_groups, head_dim
    )
    keys_local = (
        rotate(key_projected, cosine, sine_table).astype(jnp.bfloat16).reshape(tok_rows, key_width)
    )
    values_local = jnp.dot(attention_input, value_full, preferred_element_type=jnp.float32).astype(
        jnp.bfloat16
    )

    def block_scores(key_block, key_start):
        block_size = key_block.shape[0]
        key_heads = key_block.reshape(block_size, key_groups, head_dim)
        key_places = key_start + jnp.arange(block_size, dtype=jnp.int32)
        allowed = (key_places[None, :] <= positions[:, None]) | (key_places[None, :] < prefix_end)
        scores = (
            jnp.einsum("qhgd,khd->hgqk", queries, key_heads, preferred_element_type=jnp.float32)
            * score_scale
        )
        return (jnp.where(allowed, scores, -jnp.inf), key_heads)

    def attend(running, key_block, value_block, key_start):

        def compute(carried):
            run_max, run_sum, weighted = carried
            scores, key_heads = block_scores(key_block, key_start)
            value_heads = value_block.reshape(key_block.shape[0], key_groups, head_dim)
            new_max = jnp.maximum(run_max, jnp.max(scores, -1))
            weights = jnp.exp(scores - new_max[..., None])
            factor = jnp.exp(run_max - new_max)
            new_sum = run_sum * factor + jnp.sum(weights, -1)
            new_weighted = weighted * factor[..., None] + jnp.einsum(
                "hgqk,khd->hgqd",
                weights.astype(jnp.bfloat16),
                value_heads,
                preferred_element_type=jnp.float32,
            )
            return (new_max, new_sum, new_weighted)

        visible = (key_start <= last_place) | (key_start < prefix_end)
        return lax.cond(visible, compute, keep_state, running)

    stat_shape = (key_groups, head_group, tok_rows)
    start_state = (
        jnp.full(stat_shape, LOW_SCORE, jnp.float32),
        jnp.zeros(stat_shape, jnp.float32),
        jnp.zeros(stat_shape + (head_dim,), jnp.float32),
    )
    run_max, run_sum, weighted = over_key_blocks(
        (
            lax.all_gather(keys_local, "seq", axis=0, tiled=True),
            lax.all_gather(values_local, "seq", axis=0, tiled=True),
        ),
        attend,
        start_state,
    )
    log_total = run_max + jnp.log(run_sum)
    attended_heads = weighted / run_sum[..., None]
    attention_lowered = (
        attended_heads.transpose(2, 0, 1, 3).reshape(tok_rows, query_width).astype(jnp.bfloat16)
    )
    branch_output = jnp.einsum(
        "tc,dc->td", attention_lowered, output_full, preferred_element_type=jnp.float32
    )
    middle = hidden + branch_output
    inverse_expert = lax.rsqrt(jnp.mean(middle * middle, -1, keepdims=True) + NORM_EPS)
    normed_expert = middle * inverse_expert
    expert_input = (normed_expert * gain_expert.astype(jnp.float32)).astype(jnp.bfloat16)
    router_logits = jnp.dot(expert_input, router_full, preferred_element_type=jnp.float32)
    router_probs = jax.nn.softmax(router_logits, axis=-1)
    expert_count = router_full.shape[1]
    route_ids = routes[0]
    expert_range = jnp.arange(expert_count, dtype=jnp.int32)
    route_hits = jnp.sum(
        (route_ids[:, :, None] == expert_range[None, None, :]).astype(jnp.int32), 1
    )
    slot_rank = jnp.cumsum(route_hits, 0) - 1
    slot_target = jnp.where(route_hits > 0, slot_rank, CAPACITY)
    token_index = jnp.broadcast_to(
        jnp.arange(tok_rows, dtype=jnp.int32)[:, None], (tok_rows, expert_count)
    )
    expert_index = jnp.broadcast_to(expert_range[None, :], (tok_rows, expert_count))
    slot_table = (
        jnp.zeros((expert_count, CAPACITY), jnp.int32)
        .at[expert_index, slot_target]
        .set(token_index, mode="drop")
    )
    slot_live = jnp.arange(CAPACITY, dtype=jnp.int32)[None, :] < jnp.sum(route_hits, 0)[:, None]
    expert_column = expert_range[:, None]
    dispatched = expert_input[slot_table]
    slot_gates = jnp.where(slot_live, router_probs[slot_table, expert_column], 0.0)
    ff_width = down_weight.shape[2]
    grad_mid = cotangent[0].astype(jnp.float32)
    slot_grad = grad_mid[slot_table]
    out_grad = (slot_gates[..., None] * slot_grad).astype(jnp.bfloat16)
    gate_up_full, down_full = (
        lax.all_gather(gate_up_weight, ("dp", "seq"), axis=0, tiled=True),
        lax.all_gather(down_weight, ("dp", "seq"), axis=0, tiled=True),
    )
    mid_linear = jnp.einsum(
        "ecd,def->ecf", dispatched, gate_up_full, preferred_element_type=jnp.float32
    )
    activation = swiglu(mid_linear, ff_width)
    expert_out = jnp.einsum(
        "ecf,def->ecd", activation, down_full, preferred_element_type=jnp.float32
    )
    flat_slots = slot_table.reshape(-1)
    combined = (
        jnp.zeros((tok_rows, model_width), jnp.float32)
        .at[flat_slots]
        .add((slot_gates[..., None] * expert_out).reshape(-1, model_width))
    )
    mixed = (middle + combined).astype(jnp.bfloat16)
    gate_grad = jnp.where(slot_live, jnp.sum(expert_out * slot_grad, -1), 0.0)
    act_grad = jnp.einsum("ecd,def->ecf", out_grad, down_full, preferred_element_type=jnp.float32)
    mid_grad = swiglu_back(act_grad, mid_linear, ff_width)
    gate_up_term = jnp.einsum(
        "ecd,ecf->def", dispatched, mid_grad, preferred_element_type=jnp.float32
    )
    down_term = jnp.einsum("ecd,ecf->def", out_grad, activation, preferred_element_type=jnp.float32)
    summed_terms = lax.psum_scatter(
        jnp.concatenate([gate_up_term, down_term], axis=-1),
        ("dp", "seq"),
        scatter_dimension=0,
        tiled=True,
    )
    gate_up_weight_grad = summed_terms[..., : 2 * ff_width]
    down_weight_grad = summed_terms[..., 2 * ff_width :]
    dispatched_grad = jnp.einsum(
        "ecf,def->ecd", mid_grad, gate_up_full, preferred_element_type=jnp.float32
    )
    expert_in_grad = (
        jnp.zeros((tok_rows, model_width), jnp.float32)
        .at[flat_slots]
        .add(dispatched_grad.reshape(-1, model_width))
    )
    prob_grad = (
        jnp.zeros((tok_rows, expert_count), jnp.float32)
        .at[slot_table, expert_column]
        .add(gate_grad)
    )
    logit_grad = (
        router_probs * (prob_grad - jnp.sum(router_probs * prob_grad, -1, keepdims=True))
    ).astype(jnp.bfloat16)
    router_term = jnp.einsum(
        "td,te->de", expert_input, logit_grad, preferred_element_type=jnp.float32
    )
    expert_in_grad = expert_in_grad + jnp.einsum(
        "te,de->td", logit_grad, router_full, preferred_element_type=jnp.float32
    )
    expert_gain_term = jnp.sum(expert_in_grad * normed_expert, 0)
    grad_res = grad_mid + norm_back(
        expert_in_grad * gain_expert.astype(jnp.float32), normed_expert, inverse_expert
    )
    branch_grad = grad_res.astype(jnp.bfloat16)
    output_term = jnp.einsum(
        "td,tc->dc", branch_grad, attention_lowered, preferred_element_type=jnp.float32
    )
    attended_grad = jnp.dot(branch_grad, output_full, preferred_element_type=jnp.float32).astype(
        jnp.bfloat16
    )
    attended_grad_heads = attended_grad.reshape(
        tok_rows, key_groups, head_group, head_dim
    ).transpose(1, 2, 0, 3)
    delta = jnp.sum(attended_grad_heads.astype(jnp.float32) * attended_heads, -1)
    seq_total = tok_rows * lax.axis_size("seq")

    def attend_back(running, key_block, value_block, key_start):

        def compute(carried):
            query_sum, key_sum, value_sum = carried
            block_size = key_block.shape[0]
            scores, key_heads = block_scores(key_block, key_start)
            value_heads = value_block.reshape(block_size, key_groups, head_dim)
            probs_full = jnp.exp(scores - log_total[..., None])
            probs_low = probs_full.astype(jnp.bfloat16)
            value_piece = jnp.einsum(
                "hgqk,hgqd->khd", probs_low, attended_grad_heads, preferred_element_type=jnp.float32
            ).reshape(block_size, key_width)
            prob_part = jnp.einsum(
                "hgqd,khd->hgqk",
                attended_grad_heads,
                value_heads,
                preferred_element_type=jnp.float32,
            )
            score_grad = (probs_full * (prob_part - delta[..., None])).astype(jnp.bfloat16)
            query_sum = (
                query_sum
                + jnp.einsum(
                    "hgqk,khd->hgqd", score_grad, key_heads, preferred_element_type=jnp.float32
                )
                * score_scale
            )
            key_piece = (
                jnp.einsum(
                    "hgqk,qhgd->khd", score_grad, queries, preferred_element_type=jnp.float32
                )
                * score_scale
            ).reshape(block_size, key_width)
            key_sum = lax.dynamic_update_slice_in_dim(
                key_sum,
                lax.dynamic_slice_in_dim(key_sum, key_start, block_size, 0) + key_piece,
                key_start,
                0,
            )
            value_sum = lax.dynamic_update_slice_in_dim(
                value_sum,
                lax.dynamic_slice_in_dim(value_sum, key_start, block_size, 0) + value_piece,
                key_start,
                0,
            )
            return (query_sum, key_sum, value_sum)

        visible = (key_start <= last_place) | (key_start < prefix_end)
        return lax.cond(visible, compute, keep_state, running)

    back_start = (
        jnp.zeros(stat_shape + (head_dim,), jnp.float32),
        jnp.zeros((seq_total, key_width), jnp.float32),
        jnp.zeros((seq_total, key_width), jnp.float32),
    )
    query_sum, key_sum, value_sum = over_key_blocks(
        (
            lax.all_gather(keys_local, "seq", axis=0, tiled=True),
            lax.all_gather(values_local, "seq", axis=0, tiled=True),
        ),
        attend_back,
        back_start,
    )
    key_part, value_part = (
        lax.psum_scatter(
            key_sum.astype(jnp.bfloat16), "seq", scatter_dimension=0, tiled=True
        ).astype(jnp.float32),
        lax.psum_scatter(
            value_sum.astype(jnp.bfloat16), "seq", scatter_dimension=0, tiled=True
        ).astype(jnp.float32),
    )
    query_rows = query_sum.transpose(2, 0, 1, 3).reshape(tok_rows, query_heads, head_dim)
    query_grad = (
        rotate(query_rows, cosine, -sine_table).reshape(tok_rows, query_width).astype(jnp.bfloat16)
    )
    key_grad = (
        rotate(key_part.reshape(tok_rows, key_groups, head_dim), cosine, -sine_table)
        .reshape(tok_rows, key_width)
        .astype(jnp.bfloat16)
    )
    value_grad = value_part.astype(jnp.bfloat16)
    query_term = jnp.einsum(
        "td,tc->dc", attention_input, query_grad, preferred_element_type=jnp.float32
    )
    key_term = jnp.einsum(
        "td,tc->dc", attention_input, key_grad, preferred_element_type=jnp.float32
    )
    value_term = jnp.einsum(
        "td,tc->dc", attention_input, value_grad, preferred_element_type=jnp.float32
    )
    attention_in_grad = jnp.einsum(
        "tc,dc->td", query_grad, query_full, preferred_element_type=jnp.float32
    )
    attention_in_grad = attention_in_grad + jnp.einsum(
        "tc,dc->td", key_grad, key_full, preferred_element_type=jnp.float32
    )
    attention_in_grad = attention_in_grad + jnp.einsum(
        "tc,dc->td", value_grad, value_full, preferred_element_type=jnp.float32
    )
    attention_gain_term = jnp.sum(attention_in_grad * normed_attention, 0)
    tokens_grad = grad_res + norm_back(
        attention_in_grad * gain_attention.astype(jnp.float32), normed_attention, inverse_attention
    )
    summed_grads = (
        lax.psum_scatter(query_term, ("dp", "seq"), scatter_dimension=0, tiled=True),
        lax.psum_scatter(key_term, ("dp", "seq"), scatter_dimension=0, tiled=True),
        lax.psum_scatter(value_term, ("dp", "seq"), scatter_dimension=0, tiled=True),
        lax.psum_scatter(output_term, ("dp", "seq"), scatter_dimension=0, tiled=True),
        lax.psum_scatter(attention_gain_term, ("dp", "seq"), scatter_dimension=0, tiled=True),
        lax.psum_scatter(expert_gain_term, ("dp", "seq"), scatter_dimension=0, tiled=True),
        lax.psum_scatter(router_term, ("dp", "seq"), scatter_dimension=0, tiled=True),
    )
    return (
        mixed[None],
        tokens_grad[None],
        summed_grads[0],
        summed_grads[1],
        summed_grads[2],
        summed_grads[3],
        summed_grads[4],
        summed_grads[5],
        summed_grads[6],
        gate_up_weight_grad,
        down_weight_grad,
    )


def matmul(left, right, contract):
    return lax.dot_general(
        left, right, (contract, ((), ())), preferred_element_type=jnp.float32
    )


ROWS_BY_COLS = ((1,), (0,))
ROWS_BY_ROWS = ((1,), (1,))
COLS_BY_COLS = ((0,), (0,))


def split_sum_columns(terms):
    ones = jnp.ones((terms.shape[0], LANES), jnp.bfloat16)
    high = terms.astype(jnp.bfloat16)
    low = (terms - high.astype(jnp.float32)).astype(jnp.bfloat16)
    return matmul(high, ones, COLS_BY_COLS) + matmul(low, ones, COLS_BY_COLS)


def turned(value_rows):
    width = value_rows.shape[1]
    lane = lax.broadcasted_iota(jnp.int32, value_rows.shape, 1)
    ahead = pltpu.roll(value_rows, width - HALF, 1)
    behind = pltpu.roll(value_rows, HALF, 1)
    return jnp.where(lane % HEAD_WIDTH < HALF, -ahead, behind)


def spin(value_rows, cosine, sine_table):
    repeats = value_rows.shape[1] // LANES
    cos_all = jnp.concatenate([cosine] * repeats, 1) if repeats > 1 else cosine
    sin_all = jnp.concatenate([sine_table] * repeats, 1) if repeats > 1 else sine_table
    return value_rows * cos_all + turned(value_rows) * sin_all


def inverse_rms(value_rows):
    return lax.rsqrt(jnp.mean(value_rows * value_rows, -1, keepdims=True) + NORM_EPS)


def shape_of(*dims, kind=jnp.bfloat16):
    return jax.ShapeDtypeStruct(dims, kind)


VMEM_SPEC = pl.BlockSpec(memory_space=pltpu.VMEM)
SMEM_SPEC = pl.BlockSpec(memory_space=pltpu.SMEM)
ANY_SPEC = pl.BlockSpec(memory_space=pl.ANY)


class Place:
    def __init__(self):
        self.dp = lax.axis_index("dp")
        self.z = lax.axis_index("seq")
        self.lines = lax.axis_size("seq")
        self.chips = lax.axis_size("dp") // 2
        self.chip = self.dp // 2
        self.core = self.dp % 2
        self.other = 1 - self.core
        self.chip_x = self.chip + 1 - 2 * (self.chip % 2)
        self.chip_y = (self.chip + 2) % 4
        self.chip_diag = 3 - self.chip

    def ahead(self, step):
        return (self.z + step) % self.lines

    def behind(self, step):
        return (self.z + self.lines - step) % self.lines

    def line_peer(self, step):
        return (self.dp, self.ahead(step))

    def on_chip(self, chip):
        return (chip * 2 + self.core, self.z)

    def sibling(self):
        return (self.chip * 2 + self.other, self.z)


def meet(peers):
    barrier = pltpu.get_barrier_semaphore()
    for peer in peers:
        pl.semaphore_signal(barrier, inc=1, device_id=peer, device_id_type=MESH)
    pl.semaphore_wait(barrier, len(peers))


def send(source, target, send_sem, recv_sem, peer):
    copy = pltpu.make_async_remote_copy(
        src_ref=source,
        dst_ref=target,
        send_sem=send_sem,
        recv_sem=recv_sem,
        device_id=peer,
        device_id_type=MESH,
    )
    copy.start()
    return copy


def move(source, target, sem):
    copy = pltpu.make_async_copy(source, target, sem)
    copy.start()
    return copy


def all_peers(here):
    return (
        [here.line_peer(k) for k in range(1, here.lines)]
        + [here.on_chip(chip) for chip in (here.chip_x, here.chip_y, here.chip_diag)]
        + [here.sibling()]
    )


def comm_params(ident, limit=56):
    return pltpu.CompilerParams(
        collective_id=ident, has_side_effects=True, vmem_limit_bytes=limit << 20
    )


class Spread:
    def __init__(self, here, pick, target, depth, local_sem, sends, recvs):
        self.here, self.pick, self.target, self.depth = here, pick, target, depth
        self.local_sem, self.sends, self.recvs = local_sem, sends, recvs
        self.used = 0

    def put(self, source, target, peer):
        copy = send(source, target, self.sends.at[self.used], self.recvs.at[self.used], peer)
        self.used += 1
        return copy

    def row(self):
        here = self.here
        if len(self.target.shape) > 2:
            return self.target.at[here.chip, here.core, here.z]
        first = (here.dp * here.lines + here.z) * self.depth
        return self.target.at[pl.ds(pl.multiple_of(first, self.depth), self.depth)]

    def chip_rows(self, chip, part=None):
        here = self.here
        if len(self.target.shape) > 2:
            if part is None:
                return self.target.at[chip, here.core]
            return self.target.at[chip, here.core, pl.ds(part * (here.lines // 2), here.lines // 2)]
        count = here.lines * self.depth
        first = (chip * 2 + here.core) * count
        if part is not None:
            first, count = first + part * (count // 2), count // 2
        return self.target.at[pl.ds(pl.multiple_of(first, count), count)]

    def start(self):
        here = self.here
        mine = self.row()
        self.own = move(self.pick(here.z), mine, self.local_sem)
        self.line = [
            self.put(self.pick(here.ahead(k)), mine, here.line_peer(k)) for k in range(1, here.lines)
        ]

    def chips(self):
        here = self.here
        self.own.wait()
        for copy in self.line:
            copy.wait_recv()
        mine = self.chip_rows(here.chip)
        self.plane = [
            self.put(mine, mine, here.on_chip(here.chip_x)),
            self.put(mine, mine, here.on_chip(here.chip_y)),
        ]
        self.across = [self.put(mine, mine, here.sibling())]

    def turn(self):
        here = self.here
        self.corner = []
        for copy, origin, onward, part in (
            (self.plane[0], here.chip_x, here.chip_y, 0),
            (self.plane[1], here.chip_y, here.chip_x, 1),
        ):
            copy.wait_recv()
            half = self.chip_rows(origin, part)
            self.corner.append(self.put(half, half, here.on_chip(onward)))
            block = self.chip_rows(origin)
            self.across.append(self.put(block, block, here.sibling()))

    def cores(self):
        here = self.here
        for copy in self.corner:
            copy.wait_recv()
        block = self.chip_rows(here.chip_diag)
        self.across.append(self.put(block, block, here.sibling()))

    def finish(self):
        for copy in self.across:
            copy.wait_recv()

    def close(self):
        for copy in self.line + self.plane + self.corner + self.across:
            copy.wait_send()


def spread_count(lines):
    return lines - 1 + 2 + 2 + 4


class LineGather:
    def __init__(self, here, view, sends, recvs, source=None):
        self.here, self.view, self.source = here, view, source
        self.sends, self.recvs = sends, recvs

    def copy(self, way, hop, block, source=None):
        here = self.here
        step = 1 if way == 0 else here.lines - 1
        return pltpu.make_async_remote_copy(
            src_ref=self.view(block) if source is None else source,
            dst_ref=self.view(block),
            send_sem=self.sends.at[way, hop - 1],
            recv_sem=self.recvs.at[way, hop - 1],
            device_id=here.line_peer(step),
            device_id_type=MESH,
        )

    def start(self):
        here = self.here

        @pl.when(here.z < here.lines - 1)
        def rightward():
            self.copy(0, 1, here.z, self.source).start()

        @pl.when(here.z > 0)
        def leftward():
            self.copy(1, 1, here.z, self.source).start()

    def step(self, hop):
        here = self.here
        lines = here.lines

        @pl.when(here.z >= hop)
        def from_left():
            block = here.behind(hop)
            self.copy(0, hop, block).wait_recv()
            if hop < lines - 1:

                @pl.when(here.z < lines - 1)
                def onward():
                    self.copy(0, hop + 1, block).start()

        @pl.when(here.z + hop < lines)
        def from_right():
            block = here.ahead(hop)
            self.copy(1, hop, block).wait_recv()
            if hop < lines - 1:

                @pl.when(here.z > 0)
                def onward():
                    self.copy(1, hop + 1, block).start()

    def close(self):
        here = self.here
        lines = here.lines
        for hop in range(1, lines):

            @pl.when((here.z >= hop - 1) & (here.z < lines - 1))
            def rightward():
                self.copy(0, hop, here.behind(hop - 1)).wait_send()

            @pl.when((here.z + hop - 1 < lines) & (here.z > 0))
            def leftward():
                self.copy(1, hop, here.ahead(hop - 1)).wait_send()


class LineSpread:
    def __init__(self, here, view, sends, recvs, source=None):
        self.here, self.view, self.source = here, view, source
        self.sends, self.recvs = sends, recvs

    def start(self):
        here = self.here
        mine = self.view(here.z)
        self.line = [
            send(
                mine if self.source is None else self.source, mine, self.sends.at[k - 1], self.recvs.at[k - 1], here.line_peer(k)
            )
            for k in range(1, here.lines)
        ]

    def arrived(self, step):
        self.line[step - 1].wait_recv()

    def finish(self):
        for copy in self.line:
            copy.wait_recv()

    def close(self):
        for copy in self.line:
            copy.wait_send()


class LineSum:
    def __init__(self, here, parts, landed, rows, sends, recvs):
        self.here, self.parts, self.landed, self.rows = here, parts, landed, rows
        self.sends, self.recvs = sends, recvs

    def copy(self, way, hops):
        here = self.here
        step = 1 if way == 0 else here.lines - 1
        block = here.ahead(hops) if way == 0 else here.behind(hops)
        return pltpu.make_async_remote_copy(
            src_ref=self.parts.at[block, self.rows],
            dst_ref=self.landed.at[way, hops - 1, self.rows],
            send_sem=self.sends.at[way, hops - 1],
            recv_sem=self.recvs.at[way, hops - 1],
            device_id=here.line_peer(step),
            device_id_type=MESH,
        )

    def launch(self, hops):
        here = self.here

        @pl.when(here.z == 0)
        def rightward():
            self.copy(0, hops).start()

        @pl.when(here.z == here.lines - 1)
        def leftward():
            self.copy(1, hops).start()

    def step(self, hops):
        here = self.here
        lines = here.lines

        def pass_on(way):
            block = here.ahead(hops) if way == 0 else here.behind(hops)
            self.copy(way, hops + 1).wait_recv()
            self.parts[block, self.rows] = (
                self.parts[block, self.rows].astype(jnp.float32)
                + self.landed[way, hops, self.rows].astype(jnp.float32)
            ).astype(self.parts.dtype)
            self.copy(way, hops).start()

        @pl.when((here.z > 0) & (here.z + hops < lines))
        def rightward():
            pass_on(0)

        @pl.when((here.z < lines - 1) & (here.z >= hops))
        def leftward():
            pass_on(1)

    def finish(self, total):
        here = self.here
        rows = self.rows
        total[rows, :] = self.parts[here.z, rows].astype(jnp.float32)

        @pl.when(here.z > 0)
        def from_left():
            self.copy(0, 1).wait_recv()
            total[rows, :] = total[rows, :] + self.landed[0, 0, rows].astype(jnp.float32)

        @pl.when(here.z < here.lines - 1)
        def from_right():
            self.copy(1, 1).wait_recv()
            total[rows, :] = total[rows, :] + self.landed[1, 0, rows].astype(jnp.float32)

    def close(self):
        here = self.here
        for hops in range(1, here.lines):

            @pl.when(here.z + hops < here.lines)
            def rightward():
                self.copy(0, hops).wait_send()

            @pl.when(here.z >= hops)
            def leftward():
                self.copy(1, hops).wait_send()


class Halves:
    def __init__(self, *members):
        self.members = members

    def start(self):
        for member in self.members:
            member.start()

    def launch(self, hops):
        for member in self.members:
            member.launch(hops)

    def step(self, hops):
        for member in self.members:
            member.step(hops)

    def finish(self, total):
        for member in self.members:
            member.finish(total)

    def close(self):
        for member in self.members:
            member.close()


class LineSwap:
    def __init__(self, here, pick, received, sends, recvs):
        self.here, self.pick, self.received = here, pick, received
        self.sends, self.recvs = sends, recvs

    def start(self):
        here = self.here
        self.line = [
            send(
                self.pick(here.ahead(k)), self.received(k, here.z), self.sends.at[k - 1], self.recvs.at[k - 1], here.line_peer(k)
            )
            for k in range(1, here.lines)
        ]

    def finish(self):
        for copy in self.line:
            copy.wait_recv()

    def close(self):
        for copy in self.line:
            copy.wait_send()


def padded_square(block):
    filler = jnp.zeros((LANES - block.shape[0], LANES), jnp.float32)
    return jnp.concatenate([block, filler], 0).T


def row_order(depth, experts, by_expert):
    count = depth * experts
    place = lax.broadcasted_iota(jnp.int32, (count, count), 0)
    source = lax.broadcasted_iota(jnp.int32, (count, count), 1)
    if by_expert:
        wanted = place % depth * experts + place // depth
    else:
        wanted = place % experts * depth + place // experts
    return (source == wanted).astype(jnp.bfloat16)


class Fold:
    def __init__(self, here, terms, crossed, landed, last, sends, recvs):
        self.here, self.terms, self.crossed = here, terms, crossed
        self.landed, self.last = landed, last
        self.sends, self.recvs = sends, recvs
        middle = here.lines // 2
        self.parts = [(0, middle), (middle, here.lines)]

    def start(self):
        here = self.here
        self.first = send(
            self.terms.at[:, here.other], self.crossed, self.sends.at[0], self.recvs.at[0], here.sibling()
        )

    def chips(self):
        here = self.here
        self.first.wait_recv()
        for chip in range(here.chips):
            self.terms[chip, here.core] = (
                self.terms[chip, here.core].astype(jnp.float32) + self.crossed[chip].astype(jnp.float32)
            ).astype(jnp.bfloat16)
        self.one, self.straight = [], []
        for number, near in enumerate((here.chip_x, here.chip_y)):
            low, high = self.parts[number]
            for slot, chip, group in ((1, here.chip_diag, self.one), (0, near, self.straight)):
                place = 1 + number * 2 + slot
                group.append(
                    send(
                        self.terms.at[chip, here.core, low:high], self.landed.at[number, slot],
                        self.sends.at[place], self.recvs.at[place], here.on_chip(near),
                    )
                )

    def turn(self):
        here = self.here
        self.two = []
        for number, onward in enumerate((here.chip_y, here.chip_x)):
            low, high = self.parts[number]
            self.one[number].wait_recv()
            self.terms[onward, here.core, low:high] = (
                self.terms[onward, here.core, low:high].astype(jnp.float32)
                + self.landed[number, 1].astype(jnp.float32)
            ).astype(jnp.bfloat16)
            place = 5 + number
            self.two.append(
                send(
                    self.terms.at[onward, here.core, low:high], self.last.at[number],
                    self.sends.at[place], self.recvs.at[place], here.on_chip(onward),
                )
            )

    def finish(self):
        here = self.here
        for number in range(2):
            low, high = self.parts[number]
            self.straight[number].wait_recv()
            self.two[number].wait_recv()
            self.terms[here.chip, here.core, low:high] = (
                self.terms[here.chip, here.core, low:high].astype(jnp.float32)
                + self.landed[number, 0].astype(jnp.float32)
                + self.last[number].astype(jnp.float32)
            ).astype(jnp.bfloat16)

    def sums(self, z):
        return self.terms.at[self.here.chip, self.here.core, z]

    def close(self):
        for copy in [self.first] + self.one + self.straight + self.two:
            copy.wait_send()


def layer_kernel(
    prefix, tokens, query_rows, key_rows, value_rows, out_rows, router_cols, attention_gain, expert_gain, gate_up_rows, down_rows,
    cotangent, routes, cosine, sine_table,
    mixed_o, tokens_grad_o, query_o, key_o, value_o, out_o, attention_gain_o, expert_gain_o, router_o, expert_o,
    square, rows, expert_rows, tokens_all, weights, out_full, terms, cot_all, chosen_all, att_in, qkv, attended, attended_all,
    log_total, expert_in, probs, middle, slopes, acts, mids, part_mix, got_mix, mix_total, mixed, part_grad, got_grad,
    gate_grad, got_gate, grad_res, attended_grad, attended_grad_all, joined_grad, key_sum, value_sum, e_landed, e_last,
    o_terms, o_crossed, o_landed, o_last, o_lines, q_terms, q_crossed, q_landed, q_last, q_lines,
    query_s, key_s, value_s, out_s, attention_gain_s, expert_gain_s, router_s,
    local_sem, r_sends, r_recvs, o_sends, o_recvs, e_sends, e_recvs, t_sends, t_recvs, c_sends, c_recvs, k_sends, k_recvs,
    a_sends, a_recvs, m_sends, m_recvs, x_sends, x_recvs, g_sends, g_recvs, b_sends, b_recvs, p_sends, p_recvs,
    f_sends, f_recvs, of_sends, of_recvs, q_sends, q_recvs, el_sends, el_recvs, ol_sends, ol_recvs, ql_sends, ql_recvs,
    free_sem, out_sem,
):
    here = Place()
    lines = here.lines
    tok_rows, width = tokens.shape
    rows_all = lines * tok_rows
    depth = rows.shape[1]
    own_experts = terms.shape[0]
    ff_width = terms.shape[5] // 3
    chips = here.chips
    five = (chips, 2, lines, depth)
    four = (chips, lines, depth)
    query_width = lines * (qkv.shape[1] // 2)
    qkv_cols = qkv.shape[1]
    kv_cols = qkv_cols // 4
    q_cols = 2 * kv_cols
    stores = []

    def store(source, target):
        stores.append(move(source, target, out_sem.at[len(stores)]))

    gate_up_load = move(gate_up_rows, mids.at[0, ..., : 2 * ff_width], local_sem.at[0])
    down_load = move(down_rows, mids.at[0, ..., 2 * ff_width :], local_sem.at[1])
    token_load = move(tokens, tokens_all.at[here.z], local_sem.at[2])
    cot_load = move(cotangent, cot_all.at[here.z], local_sem.at[3])

    square[...] = jnp.zeros_like(square)
    square[:EXPERT_COUNT, :depth] = router_cols[...].astype(jnp.float32)
    square[EXPERT_COUNT : EXPERT_COUNT + 1, :depth] = attention_gain[...].astype(jnp.float32)
    square[EXPERT_COUNT + 1 : EXPERT_COUNT + 2, :depth] = expert_gain[...].astype(jnp.float32)
    small = square[...].T[:depth, :].astype(jnp.bfloat16)
    for line in range(lines):
        rows[line, :, :q_cols] = query_rows[:, line * q_cols : (line + 1) * q_cols]
        rows[line, :, q_cols : q_cols + kv_cols] = key_rows[:, line * kv_cols : (line + 1) * kv_cols]
        rows[line, :, q_cols + kv_cols : qkv_cols] = value_rows[:, line * kv_cols : (line + 1) * kv_cols]
        rows[line, :, qkv_cols:] = small
    meet(all_peers(here))
    rows_spread = Spread(here, lambda z: rows.at[z], weights, depth, local_sem.at[4], r_sends, r_recvs)
    half = tok_rows // 2
    token_gathers = [
        LineGather(
            here, lambda z, n=n: tokens_all.at[z, pl.ds(n * half, half)], t_sends.at[n], t_recvs.at[n], tokens.at[pl.ds(n * half, half)]
        )
        for n in range(2)
    ]
    out_spread = Spread(here, lambda z: out_rows, out_full, depth, local_sem.at[5], o_sends, o_recvs)
    chosen_swap = LineSwap(
        here, lambda z: chosen_all.at[here.z], lambda k, z: chosen_all.at[z], k_sends, k_recvs
    )
    cot_gather = Halves(
        *[
            LineGather(
                here, lambda z, n=n: cot_all.at[z, pl.ds(n * half, half)], c_sends.at[n], c_recvs.at[n], cotangent.at[pl.ds(n * half, half)]
            )
            for n in range(2)
        ]
    )
    expert_spreads = [
        Spread(
            here,
            lambda z, e=e: expert_rows.at[z, e], terms.at[e], depth, local_sem.at[6 + e], e_sends.at[e], e_recvs.at[e],
        )
        for e in range(own_experts)
    ]
    rows_spread.start()
    gate_up_load.wait()
    down_load.wait()
    order = row_order(depth, EXPERT_COUNT, True)
    expert_rows[...] = (
        matmul(order, mids[0].reshape(depth * EXPERT_COUNT, 3 * ff_width), ROWS_BY_COLS)
        .astype(jnp.bfloat16)
        .reshape(expert_rows.shape)
    )
    expert_spreads[0].start()
    token_gathers[0].start()
    token_gathers[1].start()
    expert_spreads[1].start()
    expert_id = lax.broadcasted_iota(jnp.int32, (EXPERT_COUNT, tok_rows), 0)
    chosen = jnp.zeros((EXPERT_COUNT, tok_rows), jnp.float32)
    for number in range(routes.shape[0]):
        chosen = chosen + (routes[number : number + 1, :] == expert_id).astype(jnp.float32)
    chosen_all[here.z] = chosen.astype(jnp.bfloat16)
    chosen_swap.start()
    rows_spread.chips()
    rows_spread.turn()
    rows_spread.cores()
    expert_spreads[0].chips()
    token_gathers[0].step(1)
    token_gathers[1].step(1)
    rows_spread.finish()
    columns = weights[:, qkv_cols:].astype(jnp.float32).T
    gain_attention = columns[EXPERT_COUNT : EXPERT_COUNT + 1, :]
    gain_expert = columns[EXPERT_COUNT + 1 : EXPERT_COUNT + 2, :]

    def project(source):
        block = pl.ds(pl.multiple_of(source * tok_rows, tok_rows), tok_rows)
        hidden = tokens_all[source].astype(jnp.float32)
        normed = (hidden * inverse_rms(hidden) * gain_attention).astype(jnp.bfloat16)
        att_in[block, :] = normed
        linear = matmul(normed, weights[:, :qkv_cols], ROWS_BY_COLS)
        turned_part = linear[:, : q_cols + kv_cols]
        qkv[block, : q_cols + kv_cols] = spin(turned_part, cosine[block, :], sine_table[block, :]).astype(
            jnp.bfloat16
        )
        qkv[block, q_cols + kv_cols :] = linear[:, q_cols + kv_cols :].astype(jnp.bfloat16)

    def project_hop(hop):
        @pl.when(here.z >= hop)
        def left():
            project(here.behind(hop))

        @pl.when(here.z + hop < lines)
        def right():
            project(here.ahead(hop))

    token_load.wait()
    project(here.z)
    expert_spreads[0].turn()
    expert_spreads[1].chips()
    expert_spreads[0].cores()
    for hop in range(2, lines - 1):
        token_gathers[0].step(hop)
        token_gathers[1].step(hop)
    out_spread.start()
    for spread in expert_spreads[2:]:
        spread.start()
    for hop in range(1, lines - 1):
        project_hop(hop)
    expert_spreads[1].turn()
    for gather in token_gathers:
        gather.step(lines - 1)
    project_hop(lines - 1)

    prefix_end = prefix[0]
    heads = q_cols // HEAD_WIDTH
    group = q_cols // kv_cols

    def attend(number):
        start = number * tok_rows
        block = pl.ds(start, tok_rows)
        reach = max(rows_all // 2, start + tok_rows)
        query_place = start + lax.broadcasted_iota(jnp.int32, (tok_rows, reach), 0)
        key_place = lax.broadcasted_iota(jnp.int32, (tok_rows, reach), 1)
        allowed = (key_place <= query_place) | (key_place < prefix_end)
        lanes = lax.broadcasted_iota(jnp.int32, (tok_rows, LANES), 1)
        totals = jnp.zeros((tok_rows, LANES), jnp.float32)
        outputs = []
        for head in range(heads):
            key_at = q_cols + head // group * HEAD_WIDTH
            value_at = key_at + kv_cols
            scores = matmul(
                qkv[block, head * HEAD_WIDTH : (head + 1) * HEAD_WIDTH],
                qkv[:reach, key_at : key_at + HEAD_WIDTH],
                ROWS_BY_ROWS,
            )
            scores = jnp.where(allowed, scores * SCORE_SCALE, LOW_SCORE)
            largest = jnp.max(scores, -1, keepdims=True)
            powers = jnp.exp(scores - largest)
            total = jnp.sum(powers, -1, keepdims=True)
            product = matmul(
                powers.astype(jnp.bfloat16), qkv[:reach, value_at : value_at + HEAD_WIDTH], ROWS_BY_COLS
            )
            outputs.append(product / total)
            totals = jnp.where(lanes == head, largest + jnp.log(total), totals)
        joined = jnp.concatenate(outputs, 1)
        attended[block, :] = joined
        log_total[block, :] = totals
        attended_all[here.z, block, :] = joined.astype(jnp.bfloat16)

    def mix_in(number):
        block = pl.ds(number * tok_rows, tok_rows)
        branch = matmul(attended_all[0, block, :], out_full[:, :q_cols], ROWS_BY_ROWS)
        for line in range(1, lines):
            branch = branch + matmul(
                attended_all[line, block, :], out_full[:, line * q_cols : (line + 1) * q_cols], ROWS_BY_ROWS
            )
        total = tokens_all[number].astype(jnp.float32) + branch
        lowered = (total * inverse_rms(total) * gain_expert).astype(jnp.bfloat16)
        expert_in[number] = lowered
        logits = matmul(lowered, weights[:, qkv_cols:], ROWS_BY_COLS)
        lane = lax.broadcasted_iota(jnp.int32, logits.shape, 1)
        logits = jnp.where(lane < EXPERT_COUNT, logits, LOW_SCORE)
        powers = jnp.exp(logits - jnp.max(logits, -1, keepdims=True))
        powers = jnp.where(lane < EXPERT_COUNT, powers, 0.0)
        probs[number] = powers / jnp.sum(powers, -1, keepdims=True)

        @pl.when(here.z == number)
        def keep():
            middle[...] = total


    attended_gathers = [
        LineSpread(
            here, lambda z, n=n: attended_all.at[z, pl.ds(n * tok_rows, tok_rows)], a_sends.at[n], a_recvs.at[n]
        )
        for n in range(lines)
    ]
    def gate_columns(number, e):
        chosen = padded_square(chosen_all[number].astype(jnp.float32))
        lane = lax.broadcasted_iota(jnp.int32, chosen.shape, 1)
        own = lane == here.z * own_experts + e
        picked = jnp.sum(jnp.where(own, chosen, 0.0), -1, keepdims=True)
        gate = jnp.sum(jnp.where(own, probs[number] * chosen, 0.0), -1, keepdims=True)
        return own, picked, gate

    pairs = [(a, a + 2) for a in range(0, lines, 2)]

    def gate_up_of(e):
        return terms[e, ..., : 2 * ff_width].reshape(width, 2 * ff_width)

    def down_of(e):
        return terms[e, ..., 2 * ff_width :].reshape(width, ff_width)

    def expert_forward(e, numbers):
        for low, high in numbers:
            block = pl.ds(low * tok_rows, (high - low) * tok_rows)
            inputs = jnp.concatenate([expert_in[n] for n in range(low, high)], 0)
            linear = matmul(inputs, gate_up_of(e), ROWS_BY_COLS)
            gate_part, up_part = linear[:, :ff_width], linear[:, ff_width:]
            sigmoid = 1.0 / (1.0 + jnp.exp(-gate_part))
            silu = gate_part * sigmoid
            act = silu * up_part
            slopes[e, block, :ff_width] = (
                up_part * (sigmoid * (1.0 + gate_part * (1.0 - sigmoid)))
            ).astype(jnp.bfloat16)
            slopes[e, block, ff_width:] = silu.astype(jnp.bfloat16)
            acts[e, block, :] = act.astype(jnp.bfloat16)
            gate = jnp.concatenate([gate_columns(n, e)[2] for n in range(low, high)], 0)
            mids[e, low:high, ..., 2 * ff_width :] = (
                (gate * act).astype(jnp.bfloat16).reshape(high - low, lines, depth, ff_width)
            )

    def line_sum(parts, landed, sends, recvs):
        return Halves(
            *[
                LineSum(here, parts, landed, pl.ds(n * half, half), sends.at[n], recvs.at[n])
                for n in range(2)
            ]
        )

    def mix_out(members):
        for low, high in pairs:
            total = None
            if 0 not in members:
                total = jnp.concatenate([part_mix[n] for n in range(low, high)], 0).astype(jnp.float32)
            for e in members:
                gated = mids[e, low:high, ..., 2 * ff_width :].reshape((high - low) * tok_rows, ff_width)
                term = matmul(gated, down_of(e), ROWS_BY_ROWS)
                total = term if total is None else total + term
            for n in range(low, high):
                part_mix[n] = total[(n - low) * tok_rows : (n - low + 1) * tok_rows, :].astype(jnp.bfloat16)

    def expert_back(low, members):
        block = pl.ds(pl.multiple_of(low * tok_rows, 2 * tok_rows), 2 * tok_rows)
        grad_mid = jnp.concatenate([cot_all[low], cot_all[low + 1]], 0)
        opening = 0 in members
        total = None
        if not opening:
            total = jnp.concatenate([part_grad[low], part_grad[low + 1]], 0).astype(jnp.float32)
        gate_cols = [jnp.zeros((tok_rows, LANES), jnp.float32)] * 2
        for e in members:
            act_grad = matmul(grad_mid, down_of(e), ROWS_BY_COLS)
            column = jnp.sum(act_grad * acts[e, block, :].astype(jnp.float32), -1, keepdims=True)
            gates = []
            for n in range(2):
                own, picked, gate = gate_columns(low + n, e)
                part = column[n * tok_rows : (n + 1) * tok_rows, :]
                gate_cols[n] = jnp.where(own, part * picked, gate_cols[n])
                gates.append(gate)
            act_grad = act_grad * jnp.concatenate(gates, 0)
            slope = slopes[e, block, :].astype(jnp.float32)
            mid = jnp.concatenate(
                [act_grad * slope[:, :ff_width], act_grad * slope[:, ff_width:]], 1
            ).astype(jnp.bfloat16)
            mids[e, pl.ds(low, 2), ..., : 2 * ff_width] = mid.reshape(2, lines, depth, 2 * ff_width)
            term = matmul(mid, gate_up_of(e), ROWS_BY_ROWS)
            total = term if total is None else total + term
        for n in range(2):
            part_grad[low + n] = total[n * tok_rows : (n + 1) * tok_rows, :].astype(jnp.bfloat16)
            gate_rows = gate_cols[n].T[:EXPERT_COUNT, :]
            gate_grad[low + n] = gate_rows if opening else gate_grad[low + n] + gate_rows

    folds = [
        Fold(here, terms.at[e], mids.at[e], e_landed.at[e], e_last.at[e], f_sends.at[e], f_recvs.at[e])
        for e in range(own_experts)
    ]

    def weight_terms(e):
        terms[e, ..., : 2 * ff_width] = (
            matmul(
                expert_in[...].reshape(rows_all, width),
                mids[e, ..., : 2 * ff_width].reshape(rows_all, 2 * ff_width),
                COLS_BY_COLS,
            )
            .astype(jnp.bfloat16)
            .reshape(*five, 2 * ff_width)
        )
        terms[e, ..., 2 * ff_width :] = (
            matmul(
                cot_all[...].reshape(rows_all, width),
                mids[e, ..., 2 * ff_width :].reshape(rows_all, ff_width),
                COLS_BY_COLS,
            )
            .astype(jnp.bfloat16)
            .reshape(*five, ff_width)
        )
        pl.semaphore_signal(free_sem.at[e], inc=1, device_id=here.sibling(), device_id_type=MESH)

    def fold_start(e):
        pl.semaphore_wait(free_sem.at[e], 1)
        folds[e].start()

    near = here.z // 2 * 2
    far = (near + 2) % lines
    def mix_arrived(number):
        attended_gathers[number].finish()
        mix_in(number)

    for turn in range(lines):
        attend(turn)
        attended_gathers[turn].start()
    cot_gather.start()
    early, late = cot_gather.members
    expert_spreads[1].cores()
    out_spread.chips()
    expert_spreads[2].chips()
    out_spread.turn()
    expert_spreads[3].chips()
    expert_spreads[2].turn()
    out_spread.cores()
    out_spread.finish()
    chosen_swap.finish()
    mix_arrived(0)
    mix_arrived(1)
    for e in range(2):
        expert_spreads[e].finish()
        expert_forward(e, pairs[:1])
    expert_spreads[2].cores()
    expert_spreads[3].turn()
    mix_arrived(2)
    early.step(1)
    mix_arrived(3)
    late.step(1)
    for e in range(2):
        expert_forward(e, pairs[1:])
    expert_spreads[3].cores()
    expert_spreads[2].finish()
    expert_forward(2, pairs)
    for hop in range(2, lines - 1):
        early.step(hop)
    mix_out([0, 1, 2])
    for hop in range(2, lines - 1):
        late.step(hop)
    cot_load.wait()
    near = here.z // 2 * 2
    far = (near + 2) % lines
    expert_back(near, [0, 1, 2])
    expert_spreads[3].finish()
    expert_forward(3, pairs)
    mix_out([3])
    mix_swap = line_sum(part_mix, got_mix, m_sends, m_recvs)
    mix_swap.launch(lines - 1)
    for hops in range(lines - 2, 1, -1):
        mix_swap.launch(hops)
    expert_back(near, [3])
    cot_gather.step(lines - 1)
    expert_back(far, [0])
    for spread in expert_spreads[:1]:
        spread.close()
    weight_terms(0)
    fold_start(0)
    expert_back(far, [1, 2, 3])
    for group_of in [rows_spread, out_spread, chosen_swap, cot_gather] + token_gathers + expert_spreads[1:] + attended_gathers:
        group_of.close()
    grad_swap = line_sum(part_grad, got_grad, x_sends, x_recvs)
    gate_swap = LineSwap(here, lambda z: gate_grad.at[z], lambda k, z: got_gate.at[k - 1], g_sends, g_recvs)
    attended_swap = LineSwap(
        here, lambda z: attended_grad.at[z], lambda k, z: attended_grad_all.at[z], b_sends, b_recvs
    )
    part_swap = line_sum(part_grad, got_grad, p_sends, p_recvs)
    out_fold = Fold(here, o_terms, o_crossed, o_landed, o_last, of_sends, of_recvs)
    qkv_fold = Fold(here, q_terms, q_crossed, q_landed, q_last, q_sends, q_recvs)
    expert_swaps = [
        LineSwap(here, folds[e].sums, lambda k, z, e=e: expert_rows.at[z, e], el_sends.at[e], el_recvs.at[e])
        for e in range(own_experts)
    ]
    out_swap = LineSwap(here, out_fold.sums, lambda k, z: o_lines.at[k - 1], ol_sends, ol_recvs)
    qkv_swap = LineSwap(here, qkv_fold.sums, lambda k, z: q_lines.at[z], ql_sends, ql_recvs)

    for hops in range(lines - 1, 0, -1):
        grad_swap.launch(hops)
    gate_swap.start()
    folds[0].chips()
    weight_terms(1)
    fold_start(1)
    for hops in range(lines - 2, 1, -1):
        mix_swap.step(hops)
    for hops in range(lines - 2, 1, -1):
        grad_swap.step(hops)
    folds[1].chips()
    weight_terms(2)
    fold_start(2)
    grad_swap.step(1)
    folds[0].turn()
    weight_terms(3)
    fold_start(3)
    folds[2].chips()

    gate_swap.finish()
    grad_swap.finish(grad_res)
    gate_rows = gate_grad[here.z]
    for k in range(lines - 1):
        gate_rows = gate_rows + got_gate[k]
    gates = padded_square(gate_rows)
    grad = grad_res[...]
    prob = probs[here.z]
    logit_grad = (prob * (gates - jnp.sum(prob * gates, -1, keepdims=True))).astype(jnp.bfloat16)
    grad = grad + matmul(logit_grad, weights[:, qkv_cols:], ROWS_BY_ROWS)
    hidden = middle[...]
    inverse = inverse_rms(hidden)
    normed = hidden * inverse
    scaled = grad * gain_expert
    result = cot_all[here.z].astype(jnp.float32) + inverse * (
        scaled - normed * jnp.mean(scaled * normed, -1, keepdims=True)
    )
    grad_res[...] = result
    branch = result.astype(jnp.bfloat16)
    for line in range(lines):
        attended_grad[line] = matmul(
            branch, out_full[:, line * q_cols : (line + 1) * q_cols], ROWS_BY_COLS
        ).astype(jnp.bfloat16)
    attended_swap.start()
    attended_grad_all[here.z] = attended_grad[here.z]
    own_block = pl.ds(pl.multiple_of(here.z * tok_rows, tok_rows), tok_rows)
    router_term = matmul(expert_in[here.z], logit_grad, COLS_BY_COLS)
    gain_term = split_sum_columns(grad * normed)
    lane = lax.broadcasted_iota(jnp.int32, router_term.shape, 1)
    for line in range(lines):
        o_terms[..., line * q_cols : (line + 1) * q_cols] = (
            matmul(branch, attended_all[line, own_block, :], COLS_BY_COLS).astype(jnp.bfloat16).reshape(*five, q_cols)
        )
    o_terms[..., query_width:] = (
        jnp.where(lane == EXPERT_COUNT, gain_term, router_term).astype(jnp.bfloat16).reshape(*five, LANES)
    )
    out_fold.start()
    mix_swap.launch(1)
    folds[1].turn()
    folds[3].chips()
    folds[0].finish()
    expert_swaps[0].start()
    attended_swap.finish()
    grad_swap.close()

    key_sum[...] = jnp.zeros_like(key_sum)
    value_sum[...] = jnp.zeros_like(value_sum)

    def attend_back(number):
        start = number * tok_rows
        block = pl.ds(start, tok_rows)
        reach = max(rows_all // 2, start + tok_rows)
        query_place = start + lax.broadcasted_iota(jnp.int32, (tok_rows, reach), 0)
        key_place = lax.broadcasted_iota(jnp.int32, (tok_rows, reach), 1)
        allowed = (key_place <= query_place) | (key_place < prefix_end)
        query_grads = []
        for head in range(heads):
            own = slice(head * HEAD_WIDTH, (head + 1) * HEAD_WIDTH)
            low = head // group * HEAD_WIDTH
            shared = slice(low, low + HEAD_WIDTH)
            query = qkv[block, own]
            key = qkv[:reach, q_cols + low : q_cols + low + HEAD_WIDTH]
            value = qkv[:reach, q_cols + kv_cols + low : q_cols + kv_cols + low + HEAD_WIDTH]
            grad = attended_grad_all[number, :, own]
            scores = matmul(query, key, ROWS_BY_ROWS) * SCORE_SCALE
            prob = jnp.where(allowed, jnp.exp(scores - log_total[block, head : head + 1]), 0.0)
            delta = jnp.sum(grad.astype(jnp.float32) * attended[block, own], -1, keepdims=True)
            prob_part = matmul(grad, value, ROWS_BY_ROWS)
            score_grad = (prob * (prob_part - delta)).astype(jnp.bfloat16)
            value_sum[:reach, shared] = value_sum[:reach, shared] + matmul(
                prob.astype(jnp.bfloat16), grad, COLS_BY_COLS
            )
            key_sum[:reach, shared] = key_sum[:reach, shared] + matmul(score_grad, query, COLS_BY_COLS)
            query_grads.append(matmul(score_grad, key, ROWS_BY_COLS))
        query_grad = jnp.concatenate(query_grads, 1) * SCORE_SCALE
        joined_grad[block, :q_cols] = spin(query_grad, cosine[block, :], -sine_table[block, :]).astype(
            jnp.bfloat16
        )

    for number in range(lines):
        attend_back(number)
        if number == 1:
            folds[2].turn()
            mix_swap.step(1)
    folds[1].finish()
    expert_swaps[1].start()
    out_fold.chips()
    joined_grad[:, q_cols : q_cols + kv_cols] = spin(
        key_sum[...] * SCORE_SCALE, cosine[...], -sine_table[...]
    ).astype(jnp.bfloat16)
    joined_grad[:, q_cols + kv_cols :] = value_sum[...].astype(jnp.bfloat16)
    gain_term = jnp.zeros((width, LANES), jnp.float32)
    for number in range(lines):
        block = pl.ds(number * tok_rows, tok_rows)
        hidden = tokens_all[number].astype(jnp.float32)
        normed = hidden * inverse_rms(hidden)
        part = matmul(joined_grad[block, :], weights[:, :qkv_cols], ROWS_BY_ROWS)
        part_grad[number] = part.astype(jnp.bfloat16)
        gain_term = gain_term + split_sum_columns(part * normed)
    for hops in range(lines - 1, 0, -1):
        part_swap.launch(hops)
    q_terms[..., :qkv_cols] = (
        matmul(att_in[...], joined_grad[...], COLS_BY_COLS).astype(jnp.bfloat16).reshape(*five, qkv_cols)
    )
    q_terms[..., qkv_cols:] = gain_term.astype(jnp.bfloat16).reshape(*five, LANES)
    qkv_fold.start()
    for hops in range(lines - 2, 1, -1):
        part_swap.step(hops)
    folds[3].turn()
    qkv_fold.chips()
    folds[2].finish()
    expert_swaps[2].start()
    part_swap.step(1)
    out_fold.turn()
    folds[3].finish()
    expert_swaps[3].start()
    mix_swap.finish(mix_total)
    mixed[...] = (mix_total[...] + middle[...]).astype(jnp.bfloat16)
    store(mixed, mixed_o)
    out_fold.finish()
    out_swap.start()
    qkv_fold.turn()
    qkv_fold.finish()
    qkv_swap.start()

    part_swap.finish(mix_total)
    hidden = tokens_all[here.z].astype(jnp.float32)
    inverse = inverse_rms(hidden)
    normed = hidden * inverse
    scaled = mix_total[...] * gain_attention
    mix_total[...] = grad_res[...] + inverse * (
        scaled - normed * jnp.mean(scaled * normed, -1, keepdims=True)
    )
    store(mix_total, tokens_grad_o)
    out_swap.finish()
    total = o_terms[here.chip, here.core, here.z].astype(jnp.float32)
    for k in range(lines - 1):
        total = total + o_lines[k].astype(jnp.float32)
    out_s[...] = total[:, :query_width]
    tail = padded_square(total[:, query_width:])
    router_s[...] = tail[:EXPERT_COUNT, :depth]
    expert_gain_s[...] = tail[EXPERT_COUNT : EXPERT_COUNT + 1, :depth]
    store(out_s, out_o)
    store(router_s, router_o)
    store(expert_gain_s, expert_gain_o)
    q_lines[here.z] = q_terms[here.chip, here.core, here.z]
    qkv_swap.finish()
    gain_columns = jnp.zeros((depth, LANES), jnp.float32)
    for line in range(lines):
        query_s[:, line * q_cols : (line + 1) * q_cols] = q_lines[line, :, :q_cols].astype(jnp.float32)
        key_s[:, line * kv_cols : (line + 1) * kv_cols] = q_lines[line, :, q_cols : q_cols + kv_cols].astype(
            jnp.float32
        )
        value_s[:, line * kv_cols : (line + 1) * kv_cols] = q_lines[line, :, q_cols + kv_cols : qkv_cols].astype(
            jnp.float32
        )
        gain_columns = gain_columns + q_lines[line, :, qkv_cols:].astype(jnp.float32)
    attention_gain_s[...] = padded_square(gain_columns)[:1, :depth]
    store(query_s, query_o)
    store(key_s, key_o)
    store(value_s, value_o)
    store(attention_gain_s, attention_gain_o)
    for e in range(own_experts):
        expert_rows[here.z, e] = terms[e, here.chip, here.core, here.z]
        expert_swaps[e].finish()
    store(expert_rows, expert_o)
    for group_of in (
        [gate_swap, attended_swap, part_swap, mix_swap, out_swap, qkv_swap, out_fold, qkv_fold] + folds + expert_swaps
    ):
        group_of.close()
    for copy in stores:
        copy.wait()


def deliver_kernel(*refs):
    count = (len(refs) - 4) // 3
    sources, targets, held = refs[:count], refs[count : 2 * count + 1], refs[2 * count + 1 : 3 * count + 1]
    gate_up, down, sems = refs[3 * count + 1 :]
    loads = [move(sources[n], held[n], sems.at[0, n]) for n in reversed(range(count))][::-1]
    stores = []
    depth, expert_count = gate_up.shape[:2]
    order = row_order(depth, expert_count, False)
    loads[count - 1].wait()
    rows = held[count - 1][...].reshape(expert_count * depth, gate_up.shape[2] + down.shape[2])
    gate_up[...] = matmul(order, rows[:, : gate_up.shape[2]], ROWS_BY_COLS).reshape(gate_up.shape)
    stores.append(move(gate_up, targets[count - 1], sems.at[1, count - 1]))
    down[...] = matmul(order, rows[:, gate_up.shape[2] :], ROWS_BY_COLS).reshape(down.shape)
    stores.append(move(down, targets[count], sems.at[1, count]))
    for n in range(count - 1):
        loads[n].wait()
        stores.append(move(held[n], targets[n], sems.at[1, n]))
    for copy in stores:
        copy.wait()


def fast_device(
    tokens, prefix_len, routes, cotangent, query_matrix, key_matrix, value_matrix, output_matrix,
    attention_gain, expert_gain, router_matrix, gate_up_weight, down_weight,
):
    lines = lax.axis_size("seq")
    chips = lax.axis_size("dp") // 2
    tok_rows, width = tokens.shape[1:]
    rows_all = lines * tok_rows
    depth = query_matrix.shape[0]
    query_width, key_width = query_matrix.shape[1], key_matrix.shape[1]
    q_cols, kv_cols = query_width // lines, key_width // lines
    qkv_cols = q_cols + 2 * kv_cols
    expert_count = router_matrix.shape[1]
    own_experts = expert_count // lines
    ff_width = down_weight.shape[2]
    all_ff = 3 * ff_width
    row_cols = qkv_cols + LANES
    out_cols = query_width + LANES
    half_dim = HEAD_WIDTH // 2
    low, full = jnp.bfloat16, jnp.float32

    places = np.arange(rows_all, dtype=np.float32)
    frequency = np.exp(
        np.arange(half_dim, dtype=np.float32) * np.float32(-2.0 * math.log(10000.0) / HEAD_WIDTH)
    ).astype(np.float32)
    angles = places[:, None] * frequency[None, :]
    cosine = jnp.asarray(np.tile(np.cos(angles), (1, LANES // half_dim)), jnp.float32)
    sine_table = jnp.asarray(np.tile(np.sin(angles), (1, LANES // half_dim)), jnp.float32)

    count = spread_count(lines)

    def scratch(*dims, kind=low):
        return pltpu.VMEM(dims, kind)

    def pair(*dims):
        return [pltpu.SemaphoreType.DMA(dims)] * 2

    DMA = pltpu.SemaphoreType.DMA
    by_token = (lines, tok_rows)
    five = (chips, 2, lines, depth)
    four = (chips, lines, depth)
    landed = (2, 2, lines // 2, depth)
    last = (2, lines // 2, depth)
    ends = [
        ((tok_rows, width), low), ((tok_rows, width), full), ((depth, query_width), full), ((depth, key_width), full),
        ((depth, key_width), full), ((depth, query_width), full), ((1, depth), full), ((1, depth), full), ((expert_count, depth), full),
        ((lines, own_experts, depth, all_ff), low),
    ]

    def fold_scratch(cols):
        return [scratch(*dims, cols) for dims in (five, four, landed, last)]

    results = pl.pallas_call(
        layer_kernel,
        name="layer",
        out_shape=tuple(jax.ShapeDtypeStruct(dims, kind) for dims, kind in ends),
        in_specs=[SMEM_SPEC, ANY_SPEC] + [VMEM_SPEC] * 3 + [ANY_SPEC] + [VMEM_SPEC] * 3 + [ANY_SPEC] * 3 + [VMEM_SPEC] * 3,
        out_specs=(ANY_SPEC,) * len(ends),
        scratch_shapes=[
            scratch(LANES, LANES, kind=full), scratch(lines, depth, row_cols), scratch(lines, own_experts, depth, all_ff),
            scratch(*by_token, width), scratch(width, row_cols), scratch(width, query_width), scratch(own_experts, *five, all_ff),
            scratch(*by_token, width), scratch(lines, expert_count, tok_rows), scratch(rows_all, width), scratch(rows_all, qkv_cols),
            scratch(rows_all, q_cols, kind=full), scratch(lines, rows_all, q_cols), scratch(rows_all, LANES, kind=full),
            scratch(*by_token, width), scratch(*by_token, LANES, kind=full), scratch(tok_rows, width, kind=full),
            scratch(own_experts, rows_all, 2 * ff_width), scratch(own_experts, rows_all, ff_width), scratch(own_experts, *four, all_ff),
            scratch(*by_token, width), scratch(2, lines - 1, tok_rows, width), scratch(tok_rows, width, kind=full), scratch(tok_rows, width),
            scratch(*by_token, width), scratch(2, lines - 1, tok_rows, width),
            scratch(lines, expert_count, tok_rows, kind=full), scratch(lines - 1, expert_count, tok_rows, kind=full),
            scratch(tok_rows, width, kind=full), scratch(*by_token, q_cols), scratch(*by_token, q_cols), scratch(rows_all, qkv_cols),
            scratch(rows_all, kv_cols, kind=full), scratch(rows_all, kv_cols, kind=full),
            scratch(own_experts, *landed, all_ff), scratch(own_experts, *last, all_ff),
            *fold_scratch(out_cols), scratch(lines - 1, depth, out_cols),
            *fold_scratch(row_cols), scratch(lines, depth, row_cols),
            *[scratch(*dims, kind=kind) for dims, kind in ends[2:-1]],
            DMA((6 + own_experts,)),
            *pair(count), *pair(count), *pair(own_experts, count), *pair(2, 2, lines - 1), *pair(2, 2, lines - 1), *pair(lines),
            *pair(lines, lines), *pair(2, 2, lines - 1), *pair(2, 2, lines - 1), *pair(lines), *pair(lines), *pair(2, 2, lines - 1),
            *pair(own_experts, 7), *pair(7), *pair(7), *pair(own_experts, lines), *pair(lines), *pair(lines),
            pltpu.SemaphoreType.REGULAR((own_experts,)), DMA((len(ends),)),
        ],
        compiler_params=comm_params(1, 63),
    )(
        prefix_len, tokens[0], query_matrix, key_matrix, value_matrix, output_matrix, router_matrix.T,
        attention_gain.reshape(1, depth), expert_gain.reshape(1, depth), gate_up_weight.reshape(*four, 2 * ff_width),
        down_weight.reshape(*four, ff_width), cotangent[0], routes[0].T, cosine, sine_table,
    )
    last_ends = [((depth, expert_count, 2 * ff_width), full), ((depth, expert_count, ff_width), full)]
    results = pl.pallas_call(
        deliver_kernel,
        name="deliver",
        out_shape=tuple(jax.ShapeDtypeStruct(dims, kind) for dims, kind in ends[:-1] + last_ends),
        in_specs=[ANY_SPEC] * len(ends),
        out_specs=(ANY_SPEC,) * (len(ends) + 1),
        scratch_shapes=[pltpu.VMEM(dims, kind) for dims, kind in ends + last_ends] + [DMA((2, len(ends) + 1))],
        compiler_params=pltpu.CompilerParams(vmem_limit_bytes=63 << 20),
    )(*results)
    mixed, tokens_grad, query_grad, key_grad, value_grad, out_grad, attention_gain_grad, expert_gain_grad, router_grad, gate_up_grad, down_grad = results
    return (
        mixed[None],
        tokens_grad[None],
        query_grad,
        key_grad,
        value_grad,
        out_grad,
        attention_gain_grad.reshape(depth),
        expert_gain_grad.reshape(depth),
        router_grad.T,
        gate_up_grad,
        down_grad,
    )


def solution(mesh):
    lines, chips = mesh.shape["seq"], mesh.shape["dp"] // 2
    even = KEY_HEADS % (2 * lines) == 0 and EXPERT_COUNT % lines == 0 and chips == lines
    return jax.shard_map(
        fast_device if even else per_device,
        mesh=mesh,
        in_specs=(
            P("dp", "seq", None),
            P("dp"),
            P("dp", "seq", None),
            P("dp", "seq", None),
            P(("dp", "seq"), None),
            P(("dp", "seq"), None),
            P(("dp", "seq"), None),
            P(("dp", "seq"), None),
            P(("dp", "seq")),
            P(("dp", "seq")),
            P(("dp", "seq"), None),
            P(("dp", "seq"), None, None),
            P(("dp", "seq"), None, None),
        ),
        out_specs=(
            P("dp", "seq", None),
            P("dp", "seq", None),
            P(("dp", "seq"), None),
            P(("dp", "seq"), None),
            P(("dp", "seq"), None),
            P(("dp", "seq"), None),
            P(("dp", "seq")),
            P(("dp", "seq")),
            P(("dp", "seq"), None),
            P(("dp", "seq"), None, None),
            P(("dp", "seq"), None, None),
        ),
        check_vma=False,
    )
```

```python
import math

import jax
import jax.numpy as jnp
import numpy as np
from jax import lax
from jax.experimental import pallas as pl
from jax.experimental.pallas import tpu as pltpu
from jax.sharding import PartitionSpec as P

HEAD_WIDTH = 64
CAPACITY = 96


NORM_EPS = 1e-06
LOW_SCORE = -1e30
LANES = 128
HALF = HEAD_WIDTH // 2
SCORE_SCALE = HEAD_WIDTH ** (-0.5)
EXPERT_COUNT = 16
KEY_HEADS = 8
MESH = pl.DeviceIdType.MESH


def rotary_tables(positions, head_dim):
    half_dim = head_dim // 2
    frequency = jnp.exp(
        jnp.arange(half_dim, dtype=jnp.float32) * (-2.0 * math.log(10000.0) / head_dim)
    )
    angles = positions.astype(jnp.float32)[:, None] * frequency[None, :]
    return (jnp.cos(angles), jnp.sin(angles))


def rotate(value_rows, cosine, sine_table):
    half_dim = value_rows.shape[-1] // 2
    first_half = value_rows[..., :half_dim]
    second = value_rows[..., half_dim:]
    cos_heads = cosine[:, None, :]
    sin_heads = sine_table[:, None, :]
    return jnp.concatenate(
        [first_half * cos_heads - second * sin_heads, second * cos_heads + first_half * sin_heads],
        axis=-1,
    )


def norm_back(grad_normed, normed, inverse):
    return inverse * (grad_normed - normed * jnp.mean(grad_normed * normed, -1, keepdims=True))


def keep_state(running):
    return running


def swiglu(mid_linear, ff_width):
    return (jax.nn.silu(mid_linear[..., :ff_width]) * mid_linear[..., ff_width:]).astype(
        jnp.bfloat16
    )


def swiglu_back(act_grad, mid_linear, ff_width):
    gate_part = mid_linear[..., :ff_width]
    up_part = mid_linear[..., ff_width:]
    sigmoid = jax.nn.sigmoid(gate_part)
    gate_slope = sigmoid * (1.0 + gate_part * (1.0 - sigmoid))
    return jnp.concatenate(
        [act_grad * up_part * gate_slope, act_grad * gate_part * sigmoid], axis=-1
    ).astype(jnp.bfloat16)


def over_key_blocks(pieces, block_fn, running):
    piece_rows = pieces[0].shape[0]
    block_size = math.gcd(piece_rows, 512)
    shaped = tuple(
        (piece.reshape(piece_rows // block_size, block_size, piece.shape[1]) for piece in pieces)
    )
    offsets = block_size * jnp.arange(piece_rows // block_size, dtype=jnp.int32)

    def advance(carried, block_item):
        return (block_fn(carried, block_item[0], block_item[1], block_item[2]), None)

    result_state, unused = lax.scan(advance, running, (shaped[0], shaped[1], offsets))
    return result_state


def per_device(
    tokens,
    prefix_len,
    routes,
    cotangent,
    query_matrix,
    key_matrix,
    value_matrix,
    output_matrix,
    attention_gain,
    expert_gain,
    router_matrix,
    gate_up_weight,
    down_weight,
):
    hidden = tokens[0].astype(jnp.float32)
    tok_rows, model_width = hidden.shape
    params = (
        lax.all_gather(query_matrix, ("dp", "seq"), axis=0, tiled=True),
        lax.all_gather(key_matrix, ("dp", "seq"), axis=0, tiled=True),
        lax.all_gather(value_matrix, ("dp", "seq"), axis=0, tiled=True),
        lax.all_gather(output_matrix, ("dp", "seq"), axis=0, tiled=True),
        lax.all_gather(attention_gain, ("dp", "seq"), axis=0, tiled=True),
        lax.all_gather(expert_gain, ("dp", "seq"), axis=0, tiled=True),
        lax.all_gather(router_matrix, ("dp", "seq"), axis=0, tiled=True),
    )
    query_full, key_full, value_full, output_full, gain_attention, gain_expert, router_full = params
    head_dim = HEAD_WIDTH
    query_width = query_full.shape[1]
    key_width = key_full.shape[1]
    query_heads = query_width // head_dim
    key_groups = key_width // head_dim
    head_group = query_heads // key_groups
    score_scale = head_dim ** (-0.5)
    first_place = lax.axis_index("seq") * tok_rows
    positions = first_place + jnp.arange(tok_rows, dtype=jnp.int32)
    last_place = first_place + tok_rows - 1
    prefix_end = prefix_len[0]
    cosine, sine_table = rotary_tables(positions, head_dim)
    inverse_attention = lax.rsqrt(jnp.mean(hidden * hidden, -1, keepdims=True) + NORM_EPS)
    normed_attention = hidden * inverse_attention
    attention_input = (normed_attention * gain_attention.astype(jnp.float32)).astype(jnp.bfloat16)
    query_projected = jnp.dot(
        attention_input, query_full, preferred_element_type=jnp.float32
    ).reshape(tok_rows, query_heads, head_dim)
    queries = (
        rotate(query_projected, cosine, sine_table)
        .astype(jnp.bfloat16)
        .reshape(tok_rows, key_groups, head_group, head_dim)
    )
    key_projected = jnp.dot(attention_input, key_full, preferred_element_type=jnp.float32).reshape(
        tok_rows, key_groups, head_dim
    )
    keys_local = (
        rotate(key_projected, cosine, sine_table).astype(jnp.bfloat16).reshape(tok_rows, key_width)
    )
    values_local = jnp.dot(attention_input, value_full, preferred_element_type=jnp.float32).astype(
        jnp.bfloat16
    )

    def block_scores(key_block, key_start):
        block_size = key_block.shape[0]
        key_heads = key_block.reshape(block_size, key_groups, head_dim)
        key_places = key_start + jnp.arange(block_size, dtype=jnp.int32)
        allowed = (key_places[None, :] <= positions[:, None]) | (key_places[None, :] < prefix_end)
        scores = (
            jnp.einsum("qhgd,khd->hgqk", queries, key_heads, preferred_element_type=jnp.float32)
            * score_scale
        )
        return (jnp.where(allowed, scores, -jnp.inf), key_heads)

    def attend(running, key_block, value_block, key_start):

        def compute(carried):
            run_max, run_sum, weighted = carried
            scores, key_heads = block_scores(key_block, key_start)
            value_heads = value_block.reshape(key_block.shape[0], key_groups, head_dim)
            new_max = jnp.maximum(run_max, jnp.max(scores, -1))
            weights = jnp.exp(scores - new_max[..., None])
            factor = jnp.exp(run_max - new_max)
            new_sum = run_sum * factor + jnp.sum(weights, -1)
            new_weighted = weighted * factor[..., None] + jnp.einsum(
                "hgqk,khd->hgqd",
                weights.astype(jnp.bfloat16),
                value_heads,
                preferred_element_type=jnp.float32,
            )
            return (new_max, new_sum, new_weighted)

        visible = (key_start <= last_place) | (key_start < prefix_end)
        return lax.cond(visible, compute, keep_state, running)

    stat_shape = (key_groups, head_group, tok_rows)
    start_state = (
        jnp.full(stat_shape, LOW_SCORE, jnp.float32),
        jnp.zeros(stat_shape, jnp.float32),
        jnp.zeros(stat_shape + (head_dim,), jnp.float32),
    )
    run_max, run_sum, weighted = over_key_blocks(
        (
            lax.all_gather(keys_local, "seq", axis=0, tiled=True),
            lax.all_gather(values_local, "seq", axis=0, tiled=True),
        ),
        attend,
        start_state,
    )
    log_total = run_max + jnp.log(run_sum)
    attended_heads = weighted / run_sum[..., None]
    attention_lowered = (
        attended_heads.transpose(2, 0, 1, 3).reshape(tok_rows, query_width).astype(jnp.bfloat16)
    )
    branch_output = jnp.einsum(
        "tc,dc->td", attention_lowered, output_full, preferred_element_type=jnp.float32
    )
    middle = hidden + branch_output
    inverse_expert = lax.rsqrt(jnp.mean(middle * middle, -1, keepdims=True) + NORM_EPS)
    normed_expert = middle * inverse_expert
    expert_input = (normed_expert * gain_expert.astype(jnp.float32)).astype(jnp.bfloat16)
    router_logits = jnp.dot(expert_input, router_full, preferred_element_type=jnp.float32)
    router_probs = jax.nn.softmax(router_logits, axis=-1)
    expert_count = router_full.shape[1]
    route_ids = routes[0]
    expert_range = jnp.arange(expert_count, dtype=jnp.int32)
    route_hits = jnp.sum(
        (route_ids[:, :, None] == expert_range[None, None, :]).astype(jnp.int32), 1
    )
    slot_rank = jnp.cumsum(route_hits, 0) - 1
    slot_target = jnp.where(route_hits > 0, slot_rank, CAPACITY)
    token_index = jnp.broadcast_to(
        jnp.arange(tok_rows, dtype=jnp.int32)[:, None], (tok_rows, expert_count)
    )
    expert_index = jnp.broadcast_to(expert_range[None, :], (tok_rows, expert_count))
    slot_table = (
        jnp.zeros((expert_count, CAPACITY), jnp.int32)
        .at[expert_index, slot_target]
        .set(token_index, mode="drop")
    )
    slot_live = jnp.arange(CAPACITY, dtype=jnp.int32)[None, :] < jnp.sum(route_hits, 0)[:, None]
    expert_column = expert_range[:, None]
    dispatched = expert_input[slot_table]
    slot_gates = jnp.where(slot_live, router_probs[slot_table, expert_column], 0.0)
    ff_width = down_weight.shape[2]
    grad_mid = cotangent[0].astype(jnp.float32)
    slot_grad = grad_mid[slot_table]
    out_grad = (slot_gates[..., None] * slot_grad).astype(jnp.bfloat16)
    gate_up_full, down_full = (
        lax.all_gather(gate_up_weight, ("dp", "seq"), axis=0, tiled=True),
        lax.all_gather(down_weight, ("dp", "seq"), axis=0, tiled=True),
    )
    mid_linear = jnp.einsum(
        "ecd,def->ecf", dispatched, gate_up_full, preferred_element_type=jnp.float32
    )
    activation = swiglu(mid_linear, ff_width)
    expert_out = jnp.einsum(
        "ecf,def->ecd", activation, down_full, preferred_element_type=jnp.float32
    )
    flat_slots = slot_table.reshape(-1)
    combined = (
        jnp.zeros((tok_rows, model_width), jnp.float32)
        .at[flat_slots]
        .add((slot_gates[..., None] * expert_out).reshape(-1, model_width))
    )
    mixed = (middle + combined).astype(jnp.bfloat16)
    gate_grad = jnp.where(slot_live, jnp.sum(expert_out * slot_grad, -1), 0.0)
    act_grad = jnp.einsum("ecd,def->ecf", out_grad, down_full, preferred_element_type=jnp.float32)
    mid_grad = swiglu_back(act_grad, mid_linear, ff_width)
    gate_up_term = jnp.einsum(
        "ecd,ecf->def", dispatched, mid_grad, preferred_element_type=jnp.float32
    )
    down_term = jnp.einsum("ecd,ecf->def", out_grad, activation, preferred_element_type=jnp.float32)
    summed_terms = lax.psum_scatter(
        jnp.concatenate([gate_up_term, down_term], axis=-1),
        ("dp", "seq"),
        scatter_dimension=0,
        tiled=True,
    )
    gate_up_weight_grad = summed_terms[..., : 2 * ff_width]
    down_weight_grad = summed_terms[..., 2 * ff_width :]
    dispatched_grad = jnp.einsum(
        "ecf,def->ecd", mid_grad, gate_up_full, preferred_element_type=jnp.float32
    )
    expert_in_grad = (
        jnp.zeros((tok_rows, model_width), jnp.float32)
        .at[flat_slots]
        .add(dispatched_grad.reshape(-1, model_width))
    )
    prob_grad = (
        jnp.zeros((tok_rows, expert_count), jnp.float32)
        .at[slot_table, expert_column]
        .add(gate_grad)
    )
    logit_grad = (
        router_probs * (prob_grad - jnp.sum(router_probs * prob_grad, -1, keepdims=True))
    ).astype(jnp.bfloat16)
    router_term = jnp.einsum(
        "td,te->de", expert_input, logit_grad, preferred_element_type=jnp.float32
    )
    expert_in_grad = expert_in_grad + jnp.einsum(
        "te,de->td", logit_grad, router_full, preferred_element_type=jnp.float32
    )
    expert_gain_term = jnp.sum(expert_in_grad * normed_expert, 0)
    grad_res = grad_mid + norm_back(
        expert_in_grad * gain_expert.astype(jnp.float32), normed_expert, inverse_expert
    )
    branch_grad = grad_res.astype(jnp.bfloat16)
    output_term = jnp.einsum(
        "td,tc->dc", branch_grad, attention_lowered, preferred_element_type=jnp.float32
    )
    attended_grad = jnp.dot(branch_grad, output_full, preferred_element_type=jnp.float32).astype(
        jnp.bfloat16
    )
    attended_grad_heads = attended_grad.reshape(
        tok_rows, key_groups, head_group, head_dim
    ).transpose(1, 2, 0, 3)
    delta = jnp.sum(attended_grad_heads.astype(jnp.float32) * attended_heads, -1)
    seq_total = tok_rows * lax.axis_size("seq")

    def attend_back(running, key_block, value_block, key_start):

        def compute(carried):
            query_sum, key_sum, value_sum = carried
            block_size = key_block.shape[0]
            scores, key_heads = block_scores(key_block, key_start)
            value_heads = value_block.reshape(block_size, key_groups, head_dim)
            probs_full = jnp.exp(scores - log_total[..., None])
            probs_low = probs_full.astype(jnp.bfloat16)
            value_piece = jnp.einsum(
                "hgqk,hgqd->khd", probs_low, attended_grad_heads, preferred_element_type=jnp.float32
            ).reshape(block_size, key_width)
            prob_part = jnp.einsum(
                "hgqd,khd->hgqk",
                attended_grad_heads,
                value_heads,
                preferred_element_type=jnp.float32,
            )
            score_grad = (probs_full * (prob_part - delta[..., None])).astype(jnp.bfloat16)
            query_sum = (
                query_sum
                + jnp.einsum(
                    "hgqk,khd->hgqd", score_grad, key_heads, preferred_element_type=jnp.float32
                )
                * score_scale
            )
            key_piece = (
                jnp.einsum(
                    "hgqk,qhgd->khd", score_grad, queries, preferred_element_type=jnp.float32
                )
                * score_scale
            ).reshape(block_size, key_width)
            key_sum = lax.dynamic_update_slice_in_dim(
                key_sum,
                lax.dynamic_slice_in_dim(key_sum, key_start, block_size, 0) + key_piece,
                key_start,
                0,
            )
            value_sum = lax.dynamic_update_slice_in_dim(
                value_sum,
                lax.dynamic_slice_in_dim(value_sum, key_start, block_size, 0) + value_piece,
                key_start,
                0,
            )
            return (query_sum, key_sum, value_sum)

        visible = (key_start <= last_place) | (key_start < prefix_end)
        return lax.cond(visible, compute, keep_state, running)

    back_start = (
        jnp.zeros(stat_shape + (head_dim,), jnp.float32),
        jnp.zeros((seq_total, key_width), jnp.float32),
        jnp.zeros((seq_total, key_width), jnp.float32),
    )
    query_sum, key_sum, value_sum = over_key_blocks(
        (
            lax.all_gather(keys_local, "seq", axis=0, tiled=True),
            lax.all_gather(values_local, "seq", axis=0, tiled=True),
        ),
        attend_back,
        back_start,
    )
    key_part, value_part = (
        lax.psum_scatter(
            key_sum.astype(jnp.bfloat16), "seq", scatter_dimension=0, tiled=True
        ).astype(jnp.float32),
        lax.psum_scatter(
            value_sum.astype(jnp.bfloat16), "seq", scatter_dimension=0, tiled=True
        ).astype(jnp.float32),
    )
    query_rows = query_sum.transpose(2, 0, 1, 3).reshape(tok_rows, query_heads, head_dim)
    query_grad = (
        rotate(query_rows, cosine, -sine_table).reshape(tok_rows, query_width).astype(jnp.bfloat16)
    )
    key_grad = (
        rotate(key_part.reshape(tok_rows, key_groups, head_dim), cosine, -sine_table)
        .reshape(tok_rows, key_width)
        .astype(jnp.bfloat16)
    )
    value_grad = value_part.astype(jnp.bfloat16)
    query_term = jnp.einsum(
        "td,tc->dc", attention_input, query_grad, preferred_element_type=jnp.float32
    )
    key_term = jnp.einsum(
        "td,tc->dc", attention_input, key_grad, preferred_element_type=jnp.float32
    )
    value_term = jnp.einsum(
        "td,tc->dc", attention_input, value_grad, preferred_element_type=jnp.float32
    )
    attention_in_grad = jnp.einsum(
        "tc,dc->td", query_grad, query_full, preferred_element_type=jnp.float32
    )
    attention_in_grad = attention_in_grad + jnp.einsum(
        "tc,dc->td", key_grad, key_full, preferred_element_type=jnp.float32
    )
    attention_in_grad = attention_in_grad + jnp.einsum(
        "tc,dc->td", value_grad, value_full, preferred_element_type=jnp.float32
    )
    attention_gain_term = jnp.sum(attention_in_grad * normed_attention, 0)
    tokens_grad = grad_res + norm_back(
        attention_in_grad * gain_attention.astype(jnp.float32), normed_attention, inverse_attention
    )
    summed_grads = (
        lax.psum_scatter(query_term, ("dp", "seq"), scatter_dimension=0, tiled=True),
        lax.psum_scatter(key_term, ("dp", "seq"), scatter_dimension=0, tiled=True),
        lax.psum_scatter(value_term, ("dp", "seq"), scatter_dimension=0, tiled=True),
        lax.psum_scatter(output_term, ("dp", "seq"), scatter_dimension=0, tiled=True),
        lax.psum_scatter(attention_gain_term, ("dp", "seq"), scatter_dimension=0, tiled=True),
        lax.psum_scatter(expert_gain_term, ("dp", "seq"), scatter_dimension=0, tiled=True),
        lax.psum_scatter(router_term, ("dp", "seq"), scatter_dimension=0, tiled=True),
    )
    return (
        mixed[None],
        tokens_grad[None],
        summed_grads[0],
        summed_grads[1],
        summed_grads[2],
        summed_grads[3],
        summed_grads[4],
        summed_grads[5],
        summed_grads[6],
        gate_up_weight_grad,
        down_weight_grad,
    )


def matmul(left, right, contract):
    return lax.dot_general(
        left, right, (contract, ((), ())), preferred_element_type=jnp.float32
    )


ROWS_BY_COLS = ((1,), (0,))
ROWS_BY_ROWS = ((1,), (1,))
COLS_BY_COLS = ((0,), (0,))


def split_sum_columns(terms):
    ones = jnp.ones((terms.shape[0], LANES), jnp.bfloat16)
    high = terms.astype(jnp.bfloat16)
    low = (terms - high.astype(jnp.float32)).astype(jnp.bfloat16)
    return matmul(high, ones, COLS_BY_COLS) + matmul(low, ones, COLS_BY_COLS)


def turned(value_rows):
    width = value_rows.shape[1]
    lane = lax.broadcasted_iota(jnp.int32, value_rows.shape, 1)
    ahead = pltpu.roll(value_rows, width - HALF, 1)
    behind = pltpu.roll(value_rows, HALF, 1)
    return jnp.where(lane % HEAD_WIDTH < HALF, -ahead, behind)


def spin(value_rows, cosine, sine_table):
    repeats = value_rows.shape[1] // LANES
    cos_all = jnp.concatenate([cosine] * repeats, 1) if repeats > 1 else cosine
    sin_all = jnp.concatenate([sine_table] * repeats, 1) if repeats > 1 else sine_table
    return value_rows * cos_all + turned(value_rows) * sin_all


def inverse_rms(value_rows):
    return lax.rsqrt(jnp.mean(value_rows * value_rows, -1, keepdims=True) + NORM_EPS)


def shape_of(*dims, kind=jnp.bfloat16):
    return jax.ShapeDtypeStruct(dims, kind)


VMEM_SPEC = pl.BlockSpec(memory_space=pltpu.VMEM)
SMEM_SPEC = pl.BlockSpec(memory_space=pltpu.SMEM)
ANY_SPEC = pl.BlockSpec(memory_space=pl.ANY)


class Place:
    def __init__(self):
        self.dp = lax.axis_index("dp")
        self.z = lax.axis_index("seq")
        self.lines = lax.axis_size("seq")
        self.chips = lax.axis_size("dp") // 2
        self.chip = self.dp // 2
        self.core = self.dp % 2
        self.other = 1 - self.core
        self.chip_x = self.chip + 1 - 2 * (self.chip % 2)
        self.chip_y = (self.chip + 2) % 4
        self.chip_diag = 3 - self.chip

    def ahead(self, step):
        return (self.z + step) % self.lines

    def behind(self, step):
        return (self.z + self.lines - step) % self.lines

    def line_peer(self, step):
        return (self.dp, self.ahead(step))

    def on_chip(self, chip):
        return (chip * 2 + self.core, self.z)

    def sibling(self):
        return (self.chip * 2 + self.other, self.z)


def meet(peers):
    barrier = pltpu.get_barrier_semaphore()
    for peer in peers:
        pl.semaphore_signal(barrier, inc=1, device_id=peer, device_id_type=MESH)
    pl.semaphore_wait(barrier, len(peers))


def send(source, target, send_sem, recv_sem, peer):
    copy = pltpu.make_async_remote_copy(
        src_ref=source,
        dst_ref=target,
        send_sem=send_sem,
        recv_sem=recv_sem,
        device_id=peer,
        device_id_type=MESH,
    )
    copy.start()
    return copy


def move(source, target, sem):
    copy = pltpu.make_async_copy(source, target, sem)
    copy.start()
    return copy


def all_peers(here):
    return (
        [here.line_peer(k) for k in range(1, here.lines)]
        + [here.on_chip(chip) for chip in (here.chip_x, here.chip_y, here.chip_diag)]
        + [here.sibling()]
    )


def comm_params(ident, limit=56):
    return pltpu.CompilerParams(
        collective_id=ident, has_side_effects=True, vmem_limit_bytes=limit << 20
    )


class Spread:
    def __init__(self, here, pick, target, depth, local_sem, sends, recvs):
        self.here, self.pick, self.target, self.depth = here, pick, target, depth
        self.local_sem, self.sends, self.recvs = local_sem, sends, recvs
        self.used = 0

    def put(self, source, target, peer):
        copy = send(source, target, self.sends.at[self.used], self.recvs.at[self.used], peer)
        self.used += 1
        return copy

    def row(self):
        here = self.here
        if len(self.target.shape) > 2:
            return self.target.at[here.chip, here.core, here.z]
        first = (here.dp * here.lines + here.z) * self.depth
        return self.target.at[pl.ds(pl.multiple_of(first, self.depth), self.depth)]

    def chip_rows(self, chip, part=None):
        here = self.here
        if len(self.target.shape) > 2:
            if part is None:
                return self.target.at[chip, here.core]
            return self.target.at[chip, here.core, pl.ds(part * (here.lines // 2), here.lines // 2)]
        count = here.lines * self.depth
        first = (chip * 2 + here.core) * count
        if part is not None:
            first, count = first + part * (count // 2), count // 2
        return self.target.at[pl.ds(pl.multiple_of(first, count), count)]

    def start(self):
        here = self.here
        mine = self.row()
        self.own = move(self.pick(here.z), mine, self.local_sem)
        self.line = [
            self.put(self.pick(here.ahead(k)), mine, here.line_peer(k)) for k in range(1, here.lines)
        ]

    def chips(self):
        here = self.here
        self.own.wait()
        for copy in self.line:
            copy.wait_recv()
        mine = self.chip_rows(here.chip)
        self.plane = [
            self.put(mine, mine, here.on_chip(here.chip_x)),
            self.put(mine, mine, here.on_chip(here.chip_y)),
        ]
        self.across = [self.put(mine, mine, here.sibling())]

    def turn(self):
        here = self.here
        self.corner = []
        for copy, origin, onward, part in (
            (self.plane[0], here.chip_x, here.chip_y, 0),
            (self.plane[1], here.chip_y, here.chip_x, 1),
        ):
            copy.wait_recv()
            half = self.chip_rows(origin, part)
            self.corner.append(self.put(half, half, here.on_chip(onward)))
            block = self.chip_rows(origin)
            self.across.append(self.put(block, block, here.sibling()))

    def cores(self):
        here = self.here
        for copy in self.corner:
            copy.wait_recv()
        block = self.chip_rows(here.chip_diag)
        self.across.append(self.put(block, block, here.sibling()))

    def finish(self):
        for copy in self.across:
            copy.wait_recv()

    def close(self):
        for copy in self.line + self.plane + self.corner + self.across:
            copy.wait_send()


def spread_count(lines):
    return lines - 1 + 2 + 2 + 4


class LineGather:
    def __init__(self, here, view, sends, recvs, source=None):
        self.here, self.view, self.source = here, view, source
        self.sends, self.recvs = sends, recvs

    def copy(self, way, hop, block, source=None):
        here = self.here
        step = 1 if way == 0 else here.lines - 1
        return pltpu.make_async_remote_copy(
            src_ref=self.view(block) if source is None else source,
            dst_ref=self.view(block),
            send_sem=self.sends.at[way, hop - 1],
            recv_sem=self.recvs.at[way, hop - 1],
            device_id=here.line_peer(step),
            device_id_type=MESH,
        )

    def start(self):
        here = self.here

        @pl.when(here.z < here.lines - 1)
        def rightward():
            self.copy(0, 1, here.z, self.source).start()

        @pl.when(here.z > 0)
        def leftward():
            self.copy(1, 1, here.z, self.source).start()

    def step(self, hop):
        here = self.here
        lines = here.lines

        @pl.when(here.z >= hop)
        def from_left():
            block = here.behind(hop)
            self.copy(0, hop, block).wait_recv()
            if hop < lines - 1:

                @pl.when(here.z < lines - 1)
                def onward():
                    self.copy(0, hop + 1, block).start()

        @pl.when(here.z + hop < lines)
        def from_right():
            block = here.ahead(hop)
            self.copy(1, hop, block).wait_recv()
            if hop < lines - 1:

                @pl.when(here.z > 0)
                def onward():
                    self.copy(1, hop + 1, block).start()

    def close(self):
        here = self.here
        lines = here.lines
        for hop in range(1, lines):

            @pl.when((here.z >= hop - 1) & (here.z < lines - 1))
            def rightward():
                self.copy(0, hop, here.behind(hop - 1)).wait_send()

            @pl.when((here.z + hop - 1 < lines) & (here.z > 0))
            def leftward():
                self.copy(1, hop, here.ahead(hop - 1)).wait_send()


class LineSpread:
    def __init__(self, here, view, sends, recvs, source=None):
        self.here, self.view, self.source = here, view, source
        self.sends, self.recvs = sends, recvs

    def start(self):
        here = self.here
        mine = self.view(here.z)
        self.line = [
            send(
                mine if self.source is None else self.source, mine, self.sends.at[k - 1], self.recvs.at[k - 1], here.line_peer(k)
            )
            for k in range(1, here.lines)
        ]

    def arrived(self, step):
        self.line[step - 1].wait_recv()

    def finish(self):
        for copy in self.line:
            copy.wait_recv()

    def close(self):
        for copy in self.line:
            copy.wait_send()


class LineSum:
    def __init__(self, here, parts, landed, rows, sends, recvs):
        self.here, self.parts, self.landed, self.rows = here, parts, landed, rows
        self.sends, self.recvs = sends, recvs

    def copy(self, way, hops):
        here = self.here
        step = 1 if way == 0 else here.lines - 1
        block = here.ahead(hops) if way == 0 else here.behind(hops)
        return pltpu.make_async_remote_copy(
            src_ref=self.parts.at[block, self.rows],
            dst_ref=self.landed.at[way, hops - 1, self.rows],
            send_sem=self.sends.at[way, hops - 1],
            recv_sem=self.recvs.at[way, hops - 1],
            device_id=here.line_peer(step),
            device_id_type=MESH,
        )

    def launch(self, hops):
        here = self.here

        @pl.when(here.z == 0)
        def rightward():
            self.copy(0, hops).start()

        @pl.when(here.z == here.lines - 1)
        def leftward():
            self.copy(1, hops).start()

    def step(self, hops):
        here = self.here
        lines = here.lines

        def pass_on(way):
            block = here.ahead(hops) if way == 0 else here.behind(hops)
            self.copy(way, hops + 1).wait_recv()
            self.parts[block, self.rows] = (
                self.parts[block, self.rows].astype(jnp.float32)
                + self.landed[way, hops, self.rows].astype(jnp.float32)
            ).astype(self.parts.dtype)
            self.copy(way, hops).start()

        @pl.when((here.z > 0) & (here.z + hops < lines))
        def rightward():
            pass_on(0)

        @pl.when((here.z < lines - 1) & (here.z >= hops))
        def leftward():
            pass_on(1)

    def finish(self, total):
        here = self.here
        rows = self.rows
        total[rows, :] = self.parts[here.z, rows].astype(jnp.float32)

        @pl.when(here.z > 0)
        def from_left():
            self.copy(0, 1).wait_recv()
            total[rows, :] = total[rows, :] + self.landed[0, 0, rows].astype(jnp.float32)

        @pl.when(here.z < here.lines - 1)
        def from_right():
            self.copy(1, 1).wait_recv()
            total[rows, :] = total[rows, :] + self.landed[1, 0, rows].astype(jnp.float32)

    def close(self):
        here = self.here
        for hops in range(1, here.lines):

            @pl.when(here.z + hops < here.lines)
            def rightward():
                self.copy(0, hops).wait_send()

            @pl.when(here.z >= hops)
            def leftward():
                self.copy(1, hops).wait_send()


class Halves:
    def __init__(self, *members):
        self.members = members

    def start(self):
        for member in self.members:
            member.start()

    def launch(self, hops):
        for member in self.members:
            member.launch(hops)

    def step(self, hops):
        for member in self.members:
            member.step(hops)

    def finish(self, total):
        for member in self.members:
            member.finish(total)

    def close(self):
        for member in self.members:
            member.close()


class LineSwap:
    def __init__(self, here, pick, received, sends, recvs):
        self.here, self.pick, self.received = here, pick, received
        self.sends, self.recvs = sends, recvs

    def start(self):
        here = self.here
        self.line = [
            send(
                self.pick(here.ahead(k)), self.received(k, here.z), self.sends.at[k - 1], self.recvs.at[k - 1], here.line_peer(k)
            )
            for k in range(1, here.lines)
        ]

    def finish(self):
        for copy in self.line:
            copy.wait_recv()

    def close(self):
        for copy in self.line:
            copy.wait_send()


def padded_square(block):
    filler = jnp.zeros((LANES - block.shape[0], LANES), jnp.float32)
    return jnp.concatenate([block, filler], 0).T


def row_order(depth, experts, by_expert):
    count = depth * experts
    place = lax.broadcasted_iota(jnp.int32, (count, count), 0)
    source = lax.broadcasted_iota(jnp.int32, (count, count), 1)
    if by_expert:
        wanted = place % depth * experts + place // depth
    else:
        wanted = place % experts * depth + place // experts
    return (source == wanted).astype(jnp.bfloat16)


class Fold:
    def __init__(self, here, terms, crossed, landed, last, sends, recvs):
        self.here, self.terms, self.crossed = here, terms, crossed
        self.landed, self.last = landed, last
        self.sends, self.recvs = sends, recvs
        middle = here.lines // 2
        self.parts = [(0, middle), (middle, here.lines)]

    def start(self):
        here = self.here
        self.first = send(
            self.terms.at[:, here.other], self.crossed, self.sends.at[0], self.recvs.at[0], here.sibling()
        )

    def chips(self):
        here = self.here
        self.first.wait_recv()
        for chip in range(here.chips):
            self.terms[chip, here.core] = (
                self.terms[chip, here.core].astype(jnp.float32) + self.crossed[chip].astype(jnp.float32)
            ).astype(jnp.bfloat16)
        self.one, self.straight = [], []
        for number, near in enumerate((here.chip_x, here.chip_y)):
            low, high = self.parts[number]
            for slot, chip, group in ((1, here.chip_diag, self.one), (0, near, self.straight)):
                place = 1 + number * 2 + slot
                group.append(
                    send(
                        self.terms.at[chip, here.core, low:high], self.landed.at[number, slot],
                        self.sends.at[place], self.recvs.at[place], here.on_chip(near),
                    )
                )

    def turn(self):
        here = self.here
        self.two = []
        for number, onward in enumerate((here.chip_y, here.chip_x)):
            low, high = self.parts[number]
            self.one[number].wait_recv()
            self.terms[onward, here.core, low:high] = (
                self.terms[onward, here.core, low:high].astype(jnp.float32)
                + self.landed[number, 1].astype(jnp.float32)
            ).astype(jnp.bfloat16)
            place = 5 + number
            self.two.append(
                send(
                    self.terms.at[onward, here.core, low:high], self.last.at[number],
                    self.sends.at[place], self.recvs.at[place], here.on_chip(onward),
                )
            )

    def finish(self):
        here = self.here
        for number in range(2):
            low, high = self.parts[number]
            self.straight[number].wait_recv()
            self.two[number].wait_recv()
            self.terms[here.chip, here.core, low:high] = (
                self.terms[here.chip, here.core, low:high].astype(jnp.float32)
                + self.landed[number, 0].astype(jnp.float32)
                + self.last[number].astype(jnp.float32)
            ).astype(jnp.bfloat16)

    def sums(self, z):
        return self.terms.at[self.here.chip, self.here.core, z]

    def close(self):
        for copy in [self.first] + self.one + self.straight + self.two:
            copy.wait_send()


def layer_kernel(
    prefix, tokens, query_rows, key_rows, value_rows, out_rows, router_cols, attention_gain, expert_gain, gate_up_rows, down_rows,
    cotangent, routes, cosine, sine_table,
    mixed_o, tokens_grad_o, query_o, key_o, value_o, out_o, attention_gain_o, expert_gain_o, router_o, expert_o,
    square, rows, expert_rows, tokens_all, weights, out_full, terms, cot_all, chosen_all, att_in, qkv, attended, attended_all,
    log_total, expert_in, probs, middle, slopes, acts, mids, part_mix, got_mix, mix_total, mixed, part_grad, got_grad,
    gate_grad, got_gate, grad_res, attended_grad, attended_grad_all, joined_grad, key_sum, value_sum, e_landed, e_last,
    o_terms, o_crossed, o_landed, o_last, o_lines, q_terms, q_crossed, q_landed, q_last, q_lines,
    query_s, key_s, value_s, out_s, attention_gain_s, expert_gain_s, router_s,
    local_sem, r_sends, r_recvs, o_sends, o_recvs, e_sends, e_recvs, t_sends, t_recvs, c_sends, c_recvs, k_sends, k_recvs,
    a_sends, a_recvs, m_sends, m_recvs, x_sends, x_recvs, g_sends, g_recvs, b_sends, b_recvs, p_sends, p_recvs,
    f_sends, f_recvs, of_sends, of_recvs, q_sends, q_recvs, el_sends, el_recvs, ol_sends, ol_recvs, ql_sends, ql_recvs,
    free_sem, out_sem,
):
    here = Place()
    lines = here.lines
    tok_rows, width = tokens.shape
    rows_all = lines * tok_rows
    depth = rows.shape[1]
    own_experts = terms.shape[0]
    ff_width = terms.shape[5] // 3
    chips = here.chips
    five = (chips, 2, lines, depth)
    four = (chips, lines, depth)
    query_width = lines * (qkv.shape[1] // 2)
    qkv_cols = qkv.shape[1]
    kv_cols = qkv_cols // 4
    q_cols = 2 * kv_cols
    stores = []

    def store(source, target):
        stores.append(move(source, target, out_sem.at[len(stores)]))

    gate_up_load = move(gate_up_rows, mids.at[0, ..., : 2 * ff_width], local_sem.at[0])
    down_load = move(down_rows, mids.at[0, ..., 2 * ff_width :], local_sem.at[1])
    token_load = move(tokens, tokens_all.at[here.z], local_sem.at[2])
    cot_load = move(cotangent, cot_all.at[here.z], local_sem.at[3])

    square[...] = jnp.zeros_like(square)
    square[:EXPERT_COUNT, :depth] = router_cols[...].astype(jnp.float32)
    square[EXPERT_COUNT : EXPERT_COUNT + 1, :depth] = attention_gain[...].astype(jnp.float32)
    square[EXPERT_COUNT + 1 : EXPERT_COUNT + 2, :depth] = expert_gain[...].astype(jnp.float32)
    small = square[...].T[:depth, :].astype(jnp.bfloat16)
    for line in range(lines):
        rows[line, :, :q_cols] = query_rows[:, line * q_cols : (line + 1) * q_cols]
        rows[line, :, q_cols : q_cols + kv_cols] = key_rows[:, line * kv_cols : (line + 1) * kv_cols]
        rows[line, :, q_cols + kv_cols : qkv_cols] = value_rows[:, line * kv_cols : (line + 1) * kv_cols]
        rows[line, :, qkv_cols:] = small
    meet(all_peers(here))
    rows_spread = Spread(here, lambda z: rows.at[z], weights, depth, local_sem.at[4], r_sends, r_recvs)
    half = tok_rows // 2
    token_gathers = [
        LineGather(
            here, lambda z, n=n: tokens_all.at[z, pl.ds(n * half, half)], t_sends.at[n], t_recvs.at[n], tokens.at[pl.ds(n * half, half)]
        )
        for n in range(2)
    ]
    out_spread = Spread(here, lambda z: out_rows, out_full, depth, local_sem.at[5], o_sends, o_recvs)
    chosen_swap = LineSwap(
        here, lambda z: chosen_all.at[here.z], lambda k, z: chosen_all.at[z], k_sends, k_recvs
    )
    cot_gather = Halves(
        *[
            LineGather(
                here, lambda z, n=n: cot_all.at[z, pl.ds(n * half, half)], c_sends.at[n], c_recvs.at[n], cotangent.at[pl.ds(n * half, half)]
            )
            for n in range(2)
        ]
    )
    expert_spreads = [
        Spread(
            here,
            lambda z, e=e: expert_rows.at[z, e], terms.at[e], depth, local_sem.at[6 + e], e_sends.at[e], e_recvs.at[e],
        )
        for e in range(own_experts)
    ]
    rows_spread.start()
    gate_up_load.wait()
    down_load.wait()
    order = row_order(depth, EXPERT_COUNT, True)
    expert_rows[...] = (
        matmul(order, mids[0].reshape(depth * EXPERT_COUNT, 3 * ff_width), ROWS_BY_COLS)
        .astype(jnp.bfloat16)
        .reshape(expert_rows.shape)
    )
    expert_spreads[0].start()
    token_gathers[0].start()
    token_gathers[1].start()
    expert_id = lax.broadcasted_iota(jnp.int32, (EXPERT_COUNT, tok_rows), 0)
    chosen = jnp.zeros((EXPERT_COUNT, tok_rows), jnp.float32)
    for number in range(routes.shape[0]):
        chosen = chosen + (routes[number : number + 1, :] == expert_id).astype(jnp.float32)
    chosen_all[here.z] = chosen.astype(jnp.bfloat16)
    chosen_swap.start()
    rows_spread.chips()
    rows_spread.turn()
    rows_spread.cores()
    expert_spreads[0].chips()
    token_gathers[0].step(1)
    token_gathers[1].step(1)
    expert_spreads[1].start()
    rows_spread.finish()
    columns = weights[:, qkv_cols:].astype(jnp.float32).T
    gain_attention = columns[EXPERT_COUNT : EXPERT_COUNT + 1, :]
    gain_expert = columns[EXPERT_COUNT + 1 : EXPERT_COUNT + 2, :]

    def project(source):
        block = pl.ds(pl.multiple_of(source * tok_rows, tok_rows), tok_rows)
        hidden = tokens_all[source].astype(jnp.float32)
        normed = (hidden * inverse_rms(hidden) * gain_attention).astype(jnp.bfloat16)
        att_in[block, :] = normed
        linear = matmul(normed, weights[:, :qkv_cols], ROWS_BY_COLS)
        turned_part = linear[:, : q_cols + kv_cols]
        qkv[block, : q_cols + kv_cols] = spin(turned_part, cosine[block, :], sine_table[block, :]).astype(
            jnp.bfloat16
        )
        qkv[block, q_cols + kv_cols :] = linear[:, q_cols + kv_cols :].astype(jnp.bfloat16)

    def project_hop(hop):
        @pl.when(here.z >= hop)
        def left():
            project(here.behind(hop))

        @pl.when(here.z + hop < lines)
        def right():
            project(here.ahead(hop))

    token_load.wait()
    project(here.z)
    expert_spreads[0].turn()
    expert_spreads[1].chips()
    expert_spreads[0].cores()
    for hop in range(2, lines - 1):
        token_gathers[0].step(hop)
        token_gathers[1].step(hop)
    out_spread.start()
    for spread in expert_spreads[2:]:
        spread.start()
    for hop in range(1, lines - 1):
        project_hop(hop)
    expert_spreads[1].turn()
    for gather in token_gathers:
        gather.step(lines - 1)
    project_hop(lines - 1)

    prefix_end = prefix[0]
    heads = q_cols // HEAD_WIDTH
    group = q_cols // kv_cols

    def attend(number):
        start = number * tok_rows
        block = pl.ds(start, tok_rows)
        reach = max(rows_all // 2, start + tok_rows)
        query_place = start + lax.broadcasted_iota(jnp.int32, (tok_rows, reach), 0)
        key_place = lax.broadcasted_iota(jnp.int32, (tok_rows, reach), 1)
        allowed = (key_place <= query_place) | (key_place < prefix_end)
        lanes = lax.broadcasted_iota(jnp.int32, (tok_rows, LANES), 1)
        totals = jnp.zeros((tok_rows, LANES), jnp.float32)
        outputs = []
        for head in range(heads):
            key_at = q_cols + head // group * HEAD_WIDTH
            value_at = key_at + kv_cols
            scores = matmul(
                qkv[block, head * HEAD_WIDTH : (head + 1) * HEAD_WIDTH],
                qkv[:reach, key_at : key_at + HEAD_WIDTH],
                ROWS_BY_ROWS,
            )
            scores = jnp.where(allowed, scores * SCORE_SCALE, LOW_SCORE)
            largest = jnp.max(scores, -1, keepdims=True)
            powers = jnp.exp(scores - largest)
            total = jnp.sum(powers, -1, keepdims=True)
            product = matmul(
                powers.astype(jnp.bfloat16), qkv[:reach, value_at : value_at + HEAD_WIDTH], ROWS_BY_COLS
            )
            outputs.append(product / total)
            totals = jnp.where(lanes == head, largest + jnp.log(total), totals)
        joined = jnp.concatenate(outputs, 1)
        attended[block, :] = joined
        log_total[block, :] = totals
        attended_all[here.z, block, :] = joined.astype(jnp.bfloat16)

    def mix_in(number):
        block = pl.ds(number * tok_rows, tok_rows)
        branch = matmul(attended_all[0, block, :], out_full[:, :q_cols], ROWS_BY_ROWS)
        for line in range(1, lines):
            branch = branch + matmul(
                attended_all[line, block, :], out_full[:, line * q_cols : (line + 1) * q_cols], ROWS_BY_ROWS
            )
        total = tokens_all[number].astype(jnp.float32) + branch
        lowered = (total * inverse_rms(total) * gain_expert).astype(jnp.bfloat16)
        expert_in[number] = lowered
        logits = matmul(lowered, weights[:, qkv_cols:], ROWS_BY_COLS)
        lane = lax.broadcasted_iota(jnp.int32, logits.shape, 1)
        logits = jnp.where(lane < EXPERT_COUNT, logits, LOW_SCORE)
        powers = jnp.exp(logits - jnp.max(logits, -1, keepdims=True))
        powers = jnp.where(lane < EXPERT_COUNT, powers, 0.0)
        probs[number] = powers / jnp.sum(powers, -1, keepdims=True)

        @pl.when(here.z == number)
        def keep():
            middle[...] = total


    attended_gathers = [
        LineGather(
            here, lambda z, n=n: attended_all.at[z, pl.ds(n * tok_rows, tok_rows)], a_sends.at[n], a_recvs.at[n]
        )
        for n in range(lines)
    ]
    def gate_columns(number, e):
        chosen = padded_square(chosen_all[number].astype(jnp.float32))
        lane = lax.broadcasted_iota(jnp.int32, chosen.shape, 1)
        own = lane == here.z * own_experts + e
        picked = jnp.sum(jnp.where(own, chosen, 0.0), -1, keepdims=True)
        gate = jnp.sum(jnp.where(own, probs[number] * chosen, 0.0), -1, keepdims=True)
        return own, picked, gate

    pairs = [(a, a + 2) for a in range(0, lines, 2)]

    def gate_up_of(e):
        return terms[e, ..., : 2 * ff_width].reshape(width, 2 * ff_width)

    def down_of(e):
        return terms[e, ..., 2 * ff_width :].reshape(width, ff_width)

    def expert_forward(e, numbers):
        for low, high in numbers:
            block = pl.ds(low * tok_rows, (high - low) * tok_rows)
            inputs = jnp.concatenate([expert_in[n] for n in range(low, high)], 0)
            linear = matmul(inputs, gate_up_of(e), ROWS_BY_COLS)
            gate_part, up_part = linear[:, :ff_width], linear[:, ff_width:]
            sigmoid = 1.0 / (1.0 + jnp.exp(-gate_part))
            silu = gate_part * sigmoid
            act = silu * up_part
            slopes[e, block, :ff_width] = (
                up_part * (sigmoid * (1.0 + gate_part * (1.0 - sigmoid)))
            ).astype(jnp.bfloat16)
            slopes[e, block, ff_width:] = silu.astype(jnp.bfloat16)
            acts[e, block, :] = act.astype(jnp.bfloat16)
            gate = jnp.concatenate([gate_columns(n, e)[2] for n in range(low, high)], 0)
            mids[e, low:high, ..., 2 * ff_width :] = (
                (gate * act).astype(jnp.bfloat16).reshape(high - low, lines, depth, ff_width)
            )

    def line_sum(parts, landed, sends, recvs):
        return Halves(
            *[
                LineSum(here, parts, landed, pl.ds(n * half, half), sends.at[n], recvs.at[n])
                for n in range(2)
            ]
        )

    def mix_out(members):
        for low, high in pairs:
            total = None
            if 0 not in members:
                total = jnp.concatenate([part_mix[n] for n in range(low, high)], 0).astype(jnp.float32)
            for e in members:
                gated = mids[e, low:high, ..., 2 * ff_width :].reshape((high - low) * tok_rows, ff_width)
                term = matmul(gated, down_of(e), ROWS_BY_ROWS)
                total = term if total is None else total + term
            for n in range(low, high):
                part_mix[n] = total[(n - low) * tok_rows : (n - low + 1) * tok_rows, :].astype(jnp.bfloat16)

    def expert_back(low, members):
        block = pl.ds(pl.multiple_of(low * tok_rows, 2 * tok_rows), 2 * tok_rows)
        grad_mid = jnp.concatenate([cot_all[low], cot_all[low + 1]], 0)
        opening = 0 in members
        total = None
        if not opening:
            total = jnp.concatenate([part_grad[low], part_grad[low + 1]], 0).astype(jnp.float32)
        gate_cols = [jnp.zeros((tok_rows, LANES), jnp.float32)] * 2
        for e in members:
            act_grad = matmul(grad_mid, down_of(e), ROWS_BY_COLS)
            column = jnp.sum(act_grad * acts[e, block, :].astype(jnp.float32), -1, keepdims=True)
            gates = []
            for n in range(2):
                own, picked, gate = gate_columns(low + n, e)
                part = column[n * tok_rows : (n + 1) * tok_rows, :]
                gate_cols[n] = jnp.where(own, part * picked, gate_cols[n])
                gates.append(gate)
            act_grad = act_grad * jnp.concatenate(gates, 0)
            slope = slopes[e, block, :].astype(jnp.float32)
            mid = jnp.concatenate(
                [act_grad * slope[:, :ff_width], act_grad * slope[:, ff_width:]], 1
            ).astype(jnp.bfloat16)
            mids[e, pl.ds(low, 2), ..., : 2 * ff_width] = mid.reshape(2, lines, depth, 2 * ff_width)
            term = matmul(mid, gate_up_of(e), ROWS_BY_ROWS)
            total = term if total is None else total + term
        for n in range(2):
            part_grad[low + n] = total[n * tok_rows : (n + 1) * tok_rows, :].astype(jnp.bfloat16)
            gate_rows = gate_cols[n].T[:EXPERT_COUNT, :]
            gate_grad[low + n] = gate_rows if opening else gate_grad[low + n] + gate_rows

    folds = [
        Fold(here, terms.at[e], mids.at[e], e_landed.at[e], e_last.at[e], f_sends.at[e], f_recvs.at[e])
        for e in range(own_experts)
    ]

    def weight_terms(e):
        terms[e, ..., : 2 * ff_width] = (
            matmul(
                expert_in[...].reshape(rows_all, width),
                mids[e, ..., : 2 * ff_width].reshape(rows_all, 2 * ff_width),
                COLS_BY_COLS,
            )
            .astype(jnp.bfloat16)
            .reshape(*five, 2 * ff_width)
        )
        terms[e, ..., 2 * ff_width :] = (
            matmul(
                cot_all[...].reshape(rows_all, width),
                mids[e, ..., 2 * ff_width :].reshape(rows_all, ff_width),
                COLS_BY_COLS,
            )
            .astype(jnp.bfloat16)
            .reshape(*five, ff_width)
        )
        pl.semaphore_signal(free_sem.at[e], inc=1, device_id=here.sibling(), device_id_type=MESH)

    def fold_start(e):
        pl.semaphore_wait(free_sem.at[e], 1)
        folds[e].start()

    near = here.z // 2 * 2
    far = (near + 2) % lines
    def mix_arrived(number):
        attended_gathers[number].step(lines - 1)
        mix_in(number)

    for turn in range(lines):
        attend(turn)
        attended_gathers[turn].start()
    early, late = cot_gather.members
    expert_spreads[1].cores()
    out_spread.chips()
    expert_spreads[2].chips()
    out_spread.turn()
    expert_spreads[3].chips()
    for gather in attended_gathers:
        gather.step(1)
    expert_spreads[2].turn()
    out_spread.cores()
    for gather in attended_gathers:
        gather.step(2)
    cot_gather.start()
    out_spread.finish()
    chosen_swap.finish()
    mix_arrived(0)
    mix_arrived(1)
    for e in range(2):
        expert_spreads[e].finish()
        expert_forward(e, pairs[:1])
    expert_spreads[2].cores()
    expert_spreads[3].turn()
    mix_arrived(2)
    early.step(1)
    mix_arrived(3)
    late.step(1)
    for e in range(2):
        expert_forward(e, pairs[1:])
    expert_spreads[2].finish()
    expert_forward(2, pairs)
    for hop in range(2, lines - 1):
        early.step(hop)
    mix_out([0, 1, 2])
    expert_spreads[3].cores()
    for hop in range(2, lines - 1):
        late.step(hop)
    cot_load.wait()
    near = here.z // 2 * 2
    far = (near + 2) % lines
    expert_back(near, [0, 1, 2])
    expert_spreads[3].finish()
    expert_forward(3, pairs)
    mix_out([3])
    mix_swap = line_sum(part_mix, got_mix, m_sends, m_recvs)
    mix_swap.launch(lines - 1)
    for hops in range(lines - 2, 1, -1):
        mix_swap.launch(hops)
    expert_back(near, [3])
    cot_gather.step(lines - 1)
    expert_back(far, [0])
    for spread in expert_spreads[:1]:
        spread.close()
    weight_terms(0)
    fold_start(0)
    expert_back(far, [1, 2, 3])
    for group_of in [rows_spread, out_spread, chosen_swap, cot_gather] + token_gathers + expert_spreads[1:] + attended_gathers:
        group_of.close()
    grad_swap = line_sum(part_grad, got_grad, x_sends, x_recvs)
    gate_swap = LineSwap(here, lambda z: gate_grad.at[z], lambda k, z: got_gate.at[k - 1], g_sends, g_recvs)
    attended_swap = LineSwap(
        here, lambda z: attended_grad.at[z], lambda k, z: attended_grad_all.at[z], b_sends, b_recvs
    )
    part_swap = line_sum(part_grad, got_grad, p_sends, p_recvs)
    out_fold = Fold(here, o_terms, o_crossed, o_landed, o_last, of_sends, of_recvs)
    qkv_fold = Fold(here, q_terms, q_crossed, q_landed, q_last, q_sends, q_recvs)
    expert_swaps = [
        LineSwap(here, folds[e].sums, lambda k, z, e=e: expert_rows.at[z, e], el_sends.at[e], el_recvs.at[e])
        for e in range(own_experts)
    ]
    out_swap = LineSwap(here, out_fold.sums, lambda k, z: o_lines.at[k - 1], ol_sends, ol_recvs)
    qkv_swap = LineSwap(here, qkv_fold.sums, lambda k, z: q_lines.at[z], ql_sends, ql_recvs)

    for hops in range(lines - 1, 0, -1):
        grad_swap.launch(hops)
    gate_swap.start()
    folds[0].chips()
    weight_terms(1)
    fold_start(1)
    for hops in range(lines - 2, 1, -1):
        mix_swap.step(hops)
    for hops in range(lines - 2, 1, -1):
        grad_swap.step(hops)
    folds[1].chips()
    weight_terms(2)
    fold_start(2)
    grad_swap.step(1)
    folds[0].turn()
    weight_terms(3)
    fold_start(3)
    folds[2].chips()

    gate_swap.finish()
    grad_swap.finish(grad_res)
    gate_rows = gate_grad[here.z]
    for k in range(lines - 1):
        gate_rows = gate_rows + got_gate[k]
    gates = padded_square(gate_rows)
    grad = grad_res[...]
    prob = probs[here.z]
    logit_grad = (prob * (gates - jnp.sum(prob * gates, -1, keepdims=True))).astype(jnp.bfloat16)
    grad = grad + matmul(logit_grad, weights[:, qkv_cols:], ROWS_BY_ROWS)
    hidden = middle[...]
    inverse = inverse_rms(hidden)
    normed = hidden * inverse
    scaled = grad * gain_expert
    result = cot_all[here.z].astype(jnp.float32) + inverse * (
        scaled - normed * jnp.mean(scaled * normed, -1, keepdims=True)
    )
    grad_res[...] = result
    branch = result.astype(jnp.bfloat16)
    for line in range(lines):
        attended_grad[line] = matmul(
            branch, out_full[:, line * q_cols : (line + 1) * q_cols], ROWS_BY_COLS
        ).astype(jnp.bfloat16)
    attended_swap.start()
    attended_grad_all[here.z] = attended_grad[here.z]
    own_block = pl.ds(pl.multiple_of(here.z * tok_rows, tok_rows), tok_rows)
    router_term = matmul(expert_in[here.z], logit_grad, COLS_BY_COLS)
    gain_term = split_sum_columns(grad * normed)
    lane = lax.broadcasted_iota(jnp.int32, router_term.shape, 1)
    for line in range(lines):
        o_terms[..., line * q_cols : (line + 1) * q_cols] = (
            matmul(branch, attended_all[line, own_block, :], COLS_BY_COLS).astype(jnp.bfloat16).reshape(*five, q_cols)
        )
    o_terms[..., query_width:] = (
        jnp.where(lane == EXPERT_COUNT, gain_term, router_term).astype(jnp.bfloat16).reshape(*five, LANES)
    )
    out_fold.start()
    mix_swap.launch(1)
    folds[1].turn()
    folds[3].chips()
    folds[0].finish()
    expert_swaps[0].start()
    attended_swap.finish()
    grad_swap.close()

    key_sum[...] = jnp.zeros_like(key_sum)
    value_sum[...] = jnp.zeros_like(value_sum)

    def attend_back(number):
        start = number * tok_rows
        block = pl.ds(start, tok_rows)
        reach = max(rows_all // 2, start + tok_rows)
        query_place = start + lax.broadcasted_iota(jnp.int32, (tok_rows, reach), 0)
        key_place = lax.broadcasted_iota(jnp.int32, (tok_rows, reach), 1)
        allowed = (key_place <= query_place) | (key_place < prefix_end)
        query_grads = []
        for head in range(heads):
            own = slice(head * HEAD_WIDTH, (head + 1) * HEAD_WIDTH)
            low = head // group * HEAD_WIDTH
            shared = slice(low, low + HEAD_WIDTH)
            query = qkv[block, own]
            key = qkv[:reach, q_cols + low : q_cols + low + HEAD_WIDTH]
            value = qkv[:reach, q_cols + kv_cols + low : q_cols + kv_cols + low + HEAD_WIDTH]
            grad = attended_grad_all[number, :, own]
            scores = matmul(query, key, ROWS_BY_ROWS) * SCORE_SCALE
            prob = jnp.where(allowed, jnp.exp(scores - log_total[block, head : head + 1]), 0.0)
            delta = jnp.sum(grad.astype(jnp.float32) * attended[block, own], -1, keepdims=True)
            prob_part = matmul(grad, value, ROWS_BY_ROWS)
            score_grad = (prob * (prob_part - delta)).astype(jnp.bfloat16)
            value_sum[:reach, shared] = value_sum[:reach, shared] + matmul(
                prob.astype(jnp.bfloat16), grad, COLS_BY_COLS
            )
            key_sum[:reach, shared] = key_sum[:reach, shared] + matmul(score_grad, query, COLS_BY_COLS)
            query_grads.append(matmul(score_grad, key, ROWS_BY_COLS))
        query_grad = jnp.concatenate(query_grads, 1) * SCORE_SCALE
        joined_grad[block, :q_cols] = spin(query_grad, cosine[block, :], -sine_table[block, :]).astype(
            jnp.bfloat16
        )

    for number in range(lines):
        attend_back(number)
        if number == 1:
            folds[2].turn()
            mix_swap.step(1)
    folds[1].finish()
    expert_swaps[1].start()
    out_fold.chips()
    joined_grad[:, q_cols : q_cols + kv_cols] = spin(
        key_sum[...] * SCORE_SCALE, cosine[...], -sine_table[...]
    ).astype(jnp.bfloat16)
    joined_grad[:, q_cols + kv_cols :] = value_sum[...].astype(jnp.bfloat16)
    gain_term = jnp.zeros((width, LANES), jnp.float32)
    for number in range(lines):
        block = pl.ds(number * tok_rows, tok_rows)
        hidden = tokens_all[number].astype(jnp.float32)
        normed = hidden * inverse_rms(hidden)
        part = matmul(joined_grad[block, :], weights[:, :qkv_cols], ROWS_BY_ROWS)
        part_grad[number] = part.astype(jnp.bfloat16)
        gain_term = gain_term + split_sum_columns(part * normed)
    for hops in range(lines - 1, 0, -1):
        part_swap.launch(hops)
    q_terms[..., :qkv_cols] = (
        matmul(att_in[...], joined_grad[...], COLS_BY_COLS).astype(jnp.bfloat16).reshape(*five, qkv_cols)
    )
    q_terms[..., qkv_cols:] = gain_term.astype(jnp.bfloat16).reshape(*five, LANES)
    qkv_fold.start()
    for hops in range(lines - 2, 1, -1):
        part_swap.step(hops)
    folds[3].turn()
    qkv_fold.chips()
    folds[2].finish()
    expert_swaps[2].start()
    part_swap.step(1)
    out_fold.turn()
    folds[3].finish()
    expert_swaps[3].start()
    mix_swap.finish(mix_total)
    mixed[...] = (mix_total[...] + middle[...]).astype(jnp.bfloat16)
    store(mixed, mixed_o)
    out_fold.finish()
    out_swap.start()
    qkv_fold.turn()
    qkv_fold.finish()
    qkv_swap.start()

    part_swap.finish(mix_total)
    hidden = tokens_all[here.z].astype(jnp.float32)
    inverse = inverse_rms(hidden)
    normed = hidden * inverse
    scaled = mix_total[...] * gain_attention
    mix_total[...] = grad_res[...] + inverse * (
        scaled - normed * jnp.mean(scaled * normed, -1, keepdims=True)
    )
    store(mix_total, tokens_grad_o)
    out_swap.finish()
    total = o_terms[here.chip, here.core, here.z].astype(jnp.float32)
    for k in range(lines - 1):
        total = total + o_lines[k].astype(jnp.float32)
    out_s[...] = total[:, :query_width]
    tail = padded_square(total[:, query_width:])
    router_s[...] = tail[:EXPERT_COUNT, :depth]
    expert_gain_s[...] = tail[EXPERT_COUNT : EXPERT_COUNT + 1, :depth]
    store(out_s, out_o)
    store(router_s, router_o)
    store(expert_gain_s, expert_gain_o)
    q_lines[here.z] = q_terms[here.chip, here.core, here.z]
    qkv_swap.finish()
    gain_columns = jnp.zeros((depth, LANES), jnp.float32)
    for line in range(lines):
        query_s[:, line * q_cols : (line + 1) * q_cols] = q_lines[line, :, :q_cols].astype(jnp.float32)
        key_s[:, line * kv_cols : (line + 1) * kv_cols] = q_lines[line, :, q_cols : q_cols + kv_cols].astype(
            jnp.float32
        )
        value_s[:, line * kv_cols : (line + 1) * kv_cols] = q_lines[line, :, q_cols + kv_cols : qkv_cols].astype(
            jnp.float32
        )
        gain_columns = gain_columns + q_lines[line, :, qkv_cols:].astype(jnp.float32)
    attention_gain_s[...] = padded_square(gain_columns)[:1, :depth]
    store(query_s, query_o)
    store(key_s, key_o)
    store(value_s, value_o)
    store(attention_gain_s, attention_gain_o)
    for e in range(own_experts):
        expert_rows[here.z, e] = terms[e, here.chip, here.core, here.z]
        expert_swaps[e].finish()
    store(expert_rows, expert_o)
    for group_of in (
        [gate_swap, attended_swap, part_swap, mix_swap, out_swap, qkv_swap, out_fold, qkv_fold] + folds + expert_swaps
    ):
        group_of.close()
    for copy in stores:
        copy.wait()


def deliver_kernel(*refs):
    count = (len(refs) - 4) // 3
    sources, targets, held = refs[:count], refs[count : 2 * count + 1], refs[2 * count + 1 : 3 * count + 1]
    gate_up, down, sems = refs[3 * count + 1 :]
    loads = [move(sources[n], held[n], sems.at[0, n]) for n in reversed(range(count))][::-1]
    stores = []
    depth, expert_count = gate_up.shape[:2]
    order = row_order(depth, expert_count, False)
    loads[count - 1].wait()
    rows = held[count - 1][...].reshape(expert_count * depth, gate_up.shape[2] + down.shape[2])
    gate_up[...] = matmul(order, rows[:, : gate_up.shape[2]], ROWS_BY_COLS).reshape(gate_up.shape)
    stores.append(move(gate_up, targets[count - 1], sems.at[1, count - 1]))
    down[...] = matmul(order, rows[:, gate_up.shape[2] :], ROWS_BY_COLS).reshape(down.shape)
    stores.append(move(down, targets[count], sems.at[1, count]))
    for n in range(count - 1):
        loads[n].wait()
        stores.append(move(held[n], targets[n], sems.at[1, n]))
    for copy in stores:
        copy.wait()


def fast_device(
    tokens, prefix_len, routes, cotangent, query_matrix, key_matrix, value_matrix, output_matrix,
    attention_gain, expert_gain, router_matrix, gate_up_weight, down_weight,
):
    lines = lax.axis_size("seq")
    chips = lax.axis_size("dp") // 2
    tok_rows, width = tokens.shape[1:]
    rows_all = lines * tok_rows
    depth = query_matrix.shape[0]
    query_width, key_width = query_matrix.shape[1], key_matrix.shape[1]
    q_cols, kv_cols = query_width // lines, key_width // lines
    qkv_cols = q_cols + 2 * kv_cols
    expert_count = router_matrix.shape[1]
    own_experts = expert_count // lines
    ff_width = down_weight.shape[2]
    all_ff = 3 * ff_width
    row_cols = qkv_cols + LANES
    out_cols = query_width + LANES
    half_dim = HEAD_WIDTH // 2
    low, full = jnp.bfloat16, jnp.float32

    places = np.arange(rows_all, dtype=np.float32)
    frequency = np.exp(
        np.arange(half_dim, dtype=np.float32) * np.float32(-2.0 * math.log(10000.0) / HEAD_WIDTH)
    ).astype(np.float32)
    angles = places[:, None] * frequency[None, :]
    cosine = jnp.asarray(np.tile(np.cos(angles), (1, LANES // half_dim)), jnp.float32)
    sine_table = jnp.asarray(np.tile(np.sin(angles), (1, LANES // half_dim)), jnp.float32)

    count = spread_count(lines)

    def scratch(*dims, kind=low):
        return pltpu.VMEM(dims, kind)

    def pair(*dims):
        return [pltpu.SemaphoreType.DMA(dims)] * 2

    DMA = pltpu.SemaphoreType.DMA
    by_token = (lines, tok_rows)
    five = (chips, 2, lines, depth)
    four = (chips, lines, depth)
    landed = (2, 2, lines // 2, depth)
    last = (2, lines // 2, depth)
    ends = [
        ((tok_rows, width), low), ((tok_rows, width), full), ((depth, query_width), full), ((depth, key_width), full),
        ((depth, key_width), full), ((depth, query_width), full), ((1, depth), full), ((1, depth), full), ((expert_count, depth), full),
        ((lines, own_experts, depth, all_ff), low),
    ]

    def fold_scratch(cols):
        return [scratch(*dims, cols) for dims in (five, four, landed, last)]

    results = pl.pallas_call(
        layer_kernel,
        name="layer",
        out_shape=tuple(jax.ShapeDtypeStruct(dims, kind) for dims, kind in ends),
        in_specs=[SMEM_SPEC, ANY_SPEC] + [VMEM_SPEC] * 3 + [ANY_SPEC] + [VMEM_SPEC] * 3 + [ANY_SPEC] * 3 + [VMEM_SPEC] * 3,
        out_specs=(ANY_SPEC,) * len(ends),
        scratch_shapes=[
            scratch(LANES, LANES, kind=full), scratch(lines, depth, row_cols), scratch(lines, own_experts, depth, all_ff),
            scratch(*by_token, width), scratch(width, row_cols), scratch(width, query_width), scratch(own_experts, *five, all_ff),
            scratch(*by_token, width), scratch(lines, expert_count, tok_rows), scratch(rows_all, width), scratch(rows_all, qkv_cols),
            scratch(rows_all, q_cols, kind=full), scratch(lines, rows_all, q_cols), scratch(rows_all, LANES, kind=full),
            scratch(*by_token, width), scratch(*by_token, LANES, kind=full), scratch(tok_rows, width, kind=full),
            scratch(own_experts, rows_all, 2 * ff_width), scratch(own_experts, rows_all, ff_width), scratch(own_experts, *four, all_ff),
            scratch(*by_token, width), scratch(2, lines - 1, tok_rows, width), scratch(tok_rows, width, kind=full), scratch(tok_rows, width),
            scratch(*by_token, width), scratch(2, lines - 1, tok_rows, width),
            scratch(lines, expert_count, tok_rows, kind=full), scratch(lines - 1, expert_count, tok_rows, kind=full),
            scratch(tok_rows, width, kind=full), scratch(*by_token, q_cols), scratch(*by_token, q_cols), scratch(rows_all, qkv_cols),
            scratch(rows_all, kv_cols, kind=full), scratch(rows_all, kv_cols, kind=full),
            scratch(own_experts, *landed, all_ff), scratch(own_experts, *last, all_ff),
            *fold_scratch(out_cols), scratch(lines - 1, depth, out_cols),
            *fold_scratch(row_cols), scratch(lines, depth, row_cols),
            *[scratch(*dims, kind=kind) for dims, kind in ends[2:-1]],
            DMA((6 + own_experts,)),
            *pair(count), *pair(count), *pair(own_experts, count), *pair(2, 2, lines - 1), *pair(2, 2, lines - 1), *pair(lines),
            *pair(lines, 2, lines - 1), *pair(2, 2, lines - 1), *pair(2, 2, lines - 1), *pair(lines), *pair(lines), *pair(2, 2, lines - 1),
            *pair(own_experts, 7), *pair(7), *pair(7), *pair(own_experts, lines), *pair(lines), *pair(lines),
            pltpu.SemaphoreType.REGULAR((own_experts,)), DMA((len(ends),)),
        ],
        compiler_params=comm_params(1, 63),
    )(
        prefix_len, tokens[0], query_matrix, key_matrix, value_matrix, output_matrix, router_matrix.T,
        attention_gain.reshape(1, depth), expert_gain.reshape(1, depth), gate_up_weight.reshape(*four, 2 * ff_width),
        down_weight.reshape(*four, ff_width), cotangent[0], routes[0].T, cosine, sine_table,
    )
    last_ends = [((depth, expert_count, 2 * ff_width), full), ((depth, expert_count, ff_width), full)]
    results = pl.pallas_call(
        deliver_kernel,
        name="deliver",
        out_shape=tuple(jax.ShapeDtypeStruct(dims, kind) for dims, kind in ends[:-1] + last_ends),
        in_specs=[ANY_SPEC] * len(ends),
        out_specs=(ANY_SPEC,) * (len(ends) + 1),
        scratch_shapes=[pltpu.VMEM(dims, kind) for dims, kind in ends + last_ends] + [DMA((2, len(ends) + 1))],
        compiler_params=pltpu.CompilerParams(vmem_limit_bytes=63 << 20),
    )(*results)
    mixed, tokens_grad, query_grad, key_grad, value_grad, out_grad, attention_gain_grad, expert_gain_grad, router_grad, gate_up_grad, down_grad = results
    return (
        mixed[None],
        tokens_grad[None],
        query_grad,
        key_grad,
        value_grad,
        out_grad,
        attention_gain_grad.reshape(depth),
        expert_gain_grad.reshape(depth),
        router_grad.T,
        gate_up_grad,
        down_grad,
    )


def solution(mesh):
    lines, chips = mesh.shape["seq"], mesh.shape["dp"] // 2
    even = KEY_HEADS % (2 * lines) == 0 and EXPERT_COUNT % lines == 0 and chips == lines == 4
    return jax.shard_map(
        fast_device if even else per_device,
        mesh=mesh,
        in_specs=(
            P("dp", "seq", None),
            P("dp"),
            P("dp", "seq", None),
            P("dp", "seq", None),
            P(("dp", "seq"), None),
            P(("dp", "seq"), None),
            P(("dp", "seq"), None),
            P(("dp", "seq"), None),
            P(("dp", "seq")),
            P(("dp", "seq")),
            P(("dp", "seq"), None),
            P(("dp", "seq"), None, None),
            P(("dp", "seq"), None, None),
        ),
        out_specs=(
            P("dp", "seq", None),
            P("dp", "seq", None),
            P(("dp", "seq"), None),
            P(("dp", "seq"), None),
            P(("dp", "seq"), None),
            P(("dp", "seq"), None),
            P(("dp", "seq")),
            P(("dp", "seq")),
            P(("dp", "seq"), None),
            P(("dp", "seq"), None, None),
            P(("dp", "seq"), None, None),
        ),
        check_vma=False,
    )
```

```python
import math

import jax
import jax.numpy as jnp
import numpy as np
from jax import lax
from jax.experimental import pallas as pl
from jax.experimental.pallas import tpu as pltpu
from jax.sharding import PartitionSpec as P

HEAD_WIDTH = 64
CAPACITY = 96


NORM_EPS = 1e-06
LOW_SCORE = -1e30
LANES = 128
HALF = HEAD_WIDTH // 2
SCORE_SCALE = HEAD_WIDTH ** (-0.5)
EXPERT_COUNT = 16
KEY_HEADS = 8
MESH = pl.DeviceIdType.MESH


def rotary_tables(positions, head_dim):
    half_dim = head_dim // 2
    frequency = jnp.exp(
        jnp.arange(half_dim, dtype=jnp.float32) * (-2.0 * math.log(10000.0) / head_dim)
    )
    angles = positions.astype(jnp.float32)[:, None] * frequency[None, :]
    return (jnp.cos(angles), jnp.sin(angles))


def rotate(value_rows, cosine, sine_table):
    half_dim = value_rows.shape[-1] // 2
    first_half = value_rows[..., :half_dim]
    second = value_rows[..., half_dim:]
    cos_heads = cosine[:, None, :]
    sin_heads = sine_table[:, None, :]
    return jnp.concatenate(
        [first_half * cos_heads - second * sin_heads, second * cos_heads + first_half * sin_heads],
        axis=-1,
    )


def norm_back(grad_normed, normed, inverse):
    return inverse * (grad_normed - normed * jnp.mean(grad_normed * normed, -1, keepdims=True))


def keep_state(running):
    return running


def swiglu(mid_linear, ff_width):
    return (jax.nn.silu(mid_linear[..., :ff_width]) * mid_linear[..., ff_width:]).astype(
        jnp.bfloat16
    )


def swiglu_back(act_grad, mid_linear, ff_width):
    gate_part = mid_linear[..., :ff_width]
    up_part = mid_linear[..., ff_width:]
    sigmoid = jax.nn.sigmoid(gate_part)
    gate_slope = sigmoid * (1.0 + gate_part * (1.0 - sigmoid))
    return jnp.concatenate(
        [act_grad * up_part * gate_slope, act_grad * gate_part * sigmoid], axis=-1
    ).astype(jnp.bfloat16)


def over_key_blocks(pieces, block_fn, running):
    piece_rows = pieces[0].shape[0]
    block_size = math.gcd(piece_rows, 512)
    shaped = tuple(
        (piece.reshape(piece_rows // block_size, block_size, piece.shape[1]) for piece in pieces)
    )
    offsets = block_size * jnp.arange(piece_rows // block_size, dtype=jnp.int32)

    def advance(carried, block_item):
        return (block_fn(carried, block_item[0], block_item[1], block_item[2]), None)

    result_state, unused = lax.scan(advance, running, (shaped[0], shaped[1], offsets))
    return result_state


def per_device(
    tokens,
    prefix_len,
    routes,
    cotangent,
    query_matrix,
    key_matrix,
    value_matrix,
    output_matrix,
    attention_gain,
    expert_gain,
    router_matrix,
    gate_up_weight,
    down_weight,
):
    hidden = tokens[0].astype(jnp.float32)
    tok_rows, model_width = hidden.shape
    params = (
        lax.all_gather(query_matrix, ("dp", "seq"), axis=0, tiled=True),
        lax.all_gather(key_matrix, ("dp", "seq"), axis=0, tiled=True),
        lax.all_gather(value_matrix, ("dp", "seq"), axis=0, tiled=True),
        lax.all_gather(output_matrix, ("dp", "seq"), axis=0, tiled=True),
        lax.all_gather(attention_gain, ("dp", "seq"), axis=0, tiled=True),
        lax.all_gather(expert_gain, ("dp", "seq"), axis=0, tiled=True),
        lax.all_gather(router_matrix, ("dp", "seq"), axis=0, tiled=True),
    )
    query_full, key_full, value_full, output_full, gain_attention, gain_expert, router_full = params
    head_dim = HEAD_WIDTH
    query_width = query_full.shape[1]
    key_width = key_full.shape[1]
    query_heads = query_width // head_dim
    key_groups = key_width // head_dim
    head_group = query_heads // key_groups
    score_scale = head_dim ** (-0.5)
    first_place = lax.axis_index("seq") * tok_rows
    positions = first_place + jnp.arange(tok_rows, dtype=jnp.int32)
    last_place = first_place + tok_rows - 1
    prefix_end = prefix_len[0]
    cosine, sine_table = rotary_tables(positions, head_dim)
    inverse_attention = lax.rsqrt(jnp.mean(hidden * hidden, -1, keepdims=True) + NORM_EPS)
    normed_attention = hidden * inverse_attention
    attention_input = (normed_attention * gain_attention.astype(jnp.float32)).astype(jnp.bfloat16)
    query_projected = jnp.dot(
        attention_input, query_full, preferred_element_type=jnp.float32
    ).reshape(tok_rows, query_heads, head_dim)
    queries = (
        rotate(query_projected, cosine, sine_table)
        .astype(jnp.bfloat16)
        .reshape(tok_rows, key_groups, head_group, head_dim)
    )
    key_projected = jnp.dot(attention_input, key_full, preferred_element_type=jnp.float32).reshape(
        tok_rows, key_groups, head_dim
    )
    keys_local = (
        rotate(key_projected, cosine, sine_table).astype(jnp.bfloat16).reshape(tok_rows, key_width)
    )
    values_local = jnp.dot(attention_input, value_full, preferred_element_type=jnp.float32).astype(
        jnp.bfloat16
    )

    def block_scores(key_block, key_start):
        block_size = key_block.shape[0]
        key_heads = key_block.reshape(block_size, key_groups, head_dim)
        key_places = key_start + jnp.arange(block_size, dtype=jnp.int32)
        allowed = (key_places[None, :] <= positions[:, None]) | (key_places[None, :] < prefix_end)
        scores = (
            jnp.einsum("qhgd,khd->hgqk", queries, key_heads, preferred_element_type=jnp.float32)
            * score_scale
        )
        return (jnp.where(allowed, scores, -jnp.inf), key_heads)

    def attend(running, key_block, value_block, key_start):

        def compute(carried):
            run_max, run_sum, weighted = carried
            scores, key_heads = block_scores(key_block, key_start)
            value_heads = value_block.reshape(key_block.shape[0], key_groups, head_dim)
            new_max = jnp.maximum(run_max, jnp.max(scores, -1))
            weights = jnp.exp(scores - new_max[..., None])
            factor = jnp.exp(run_max - new_max)
            new_sum = run_sum * factor + jnp.sum(weights, -1)
            new_weighted = weighted * factor[..., None] + jnp.einsum(
                "hgqk,khd->hgqd",
                weights.astype(jnp.bfloat16),
                value_heads,
                preferred_element_type=jnp.float32,
            )
            return (new_max, new_sum, new_weighted)

        visible = (key_start <= last_place) | (key_start < prefix_end)
        return lax.cond(visible, compute, keep_state, running)

    stat_shape = (key_groups, head_group, tok_rows)
    start_state = (
        jnp.full(stat_shape, LOW_SCORE, jnp.float32),
        jnp.zeros(stat_shape, jnp.float32),
        jnp.zeros(stat_shape + (head_dim,), jnp.float32),
    )
    run_max, run_sum, weighted = over_key_blocks(
        (
            lax.all_gather(keys_local, "seq", axis=0, tiled=True),
            lax.all_gather(values_local, "seq", axis=0, tiled=True),
        ),
        attend,
        start_state,
    )
    log_total = run_max + jnp.log(run_sum)
    attended_heads = weighted / run_sum[..., None]
    attention_lowered = (
        attended_heads.transpose(2, 0, 1, 3).reshape(tok_rows, query_width).astype(jnp.bfloat16)
    )
    branch_output = jnp.einsum(
        "tc,dc->td", attention_lowered, output_full, preferred_element_type=jnp.float32
    )
    middle = hidden + branch_output
    inverse_expert = lax.rsqrt(jnp.mean(middle * middle, -1, keepdims=True) + NORM_EPS)
    normed_expert = middle * inverse_expert
    expert_input = (normed_expert * gain_expert.astype(jnp.float32)).astype(jnp.bfloat16)
    router_logits = jnp.dot(expert_input, router_full, preferred_element_type=jnp.float32)
    router_probs = jax.nn.softmax(router_logits, axis=-1)
    expert_count = router_full.shape[1]
    route_ids = routes[0]
    expert_range = jnp.arange(expert_count, dtype=jnp.int32)
    route_hits = jnp.sum(
        (route_ids[:, :, None] == expert_range[None, None, :]).astype(jnp.int32), 1
    )
    slot_rank = jnp.cumsum(route_hits, 0) - 1
    slot_target = jnp.where(route_hits > 0, slot_rank, CAPACITY)
    token_index = jnp.broadcast_to(
        jnp.arange(tok_rows, dtype=jnp.int32)[:, None], (tok_rows, expert_count)
    )
    expert_index = jnp.broadcast_to(expert_range[None, :], (tok_rows, expert_count))
    slot_table = (
        jnp.zeros((expert_count, CAPACITY), jnp.int32)
        .at[expert_index, slot_target]
        .set(token_index, mode="drop")
    )
    slot_live = jnp.arange(CAPACITY, dtype=jnp.int32)[None, :] < jnp.sum(route_hits, 0)[:, None]
    expert_column = expert_range[:, None]
    dispatched = expert_input[slot_table]
    slot_gates = jnp.where(slot_live, router_probs[slot_table, expert_column], 0.0)
    ff_width = down_weight.shape[2]
    grad_mid = cotangent[0].astype(jnp.float32)
    slot_grad = grad_mid[slot_table]
    out_grad = (slot_gates[..., None] * slot_grad).astype(jnp.bfloat16)
    gate_up_full, down_full = (
        lax.all_gather(gate_up_weight, ("dp", "seq"), axis=0, tiled=True),
        lax.all_gather(down_weight, ("dp", "seq"), axis=0, tiled=True),
    )
    mid_linear = jnp.einsum(
        "ecd,def->ecf", dispatched, gate_up_full, preferred_element_type=jnp.float32
    )
    activation = swiglu(mid_linear, ff_width)
    expert_out = jnp.einsum(
        "ecf,def->ecd", activation, down_full, preferred_element_type=jnp.float32
    )
    flat_slots = slot_table.reshape(-1)
    combined = (
        jnp.zeros((tok_rows, model_width), jnp.float32)
        .at[flat_slots]
        .add((slot_gates[..., None] * expert_out).reshape(-1, model_width))
    )
    mixed = (middle + combined).astype(jnp.bfloat16)
    gate_grad = jnp.where(slot_live, jnp.sum(expert_out * slot_grad, -1), 0.0)
    act_grad = jnp.einsum("ecd,def->ecf", out_grad, down_full, preferred_element_type=jnp.float32)
    mid_grad = swiglu_back(act_grad, mid_linear, ff_width)
    gate_up_term = jnp.einsum(
        "ecd,ecf->def", dispatched, mid_grad, preferred_element_type=jnp.float32
    )
    down_term = jnp.einsum("ecd,ecf->def", out_grad, activation, preferred_element_type=jnp.float32)
    summed_terms = lax.psum_scatter(
        jnp.concatenate([gate_up_term, down_term], axis=-1),
        ("dp", "seq"),
        scatter_dimension=0,
        tiled=True,
    )
    gate_up_weight_grad = summed_terms[..., : 2 * ff_width]
    down_weight_grad = summed_terms[..., 2 * ff_width :]
    dispatched_grad = jnp.einsum(
        "ecf,def->ecd", mid_grad, gate_up_full, preferred_element_type=jnp.float32
    )
    expert_in_grad = (
        jnp.zeros((tok_rows, model_width), jnp.float32)
        .at[flat_slots]
        .add(dispatched_grad.reshape(-1, model_width))
    )
    prob_grad = (
        jnp.zeros((tok_rows, expert_count), jnp.float32)
        .at[slot_table, expert_column]
        .add(gate_grad)
    )
    logit_grad = (
        router_probs * (prob_grad - jnp.sum(router_probs * prob_grad, -1, keepdims=True))
    ).astype(jnp.bfloat16)
    router_term = jnp.einsum(
        "td,te->de", expert_input, logit_grad, preferred_element_type=jnp.float32
    )
    expert_in_grad = expert_in_grad + jnp.einsum(
        "te,de->td", logit_grad, router_full, preferred_element_type=jnp.float32
    )
    expert_gain_term = jnp.sum(expert_in_grad * normed_expert, 0)
    grad_res = grad_mid + norm_back(
        expert_in_grad * gain_expert.astype(jnp.float32), normed_expert, inverse_expert
    )
    branch_grad = grad_res.astype(jnp.bfloat16)
    output_term = jnp.einsum(
        "td,tc->dc", branch_grad, attention_lowered, preferred_element_type=jnp.float32
    )
    attended_grad = jnp.dot(branch_grad, output_full, preferred_element_type=jnp.float32).astype(
        jnp.bfloat16
    )
    attended_grad_heads = attended_grad.reshape(
        tok_rows, key_groups, head_group, head_dim
    ).transpose(1, 2, 0, 3)
    delta = jnp.sum(attended_grad_heads.astype(jnp.float32) * attended_heads, -1)
    seq_total = tok_rows * lax.axis_size("seq")

    def attend_back(running, key_block, value_block, key_start):

        def compute(carried):
            query_sum, key_sum, value_sum = carried
            block_size = key_block.shape[0]
            scores, key_heads = block_scores(key_block, key_start)
            value_heads = value_block.reshape(block_size, key_groups, head_dim)
            probs_full = jnp.exp(scores - log_total[..., None])
            probs_low = probs_full.astype(jnp.bfloat16)
            value_piece = jnp.einsum(
                "hgqk,hgqd->khd", probs_low, attended_grad_heads, preferred_element_type=jnp.float32
            ).reshape(block_size, key_width)
            prob_part = jnp.einsum(
                "hgqd,khd->hgqk",
                attended_grad_heads,
                value_heads,
                preferred_element_type=jnp.float32,
            )
            score_grad = (probs_full * (prob_part - delta[..., None])).astype(jnp.bfloat16)
            query_sum = (
                query_sum
                + jnp.einsum(
                    "hgqk,khd->hgqd", score_grad, key_heads, preferred_element_type=jnp.float32
                )
                * score_scale
            )
            key_piece = (
                jnp.einsum(
                    "hgqk,qhgd->khd", score_grad, queries, preferred_element_type=jnp.float32
                )
                * score_scale
            ).reshape(block_size, key_width)
            key_sum = lax.dynamic_update_slice_in_dim(
                key_sum,
                lax.dynamic_slice_in_dim(key_sum, key_start, block_size, 0) + key_piece,
                key_start,
                0,
            )
            value_sum = lax.dynamic_update_slice_in_dim(
                value_sum,
                lax.dynamic_slice_in_dim(value_sum, key_start, block_size, 0) + value_piece,
                key_start,
                0,
            )
            return (query_sum, key_sum, value_sum)

        visible = (key_start <= last_place) | (key_start < prefix_end)
        return lax.cond(visible, compute, keep_state, running)

    back_start = (
        jnp.zeros(stat_shape + (head_dim,), jnp.float32),
        jnp.zeros((seq_total, key_width), jnp.float32),
        jnp.zeros((seq_total, key_width), jnp.float32),
    )
    query_sum, key_sum, value_sum = over_key_blocks(
        (
            lax.all_gather(keys_local, "seq", axis=0, tiled=True),
            lax.all_gather(values_local, "seq", axis=0, tiled=True),
        ),
        attend_back,
        back_start,
    )
    key_part, value_part = (
        lax.psum_scatter(
            key_sum.astype(jnp.bfloat16), "seq", scatter_dimension=0, tiled=True
        ).astype(jnp.float32),
        lax.psum_scatter(
            value_sum.astype(jnp.bfloat16), "seq", scatter_dimension=0, tiled=True
        ).astype(jnp.float32),
    )
    query_rows = query_sum.transpose(2, 0, 1, 3).reshape(tok_rows, query_heads, head_dim)
    query_grad = (
        rotate(query_rows, cosine, -sine_table).reshape(tok_rows, query_width).astype(jnp.bfloat16)
    )
    key_grad = (
        rotate(key_part.reshape(tok_rows, key_groups, head_dim), cosine, -sine_table)
        .reshape(tok_rows, key_width)
        .astype(jnp.bfloat16)
    )
    value_grad = value_part.astype(jnp.bfloat16)
    query_term = jnp.einsum(
        "td,tc->dc", attention_input, query_grad, preferred_element_type=jnp.float32
    )
    key_term = jnp.einsum(
        "td,tc->dc", attention_input, key_grad, preferred_element_type=jnp.float32
    )
    value_term = jnp.einsum(
        "td,tc->dc", attention_input, value_grad, preferred_element_type=jnp.float32
    )
    attention_in_grad = jnp.einsum(
        "tc,dc->td", query_grad, query_full, preferred_element_type=jnp.float32
    )
    attention_in_grad = attention_in_grad + jnp.einsum(
        "tc,dc->td", key_grad, key_full, preferred_element_type=jnp.float32
    )
    attention_in_grad = attention_in_grad + jnp.einsum(
        "tc,dc->td", value_grad, value_full, preferred_element_type=jnp.float32
    )
    attention_gain_term = jnp.sum(attention_in_grad * normed_attention, 0)
    tokens_grad = grad_res + norm_back(
        attention_in_grad * gain_attention.astype(jnp.float32), normed_attention, inverse_attention
    )
    summed_grads = (
        lax.psum_scatter(query_term, ("dp", "seq"), scatter_dimension=0, tiled=True),
        lax.psum_scatter(key_term, ("dp", "seq"), scatter_dimension=0, tiled=True),
        lax.psum_scatter(value_term, ("dp", "seq"), scatter_dimension=0, tiled=True),
        lax.psum_scatter(output_term, ("dp", "seq"), scatter_dimension=0, tiled=True),
        lax.psum_scatter(attention_gain_term, ("dp", "seq"), scatter_dimension=0, tiled=True),
        lax.psum_scatter(expert_gain_term, ("dp", "seq"), scatter_dimension=0, tiled=True),
        lax.psum_scatter(router_term, ("dp", "seq"), scatter_dimension=0, tiled=True),
    )
    return (
        mixed[None],
        tokens_grad[None],
        summed_grads[0],
        summed_grads[1],
        summed_grads[2],
        summed_grads[3],
        summed_grads[4],
        summed_grads[5],
        summed_grads[6],
        gate_up_weight_grad,
        down_weight_grad,
    )


def matmul(left, right, contract):
    return lax.dot_general(
        left, right, (contract, ((), ())), preferred_element_type=jnp.float32
    )


ROWS_BY_COLS = ((1,), (0,))
ROWS_BY_ROWS = ((1,), (1,))
COLS_BY_COLS = ((0,), (0,))


def split_sum_columns(terms):
    ones = jnp.ones((terms.shape[0], LANES), jnp.bfloat16)
    high = terms.astype(jnp.bfloat16)
    low = (terms - high.astype(jnp.float32)).astype(jnp.bfloat16)
    return matmul(high, ones, COLS_BY_COLS) + matmul(low, ones, COLS_BY_COLS)


def turned(value_rows):
    width = value_rows.shape[1]
    lane = lax.broadcasted_iota(jnp.int32, value_rows.shape, 1)
    ahead = pltpu.roll(value_rows, width - HALF, 1)
    behind = pltpu.roll(value_rows, HALF, 1)
    return jnp.where(lane % HEAD_WIDTH < HALF, -ahead, behind)


def spin(value_rows, cosine, sine_table):
    repeats = value_rows.shape[1] // LANES
    cos_all = jnp.concatenate([cosine] * repeats, 1) if repeats > 1 else cosine
    sin_all = jnp.concatenate([sine_table] * repeats, 1) if repeats > 1 else sine_table
    return value_rows * cos_all + turned(value_rows) * sin_all


def inverse_rms(value_rows):
    return lax.rsqrt(jnp.mean(value_rows * value_rows, -1, keepdims=True) + NORM_EPS)


def shape_of(*dims, kind=jnp.bfloat16):
    return jax.ShapeDtypeStruct(dims, kind)


VMEM_SPEC = pl.BlockSpec(memory_space=pltpu.VMEM)
SMEM_SPEC = pl.BlockSpec(memory_space=pltpu.SMEM)
ANY_SPEC = pl.BlockSpec(memory_space=pl.ANY)


class Place:
    def __init__(self):
        self.dp = lax.axis_index("dp")
        self.z = lax.axis_index("seq")
        self.lines = lax.axis_size("seq")
        self.chips = lax.axis_size("dp") // 2
        self.chip = self.dp // 2
        self.core = self.dp % 2
        self.other = 1 - self.core
        self.chip_x = self.chip + 1 - 2 * (self.chip % 2)
        self.chip_y = (self.chip + 2) % 4
        self.chip_diag = 3 - self.chip

    def ahead(self, step):
        return (self.z + step) % self.lines

    def behind(self, step):
        return (self.z + self.lines - step) % self.lines

    def line_peer(self, step):
        return (self.dp, self.ahead(step))

    def on_chip(self, chip):
        return (chip * 2 + self.core, self.z)

    def sibling(self):
        return (self.chip * 2 + self.other, self.z)


def meet(peers):
    barrier = pltpu.get_barrier_semaphore()
    for peer in peers:
        pl.semaphore_signal(barrier, inc=1, device_id=peer, device_id_type=MESH)
    pl.semaphore_wait(barrier, len(peers))


def send(source, target, send_sem, recv_sem, peer):
    copy = pltpu.make_async_remote_copy(
        src_ref=source,
        dst_ref=target,
        send_sem=send_sem,
        recv_sem=recv_sem,
        device_id=peer,
        device_id_type=MESH,
    )
    copy.start()
    return copy


def move(source, target, sem):
    copy = pltpu.make_async_copy(source, target, sem)
    copy.start()
    return copy


def all_peers(here):
    return (
        [here.line_peer(k) for k in range(1, here.lines)]
        + [here.on_chip(chip) for chip in (here.chip_x, here.chip_y, here.chip_diag)]
        + [here.sibling()]
    )


def comm_params(ident, limit=56):
    return pltpu.CompilerParams(
        collective_id=ident, has_side_effects=True, vmem_limit_bytes=limit << 20
    )


class Spread:
    def __init__(self, here, pick, target, depth, local_sem, sends, recvs):
        self.here, self.pick, self.target, self.depth = here, pick, target, depth
        self.local_sem, self.sends, self.recvs = local_sem, sends, recvs
        self.used = 0

    def put(self, source, target, peer):
        copy = send(source, target, self.sends.at[self.used], self.recvs.at[self.used], peer)
        self.used += 1
        return copy

    def row(self):
        here = self.here
        if len(self.target.shape) > 2:
            return self.target.at[here.chip, here.core, here.z]
        first = (here.dp * here.lines + here.z) * self.depth
        return self.target.at[pl.ds(pl.multiple_of(first, self.depth), self.depth)]

    def chip_rows(self, chip, part=None):
        here = self.here
        if len(self.target.shape) > 2:
            if part is None:
                return self.target.at[chip, here.core]
            return self.target.at[chip, here.core, pl.ds(part * (here.lines // 2), here.lines // 2)]
        count = here.lines * self.depth
        first = (chip * 2 + here.core) * count
        if part is not None:
            first, count = first + part * (count // 2), count // 2
        return self.target.at[pl.ds(pl.multiple_of(first, count), count)]

    def start(self):
        here = self.here
        mine = self.row()
        self.own = move(self.pick(here.z), mine, self.local_sem)
        self.line = [
            self.put(self.pick(here.ahead(k)), mine, here.line_peer(k)) for k in range(1, here.lines)
        ]

    def chips(self):
        here = self.here
        self.own.wait()
        for copy in self.line:
            copy.wait_recv()
        mine = self.chip_rows(here.chip)
        self.plane = [
            self.put(mine, mine, here.on_chip(here.chip_x)),
            self.put(mine, mine, here.on_chip(here.chip_y)),
        ]
        self.across = [self.put(mine, mine, here.sibling())]

    def turn(self):
        here = self.here
        self.corner = []
        for copy, origin, onward, part in (
            (self.plane[0], here.chip_x, here.chip_y, 0),
            (self.plane[1], here.chip_y, here.chip_x, 1),
        ):
            copy.wait_recv()
            half = self.chip_rows(origin, part)
            self.corner.append(self.put(half, half, here.on_chip(onward)))
            block = self.chip_rows(origin)
            self.across.append(self.put(block, block, here.sibling()))

    def cores(self):
        here = self.here
        for copy in self.corner:
            copy.wait_recv()
        block = self.chip_rows(here.chip_diag)
        self.across.append(self.put(block, block, here.sibling()))

    def finish(self):
        for copy in self.across:
            copy.wait_recv()

    def close(self):
        for copy in self.line + self.plane + self.corner + self.across:
            copy.wait_send()


def spread_count(lines):
    return lines - 1 + 2 + 2 + 4


class LineGather:
    def __init__(self, here, view, sends, recvs, source=None):
        self.here, self.view, self.source = here, view, source
        self.sends, self.recvs = sends, recvs

    def copy(self, way, hop, block, source=None):
        here = self.here
        step = 1 if way == 0 else here.lines - 1
        return pltpu.make_async_remote_copy(
            src_ref=self.view(block) if source is None else source,
            dst_ref=self.view(block),
            send_sem=self.sends.at[way, hop - 1],
            recv_sem=self.recvs.at[way, hop - 1],
            device_id=here.line_peer(step),
            device_id_type=MESH,
        )

    def start(self):
        here = self.here

        @pl.when(here.z < here.lines - 1)
        def rightward():
            self.copy(0, 1, here.z, self.source).start()

        @pl.when(here.z > 0)
        def leftward():
            self.copy(1, 1, here.z, self.source).start()

    def step(self, hop):
        here = self.here
        lines = here.lines

        @pl.when(here.z >= hop)
        def from_left():
            block = here.behind(hop)
            self.copy(0, hop, block).wait_recv()
            if hop < lines - 1:

                @pl.when(here.z < lines - 1)
                def onward():
                    self.copy(0, hop + 1, block).start()

        @pl.when(here.z + hop < lines)
        def from_right():
            block = here.ahead(hop)
            self.copy(1, hop, block).wait_recv()
            if hop < lines - 1:

                @pl.when(here.z > 0)
                def onward():
                    self.copy(1, hop + 1, block).start()

    def close(self):
        here = self.here
        lines = here.lines
        for hop in range(1, lines):

            @pl.when((here.z >= hop - 1) & (here.z < lines - 1))
            def rightward():
                self.copy(0, hop, here.behind(hop - 1)).wait_send()

            @pl.when((here.z + hop - 1 < lines) & (here.z > 0))
            def leftward():
                self.copy(1, hop, here.ahead(hop - 1)).wait_send()


class LineSpread:
    def __init__(self, here, view, sends, recvs, source=None):
        self.here, self.view, self.source = here, view, source
        self.sends, self.recvs = sends, recvs

    def start(self):
        here = self.here
        mine = self.view(here.z)
        self.line = [
            send(
                mine if self.source is None else self.source, mine, self.sends.at[k - 1], self.recvs.at[k - 1], here.line_peer(k)
            )
            for k in range(1, here.lines)
        ]

    def arrived(self, step):
        self.line[step - 1].wait_recv()

    def finish(self):
        for copy in self.line:
            copy.wait_recv()

    def close(self):
        for copy in self.line:
            copy.wait_send()


class LineSum:
    def __init__(self, here, parts, landed, rows, sends, recvs):
        self.here, self.parts, self.landed, self.rows = here, parts, landed, rows
        self.sends, self.recvs = sends, recvs

    def copy(self, way, hops):
        here = self.here
        step = 1 if way == 0 else here.lines - 1
        block = here.ahead(hops) if way == 0 else here.behind(hops)
        return pltpu.make_async_remote_copy(
            src_ref=self.parts.at[block, self.rows],
            dst_ref=self.landed.at[way, hops - 1, self.rows],
            send_sem=self.sends.at[way, hops - 1],
            recv_sem=self.recvs.at[way, hops - 1],
            device_id=here.line_peer(step),
            device_id_type=MESH,
        )

    def launch(self, hops):
        here = self.here

        @pl.when(here.z == 0)
        def rightward():
            self.copy(0, hops).start()

        @pl.when(here.z == here.lines - 1)
        def leftward():
            self.copy(1, hops).start()

    def step(self, hops):
        here = self.here
        lines = here.lines

        def pass_on(way):
            block = here.ahead(hops) if way == 0 else here.behind(hops)
            self.copy(way, hops + 1).wait_recv()
            self.parts[block, self.rows] = (
                self.parts[block, self.rows].astype(jnp.float32)
                + self.landed[way, hops, self.rows].astype(jnp.float32)
            ).astype(self.parts.dtype)
            self.copy(way, hops).start()

        @pl.when((here.z > 0) & (here.z + hops < lines))
        def rightward():
            pass_on(0)

        @pl.when((here.z < lines - 1) & (here.z >= hops))
        def leftward():
            pass_on(1)

    def finish(self, total):
        here = self.here
        rows = self.rows
        total[rows, :] = self.parts[here.z, rows].astype(jnp.float32)

        @pl.when(here.z > 0)
        def from_left():
            self.copy(0, 1).wait_recv()
            total[rows, :] = total[rows, :] + self.landed[0, 0, rows].astype(jnp.float32)

        @pl.when(here.z < here.lines - 1)
        def from_right():
            self.copy(1, 1).wait_recv()
            total[rows, :] = total[rows, :] + self.landed[1, 0, rows].astype(jnp.float32)

    def close(self):
        here = self.here
        for hops in range(1, here.lines):

            @pl.when(here.z + hops < here.lines)
            def rightward():
                self.copy(0, hops).wait_send()

            @pl.when(here.z >= hops)
            def leftward():
                self.copy(1, hops).wait_send()


class Halves:
    def __init__(self, *members):
        self.members = members

    def start(self):
        for member in self.members:
            member.start()

    def launch(self, hops):
        for member in self.members:
            member.launch(hops)

    def step(self, hops):
        for member in self.members:
            member.step(hops)

    def finish(self, total):
        for member in self.members:
            member.finish(total)

    def close(self):
        for member in self.members:
            member.close()


class LineSwap:
    def __init__(self, here, pick, received, sends, recvs):
        self.here, self.pick, self.received = here, pick, received
        self.sends, self.recvs = sends, recvs

    def start(self):
        here = self.here
        self.line = [
            send(
                self.pick(here.ahead(k)), self.received(k, here.z), self.sends.at[k - 1], self.recvs.at[k - 1], here.line_peer(k)
            )
            for k in range(1, here.lines)
        ]

    def finish(self):
        for copy in self.line:
            copy.wait_recv()

    def close(self):
        for copy in self.line:
            copy.wait_send()


def padded_square(block):
    filler = jnp.zeros((LANES - block.shape[0], LANES), jnp.float32)
    return jnp.concatenate([block, filler], 0).T


def row_order(depth, experts, by_expert):
    count = depth * experts
    place = lax.broadcasted_iota(jnp.int32, (count, count), 0)
    source = lax.broadcasted_iota(jnp.int32, (count, count), 1)
    if by_expert:
        wanted = place % depth * experts + place // depth
    else:
        wanted = place % experts * depth + place // experts
    return (source == wanted).astype(jnp.bfloat16)


class Fold:
    def __init__(self, here, terms, crossed, landed, last, sends, recvs):
        self.here, self.terms, self.crossed = here, terms, crossed
        self.landed, self.last = landed, last
        self.sends, self.recvs = sends, recvs
        middle = here.lines // 2
        self.parts = [(0, middle), (middle, here.lines)]

    def start(self):
        here = self.here
        self.first = send(
            self.terms.at[:, here.other], self.crossed, self.sends.at[0], self.recvs.at[0], here.sibling()
        )

    def chips(self):
        here = self.here
        self.first.wait_recv()
        for chip in range(here.chips):
            self.terms[chip, here.core] = (
                self.terms[chip, here.core].astype(jnp.float32) + self.crossed[chip].astype(jnp.float32)
            ).astype(jnp.bfloat16)
        self.one, self.straight = [], []
        for number, near in enumerate((here.chip_x, here.chip_y)):
            low, high = self.parts[number]
            for slot, chip, group in ((1, here.chip_diag, self.one), (0, near, self.straight)):
                place = 1 + number * 2 + slot
                group.append(
                    send(
                        self.terms.at[chip, here.core, low:high], self.landed.at[number, slot],
                        self.sends.at[place], self.recvs.at[place], here.on_chip(near),
                    )
                )

    def turn(self):
        here = self.here
        self.two = []
        for number, onward in enumerate((here.chip_y, here.chip_x)):
            low, high = self.parts[number]
            self.one[number].wait_recv()
            self.terms[onward, here.core, low:high] = (
                self.terms[onward, here.core, low:high].astype(jnp.float32)
                + self.landed[number, 1].astype(jnp.float32)
            ).astype(jnp.bfloat16)
            place = 5 + number
            self.two.append(
                send(
                    self.terms.at[onward, here.core, low:high], self.last.at[number],
                    self.sends.at[place], self.recvs.at[place], here.on_chip(onward),
                )
            )

    def finish(self):
        here = self.here
        for number in range(2):
            low, high = self.parts[number]
            self.straight[number].wait_recv()
            self.two[number].wait_recv()
            self.terms[here.chip, here.core, low:high] = (
                self.terms[here.chip, here.core, low:high].astype(jnp.float32)
                + self.landed[number, 0].astype(jnp.float32)
                + self.last[number].astype(jnp.float32)
            ).astype(jnp.bfloat16)

    def sums(self, z):
        return self.terms.at[self.here.chip, self.here.core, z]

    def close(self):
        for copy in [self.first] + self.one + self.straight + self.two:
            copy.wait_send()


def layer_kernel(
    prefix, tokens, query_rows, key_rows, value_rows, out_rows, router_cols, attention_gain, expert_gain, gate_up_rows, down_rows,
    cotangent, routes, cosine, sine_table,
    mixed_o, tokens_grad_o, query_o, key_o, value_o, out_o, attention_gain_o, expert_gain_o, router_o, expert_o,
    square, rows, expert_rows, tokens_all, weights, out_full, terms, cot_all, chosen_all, att_in, qkv, attended, attended_all,
    log_total, expert_in, probs, middle, slopes, acts, mids, part_mix, got_mix, mix_total, mixed, part_grad, got_grad,
    gate_grad, got_gate, grad_res, attended_grad, attended_grad_all, joined_grad, key_sum, value_sum, e_landed, e_last,
    o_terms, o_crossed, o_landed, o_last, o_lines, q_terms, q_crossed, q_landed, q_last, q_lines,
    query_s, key_s, value_s, out_s, attention_gain_s, expert_gain_s, router_s,
    local_sem, r_sends, r_recvs, o_sends, o_recvs, e_sends, e_recvs, t_sends, t_recvs, c_sends, c_recvs, k_sends, k_recvs,
    a_sends, a_recvs, m_sends, m_recvs, x_sends, x_recvs, g_sends, g_recvs, b_sends, b_recvs, p_sends, p_recvs,
    f_sends, f_recvs, of_sends, of_recvs, q_sends, q_recvs, el_sends, el_recvs, ol_sends, ol_recvs, ql_sends, ql_recvs,
    free_sem, out_sem,
):
    here = Place()
    lines = here.lines
    tok_rows, width = tokens.shape
    rows_all = lines * tok_rows
    depth = rows.shape[1]
    own_experts = terms.shape[0]
    ff_width = terms.shape[5] // 3
    chips = here.chips
    five = (chips, 2, lines, depth)
    four = (chips, lines, depth)
    query_width = lines * (qkv.shape[1] // 2)
    qkv_cols = qkv.shape[1]
    kv_cols = qkv_cols // 4
    q_cols = 2 * kv_cols
    stores = []

    def store(source, target):
        stores.append(move(source, target, out_sem.at[len(stores)]))

    gate_up_load = move(gate_up_rows, mids.at[0, ..., : 2 * ff_width], local_sem.at[0])
    down_load = move(down_rows, mids.at[0, ..., 2 * ff_width :], local_sem.at[1])
    token_load = move(tokens, tokens_all.at[here.z], local_sem.at[2])
    cot_load = move(cotangent, cot_all.at[here.z], local_sem.at[3])

    square[...] = jnp.zeros_like(square)
    square[:EXPERT_COUNT, :depth] = router_cols[...].astype(jnp.float32)
    square[EXPERT_COUNT : EXPERT_COUNT + 1, :depth] = attention_gain[...].astype(jnp.float32)
    square[EXPERT_COUNT + 1 : EXPERT_COUNT + 2, :depth] = expert_gain[...].astype(jnp.float32)
    small = square[...].T[:depth, :].astype(jnp.bfloat16)
    for line in range(lines):
        rows[line, :, :q_cols] = query_rows[:, line * q_cols : (line + 1) * q_cols]
        rows[line, :, q_cols : q_cols + kv_cols] = key_rows[:, line * kv_cols : (line + 1) * kv_cols]
        rows[line, :, q_cols + kv_cols : qkv_cols] = value_rows[:, line * kv_cols : (line + 1) * kv_cols]
        rows[line, :, qkv_cols:] = small
    meet(all_peers(here))
    rows_spread = Spread(here, lambda z: rows.at[z], weights, depth, local_sem.at[4], r_sends, r_recvs)
    half = tok_rows // 2
    token_gathers = [
        LineGather(
            here, lambda z, n=n: tokens_all.at[z, pl.ds(n * half, half)], t_sends.at[n], t_recvs.at[n], tokens.at[pl.ds(n * half, half)]
        )
        for n in range(2)
    ]
    out_spread = Spread(here, lambda z: out_rows, out_full, depth, local_sem.at[5], o_sends, o_recvs)
    chosen_swap = LineSwap(
        here, lambda z: chosen_all.at[here.z], lambda k, z: chosen_all.at[z], k_sends, k_recvs
    )
    cot_gather = Halves(
        *[
            LineGather(
                here, lambda z, n=n: cot_all.at[z, pl.ds(n * half, half)], c_sends.at[n], c_recvs.at[n], cotangent.at[pl.ds(n * half, half)]
            )
            for n in range(2)
        ]
    )
    expert_spreads = [
        Spread(
            here,
            lambda z, e=e: expert_rows.at[z, e], terms.at[e], depth, local_sem.at[6 + e], e_sends.at[e], e_recvs.at[e],
        )
        for e in range(own_experts)
    ]
    rows_spread.start()
    gate_up_load.wait()
    down_load.wait()
    order = row_order(depth, EXPERT_COUNT, True)
    expert_rows[...] = (
        matmul(order, mids[0].reshape(depth * EXPERT_COUNT, 3 * ff_width), ROWS_BY_COLS)
        .astype(jnp.bfloat16)
        .reshape(expert_rows.shape)
    )
    expert_spreads[0].start()
    token_gathers[0].start()
    token_gathers[1].start()
    expert_id = lax.broadcasted_iota(jnp.int32, (EXPERT_COUNT, tok_rows), 0)
    chosen = jnp.zeros((EXPERT_COUNT, tok_rows), jnp.float32)
    for number in range(routes.shape[0]):
        chosen = chosen + (routes[number : number + 1, :] == expert_id).astype(jnp.float32)
    chosen_all[here.z] = chosen.astype(jnp.bfloat16)
    chosen_swap.start()
    rows_spread.chips()
    rows_spread.turn()
    rows_spread.cores()
    expert_spreads[0].chips()
    token_gathers[0].step(1)
    token_gathers[1].step(1)
    expert_spreads[1].start()
    rows_spread.finish()
    columns = weights[:, qkv_cols:].astype(jnp.float32).T
    gain_attention = columns[EXPERT_COUNT : EXPERT_COUNT + 1, :]
    gain_expert = columns[EXPERT_COUNT + 1 : EXPERT_COUNT + 2, :]

    def project(source):
        block = pl.ds(pl.multiple_of(source * tok_rows, tok_rows), tok_rows)
        hidden = tokens_all[source].astype(jnp.float32)
        normed = (hidden * inverse_rms(hidden) * gain_attention).astype(jnp.bfloat16)
        att_in[block, :] = normed
        linear = matmul(normed, weights[:, :qkv_cols], ROWS_BY_COLS)
        turned_part = linear[:, : q_cols + kv_cols]
        qkv[block, : q_cols + kv_cols] = spin(turned_part, cosine[block, :], sine_table[block, :]).astype(
            jnp.bfloat16
        )
        qkv[block, q_cols + kv_cols :] = linear[:, q_cols + kv_cols :].astype(jnp.bfloat16)

    def project_hop(hop):
        @pl.when(here.z >= hop)
        def left():
            project(here.behind(hop))

        @pl.when(here.z + hop < lines)
        def right():
            project(here.ahead(hop))

    token_load.wait()
    project(here.z)
    expert_spreads[0].turn()
    expert_spreads[1].chips()
    expert_spreads[0].cores()
    for hop in range(2, lines - 1):
        token_gathers[0].step(hop)
        token_gathers[1].step(hop)
    out_spread.start()
    for spread in expert_spreads[2:]:
        spread.start()
    for hop in range(1, lines - 1):
        project_hop(hop)
    expert_spreads[1].turn()
    for gather in token_gathers:
        gather.step(lines - 1)
    project_hop(lines - 1)

    prefix_end = prefix[0]
    heads = q_cols // HEAD_WIDTH
    group = q_cols // kv_cols

    def attend(number):
        start = number * tok_rows
        block = pl.ds(start, tok_rows)
        reach = max(rows_all // 2, start + tok_rows)
        query_place = start + lax.broadcasted_iota(jnp.int32, (tok_rows, reach), 0)
        key_place = lax.broadcasted_iota(jnp.int32, (tok_rows, reach), 1)
        allowed = (key_place <= query_place) | (key_place < prefix_end)
        lanes = lax.broadcasted_iota(jnp.int32, (tok_rows, LANES), 1)
        totals = jnp.zeros((tok_rows, LANES), jnp.float32)
        outputs = []
        for head in range(heads):
            key_at = q_cols + head // group * HEAD_WIDTH
            value_at = key_at + kv_cols
            scores = matmul(
                qkv[block, head * HEAD_WIDTH : (head + 1) * HEAD_WIDTH],
                qkv[:reach, key_at : key_at + HEAD_WIDTH],
                ROWS_BY_ROWS,
            )
            scores = jnp.where(allowed, scores * SCORE_SCALE, LOW_SCORE)
            largest = jnp.max(scores, -1, keepdims=True)
            powers = jnp.exp(scores - largest)
            total = jnp.sum(powers, -1, keepdims=True)
            product = matmul(
                powers.astype(jnp.bfloat16), qkv[:reach, value_at : value_at + HEAD_WIDTH], ROWS_BY_COLS
            )
            outputs.append(product / total)
            totals = jnp.where(lanes == head, largest + jnp.log(total), totals)
        joined = jnp.concatenate(outputs, 1)
        attended[block, :] = joined
        log_total[block, :] = totals
        attended_all[here.z, block, :] = joined.astype(jnp.bfloat16)

    def mix_in(number):
        block = pl.ds(number * tok_rows, tok_rows)
        branch = matmul(attended_all[0, block, :], out_full[:, :q_cols], ROWS_BY_ROWS)
        for line in range(1, lines):
            branch = branch + matmul(
                attended_all[line, block, :], out_full[:, line * q_cols : (line + 1) * q_cols], ROWS_BY_ROWS
            )
        total = tokens_all[number].astype(jnp.float32) + branch
        lowered = (total * inverse_rms(total) * gain_expert).astype(jnp.bfloat16)
        expert_in[number] = lowered
        logits = matmul(lowered, weights[:, qkv_cols:], ROWS_BY_COLS)
        lane = lax.broadcasted_iota(jnp.int32, logits.shape, 1)
        logits = jnp.where(lane < EXPERT_COUNT, logits, LOW_SCORE)
        powers = jnp.exp(logits - jnp.max(logits, -1, keepdims=True))
        powers = jnp.where(lane < EXPERT_COUNT, powers, 0.0)
        probs[number] = powers / jnp.sum(powers, -1, keepdims=True)

        @pl.when(here.z == number)
        def keep():
            middle[...] = total


    attended_gathers = [
        LineGather(
            here, lambda z, n=n: attended_all.at[z, pl.ds(n * tok_rows, tok_rows)], a_sends.at[n], a_recvs.at[n]
        )
        for n in range(lines)
    ]
    def gate_columns(number, e):
        chosen = padded_square(chosen_all[number].astype(jnp.float32))
        lane = lax.broadcasted_iota(jnp.int32, chosen.shape, 1)
        own = lane == here.z * own_experts + e
        picked = jnp.sum(jnp.where(own, chosen, 0.0), -1, keepdims=True)
        gate = jnp.sum(jnp.where(own, probs[number] * chosen, 0.0), -1, keepdims=True)
        return own, picked, gate

    pairs = [(a, a + 2) for a in range(0, lines, 2)]

    def gate_up_of(e):
        return terms[e, ..., : 2 * ff_width].reshape(width, 2 * ff_width)

    def down_of(e):
        return terms[e, ..., 2 * ff_width :].reshape(width, ff_width)

    def expert_forward(e, numbers):
        for low, high in numbers:
            block = pl.ds(low * tok_rows, (high - low) * tok_rows)
            inputs = jnp.concatenate([expert_in[n] for n in range(low, high)], 0)
            linear = matmul(inputs, gate_up_of(e), ROWS_BY_COLS)
            gate_part, up_part = linear[:, :ff_width], linear[:, ff_width:]
            sigmoid = 1.0 / (1.0 + jnp.exp(-gate_part))
            silu = gate_part * sigmoid
            act = silu * up_part
            slopes[e, block, :ff_width] = (
                up_part * (sigmoid * (1.0 + gate_part * (1.0 - sigmoid)))
            ).astype(jnp.bfloat16)
            slopes[e, block, ff_width:] = silu.astype(jnp.bfloat16)
            acts[e, block, :] = act.astype(jnp.bfloat16)
            gate = jnp.concatenate([gate_columns(n, e)[2] for n in range(low, high)], 0)
            mids[e, low:high, ..., 2 * ff_width :] = (
                (gate * act).astype(jnp.bfloat16).reshape(high - low, lines, depth, ff_width)
            )

    def line_sum(parts, landed, sends, recvs):
        return Halves(
            *[
                LineSum(here, parts, landed, pl.ds(n * half, half), sends.at[n], recvs.at[n])
                for n in range(2)
            ]
        )

    def mix_out(members):
        for low, high in pairs:
            total = None
            if 0 not in members:
                total = jnp.concatenate([part_mix[n] for n in range(low, high)], 0).astype(jnp.float32)
            for e in members:
                gated = mids[e, low:high, ..., 2 * ff_width :].reshape((high - low) * tok_rows, ff_width)
                term = matmul(gated, down_of(e), ROWS_BY_ROWS)
                total = term if total is None else total + term
            for n in range(low, high):
                part_mix[n] = total[(n - low) * tok_rows : (n - low + 1) * tok_rows, :].astype(jnp.bfloat16)

    def expert_back(low, members):
        block = pl.ds(pl.multiple_of(low * tok_rows, 2 * tok_rows), 2 * tok_rows)
        grad_mid = jnp.concatenate([cot_all[low], cot_all[low + 1]], 0)
        opening = 0 in members
        total = None
        if not opening:
            total = jnp.concatenate([part_grad[low], part_grad[low + 1]], 0).astype(jnp.float32)
        gate_cols = [jnp.zeros((tok_rows, LANES), jnp.float32)] * 2
        for e in members:
            act_grad = matmul(grad_mid, down_of(e), ROWS_BY_COLS)
            column = jnp.sum(act_grad * acts[e, block, :].astype(jnp.float32), -1, keepdims=True)
            gates = []
            for n in range(2):
                own, picked, gate = gate_columns(low + n, e)
                part = column[n * tok_rows : (n + 1) * tok_rows, :]
                gate_cols[n] = jnp.where(own, part * picked, gate_cols[n])
                gates.append(gate)
            act_grad = act_grad * jnp.concatenate(gates, 0)
            slope = slopes[e, block, :].astype(jnp.float32)
            mid = jnp.concatenate(
                [act_grad * slope[:, :ff_width], act_grad * slope[:, ff_width:]], 1
            ).astype(jnp.bfloat16)
            mids[e, pl.ds(low, 2), ..., : 2 * ff_width] = mid.reshape(2, lines, depth, 2 * ff_width)
            term = matmul(mid, gate_up_of(e), ROWS_BY_ROWS)
            total = term if total is None else total + term
        for n in range(2):
            part_grad[low + n] = total[n * tok_rows : (n + 1) * tok_rows, :].astype(jnp.bfloat16)
            gate_rows = gate_cols[n].T[:EXPERT_COUNT, :]
            gate_grad[low + n] = gate_rows if opening else gate_grad[low + n] + gate_rows

    folds = [
        Fold(here, terms.at[e], mids.at[e], e_landed.at[e], e_last.at[e], f_sends.at[e], f_recvs.at[e])
        for e in range(own_experts)
    ]

    def weight_terms(e):
        terms[e, ..., : 2 * ff_width] = (
            matmul(
                expert_in[...].reshape(rows_all, width),
                mids[e, ..., : 2 * ff_width].reshape(rows_all, 2 * ff_width),
                COLS_BY_COLS,
            )
            .astype(jnp.bfloat16)
            .reshape(*five, 2 * ff_width)
        )
        terms[e, ..., 2 * ff_width :] = (
            matmul(
                cot_all[...].reshape(rows_all, width),
                mids[e, ..., 2 * ff_width :].reshape(rows_all, ff_width),
                COLS_BY_COLS,
            )
            .astype(jnp.bfloat16)
            .reshape(*five, ff_width)
        )
        pl.semaphore_signal(free_sem.at[e], inc=1, device_id=here.sibling(), device_id_type=MESH)

    def fold_start(e):
        pl.semaphore_wait(free_sem.at[e], 1)
        folds[e].start()

    near = here.z // 2 * 2
    far = (near + 2) % lines
    def mix_arrived(number):
        attended_gathers[number].step(lines - 1)
        mix_in(number)

    out_spread.chips()
    for turn in range(lines):
        attend(turn)
        attended_gathers[turn].start()
    early, late = cot_gather.members
    expert_spreads[1].cores()
    expert_spreads[2].chips()
    out_spread.turn()
    expert_spreads[3].chips()
    for gather in attended_gathers:
        gather.step(1)
    expert_spreads[2].turn()
    out_spread.cores()
    for gather in attended_gathers:
        gather.step(2)
    cot_gather.start()
    out_spread.finish()
    chosen_swap.finish()
    mix_arrived(0)
    mix_arrived(1)
    for e in range(2):
        expert_spreads[e].finish()
        expert_forward(e, pairs[:1])
    mix_arrived(2)
    mix_arrived(3)
    expert_spreads[2].cores()
    expert_spreads[3].turn()
    early.step(1)
    late.step(1)
    for e in range(2):
        expert_forward(e, pairs[1:])
    expert_spreads[2].finish()
    expert_forward(2, pairs)
    for hop in range(2, lines - 1):
        early.step(hop)
    mix_out([0, 1, 2])
    expert_spreads[3].cores()
    for hop in range(2, lines - 1):
        late.step(hop)
    cot_load.wait()
    near = here.z // 2 * 2
    far = (near + 2) % lines
    expert_back(near, [0, 1, 2])
    expert_spreads[3].finish()
    expert_forward(3, pairs)
    mix_out([3])
    mix_swap = line_sum(part_mix, got_mix, m_sends, m_recvs)
    mix_swap.launch(lines - 1)
    for hops in range(lines - 2, 1, -1):
        mix_swap.launch(hops)
    expert_back(near, [3])
    cot_gather.step(lines - 1)
    expert_back(far, [0])
    for spread in expert_spreads[:1]:
        spread.close()
    weight_terms(0)
    fold_start(0)
    expert_back(far, [1, 2, 3])
    for group_of in [rows_spread, out_spread, chosen_swap, cot_gather] + token_gathers + expert_spreads[1:] + attended_gathers:
        group_of.close()
    grad_swap = line_sum(part_grad, got_grad, x_sends, x_recvs)
    gate_swap = LineSwap(here, lambda z: gate_grad.at[z], lambda k, z: got_gate.at[k - 1], g_sends, g_recvs)
    attended_swap = LineSwap(
        here, lambda z: attended_grad.at[z], lambda k, z: attended_grad_all.at[z], b_sends, b_recvs
    )
    part_swap = line_sum(part_grad, got_grad, p_sends, p_recvs)
    out_fold = Fold(here, o_terms, o_crossed, o_landed, o_last, of_sends, of_recvs)
    qkv_fold = Fold(here, q_terms, q_crossed, q_landed, q_last, q_sends, q_recvs)
    expert_swaps = [
        LineSwap(here, folds[e].sums, lambda k, z, e=e: expert_rows.at[z, e], el_sends.at[e], el_recvs.at[e])
        for e in range(own_experts)
    ]
    out_swap = LineSwap(here, out_fold.sums, lambda k, z: o_lines.at[k - 1], ol_sends, ol_recvs)
    qkv_swap = LineSwap(here, qkv_fold.sums, lambda k, z: q_lines.at[z], ql_sends, ql_recvs)

    for hops in range(lines - 1, 0, -1):
        grad_swap.launch(hops)
    gate_swap.start()
    folds[0].chips()
    weight_terms(1)
    fold_start(1)
    for hops in range(lines - 2, 1, -1):
        mix_swap.step(hops)
    for hops in range(lines - 2, 1, -1):
        grad_swap.step(hops)
    folds[1].chips()
    weight_terms(2)
    fold_start(2)
    grad_swap.step(1)
    folds[0].turn()
    weight_terms(3)
    fold_start(3)
    folds[2].chips()

    gate_swap.finish()
    grad_swap.finish(grad_res)
    gate_rows = gate_grad[here.z]
    for k in range(lines - 1):
        gate_rows = gate_rows + got_gate[k]
    gates = padded_square(gate_rows)
    grad = grad_res[...]
    prob = probs[here.z]
    logit_grad = (prob * (gates - jnp.sum(prob * gates, -1, keepdims=True))).astype(jnp.bfloat16)
    grad = grad + matmul(logit_grad, weights[:, qkv_cols:], ROWS_BY_ROWS)
    hidden = middle[...]
    inverse = inverse_rms(hidden)
    normed = hidden * inverse
    scaled = grad * gain_expert
    result = cot_all[here.z].astype(jnp.float32) + inverse * (
        scaled - normed * jnp.mean(scaled * normed, -1, keepdims=True)
    )
    grad_res[...] = result
    branch = result.astype(jnp.bfloat16)
    for line in range(lines):
        attended_grad[line] = matmul(
            branch, out_full[:, line * q_cols : (line + 1) * q_cols], ROWS_BY_COLS
        ).astype(jnp.bfloat16)
    attended_swap.start()
    attended_grad_all[here.z] = attended_grad[here.z]
    own_block = pl.ds(pl.multiple_of(here.z * tok_rows, tok_rows), tok_rows)
    router_term = matmul(expert_in[here.z], logit_grad, COLS_BY_COLS)
    gain_term = split_sum_columns(grad * normed)
    lane = lax.broadcasted_iota(jnp.int32, router_term.shape, 1)
    for line in range(lines):
        o_terms[..., line * q_cols : (line + 1) * q_cols] = (
            matmul(branch, attended_all[line, own_block, :], COLS_BY_COLS).astype(jnp.bfloat16).reshape(*five, q_cols)
        )
    o_terms[..., query_width:] = (
        jnp.where(lane == EXPERT_COUNT, gain_term, router_term).astype(jnp.bfloat16).reshape(*five, LANES)
    )
    out_fold.start()
    mix_swap.launch(1)
    folds[1].turn()
    folds[3].chips()
    folds[0].finish()
    expert_swaps[0].start()
    attended_swap.finish()
    grad_swap.close()

    key_sum[...] = jnp.zeros_like(key_sum)
    value_sum[...] = jnp.zeros_like(value_sum)

    def attend_back(number):
        start = number * tok_rows
        block = pl.ds(start, tok_rows)
        reach = max(rows_all // 2, start + tok_rows)
        query_place = start + lax.broadcasted_iota(jnp.int32, (tok_rows, reach), 0)
        key_place = lax.broadcasted_iota(jnp.int32, (tok_rows, reach), 1)
        allowed = (key_place <= query_place) | (key_place < prefix_end)
        query_grads = []
        for head in range(heads):
            own = slice(head * HEAD_WIDTH, (head + 1) * HEAD_WIDTH)
            low = head // group * HEAD_WIDTH
            shared = slice(low, low + HEAD_WIDTH)
            query = qkv[block, own]
            key = qkv[:reach, q_cols + low : q_cols + low + HEAD_WIDTH]
            value = qkv[:reach, q_cols + kv_cols + low : q_cols + kv_cols + low + HEAD_WIDTH]
            grad = attended_grad_all[number, :, own]
            scores = matmul(query, key, ROWS_BY_ROWS) * SCORE_SCALE
            prob = jnp.where(allowed, jnp.exp(scores - log_total[block, head : head + 1]), 0.0)
            delta = jnp.sum(grad.astype(jnp.float32) * attended[block, own], -1, keepdims=True)
            prob_part = matmul(grad, value, ROWS_BY_ROWS)
            score_grad = (prob * (prob_part - delta)).astype(jnp.bfloat16)
            value_sum[:reach, shared] = value_sum[:reach, shared] + matmul(
                prob.astype(jnp.bfloat16), grad, COLS_BY_COLS
            )
            key_sum[:reach, shared] = key_sum[:reach, shared] + matmul(score_grad, query, COLS_BY_COLS)
            query_grads.append(matmul(score_grad, key, ROWS_BY_COLS))
        query_grad = jnp.concatenate(query_grads, 1) * SCORE_SCALE
        joined_grad[block, :q_cols] = spin(query_grad, cosine[block, :], -sine_table[block, :]).astype(
            jnp.bfloat16
        )

    for number in range(lines):
        attend_back(number)
        if number == 1:
            folds[2].turn()
            mix_swap.step(1)
    folds[1].finish()
    expert_swaps[1].start()
    out_fold.chips()
    joined_grad[:, q_cols : q_cols + kv_cols] = spin(
        key_sum[...] * SCORE_SCALE, cosine[...], -sine_table[...]
    ).astype(jnp.bfloat16)
    joined_grad[:, q_cols + kv_cols :] = value_sum[...].astype(jnp.bfloat16)
    gain_term = jnp.zeros((width, LANES), jnp.float32)
    for number in range(lines):
        block = pl.ds(number * tok_rows, tok_rows)
        hidden = tokens_all[number].astype(jnp.float32)
        normed = hidden * inverse_rms(hidden)
        part = matmul(joined_grad[block, :], weights[:, :qkv_cols], ROWS_BY_ROWS)
        part_grad[number] = part.astype(jnp.bfloat16)
        gain_term = gain_term + split_sum_columns(part * normed)
    for hops in range(lines - 1, 0, -1):
        part_swap.launch(hops)
    q_terms[..., :qkv_cols] = (
        matmul(att_in[...], joined_grad[...], COLS_BY_COLS).astype(jnp.bfloat16).reshape(*five, qkv_cols)
    )
    q_terms[..., qkv_cols:] = gain_term.astype(jnp.bfloat16).reshape(*five, LANES)
    qkv_fold.start()
    for hops in range(lines - 2, 1, -1):
        part_swap.step(hops)
    folds[3].turn()
    qkv_fold.chips()
    folds[2].finish()
    expert_swaps[2].start()
    part_swap.step(1)
    out_fold.turn()
    folds[3].finish()
    expert_swaps[3].start()
    mix_swap.finish(mix_total)
    mixed[...] = (mix_total[...] + middle[...]).astype(jnp.bfloat16)
    store(mixed, mixed_o)
    out_fold.finish()
    out_swap.start()
    qkv_fold.turn()
    qkv_fold.finish()
    qkv_swap.start()

    part_swap.finish(mix_total)
    hidden = tokens_all[here.z].astype(jnp.float32)
    inverse = inverse_rms(hidden)
    normed = hidden * inverse
    scaled = mix_total[...] * gain_attention
    mix_total[...] = grad_res[...] + inverse * (
        scaled - normed * jnp.mean(scaled * normed, -1, keepdims=True)
    )
    store(mix_total, tokens_grad_o)
    out_swap.finish()
    total = o_terms[here.chip, here.core, here.z].astype(jnp.float32)
    for k in range(lines - 1):
        total = total + o_lines[k].astype(jnp.float32)
    out_s[...] = total[:, :query_width]
    tail = padded_square(total[:, query_width:])
    router_s[...] = tail[:EXPERT_COUNT, :depth]
    expert_gain_s[...] = tail[EXPERT_COUNT : EXPERT_COUNT + 1, :depth]
    store(out_s, out_o)
    store(router_s, router_o)
    store(expert_gain_s, expert_gain_o)
    q_lines[here.z] = q_terms[here.chip, here.core, here.z]
    qkv_swap.finish()
    gain_columns = jnp.zeros((depth, LANES), jnp.float32)
    for line in range(lines):
        query_s[:, line * q_cols : (line + 1) * q_cols] = q_lines[line, :, :q_cols].astype(jnp.float32)
        key_s[:, line * kv_cols : (line + 1) * kv_cols] = q_lines[line, :, q_cols : q_cols + kv_cols].astype(
            jnp.float32
        )
        value_s[:, line * kv_cols : (line + 1) * kv_cols] = q_lines[line, :, q_cols + kv_cols : qkv_cols].astype(
            jnp.float32
        )
        gain_columns = gain_columns + q_lines[line, :, qkv_cols:].astype(jnp.float32)
    attention_gain_s[...] = padded_square(gain_columns)[:1, :depth]
    store(query_s, query_o)
    store(key_s, key_o)
    store(value_s, value_o)
    store(attention_gain_s, attention_gain_o)
    for e in range(own_experts):
        expert_rows[here.z, e] = terms[e, here.chip, here.core, here.z]
        expert_swaps[e].finish()
    store(expert_rows, expert_o)
    for group_of in (
        [gate_swap, attended_swap, part_swap, mix_swap, out_swap, qkv_swap, out_fold, qkv_fold] + folds + expert_swaps
    ):
        group_of.close()
    for copy in stores:
        copy.wait()


def deliver_kernel(*refs):
    count = (len(refs) - 4) // 3
    sources, targets, held = refs[:count], refs[count : 2 * count + 1], refs[2 * count + 1 : 3 * count + 1]
    gate_up, down, sems = refs[3 * count + 1 :]
    loads = [move(sources[n], held[n], sems.at[0, n]) for n in reversed(range(count))][::-1]
    stores = []
    depth, expert_count = gate_up.shape[:2]
    order = row_order(depth, expert_count, False)
    loads[count - 1].wait()
    rows = held[count - 1][...].reshape(expert_count * depth, gate_up.shape[2] + down.shape[2])
    gate_up[...] = matmul(order, rows[:, : gate_up.shape[2]], ROWS_BY_COLS).reshape(gate_up.shape)
    stores.append(move(gate_up, targets[count - 1], sems.at[1, count - 1]))
    down[...] = matmul(order, rows[:, gate_up.shape[2] :], ROWS_BY_COLS).reshape(down.shape)
    stores.append(move(down, targets[count], sems.at[1, count]))
    for n in range(count - 1):
        loads[n].wait()
        stores.append(move(held[n], targets[n], sems.at[1, n]))
    for copy in stores:
        copy.wait()


def fast_device(
    tokens, prefix_len, routes, cotangent, query_matrix, key_matrix, value_matrix, output_matrix,
    attention_gain, expert_gain, router_matrix, gate_up_weight, down_weight,
):
    lines = lax.axis_size("seq")
    chips = lax.axis_size("dp") // 2
    tok_rows, width = tokens.shape[1:]
    rows_all = lines * tok_rows
    depth = query_matrix.shape[0]
    query_width, key_width = query_matrix.shape[1], key_matrix.shape[1]
    q_cols, kv_cols = query_width // lines, key_width // lines
    qkv_cols = q_cols + 2 * kv_cols
    expert_count = router_matrix.shape[1]
    own_experts = expert_count // lines
    ff_width = down_weight.shape[2]
    all_ff = 3 * ff_width
    row_cols = qkv_cols + LANES
    out_cols = query_width + LANES
    half_dim = HEAD_WIDTH // 2
    low, full = jnp.bfloat16, jnp.float32

    places = np.arange(rows_all, dtype=np.float32)
    frequency = np.exp(
        np.arange(half_dim, dtype=np.float32) * np.float32(-2.0 * math.log(10000.0) / HEAD_WIDTH)
    ).astype(np.float32)
    angles = places[:, None] * frequency[None, :]
    cosine = jnp.asarray(np.tile(np.cos(angles), (1, LANES // half_dim)), jnp.float32)
    sine_table = jnp.asarray(np.tile(np.sin(angles), (1, LANES // half_dim)), jnp.float32)

    count = spread_count(lines)

    def scratch(*dims, kind=low):
        return pltpu.VMEM(dims, kind)

    def pair(*dims):
        return [pltpu.SemaphoreType.DMA(dims)] * 2

    DMA = pltpu.SemaphoreType.DMA
    by_token = (lines, tok_rows)
    five = (chips, 2, lines, depth)
    four = (chips, lines, depth)
    landed = (2, 2, lines // 2, depth)
    last = (2, lines // 2, depth)
    ends = [
        ((tok_rows, width), low), ((tok_rows, width), full), ((depth, query_width), full), ((depth, key_width), full),
        ((depth, key_width), full), ((depth, query_width), full), ((1, depth), full), ((1, depth), full), ((expert_count, depth), full),
        ((lines, own_experts, depth, all_ff), low),
    ]

    def fold_scratch(cols):
        return [scratch(*dims, cols) for dims in (five, four, landed, last)]

    results = pl.pallas_call(
        layer_kernel,
        name="layer",
        out_shape=tuple(jax.ShapeDtypeStruct(dims, kind) for dims, kind in ends),
        in_specs=[SMEM_SPEC, ANY_SPEC] + [VMEM_SPEC] * 3 + [ANY_SPEC] + [VMEM_SPEC] * 3 + [ANY_SPEC] * 3 + [VMEM_SPEC] * 3,
        out_specs=(ANY_SPEC,) * len(ends),
        scratch_shapes=[
            scratch(LANES, LANES, kind=full), scratch(lines, depth, row_cols), scratch(lines, own_experts, depth, all_ff),
            scratch(*by_token, width), scratch(width, row_cols), scratch(width, query_width), scratch(own_experts, *five, all_ff),
            scratch(*by_token, width), scratch(lines, expert_count, tok_rows), scratch(rows_all, width), scratch(rows_all, qkv_cols),
            scratch(rows_all, q_cols, kind=full), scratch(lines, rows_all, q_cols), scratch(rows_all, LANES, kind=full),
            scratch(*by_token, width), scratch(*by_token, LANES, kind=full), scratch(tok_rows, width, kind=full),
            scratch(own_experts, rows_all, 2 * ff_width), scratch(own_experts, rows_all, ff_width), scratch(own_experts, *four, all_ff),
            scratch(*by_token, width), scratch(2, lines - 1, tok_rows, width), scratch(tok_rows, width, kind=full), scratch(tok_rows, width),
            scratch(*by_token, width), scratch(2, lines - 1, tok_rows, width),
            scratch(lines, expert_count, tok_rows, kind=full), scratch(lines - 1, expert_count, tok_rows, kind=full),
            scratch(tok_rows, width, kind=full), scratch(*by_token, q_cols), scratch(*by_token, q_cols), scratch(rows_all, qkv_cols),
            scratch(rows_all, kv_cols, kind=full), scratch(rows_all, kv_cols, kind=full),
            scratch(own_experts, *landed, all_ff), scratch(own_experts, *last, all_ff),
            *fold_scratch(out_cols), scratch(lines - 1, depth, out_cols),
            *fold_scratch(row_cols), scratch(lines, depth, row_cols),
            *[scratch(*dims, kind=kind) for dims, kind in ends[2:-1]],
            DMA((6 + own_experts,)),
            *pair(count), *pair(count), *pair(own_experts, count), *pair(2, 2, lines - 1), *pair(2, 2, lines - 1), *pair(lines),
            *pair(lines, 2, lines - 1), *pair(2, 2, lines - 1), *pair(2, 2, lines - 1), *pair(lines), *pair(lines), *pair(2, 2, lines - 1),
            *pair(own_experts, 7), *pair(7), *pair(7), *pair(own_experts, lines), *pair(lines), *pair(lines),
            pltpu.SemaphoreType.REGULAR((own_experts,)), DMA((len(ends),)),
        ],
        compiler_params=comm_params(1, 63),
    )(
        prefix_len, tokens[0], query_matrix, key_matrix, value_matrix, output_matrix, router_matrix.T,
        attention_gain.reshape(1, depth), expert_gain.reshape(1, depth), gate_up_weight.reshape(*four, 2 * ff_width),
        down_weight.reshape(*four, ff_width), cotangent[0], routes[0].T, cosine, sine_table,
    )
    last_ends = [((depth, expert_count, 2 * ff_width), full), ((depth, expert_count, ff_width), full)]
    results = pl.pallas_call(
        deliver_kernel,
        name="deliver",
        out_shape=tuple(jax.ShapeDtypeStruct(dims, kind) for dims, kind in ends[:-1] + last_ends),
        in_specs=[ANY_SPEC] * len(ends),
        out_specs=(ANY_SPEC,) * (len(ends) + 1),
        scratch_shapes=[pltpu.VMEM(dims, kind) for dims, kind in ends + last_ends] + [DMA((2, len(ends) + 1))],
        compiler_params=pltpu.CompilerParams(vmem_limit_bytes=63 << 20),
    )(*results)
    mixed, tokens_grad, query_grad, key_grad, value_grad, out_grad, attention_gain_grad, expert_gain_grad, router_grad, gate_up_grad, down_grad = results
    return (
        mixed[None],
        tokens_grad[None],
        query_grad,
        key_grad,
        value_grad,
        out_grad,
        attention_gain_grad.reshape(depth),
        expert_gain_grad.reshape(depth),
        router_grad.T,
        gate_up_grad,
        down_grad,
    )


def solution(mesh):
    lines, chips = mesh.shape["seq"], mesh.shape["dp"] // 2
    even = KEY_HEADS % (2 * lines) == 0 and EXPERT_COUNT % lines == 0 and chips == lines == 4
    return jax.shard_map(
        fast_device if even else per_device,
        mesh=mesh,
        in_specs=(
            P("dp", "seq", None),
            P("dp"),
            P("dp", "seq", None),
            P("dp", "seq", None),
            P(("dp", "seq"), None),
            P(("dp", "seq"), None),
            P(("dp", "seq"), None),
            P(("dp", "seq"), None),
            P(("dp", "seq")),
            P(("dp", "seq")),
            P(("dp", "seq"), None),
            P(("dp", "seq"), None, None),
            P(("dp", "seq"), None, None),
        ),
        out_specs=(
            P("dp", "seq", None),
            P("dp", "seq", None),
            P(("dp", "seq"), None),
            P(("dp", "seq"), None),
            P(("dp", "seq"), None),
            P(("dp", "seq"), None),
            P(("dp", "seq")),
            P(("dp", "seq")),
            P(("dp", "seq"), None),
            P(("dp", "seq"), None, None),
            P(("dp", "seq"), None, None),
        ),
        check_vma=False,
    )
```

```python
import math

import jax
import jax.numpy as jnp
import numpy as np
from jax import lax
from jax.experimental import pallas as pl
from jax.experimental.pallas import tpu as pltpu
from jax.sharding import PartitionSpec as P

HEAD_WIDTH = 64
CAPACITY = 96


NORM_EPS = 1e-06
LOW_SCORE = -1e30
LANES = 128
HALF = HEAD_WIDTH // 2
SCORE_SCALE = HEAD_WIDTH ** (-0.5)
EXPERT_COUNT = 16
KEY_HEADS = 8
MESH = pl.DeviceIdType.MESH


def rotary_tables(positions, head_dim):
    half_dim = head_dim // 2
    frequency = jnp.exp(
        jnp.arange(half_dim, dtype=jnp.float32) * (-2.0 * math.log(10000.0) / head_dim)
    )
    angles = positions.astype(jnp.float32)[:, None] * frequency[None, :]
    return (jnp.cos(angles), jnp.sin(angles))


def rotate(value_rows, cosine, sine_table):
    half_dim = value_rows.shape[-1] // 2
    first_half = value_rows[..., :half_dim]
    second = value_rows[..., half_dim:]
    cos_heads = cosine[:, None, :]
    sin_heads = sine_table[:, None, :]
    return jnp.concatenate(
        [first_half * cos_heads - second * sin_heads, second * cos_heads + first_half * sin_heads],
        axis=-1,
    )


def norm_back(grad_normed, normed, inverse):
    return inverse * (grad_normed - normed * jnp.mean(grad_normed * normed, -1, keepdims=True))


def keep_state(running):
    return running


def swiglu(mid_linear, ff_width):
    return (jax.nn.silu(mid_linear[..., :ff_width]) * mid_linear[..., ff_width:]).astype(
        jnp.bfloat16
    )


def swiglu_back(act_grad, mid_linear, ff_width):
    gate_part = mid_linear[..., :ff_width]
    up_part = mid_linear[..., ff_width:]
    sigmoid = jax.nn.sigmoid(gate_part)
    gate_slope = sigmoid * (1.0 + gate_part * (1.0 - sigmoid))
    return jnp.concatenate(
        [act_grad * up_part * gate_slope, act_grad * gate_part * sigmoid], axis=-1
    ).astype(jnp.bfloat16)


def over_key_blocks(pieces, block_fn, running):
    piece_rows = pieces[0].shape[0]
    block_size = math.gcd(piece_rows, 512)
    shaped = tuple(
        (piece.reshape(piece_rows // block_size, block_size, piece.shape[1]) for piece in pieces)
    )
    offsets = block_size * jnp.arange(piece_rows // block_size, dtype=jnp.int32)

    def advance(carried, block_item):
        return (block_fn(carried, block_item[0], block_item[1], block_item[2]), None)

    result_state, unused = lax.scan(advance, running, (shaped[0], shaped[1], offsets))
    return result_state


def per_device(
    tokens,
    prefix_len,
    routes,
    cotangent,
    query_matrix,
    key_matrix,
    value_matrix,
    output_matrix,
    attention_gain,
    expert_gain,
    router_matrix,
    gate_up_weight,
    down_weight,
):
    hidden = tokens[0].astype(jnp.float32)
    tok_rows, model_width = hidden.shape
    params = (
        lax.all_gather(query_matrix, ("dp", "seq"), axis=0, tiled=True),
        lax.all_gather(key_matrix, ("dp", "seq"), axis=0, tiled=True),
        lax.all_gather(value_matrix, ("dp", "seq"), axis=0, tiled=True),
        lax.all_gather(output_matrix, ("dp", "seq"), axis=0, tiled=True),
        lax.all_gather(attention_gain, ("dp", "seq"), axis=0, tiled=True),
        lax.all_gather(expert_gain, ("dp", "seq"), axis=0, tiled=True),
        lax.all_gather(router_matrix, ("dp", "seq"), axis=0, tiled=True),
    )
    query_full, key_full, value_full, output_full, gain_attention, gain_expert, router_full = params
    head_dim = HEAD_WIDTH
    query_width = query_full.shape[1]
    key_width = key_full.shape[1]
    query_heads = query_width // head_dim
    key_groups = key_width // head_dim
    head_group = query_heads // key_groups
    score_scale = head_dim ** (-0.5)
    first_place = lax.axis_index("seq") * tok_rows
    positions = first_place + jnp.arange(tok_rows, dtype=jnp.int32)
    last_place = first_place + tok_rows - 1
    prefix_end = prefix_len[0]
    cosine, sine_table = rotary_tables(positions, head_dim)
    inverse_attention = lax.rsqrt(jnp.mean(hidden * hidden, -1, keepdims=True) + NORM_EPS)
    normed_attention = hidden * inverse_attention
    attention_input = (normed_attention * gain_attention.astype(jnp.float32)).astype(jnp.bfloat16)
    query_projected = jnp.dot(
        attention_input, query_full, preferred_element_type=jnp.float32
    ).reshape(tok_rows, query_heads, head_dim)
    queries = (
        rotate(query_projected, cosine, sine_table)
        .astype(jnp.bfloat16)
        .reshape(tok_rows, key_groups, head_group, head_dim)
    )
    key_projected = jnp.dot(attention_input, key_full, preferred_element_type=jnp.float32).reshape(
        tok_rows, key_groups, head_dim
    )
    keys_local = (
        rotate(key_projected, cosine, sine_table).astype(jnp.bfloat16).reshape(tok_rows, key_width)
    )
    values_local = jnp.dot(attention_input, value_full, preferred_element_type=jnp.float32).astype(
        jnp.bfloat16
    )

    def block_scores(key_block, key_start):
        block_size = key_block.shape[0]
        key_heads = key_block.reshape(block_size, key_groups, head_dim)
        key_places = key_start + jnp.arange(block_size, dtype=jnp.int32)
        allowed = (key_places[None, :] <= positions[:, None]) | (key_places[None, :] < prefix_end)
        scores = (
            jnp.einsum("qhgd,khd->hgqk", queries, key_heads, preferred_element_type=jnp.float32)
            * score_scale
        )
        return (jnp.where(allowed, scores, -jnp.inf), key_heads)

    def attend(running, key_block, value_block, key_start):

        def compute(carried):
            run_max, run_sum, weighted = carried
            scores, key_heads = block_scores(key_block, key_start)
            value_heads = value_block.reshape(key_block.shape[0], key_groups, head_dim)
            new_max = jnp.maximum(run_max, jnp.max(scores, -1))
            weights = jnp.exp(scores - new_max[..., None])
            factor = jnp.exp(run_max - new_max)
            new_sum = run_sum * factor + jnp.sum(weights, -1)
            new_weighted = weighted * factor[..., None] + jnp.einsum(
                "hgqk,khd->hgqd",
                weights.astype(jnp.bfloat16),
                value_heads,
                preferred_element_type=jnp.float32,
            )
            return (new_max, new_sum, new_weighted)

        visible = (key_start <= last_place) | (key_start < prefix_end)
        return lax.cond(visible, compute, keep_state, running)

    stat_shape = (key_groups, head_group, tok_rows)
    start_state = (
        jnp.full(stat_shape, LOW_SCORE, jnp.float32),
        jnp.zeros(stat_shape, jnp.float32),
        jnp.zeros(stat_shape + (head_dim,), jnp.float32),
    )
    run_max, run_sum, weighted = over_key_blocks(
        (
            lax.all_gather(keys_local, "seq", axis=0, tiled=True),
            lax.all_gather(values_local, "seq", axis=0, tiled=True),
        ),
        attend,
        start_state,
    )
    log_total = run_max + jnp.log(run_sum)
    attended_heads = weighted / run_sum[..., None]
    attention_lowered = (
        attended_heads.transpose(2, 0, 1, 3).reshape(tok_rows, query_width).astype(jnp.bfloat16)
    )
    branch_output = jnp.einsum(
        "tc,dc->td", attention_lowered, output_full, preferred_element_type=jnp.float32
    )
    middle = hidden + branch_output
    inverse_expert = lax.rsqrt(jnp.mean(middle * middle, -1, keepdims=True) + NORM_EPS)
    normed_expert = middle * inverse_expert
    expert_input = (normed_expert * gain_expert.astype(jnp.float32)).astype(jnp.bfloat16)
    router_logits = jnp.dot(expert_input, router_full, preferred_element_type=jnp.float32)
    router_probs = jax.nn.softmax(router_logits, axis=-1)
    expert_count = router_full.shape[1]
    route_ids = routes[0]
    expert_range = jnp.arange(expert_count, dtype=jnp.int32)
    route_hits = jnp.sum(
        (route_ids[:, :, None] == expert_range[None, None, :]).astype(jnp.int32), 1
    )
    slot_rank = jnp.cumsum(route_hits, 0) - 1
    slot_target = jnp.where(route_hits > 0, slot_rank, CAPACITY)
    token_index = jnp.broadcast_to(
        jnp.arange(tok_rows, dtype=jnp.int32)[:, None], (tok_rows, expert_count)
    )
    expert_index = jnp.broadcast_to(expert_range[None, :], (tok_rows, expert_count))
    slot_table = (
        jnp.zeros((expert_count, CAPACITY), jnp.int32)
        .at[expert_index, slot_target]
        .set(token_index, mode="drop")
    )
    slot_live = jnp.arange(CAPACITY, dtype=jnp.int32)[None, :] < jnp.sum(route_hits, 0)[:, None]
    expert_column = expert_range[:, None]
    dispatched = expert_input[slot_table]
    slot_gates = jnp.where(slot_live, router_probs[slot_table, expert_column], 0.0)
    ff_width = down_weight.shape[2]
    grad_mid = cotangent[0].astype(jnp.float32)
    slot_grad = grad_mid[slot_table]
    out_grad = (slot_gates[..., None] * slot_grad).astype(jnp.bfloat16)
    gate_up_full, down_full = (
        lax.all_gather(gate_up_weight, ("dp", "seq"), axis=0, tiled=True),
        lax.all_gather(down_weight, ("dp", "seq"), axis=0, tiled=True),
    )
    mid_linear = jnp.einsum(
        "ecd,def->ecf", dispatched, gate_up_full, preferred_element_type=jnp.float32
    )
    activation = swiglu(mid_linear, ff_width)
    expert_out = jnp.einsum(
        "ecf,def->ecd", activation, down_full, preferred_element_type=jnp.float32
    )
    flat_slots = slot_table.reshape(-1)
    combined = (
        jnp.zeros((tok_rows, model_width), jnp.float32)
        .at[flat_slots]
        .add((slot_gates[..., None] * expert_out).reshape(-1, model_width))
    )
    mixed = (middle + combined).astype(jnp.bfloat16)
    gate_grad = jnp.where(slot_live, jnp.sum(expert_out * slot_grad, -1), 0.0)
    act_grad = jnp.einsum("ecd,def->ecf", out_grad, down_full, preferred_element_type=jnp.float32)
    mid_grad = swiglu_back(act_grad, mid_linear, ff_width)
    gate_up_term = jnp.einsum(
        "ecd,ecf->def", dispatched, mid_grad, preferred_element_type=jnp.float32
    )
    down_term = jnp.einsum("ecd,ecf->def", out_grad, activation, preferred_element_type=jnp.float32)
    summed_terms = lax.psum_scatter(
        jnp.concatenate([gate_up_term, down_term], axis=-1),
        ("dp", "seq"),
        scatter_dimension=0,
        tiled=True,
    )
    gate_up_weight_grad = summed_terms[..., : 2 * ff_width]
    down_weight_grad = summed_terms[..., 2 * ff_width :]
    dispatched_grad = jnp.einsum(
        "ecf,def->ecd", mid_grad, gate_up_full, preferred_element_type=jnp.float32
    )
    expert_in_grad = (
        jnp.zeros((tok_rows, model_width), jnp.float32)
        .at[flat_slots]
        .add(dispatched_grad.reshape(-1, model_width))
    )
    prob_grad = (
        jnp.zeros((tok_rows, expert_count), jnp.float32)
        .at[slot_table, expert_column]
        .add(gate_grad)
    )
    logit_grad = (
        router_probs * (prob_grad - jnp.sum(router_probs * prob_grad, -1, keepdims=True))
    ).astype(jnp.bfloat16)
    router_term = jnp.einsum(
        "td,te->de", expert_input, logit_grad, preferred_element_type=jnp.float32
    )
    expert_in_grad = expert_in_grad + jnp.einsum(
        "te,de->td", logit_grad, router_full, preferred_element_type=jnp.float32
    )
    expert_gain_term = jnp.sum(expert_in_grad * normed_expert, 0)
    grad_res = grad_mid + norm_back(
        expert_in_grad * gain_expert.astype(jnp.float32), normed_expert, inverse_expert
    )
    branch_grad = grad_res.astype(jnp.bfloat16)
    output_term = jnp.einsum(
        "td,tc->dc", branch_grad, attention_lowered, preferred_element_type=jnp.float32
    )
    attended_grad = jnp.dot(branch_grad, output_full, preferred_element_type=jnp.float32).astype(
        jnp.bfloat16
    )
    attended_grad_heads = attended_grad.reshape(
        tok_rows, key_groups, head_group, head_dim
    ).transpose(1, 2, 0, 3)
    delta = jnp.sum(attended_grad_heads.astype(jnp.float32) * attended_heads, -1)
    seq_total = tok_rows * lax.axis_size("seq")

    def attend_back(running, key_block, value_block, key_start):

        def compute(carried):
            query_sum, key_sum, value_sum = carried
            block_size = key_block.shape[0]
            scores, key_heads = block_scores(key_block, key_start)
            value_heads = value_block.reshape(block_size, key_groups, head_dim)
            probs_full = jnp.exp(scores - log_total[..., None])
            probs_low = probs_full.astype(jnp.bfloat16)
            value_piece = jnp.einsum(
                "hgqk,hgqd->khd", probs_low, attended_grad_heads, preferred_element_type=jnp.float32
            ).reshape(block_size, key_width)
            prob_part = jnp.einsum(
                "hgqd,khd->hgqk",
                attended_grad_heads,
                value_heads,
                preferred_element_type=jnp.float32,
            )
            score_grad = (probs_full * (prob_part - delta[..., None])).astype(jnp.bfloat16)
            query_sum = (
                query_sum
                + jnp.einsum(
                    "hgqk,khd->hgqd", score_grad, key_heads, preferred_element_type=jnp.float32
                )
                * score_scale
            )
            key_piece = (
                jnp.einsum(
                    "hgqk,qhgd->khd", score_grad, queries, preferred_element_type=jnp.float32
                )
                * score_scale
            ).reshape(block_size, key_width)
            key_sum = lax.dynamic_update_slice_in_dim(
                key_sum,
                lax.dynamic_slice_in_dim(key_sum, key_start, block_size, 0) + key_piece,
                key_start,
                0,
            )
            value_sum = lax.dynamic_update_slice_in_dim(
                value_sum,
                lax.dynamic_slice_in_dim(value_sum, key_start, block_size, 0) + value_piece,
                key_start,
                0,
            )
            return (query_sum, key_sum, value_sum)

        visible = (key_start <= last_place) | (key_start < prefix_end)
        return lax.cond(visible, compute, keep_state, running)

    back_start = (
        jnp.zeros(stat_shape + (head_dim,), jnp.float32),
        jnp.zeros((seq_total, key_width), jnp.float32),
        jnp.zeros((seq_total, key_width), jnp.float32),
    )
    query_sum, key_sum, value_sum = over_key_blocks(
        (
            lax.all_gather(keys_local, "seq", axis=0, tiled=True),
            lax.all_gather(values_local, "seq", axis=0, tiled=True),
        ),
        attend_back,
        back_start,
    )
    key_part, value_part = (
        lax.psum_scatter(
            key_sum.astype(jnp.bfloat16), "seq", scatter_dimension=0, tiled=True
        ).astype(jnp.float32),
        lax.psum_scatter(
            value_sum.astype(jnp.bfloat16), "seq", scatter_dimension=0, tiled=True
        ).astype(jnp.float32),
    )
    query_rows = query_sum.transpose(2, 0, 1, 3).reshape(tok_rows, query_heads, head_dim)
    query_grad = (
        rotate(query_rows, cosine, -sine_table).reshape(tok_rows, query_width).astype(jnp.bfloat16)
    )
    key_grad = (
        rotate(key_part.reshape(tok_rows, key_groups, head_dim), cosine, -sine_table)
        .reshape(tok_rows, key_width)
        .astype(jnp.bfloat16)
    )
    value_grad = value_part.astype(jnp.bfloat16)
    query_term = jnp.einsum(
        "td,tc->dc", attention_input, query_grad, preferred_element_type=jnp.float32
    )
    key_term = jnp.einsum(
        "td,tc->dc", attention_input, key_grad, preferred_element_type=jnp.float32
    )
    value_term = jnp.einsum(
        "td,tc->dc", attention_input, value_grad, preferred_element_type=jnp.float32
    )
    attention_in_grad = jnp.einsum(
        "tc,dc->td", query_grad, query_full, preferred_element_type=jnp.float32
    )
    attention_in_grad = attention_in_grad + jnp.einsum(
        "tc,dc->td", key_grad, key_full, preferred_element_type=jnp.float32
    )
    attention_in_grad = attention_in_grad + jnp.einsum(
        "tc,dc->td", value_grad, value_full, preferred_element_type=jnp.float32
    )
    attention_gain_term = jnp.sum(attention_in_grad * normed_attention, 0)
    tokens_grad = grad_res + norm_back(
        attention_in_grad * gain_attention.astype(jnp.float32), normed_attention, inverse_attention
    )
    summed_grads = (
        lax.psum_scatter(query_term, ("dp", "seq"), scatter_dimension=0, tiled=True),
        lax.psum_scatter(key_term, ("dp", "seq"), scatter_dimension=0, tiled=True),
        lax.psum_scatter(value_term, ("dp", "seq"), scatter_dimension=0, tiled=True),
        lax.psum_scatter(output_term, ("dp", "seq"), scatter_dimension=0, tiled=True),
        lax.psum_scatter(attention_gain_term, ("dp", "seq"), scatter_dimension=0, tiled=True),
        lax.psum_scatter(expert_gain_term, ("dp", "seq"), scatter_dimension=0, tiled=True),
        lax.psum_scatter(router_term, ("dp", "seq"), scatter_dimension=0, tiled=True),
    )
    return (
        mixed[None],
        tokens_grad[None],
        summed_grads[0],
        summed_grads[1],
        summed_grads[2],
        summed_grads[3],
        summed_grads[4],
        summed_grads[5],
        summed_grads[6],
        gate_up_weight_grad,
        down_weight_grad,
    )


def matmul(left, right, contract):
    return lax.dot_general(
        left, right, (contract, ((), ())), preferred_element_type=jnp.float32
    )


ROWS_BY_COLS = ((1,), (0,))
ROWS_BY_ROWS = ((1,), (1,))
COLS_BY_COLS = ((0,), (0,))


def split_sum_columns(terms):
    ones = jnp.ones((terms.shape[0], LANES), jnp.bfloat16)
    high = terms.astype(jnp.bfloat16)
    low = (terms - high.astype(jnp.float32)).astype(jnp.bfloat16)
    return matmul(high, ones, COLS_BY_COLS) + matmul(low, ones, COLS_BY_COLS)


def turned(value_rows):
    width = value_rows.shape[1]
    lane = lax.broadcasted_iota(jnp.int32, value_rows.shape, 1)
    ahead = pltpu.roll(value_rows, width - HALF, 1)
    behind = pltpu.roll(value_rows, HALF, 1)
    return jnp.where(lane % HEAD_WIDTH < HALF, -ahead, behind)


def spin(value_rows, cosine, sine_table):
    repeats = value_rows.shape[1] // LANES
    cos_all = jnp.concatenate([cosine] * repeats, 1) if repeats > 1 else cosine
    sin_all = jnp.concatenate([sine_table] * repeats, 1) if repeats > 1 else sine_table
    return value_rows * cos_all + turned(value_rows) * sin_all


def inverse_rms(value_rows):
    return lax.rsqrt(jnp.mean(value_rows * value_rows, -1, keepdims=True) + NORM_EPS)


def shape_of(*dims, kind=jnp.bfloat16):
    return jax.ShapeDtypeStruct(dims, kind)


VMEM_SPEC = pl.BlockSpec(memory_space=pltpu.VMEM)
SMEM_SPEC = pl.BlockSpec(memory_space=pltpu.SMEM)
ANY_SPEC = pl.BlockSpec(memory_space=pl.ANY)


class Place:
    def __init__(self):
        self.dp = lax.axis_index("dp")
        self.z = lax.axis_index("seq")
        self.lines = lax.axis_size("seq")
        self.chips = lax.axis_size("dp") // 2
        self.chip = self.dp // 2
        self.core = self.dp % 2
        self.other = 1 - self.core
        self.chip_x = self.chip + 1 - 2 * (self.chip % 2)
        self.chip_y = (self.chip + 2) % 4
        self.chip_diag = 3 - self.chip

    def ahead(self, step):
        return (self.z + step) % self.lines

    def behind(self, step):
        return (self.z + self.lines - step) % self.lines

    def line_peer(self, step):
        return (self.dp, self.ahead(step))

    def on_chip(self, chip):
        return (chip * 2 + self.core, self.z)

    def sibling(self):
        return (self.chip * 2 + self.other, self.z)


def meet(peers):
    barrier = pltpu.get_barrier_semaphore()
    for peer in peers:
        pl.semaphore_signal(barrier, inc=1, device_id=peer, device_id_type=MESH)
    pl.semaphore_wait(barrier, len(peers))


def send(source, target, send_sem, recv_sem, peer):
    copy = pltpu.make_async_remote_copy(
        src_ref=source,
        dst_ref=target,
        send_sem=send_sem,
        recv_sem=recv_sem,
        device_id=peer,
        device_id_type=MESH,
    )
    copy.start()
    return copy


def move(source, target, sem):
    copy = pltpu.make_async_copy(source, target, sem)
    copy.start()
    return copy


def all_peers(here):
    return (
        [here.line_peer(k) for k in range(1, here.lines)]
        + [here.on_chip(chip) for chip in (here.chip_x, here.chip_y, here.chip_diag)]
        + [here.sibling()]
    )


def comm_params(ident, limit=56):
    return pltpu.CompilerParams(
        collective_id=ident, has_side_effects=True, vmem_limit_bytes=limit << 20
    )


class Spread:
    def __init__(self, here, pick, target, depth, local_sem, sends, recvs):
        self.here, self.pick, self.target, self.depth = here, pick, target, depth
        self.local_sem, self.sends, self.recvs = local_sem, sends, recvs
        self.used = 0

    def put(self, source, target, peer):
        copy = send(source, target, self.sends.at[self.used], self.recvs.at[self.used], peer)
        self.used += 1
        return copy

    def row(self):
        here = self.here
        if len(self.target.shape) > 2:
            return self.target.at[here.chip, here.core, here.z]
        first = (here.dp * here.lines + here.z) * self.depth
        return self.target.at[pl.ds(pl.multiple_of(first, self.depth), self.depth)]

    def chip_rows(self, chip, part=None):
        here = self.here
        if len(self.target.shape) > 2:
            if part is None:
                return self.target.at[chip, here.core]
            return self.target.at[chip, here.core, pl.ds(part * (here.lines // 2), here.lines // 2)]
        count = here.lines * self.depth
        first = (chip * 2 + here.core) * count
        if part is not None:
            first, count = first + part * (count // 2), count // 2
        return self.target.at[pl.ds(pl.multiple_of(first, count), count)]

    def start(self):
        here = self.here
        mine = self.row()
        self.own = move(self.pick(here.z), mine, self.local_sem)
        self.line = [
            self.put(self.pick(here.ahead(k)), mine, here.line_peer(k)) for k in range(1, here.lines)
        ]

    def chips(self):
        here = self.here
        self.own.wait()
        for copy in self.line:
            copy.wait_recv()
        mine = self.chip_rows(here.chip)
        self.plane = [
            self.put(mine, mine, here.on_chip(here.chip_x)),
            self.put(mine, mine, here.on_chip(here.chip_y)),
        ]
        self.across = [self.put(mine, mine, here.sibling())]

    def turn(self):
        here = self.here
        self.corner = []
        for copy, origin, onward, part in (
            (self.plane[0], here.chip_x, here.chip_y, 0),
            (self.plane[1], here.chip_y, here.chip_x, 1),
        ):
            copy.wait_recv()
            half = self.chip_rows(origin, part)
            self.corner.append(self.put(half, half, here.on_chip(onward)))
            block = self.chip_rows(origin)
            self.across.append(self.put(block, block, here.sibling()))

    def cores(self):
        here = self.here
        for copy in self.corner:
            copy.wait_recv()
        block = self.chip_rows(here.chip_diag)
        self.across.append(self.put(block, block, here.sibling()))

    def finish(self):
        for copy in self.across:
            copy.wait_recv()

    def close(self):
        for copy in self.line + self.plane + self.corner + self.across:
            copy.wait_send()


def spread_count(lines):
    return lines - 1 + 2 + 2 + 4


class LineGather:
    def __init__(self, here, view, sends, recvs, source=None):
        self.here, self.view, self.source = here, view, source
        self.sends, self.recvs = sends, recvs

    def copy(self, way, hop, block, source=None):
        here = self.here
        step = 1 if way == 0 else here.lines - 1
        return pltpu.make_async_remote_copy(
            src_ref=self.view(block) if source is None else source,
            dst_ref=self.view(block),
            send_sem=self.sends.at[way, hop - 1],
            recv_sem=self.recvs.at[way, hop - 1],
            device_id=here.line_peer(step),
            device_id_type=MESH,
        )

    def start(self):
        here = self.here

        @pl.when(here.z < here.lines - 1)
        def rightward():
            self.copy(0, 1, here.z, self.source).start()

        @pl.when(here.z > 0)
        def leftward():
            self.copy(1, 1, here.z, self.source).start()

    def step(self, hop):
        here = self.here
        lines = here.lines

        @pl.when(here.z >= hop)
        def from_left():
            block = here.behind(hop)
            self.copy(0, hop, block).wait_recv()
            if hop < lines - 1:

                @pl.when(here.z < lines - 1)
                def onward():
                    self.copy(0, hop + 1, block).start()

        @pl.when(here.z + hop < lines)
        def from_right():
            block = here.ahead(hop)
            self.copy(1, hop, block).wait_recv()
            if hop < lines - 1:

                @pl.when(here.z > 0)
                def onward():
                    self.copy(1, hop + 1, block).start()

    def close(self):
        here = self.here
        lines = here.lines
        for hop in range(1, lines):

            @pl.when((here.z >= hop - 1) & (here.z < lines - 1))
            def rightward():
                self.copy(0, hop, here.behind(hop - 1)).wait_send()

            @pl.when((here.z + hop - 1 < lines) & (here.z > 0))
            def leftward():
                self.copy(1, hop, here.ahead(hop - 1)).wait_send()


class LineSpread:
    def __init__(self, here, view, sends, recvs, source=None):
        self.here, self.view, self.source = here, view, source
        self.sends, self.recvs = sends, recvs

    def start(self):
        here = self.here
        mine = self.view(here.z)
        self.line = [
            send(
                mine if self.source is None else self.source, mine, self.sends.at[k - 1], self.recvs.at[k - 1], here.line_peer(k)
            )
            for k in range(1, here.lines)
        ]

    def arrived(self, step):
        self.line[step - 1].wait_recv()

    def finish(self):
        for copy in self.line:
            copy.wait_recv()

    def close(self):
        for copy in self.line:
            copy.wait_send()


class LineSum:
    def __init__(self, here, parts, landed, rows, sends, recvs):
        self.here, self.parts, self.landed, self.rows = here, parts, landed, rows
        self.sends, self.recvs = sends, recvs

    def copy(self, way, hops):
        here = self.here
        step = 1 if way == 0 else here.lines - 1
        block = here.ahead(hops) if way == 0 else here.behind(hops)
        return pltpu.make_async_remote_copy(
            src_ref=self.parts.at[block, self.rows],
            dst_ref=self.landed.at[way, hops - 1, self.rows],
            send_sem=self.sends.at[way, hops - 1],
            recv_sem=self.recvs.at[way, hops - 1],
            device_id=here.line_peer(step),
            device_id_type=MESH,
        )

    def launch(self, hops):
        here = self.here

        @pl.when(here.z == 0)
        def rightward():
            self.copy(0, hops).start()

        @pl.when(here.z == here.lines - 1)
        def leftward():
            self.copy(1, hops).start()

    def step(self, hops):
        here = self.here
        lines = here.lines

        def pass_on(way):
            block = here.ahead(hops) if way == 0 else here.behind(hops)
            self.copy(way, hops + 1).wait_recv()
            self.parts[block, self.rows] = (
                self.parts[block, self.rows].astype(jnp.float32)
                + self.landed[way, hops, self.rows].astype(jnp.float32)
            ).astype(self.parts.dtype)
            self.copy(way, hops).start()

        @pl.when((here.z > 0) & (here.z + hops < lines))
        def rightward():
            pass_on(0)

        @pl.when((here.z < lines - 1) & (here.z >= hops))
        def leftward():
            pass_on(1)

    def finish(self, total):
        here = self.here
        rows = self.rows
        total[rows, :] = self.parts[here.z, rows].astype(jnp.float32)

        @pl.when(here.z > 0)
        def from_left():
            self.copy(0, 1).wait_recv()
            total[rows, :] = total[rows, :] + self.landed[0, 0, rows].astype(jnp.float32)

        @pl.when(here.z < here.lines - 1)
        def from_right():
            self.copy(1, 1).wait_recv()
            total[rows, :] = total[rows, :] + self.landed[1, 0, rows].astype(jnp.float32)

    def close(self):
        here = self.here
        for hops in range(1, here.lines):

            @pl.when(here.z + hops < here.lines)
            def rightward():
                self.copy(0, hops).wait_send()

            @pl.when(here.z >= hops)
            def leftward():
                self.copy(1, hops).wait_send()


class Halves:
    def __init__(self, *members):
        self.members = members

    def start(self):
        for member in self.members:
            member.start()

    def launch(self, hops):
        for member in self.members:
            member.launch(hops)

    def step(self, hops):
        for member in self.members:
            member.step(hops)

    def finish(self, total):
        for member in self.members:
            member.finish(total)

    def close(self):
        for member in self.members:
            member.close()


class LineSwap:
    def __init__(self, here, pick, received, sends, recvs):
        self.here, self.pick, self.received = here, pick, received
        self.sends, self.recvs = sends, recvs

    def start(self):
        here = self.here
        self.line = [
            send(
                self.pick(here.ahead(k)), self.received(k, here.z), self.sends.at[k - 1], self.recvs.at[k - 1], here.line_peer(k)
            )
            for k in range(1, here.lines)
        ]

    def finish(self):
        for copy in self.line:
            copy.wait_recv()

    def close(self):
        for copy in self.line:
            copy.wait_send()


def padded_square(block):
    filler = jnp.zeros((LANES - block.shape[0], LANES), jnp.float32)
    return jnp.concatenate([block, filler], 0).T


def row_order(depth, experts, by_expert):
    count = depth * experts
    place = lax.broadcasted_iota(jnp.int32, (count, count), 0)
    source = lax.broadcasted_iota(jnp.int32, (count, count), 1)
    if by_expert:
        wanted = place % depth * experts + place // depth
    else:
        wanted = place % experts * depth + place // experts
    return (source == wanted).astype(jnp.bfloat16)


class Fold:
    def __init__(self, here, terms, crossed, landed, last, sends, recvs):
        self.here, self.terms, self.crossed = here, terms, crossed
        self.landed, self.last = landed, last
        self.sends, self.recvs = sends, recvs
        middle = here.lines // 2
        self.parts = [(0, middle), (middle, here.lines)]

    def start(self):
        here = self.here
        self.first = send(
            self.terms.at[:, here.other], self.crossed, self.sends.at[0], self.recvs.at[0], here.sibling()
        )

    def chips(self):
        here = self.here
        self.first.wait_recv()
        for chip in range(here.chips):
            self.terms[chip, here.core] = (
                self.terms[chip, here.core].astype(jnp.float32) + self.crossed[chip].astype(jnp.float32)
            ).astype(jnp.bfloat16)
        self.one, self.straight = [], []
        for number, near in enumerate((here.chip_x, here.chip_y)):
            low, high = self.parts[number]
            for slot, chip, group in ((1, here.chip_diag, self.one), (0, near, self.straight)):
                place = 1 + number * 2 + slot
                group.append(
                    send(
                        self.terms.at[chip, here.core, low:high], self.landed.at[number, slot],
                        self.sends.at[place], self.recvs.at[place], here.on_chip(near),
                    )
                )

    def turn(self):
        here = self.here
        self.two = []
        for number, onward in enumerate((here.chip_y, here.chip_x)):
            low, high = self.parts[number]
            self.one[number].wait_recv()
            self.terms[onward, here.core, low:high] = (
                self.terms[onward, here.core, low:high].astype(jnp.float32)
                + self.landed[number, 1].astype(jnp.float32)
            ).astype(jnp.bfloat16)
            place = 5 + number
            self.two.append(
                send(
                    self.terms.at[onward, here.core, low:high], self.last.at[number],
                    self.sends.at[place], self.recvs.at[place], here.on_chip(onward),
                )
            )

    def finish(self):
        here = self.here
        for number in range(2):
            low, high = self.parts[number]
            self.straight[number].wait_recv()
            self.two[number].wait_recv()
            self.terms[here.chip, here.core, low:high] = (
                self.terms[here.chip, here.core, low:high].astype(jnp.float32)
                + self.landed[number, 0].astype(jnp.float32)
                + self.last[number].astype(jnp.float32)
            ).astype(jnp.bfloat16)

    def sums(self, z):
        return self.terms.at[self.here.chip, self.here.core, z]

    def close(self):
        for copy in [self.first] + self.one + self.straight + self.two:
            copy.wait_send()


def layer_kernel(
    prefix, tokens, query_rows, key_rows, value_rows, out_rows, router_cols, attention_gain, expert_gain, gate_up_rows, down_rows,
    cotangent, routes, cosine, sine_table,
    mixed_o, tokens_grad_o, query_o, key_o, value_o, out_o, attention_gain_o, expert_gain_o, router_o, expert_o,
    square, rows, expert_rows, tokens_all, weights, out_full, terms, cot_all, chosen_all, att_in, qkv, attended, attended_all,
    log_total, expert_in, probs, middle, slopes, acts, mids, part_mix, got_mix, mix_total, mixed, part_grad, got_grad,
    gate_grad, got_gate, grad_res, attended_grad, attended_grad_all, joined_grad, key_sum, value_sum, e_landed, e_last,
    o_terms, o_crossed, o_landed, o_last, o_lines, q_terms, q_crossed, q_landed, q_last, q_lines,
    query_s, key_s, value_s, out_s, attention_gain_s, expert_gain_s, router_s,
    local_sem, r_sends, r_recvs, o_sends, o_recvs, e_sends, e_recvs, t_sends, t_recvs, c_sends, c_recvs, k_sends, k_recvs,
    a_sends, a_recvs, m_sends, m_recvs, x_sends, x_recvs, g_sends, g_recvs, b_sends, b_recvs, p_sends, p_recvs,
    f_sends, f_recvs, of_sends, of_recvs, q_sends, q_recvs, el_sends, el_recvs, ol_sends, ol_recvs, ql_sends, ql_recvs,
    free_sem, out_sem,
):
    here = Place()
    lines = here.lines
    tok_rows, width = tokens.shape
    rows_all = lines * tok_rows
    depth = rows.shape[1]
    own_experts = terms.shape[0]
    ff_width = terms.shape[5] // 3
    chips = here.chips
    five = (chips, 2, lines, depth)
    four = (chips, lines, depth)
    query_width = lines * (qkv.shape[1] // 2)
    qkv_cols = qkv.shape[1]
    kv_cols = qkv_cols // 4
    q_cols = 2 * kv_cols
    stores = []

    def store(source, target):
        stores.append(move(source, target, out_sem.at[len(stores)]))

    gate_up_load = move(gate_up_rows, mids.at[0, ..., : 2 * ff_width], local_sem.at[0])
    down_load = move(down_rows, mids.at[0, ..., 2 * ff_width :], local_sem.at[1])
    token_load = move(tokens, tokens_all.at[here.z], local_sem.at[2])
    cot_load = move(cotangent, cot_all.at[here.z], local_sem.at[3])

    square[...] = jnp.zeros_like(square)
    square[:EXPERT_COUNT, :depth] = router_cols[...].astype(jnp.float32)
    square[EXPERT_COUNT : EXPERT_COUNT + 1, :depth] = attention_gain[...].astype(jnp.float32)
    square[EXPERT_COUNT + 1 : EXPERT_COUNT + 2, :depth] = expert_gain[...].astype(jnp.float32)
    small = square[...].T[:depth, :].astype(jnp.bfloat16)
    for line in range(lines):
        rows[line, :, :q_cols] = query_rows[:, line * q_cols : (line + 1) * q_cols]
        rows[line, :, q_cols : q_cols + kv_cols] = key_rows[:, line * kv_cols : (line + 1) * kv_cols]
        rows[line, :, q_cols + kv_cols : qkv_cols] = value_rows[:, line * kv_cols : (line + 1) * kv_cols]
        rows[line, :, qkv_cols:] = small
    meet(all_peers(here))
    rows_spread = Spread(here, lambda z: rows.at[z], weights, depth, local_sem.at[4], r_sends, r_recvs)
    half = tok_rows // 2
    token_gathers = [
        LineGather(
            here, lambda z, n=n: tokens_all.at[z, pl.ds(n * half, half)], t_sends.at[n], t_recvs.at[n], tokens.at[pl.ds(n * half, half)]
        )
        for n in range(2)
    ]
    out_spread = Spread(here, lambda z: out_rows, out_full, depth, local_sem.at[5], o_sends, o_recvs)
    chosen_swap = LineSwap(
        here, lambda z: chosen_all.at[here.z], lambda k, z: chosen_all.at[z], k_sends, k_recvs
    )
    cot_gather = Halves(
        *[
            LineGather(
                here, lambda z, n=n: cot_all.at[z, pl.ds(n * half, half)], c_sends.at[n], c_recvs.at[n], cotangent.at[pl.ds(n * half, half)]
            )
            for n in range(2)
        ]
    )
    expert_spreads = [
        Spread(
            here,
            lambda z, e=e: expert_rows.at[z, e], terms.at[e], depth, local_sem.at[6 + e], e_sends.at[e], e_recvs.at[e],
        )
        for e in range(own_experts)
    ]
    rows_spread.start()
    gate_up_load.wait()
    down_load.wait()
    order = row_order(depth, EXPERT_COUNT, True)
    expert_rows[...] = (
        matmul(order, mids[0].reshape(depth * EXPERT_COUNT, 3 * ff_width), ROWS_BY_COLS)
        .astype(jnp.bfloat16)
        .reshape(expert_rows.shape)
    )
    expert_spreads[0].start()
    token_gathers[0].start()
    token_gathers[1].start()
    expert_id = lax.broadcasted_iota(jnp.int32, (EXPERT_COUNT, tok_rows), 0)
    chosen = jnp.zeros((EXPERT_COUNT, tok_rows), jnp.float32)
    for number in range(routes.shape[0]):
        chosen = chosen + (routes[number : number + 1, :] == expert_id).astype(jnp.float32)
    chosen_all[here.z] = chosen.astype(jnp.bfloat16)
    chosen_swap.start()
    rows_spread.chips()
    rows_spread.turn()
    rows_spread.cores()
    expert_spreads[0].chips()
    token_gathers[0].step(1)
    token_gathers[1].step(1)
    expert_spreads[1].start()
    rows_spread.finish()
    columns = weights[:, qkv_cols:].astype(jnp.float32).T
    gain_attention = columns[EXPERT_COUNT : EXPERT_COUNT + 1, :]
    gain_expert = columns[EXPERT_COUNT + 1 : EXPERT_COUNT + 2, :]

    def project(source):
        block = pl.ds(pl.multiple_of(source * tok_rows, tok_rows), tok_rows)
        hidden = tokens_all[source].astype(jnp.float32)
        normed = (hidden * inverse_rms(hidden) * gain_attention).astype(jnp.bfloat16)
        att_in[block, :] = normed
        linear = matmul(normed, weights[:, :qkv_cols], ROWS_BY_COLS)
        turned_part = linear[:, : q_cols + kv_cols]
        qkv[block, : q_cols + kv_cols] = spin(turned_part, cosine[block, :], sine_table[block, :]).astype(
            jnp.bfloat16
        )
        qkv[block, q_cols + kv_cols :] = linear[:, q_cols + kv_cols :].astype(jnp.bfloat16)

    def project_hop(hop):
        @pl.when(here.z >= hop)
        def left():
            project(here.behind(hop))

        @pl.when(here.z + hop < lines)
        def right():
            project(here.ahead(hop))

    token_load.wait()
    project(here.z)
    expert_spreads[0].turn()
    expert_spreads[1].chips()
    expert_spreads[0].cores()
    for hop in range(2, lines - 1):
        token_gathers[0].step(hop)
        token_gathers[1].step(hop)
    out_spread.start()
    for spread in expert_spreads[2:]:
        spread.start()
    for hop in range(1, lines - 1):
        project_hop(hop)
    expert_spreads[1].turn()
    for gather in token_gathers:
        gather.step(lines - 1)
    project_hop(lines - 1)

    prefix_end = prefix[0]
    heads = q_cols // HEAD_WIDTH
    group = q_cols // kv_cols

    def attend(number):
        start = number * tok_rows
        block = pl.ds(start, tok_rows)
        reach = max(rows_all // 2, start + tok_rows)
        query_place = start + lax.broadcasted_iota(jnp.int32, (tok_rows, reach), 0)
        key_place = lax.broadcasted_iota(jnp.int32, (tok_rows, reach), 1)
        allowed = (key_place <= query_place) | (key_place < prefix_end)
        lanes = lax.broadcasted_iota(jnp.int32, (tok_rows, LANES), 1)
        totals = jnp.zeros((tok_rows, LANES), jnp.float32)
        outputs = []
        for head in range(heads):
            key_at = q_cols + head // group * HEAD_WIDTH
            value_at = key_at + kv_cols
            scores = matmul(
                qkv[block, head * HEAD_WIDTH : (head + 1) * HEAD_WIDTH],
                qkv[:reach, key_at : key_at + HEAD_WIDTH],
                ROWS_BY_ROWS,
            )
            scores = jnp.where(allowed, scores * SCORE_SCALE, LOW_SCORE)
            largest = jnp.max(scores, -1, keepdims=True)
            powers = jnp.exp(scores - largest)
            total = jnp.sum(powers, -1, keepdims=True)
            product = matmul(
                powers.astype(jnp.bfloat16), qkv[:reach, value_at : value_at + HEAD_WIDTH], ROWS_BY_COLS
            )
            outputs.append(product / total)
            totals = jnp.where(lanes == head, largest + jnp.log(total), totals)
        joined = jnp.concatenate(outputs, 1)
        attended[block, :] = joined
        log_total[block, :] = totals
        attended_all[here.z, block, :] = joined.astype(jnp.bfloat16)

    def mix_in(number):
        block = pl.ds(number * tok_rows, tok_rows)
        branch = matmul(attended_all[0, block, :], out_full[:, :q_cols], ROWS_BY_ROWS)
        for line in range(1, lines):
            branch = branch + matmul(
                attended_all[line, block, :], out_full[:, line * q_cols : (line + 1) * q_cols], ROWS_BY_ROWS
            )
        total = tokens_all[number].astype(jnp.float32) + branch
        lowered = (total * inverse_rms(total) * gain_expert).astype(jnp.bfloat16)
        expert_in[number] = lowered
        logits = matmul(lowered, weights[:, qkv_cols:], ROWS_BY_COLS)
        lane = lax.broadcasted_iota(jnp.int32, logits.shape, 1)
        logits = jnp.where(lane < EXPERT_COUNT, logits, LOW_SCORE)
        powers = jnp.exp(logits - jnp.max(logits, -1, keepdims=True))
        powers = jnp.where(lane < EXPERT_COUNT, powers, 0.0)
        probs[number] = powers / jnp.sum(powers, -1, keepdims=True)

        @pl.when(here.z == number)
        def keep():
            middle[...] = total


    attended_gathers = [
        LineGather(
            here, lambda z, n=n: attended_all.at[z, pl.ds(n * tok_rows, tok_rows)], a_sends.at[n], a_recvs.at[n]
        )
        for n in range(lines)
    ]
    def gate_columns(number, e):
        chosen = padded_square(chosen_all[number].astype(jnp.float32))
        lane = lax.broadcasted_iota(jnp.int32, chosen.shape, 1)
        own = lane == here.z * own_experts + e
        picked = jnp.sum(jnp.where(own, chosen, 0.0), -1, keepdims=True)
        gate = jnp.sum(jnp.where(own, probs[number] * chosen, 0.0), -1, keepdims=True)
        return own, picked, gate

    pairs = [(a, a + 2) for a in range(0, lines, 2)]

    def gate_up_of(e):
        return terms[e, ..., : 2 * ff_width].reshape(width, 2 * ff_width)

    def down_of(e):
        return terms[e, ..., 2 * ff_width :].reshape(width, ff_width)

    def expert_forward(e, numbers):
        for low, high in numbers:
            block = pl.ds(low * tok_rows, (high - low) * tok_rows)
            inputs = jnp.concatenate([expert_in[n] for n in range(low, high)], 0)
            linear = matmul(inputs, gate_up_of(e), ROWS_BY_COLS)
            gate_part, up_part = linear[:, :ff_width], linear[:, ff_width:]
            sigmoid = 1.0 / (1.0 + jnp.exp(-gate_part))
            silu = gate_part * sigmoid
            act = silu * up_part
            slopes[e, block, :ff_width] = (
                up_part * (sigmoid * (1.0 + gate_part * (1.0 - sigmoid)))
            ).astype(jnp.bfloat16)
            slopes[e, block, ff_width:] = silu.astype(jnp.bfloat16)
            acts[e, block, :] = act.astype(jnp.bfloat16)
            gate = jnp.concatenate([gate_columns(n, e)[2] for n in range(low, high)], 0)
            mids[e, low:high, ..., 2 * ff_width :] = (
                (gate * act).astype(jnp.bfloat16).reshape(high - low, lines, depth, ff_width)
            )

    def line_sum(parts, landed, sends, recvs):
        return Halves(
            *[
                LineSum(here, parts, landed, pl.ds(n * half, half), sends.at[n], recvs.at[n])
                for n in range(2)
            ]
        )

    def mix_out(members):
        for low, high in pairs:
            total = None
            if 0 not in members:
                total = jnp.concatenate([part_mix[n] for n in range(low, high)], 0).astype(jnp.float32)
            for e in members:
                gated = mids[e, low:high, ..., 2 * ff_width :].reshape((high - low) * tok_rows, ff_width)
                term = matmul(gated, down_of(e), ROWS_BY_ROWS)
                total = term if total is None else total + term
            for n in range(low, high):
                part_mix[n] = total[(n - low) * tok_rows : (n - low + 1) * tok_rows, :].astype(jnp.bfloat16)

    def expert_back(low, members):
        block = pl.ds(pl.multiple_of(low * tok_rows, 2 * tok_rows), 2 * tok_rows)
        grad_mid = jnp.concatenate([cot_all[low], cot_all[low + 1]], 0)
        opening = 0 in members
        total = None
        if not opening:
            total = jnp.concatenate([part_grad[low], part_grad[low + 1]], 0).astype(jnp.float32)
        gate_cols = [jnp.zeros((tok_rows, LANES), jnp.float32)] * 2
        for e in members:
            act_grad = matmul(grad_mid, down_of(e), ROWS_BY_COLS)
            column = jnp.sum(act_grad * acts[e, block, :].astype(jnp.float32), -1, keepdims=True)
            gates = []
            for n in range(2):
                own, picked, gate = gate_columns(low + n, e)
                part = column[n * tok_rows : (n + 1) * tok_rows, :]
                gate_cols[n] = jnp.where(own, part * picked, gate_cols[n])
                gates.append(gate)
            act_grad = act_grad * jnp.concatenate(gates, 0)
            slope = slopes[e, block, :].astype(jnp.float32)
            mid = jnp.concatenate(
                [act_grad * slope[:, :ff_width], act_grad * slope[:, ff_width:]], 1
            ).astype(jnp.bfloat16)
            mids[e, pl.ds(low, 2), ..., : 2 * ff_width] = mid.reshape(2, lines, depth, 2 * ff_width)
            term = matmul(mid, gate_up_of(e), ROWS_BY_ROWS)
            total = term if total is None else total + term
        for n in range(2):
            part_grad[low + n] = total[n * tok_rows : (n + 1) * tok_rows, :].astype(jnp.bfloat16)
            gate_rows = gate_cols[n].T[:EXPERT_COUNT, :]
            gate_grad[low + n] = gate_rows if opening else gate_grad[low + n] + gate_rows

    folds = [
        Fold(here, terms.at[e], mids.at[e], e_landed.at[e], e_last.at[e], f_sends.at[e], f_recvs.at[e])
        for e in range(own_experts)
    ]

    def weight_terms(e):
        terms[e, ..., : 2 * ff_width] = (
            matmul(
                expert_in[...].reshape(rows_all, width),
                mids[e, ..., : 2 * ff_width].reshape(rows_all, 2 * ff_width),
                COLS_BY_COLS,
            )
            .astype(jnp.bfloat16)
            .reshape(*five, 2 * ff_width)
        )
        terms[e, ..., 2 * ff_width :] = (
            matmul(
                cot_all[...].reshape(rows_all, width),
                mids[e, ..., 2 * ff_width :].reshape(rows_all, ff_width),
                COLS_BY_COLS,
            )
            .astype(jnp.bfloat16)
            .reshape(*five, ff_width)
        )
        pl.semaphore_signal(free_sem.at[e], inc=1, device_id=here.sibling(), device_id_type=MESH)

    def fold_start(e):
        pl.semaphore_wait(free_sem.at[e], 1)
        folds[e].start()

    near = here.z // 2 * 2
    far = (near + 2) % lines
    def mix_arrived(number):
        attended_gathers[number].step(lines - 1)
        mix_in(number)

    out_spread.chips()
    for turn in range(lines):
        attend(turn)
        attended_gathers[turn].start()
    early, late = cot_gather.members
    expert_spreads[1].cores()
    expert_spreads[2].chips()
    out_spread.turn()
    expert_spreads[3].chips()
    for gather in attended_gathers:
        gather.step(1)
    expert_spreads[2].turn()
    out_spread.cores()
    for gather in attended_gathers:
        gather.step(2)
    cot_gather.start()
    out_spread.finish()
    chosen_swap.finish()
    mix_arrived(0)
    mix_arrived(1)
    for e in range(2):
        expert_spreads[e].finish()
        expert_forward(e, pairs[:1])
    mix_arrived(2)
    mix_arrived(3)
    expert_spreads[2].cores()
    expert_spreads[3].turn()
    early.step(1)
    late.step(1)
    for e in range(2):
        expert_forward(e, pairs[1:])
    expert_spreads[2].finish()
    expert_forward(2, pairs)
    for hop in range(2, lines - 1):
        early.step(hop)
    mix_out([0, 1, 2])
    expert_spreads[3].cores()
    for hop in range(2, lines - 1):
        late.step(hop)
    cot_load.wait()
    near = here.z // 2 * 2
    far = (near + 2) % lines
    expert_spreads[3].finish()
    expert_forward(3, pairs)
    mix_out([3])
    mix_swap = line_sum(part_mix, got_mix, m_sends, m_recvs)
    mix_swap.launch(lines - 1)
    for hops in range(lines - 2, 1, -1):
        mix_swap.launch(hops)
    expert_back(near, [0, 1, 2, 3])
    cot_gather.step(lines - 1)
    expert_back(far, [0])
    for spread in expert_spreads[:1]:
        spread.close()
    weight_terms(0)
    fold_start(0)
    expert_back(far, [1, 2, 3])
    for group_of in [rows_spread, out_spread, chosen_swap, cot_gather] + token_gathers + expert_spreads[1:] + attended_gathers:
        group_of.close()
    grad_swap = line_sum(part_grad, got_grad, x_sends, x_recvs)
    gate_swap = LineSwap(here, lambda z: gate_grad.at[z], lambda k, z: got_gate.at[k - 1], g_sends, g_recvs)
    attended_swap = LineSwap(
        here, lambda z: attended_grad.at[z], lambda k, z: attended_grad_all.at[z], b_sends, b_recvs
    )
    part_swap = line_sum(part_grad, got_grad, p_sends, p_recvs)
    out_fold = Fold(here, o_terms, o_crossed, o_landed, o_last, of_sends, of_recvs)
    qkv_fold = Fold(here, q_terms, q_crossed, q_landed, q_last, q_sends, q_recvs)
    expert_swaps = [
        LineSwap(here, folds[e].sums, lambda k, z, e=e: expert_rows.at[z, e], el_sends.at[e], el_recvs.at[e])
        for e in range(own_experts)
    ]
    out_swap = LineSwap(here, out_fold.sums, lambda k, z: o_lines.at[k - 1], ol_sends, ol_recvs)
    qkv_swap = LineSwap(here, qkv_fold.sums, lambda k, z: q_lines.at[z], ql_sends, ql_recvs)

    for hops in range(lines - 1, 0, -1):
        grad_swap.launch(hops)
    gate_swap.start()
    folds[0].chips()
    weight_terms(1)
    fold_start(1)
    for hops in range(lines - 2, 1, -1):
        mix_swap.step(hops)
    for hops in range(lines - 2, 1, -1):
        grad_swap.step(hops)
    folds[1].chips()
    weight_terms(2)
    fold_start(2)
    grad_swap.step(1)
    folds[0].turn()
    weight_terms(3)
    fold_start(3)
    folds[2].chips()

    gate_swap.finish()
    grad_swap.finish(grad_res)
    gate_rows = gate_grad[here.z]
    for k in range(lines - 1):
        gate_rows = gate_rows + got_gate[k]
    gates = padded_square(gate_rows)
    grad = grad_res[...]
    prob = probs[here.z]
    logit_grad = (prob * (gates - jnp.sum(prob * gates, -1, keepdims=True))).astype(jnp.bfloat16)
    grad = grad + matmul(logit_grad, weights[:, qkv_cols:], ROWS_BY_ROWS)
    hidden = middle[...]
    inverse = inverse_rms(hidden)
    normed = hidden * inverse
    scaled = grad * gain_expert
    result = cot_all[here.z].astype(jnp.float32) + inverse * (
        scaled - normed * jnp.mean(scaled * normed, -1, keepdims=True)
    )
    grad_res[...] = result
    branch = result.astype(jnp.bfloat16)
    for line in range(lines):
        attended_grad[line] = matmul(
            branch, out_full[:, line * q_cols : (line + 1) * q_cols], ROWS_BY_COLS
        ).astype(jnp.bfloat16)
    attended_swap.start()
    attended_grad_all[here.z] = attended_grad[here.z]
    own_block = pl.ds(pl.multiple_of(here.z * tok_rows, tok_rows), tok_rows)
    router_term = matmul(expert_in[here.z], logit_grad, COLS_BY_COLS)
    gain_term = split_sum_columns(grad * normed)
    lane = lax.broadcasted_iota(jnp.int32, router_term.shape, 1)
    for line in range(lines):
        o_terms[..., line * q_cols : (line + 1) * q_cols] = (
            matmul(branch, attended_all[line, own_block, :], COLS_BY_COLS).astype(jnp.bfloat16).reshape(*five, q_cols)
        )
    o_terms[..., query_width:] = (
        jnp.where(lane == EXPERT_COUNT, gain_term, router_term).astype(jnp.bfloat16).reshape(*five, LANES)
    )
    out_fold.start()
    mix_swap.launch(1)
    folds[1].turn()
    folds[3].chips()
    folds[0].finish()
    expert_swaps[0].start()
    attended_swap.finish()
    grad_swap.close()

    key_sum[...] = jnp.zeros_like(key_sum)
    value_sum[...] = jnp.zeros_like(value_sum)

    def attend_back(number):
        start = number * tok_rows
        block = pl.ds(start, tok_rows)
        reach = max(rows_all // 2, start + tok_rows)
        query_place = start + lax.broadcasted_iota(jnp.int32, (tok_rows, reach), 0)
        key_place = lax.broadcasted_iota(jnp.int32, (tok_rows, reach), 1)
        allowed = (key_place <= query_place) | (key_place < prefix_end)
        query_grads = []
        for head in range(heads):
            own = slice(head * HEAD_WIDTH, (head + 1) * HEAD_WIDTH)
            low = head // group * HEAD_WIDTH
            shared = slice(low, low + HEAD_WIDTH)
            query = qkv[block, own]
            key = qkv[:reach, q_cols + low : q_cols + low + HEAD_WIDTH]
            value = qkv[:reach, q_cols + kv_cols + low : q_cols + kv_cols + low + HEAD_WIDTH]
            grad = attended_grad_all[number, :, own]
            scores = matmul(query, key, ROWS_BY_ROWS) * SCORE_SCALE
            prob = jnp.where(allowed, jnp.exp(scores - log_total[block, head : head + 1]), 0.0)
            delta = jnp.sum(grad.astype(jnp.float32) * attended[block, own], -1, keepdims=True)
            prob_part = matmul(grad, value, ROWS_BY_ROWS)
            score_grad = (prob * (prob_part - delta)).astype(jnp.bfloat16)
            value_sum[:reach, shared] = value_sum[:reach, shared] + matmul(
                prob.astype(jnp.bfloat16), grad, COLS_BY_COLS
            )
            key_sum[:reach, shared] = key_sum[:reach, shared] + matmul(score_grad, query, COLS_BY_COLS)
            query_grads.append(matmul(score_grad, key, ROWS_BY_COLS))
        query_grad = jnp.concatenate(query_grads, 1) * SCORE_SCALE
        joined_grad[block, :q_cols] = spin(query_grad, cosine[block, :], -sine_table[block, :]).astype(
            jnp.bfloat16
        )

    for number in range(lines):
        attend_back(number)
        if number == 1:
            folds[2].turn()
            mix_swap.step(1)
    folds[1].finish()
    expert_swaps[1].start()
    out_fold.chips()
    joined_grad[:, q_cols : q_cols + kv_cols] = spin(
        key_sum[...] * SCORE_SCALE, cosine[...], -sine_table[...]
    ).astype(jnp.bfloat16)
    joined_grad[:, q_cols + kv_cols :] = value_sum[...].astype(jnp.bfloat16)
    gain_term = jnp.zeros((width, LANES), jnp.float32)
    for number in range(lines):
        block = pl.ds(number * tok_rows, tok_rows)
        hidden = tokens_all[number].astype(jnp.float32)
        normed = hidden * inverse_rms(hidden)
        part = matmul(joined_grad[block, :], weights[:, :qkv_cols], ROWS_BY_ROWS)
        part_grad[number] = part.astype(jnp.bfloat16)
        gain_term = gain_term + split_sum_columns(part * normed)
    for hops in range(lines - 1, 0, -1):
        part_swap.launch(hops)
    q_terms[..., :qkv_cols] = (
        matmul(att_in[...], joined_grad[...], COLS_BY_COLS).astype(jnp.bfloat16).reshape(*five, qkv_cols)
    )
    q_terms[..., qkv_cols:] = gain_term.astype(jnp.bfloat16).reshape(*five, LANES)
    qkv_fold.start()
    for hops in range(lines - 2, 1, -1):
        part_swap.step(hops)
    folds[3].turn()
    qkv_fold.chips()
    folds[2].finish()
    expert_swaps[2].start()
    part_swap.step(1)
    out_fold.turn()
    folds[3].finish()
    expert_swaps[3].start()
    mix_swap.finish(mix_total)
    mixed[...] = (mix_total[...] + middle[...]).astype(jnp.bfloat16)
    store(mixed, mixed_o)
    out_fold.finish()
    out_swap.start()
    qkv_fold.turn()
    qkv_fold.finish()
    qkv_swap.start()

    part_swap.finish(mix_total)
    hidden = tokens_all[here.z].astype(jnp.float32)
    inverse = inverse_rms(hidden)
    normed = hidden * inverse
    scaled = mix_total[...] * gain_attention
    mix_total[...] = grad_res[...] + inverse * (
        scaled - normed * jnp.mean(scaled * normed, -1, keepdims=True)
    )
    store(mix_total, tokens_grad_o)
    out_swap.finish()
    total = o_terms[here.chip, here.core, here.z].astype(jnp.float32)
    for k in range(lines - 1):
        total = total + o_lines[k].astype(jnp.float32)
    out_s[...] = total[:, :query_width]
    tail = padded_square(total[:, query_width:])
    router_s[...] = tail[:EXPERT_COUNT, :depth]
    expert_gain_s[...] = tail[EXPERT_COUNT : EXPERT_COUNT + 1, :depth]
    store(out_s, out_o)
    store(router_s, router_o)
    store(expert_gain_s, expert_gain_o)
    q_lines[here.z] = q_terms[here.chip, here.core, here.z]
    qkv_swap.finish()
    gain_columns = jnp.zeros((depth, LANES), jnp.float32)
    for line in range(lines):
        query_s[:, line * q_cols : (line + 1) * q_cols] = q_lines[line, :, :q_cols].astype(jnp.float32)
        key_s[:, line * kv_cols : (line + 1) * kv_cols] = q_lines[line, :, q_cols : q_cols + kv_cols].astype(
            jnp.float32
        )
        value_s[:, line * kv_cols : (line + 1) * kv_cols] = q_lines[line, :, q_cols + kv_cols : qkv_cols].astype(
            jnp.float32
        )
        gain_columns = gain_columns + q_lines[line, :, qkv_cols:].astype(jnp.float32)
    attention_gain_s[...] = padded_square(gain_columns)[:1, :depth]
    store(query_s, query_o)
    store(key_s, key_o)
    store(value_s, value_o)
    store(attention_gain_s, attention_gain_o)
    for e in range(own_experts):
        expert_rows[here.z, e] = terms[e, here.chip, here.core, here.z]
        expert_swaps[e].finish()
    store(expert_rows, expert_o)
    for group_of in (
        [gate_swap, attended_swap, part_swap, mix_swap, out_swap, qkv_swap, out_fold, qkv_fold] + folds + expert_swaps
    ):
        group_of.close()
    for copy in stores:
        copy.wait()


def deliver_kernel(*refs):
    count = (len(refs) - 4) // 3
    sources, targets, held = refs[:count], refs[count : 2 * count + 1], refs[2 * count + 1 : 3 * count + 1]
    gate_up, down, sems = refs[3 * count + 1 :]
    loads = [move(sources[n], held[n], sems.at[0, n]) for n in reversed(range(count))][::-1]
    stores = []
    depth, expert_count = gate_up.shape[:2]
    order = row_order(depth, expert_count, False)
    loads[count - 1].wait()
    rows = held[count - 1][...].reshape(expert_count * depth, gate_up.shape[2] + down.shape[2])
    gate_up[...] = matmul(order, rows[:, : gate_up.shape[2]], ROWS_BY_COLS).reshape(gate_up.shape)
    stores.append(move(gate_up, targets[count - 1], sems.at[1, count - 1]))
    down[...] = matmul(order, rows[:, gate_up.shape[2] :], ROWS_BY_COLS).reshape(down.shape)
    stores.append(move(down, targets[count], sems.at[1, count]))
    for n in range(count - 1):
        loads[n].wait()
        stores.append(move(held[n], targets[n], sems.at[1, n]))
    for copy in stores:
        copy.wait()


def fast_device(
    tokens, prefix_len, routes, cotangent, query_matrix, key_matrix, value_matrix, output_matrix,
    attention_gain, expert_gain, router_matrix, gate_up_weight, down_weight,
):
    lines = lax.axis_size("seq")
    chips = lax.axis_size("dp") // 2
    tok_rows, width = tokens.shape[1:]
    rows_all = lines * tok_rows
    depth = query_matrix.shape[0]
    query_width, key_width = query_matrix.shape[1], key_matrix.shape[1]
    q_cols, kv_cols = query_width // lines, key_width // lines
    qkv_cols = q_cols + 2 * kv_cols
    expert_count = router_matrix.shape[1]
    own_experts = expert_count // lines
    ff_width = down_weight.shape[2]
    all_ff = 3 * ff_width
    row_cols = qkv_cols + LANES
    out_cols = query_width + LANES
    half_dim = HEAD_WIDTH // 2
    low, full = jnp.bfloat16, jnp.float32

    places = np.arange(rows_all, dtype=np.float32)
    frequency = np.exp(
        np.arange(half_dim, dtype=np.float32) * np.float32(-2.0 * math.log(10000.0) / HEAD_WIDTH)
    ).astype(np.float32)
    angles = places[:, None] * frequency[None, :]
    cosine = jnp.asarray(np.tile(np.cos(angles), (1, LANES // half_dim)), jnp.float32)
    sine_table = jnp.asarray(np.tile(np.sin(angles), (1, LANES // half_dim)), jnp.float32)

    count = spread_count(lines)

    def scratch(*dims, kind=low):
        return pltpu.VMEM(dims, kind)

    def pair(*dims):
        return [pltpu.SemaphoreType.DMA(dims)] * 2

    DMA = pltpu.SemaphoreType.DMA
    by_token = (lines, tok_rows)
    five = (chips, 2, lines, depth)
    four = (chips, lines, depth)
    landed = (2, 2, lines // 2, depth)
    last = (2, lines // 2, depth)
    ends = [
        ((tok_rows, width), low), ((tok_rows, width), full), ((depth, query_width), full), ((depth, key_width), full),
        ((depth, key_width), full), ((depth, query_width), full), ((1, depth), full), ((1, depth), full), ((expert_count, depth), full),
        ((lines, own_experts, depth, all_ff), low),
    ]

    def fold_scratch(cols):
        return [scratch(*dims, cols) for dims in (five, four, landed, last)]

    results = pl.pallas_call(
        layer_kernel,
        name="layer",
        out_shape=tuple(jax.ShapeDtypeStruct(dims, kind) for dims, kind in ends),
        in_specs=[SMEM_SPEC, ANY_SPEC] + [VMEM_SPEC] * 3 + [ANY_SPEC] + [VMEM_SPEC] * 3 + [ANY_SPEC] * 3 + [VMEM_SPEC] * 3,
        out_specs=(ANY_SPEC,) * len(ends),
        scratch_shapes=[
            scratch(LANES, LANES, kind=full), scratch(lines, depth, row_cols), scratch(lines, own_experts, depth, all_ff),
            scratch(*by_token, width), scratch(width, row_cols), scratch(width, query_width), scratch(own_experts, *five, all_ff),
            scratch(*by_token, width), scratch(lines, expert_count, tok_rows), scratch(rows_all, width), scratch(rows_all, qkv_cols),
            scratch(rows_all, q_cols, kind=full), scratch(lines, rows_all, q_cols), scratch(rows_all, LANES, kind=full),
            scratch(*by_token, width), scratch(*by_token, LANES, kind=full), scratch(tok_rows, width, kind=full),
            scratch(own_experts, rows_all, 2 * ff_width), scratch(own_experts, rows_all, ff_width), scratch(own_experts, *four, all_ff),
            scratch(*by_token, width), scratch(2, lines - 1, tok_rows, width), scratch(tok_rows, width, kind=full), scratch(tok_rows, width),
            scratch(*by_token, width), scratch(2, lines - 1, tok_rows, width),
            scratch(lines, expert_count, tok_rows, kind=full), scratch(lines - 1, expert_count, tok_rows, kind=full),
            scratch(tok_rows, width, kind=full), scratch(*by_token, q_cols), scratch(*by_token, q_cols), scratch(rows_all, qkv_cols),
            scratch(rows_all, kv_cols, kind=full), scratch(rows_all, kv_cols, kind=full),
            scratch(own_experts, *landed, all_ff), scratch(own_experts, *last, all_ff),
            *fold_scratch(out_cols), scratch(lines - 1, depth, out_cols),
            *fold_scratch(row_cols), scratch(lines, depth, row_cols),
            *[scratch(*dims, kind=kind) for dims, kind in ends[2:-1]],
            DMA((6 + own_experts,)),
            *pair(count), *pair(count), *pair(own_experts, count), *pair(2, 2, lines - 1), *pair(2, 2, lines - 1), *pair(lines),
            *pair(lines, 2, lines - 1), *pair(2, 2, lines - 1), *pair(2, 2, lines - 1), *pair(lines), *pair(lines), *pair(2, 2, lines - 1),
            *pair(own_experts, 7), *pair(7), *pair(7), *pair(own_experts, lines), *pair(lines), *pair(lines),
            pltpu.SemaphoreType.REGULAR((own_experts,)), DMA((len(ends),)),
        ],
        compiler_params=comm_params(1, 63),
    )(
        prefix_len, tokens[0], query_matrix, key_matrix, value_matrix, output_matrix, router_matrix.T,
        attention_gain.reshape(1, depth), expert_gain.reshape(1, depth), gate_up_weight.reshape(*four, 2 * ff_width),
        down_weight.reshape(*four, ff_width), cotangent[0], routes[0].T, cosine, sine_table,
    )
    last_ends = [((depth, expert_count, 2 * ff_width), full), ((depth, expert_count, ff_width), full)]
    results = pl.pallas_call(
        deliver_kernel,
        name="deliver",
        out_shape=tuple(jax.ShapeDtypeStruct(dims, kind) for dims, kind in ends[:-1] + last_ends),
        in_specs=[ANY_SPEC] * len(ends),
        out_specs=(ANY_SPEC,) * (len(ends) + 1),
        scratch_shapes=[pltpu.VMEM(dims, kind) for dims, kind in ends + last_ends] + [DMA((2, len(ends) + 1))],
        compiler_params=pltpu.CompilerParams(vmem_limit_bytes=63 << 20),
    )(*results)
    mixed, tokens_grad, query_grad, key_grad, value_grad, out_grad, attention_gain_grad, expert_gain_grad, router_grad, gate_up_grad, down_grad = results
    return (
        mixed[None],
        tokens_grad[None],
        query_grad,
        key_grad,
        value_grad,
        out_grad,
        attention_gain_grad.reshape(depth),
        expert_gain_grad.reshape(depth),
        router_grad.T,
        gate_up_grad,
        down_grad,
    )


def solution(mesh):
    lines, chips = mesh.shape["seq"], mesh.shape["dp"] // 2
    even = KEY_HEADS % (2 * lines) == 0 and EXPERT_COUNT % lines == 0 and chips == lines == 4
    return jax.shard_map(
        fast_device if even else per_device,
        mesh=mesh,
        in_specs=(
            P("dp", "seq", None),
            P("dp"),
            P("dp", "seq", None),
            P("dp", "seq", None),
            P(("dp", "seq"), None),
            P(("dp", "seq"), None),
            P(("dp", "seq"), None),
            P(("dp", "seq"), None),
            P(("dp", "seq")),
            P(("dp", "seq")),
            P(("dp", "seq"), None),
            P(("dp", "seq"), None, None),
            P(("dp", "seq"), None, None),
        ),
        out_specs=(
            P("dp", "seq", None),
            P("dp", "seq", None),
            P(("dp", "seq"), None),
            P(("dp", "seq"), None),
            P(("dp", "seq"), None),
            P(("dp", "seq"), None),
            P(("dp", "seq")),
            P(("dp", "seq")),
            P(("dp", "seq"), None),
            P(("dp", "seq"), None, None),
            P(("dp", "seq"), None, None),
        ),
        check_vma=False,
    )
```
